128 devices in a mesh: dp: 4 (over z), row: 8 (over x, core), col: 4 (over y).
Axes of the slice: x: 4, y: 4, z: 4, core: 2. Of those that a mesh axis runs over, the one named last changes fastest.
Arguments:
- hidden: bfloat16 [16384, 1280], P(('dp', 'row'), 'col'), may hold values from -0.15625 to 0.15625
- teacher: bfloat16 [16384, 1280], P(('dp', 'row'), 'col'), may hold values from -0.15625 to 0.15625
- valid_mask: int32 [16384], P(('dp', 'row')), may hold values from 0 to 1
- segments: int32 [4, 4096], P('dp'), may hold values from 0 to 2, never falling along the last dimension, each value on 1 to 2048 neighbouring positions
- query_weight: bfloat16 [1280, 1280], P(('dp', 'row'), 'col'), may hold values from -0.15625 to 0.15625
- key_weight: bfloat16 [1280, 1280], P(('dp', 'row'), 'col'), may hold values from -0.15625 to 0.15625
- value_weight: bfloat16 [1280, 1280], P(('dp', 'row'), 'col'), may hold values from -0.15625 to 0.15625
- out_weight: bfloat16 [1280, 1280], P('col', ('dp', 'row')), may hold values from -1.5 to 1.5
- gate_weight: bfloat16 [1280, 5120], P(('dp', 'row'), 'col'), may hold values from -0.15625 to 0.15625
- up_weight: bfloat16 [1280, 5120], P(('dp', 'row'), 'col'), may hold values from -0.15625 to 0.15625
- down_weight: bfloat16 [5120, 1280], P('col', ('dp', 'row')), may hold values from -0.078125 to 0.078125
- attention_rate: float32 [1280], P('col'), may hold values from 0.1 to 0.6
- feedforward_rate: float32 [1280], P('col'), may hold values from 0.1 to 0.6
- score_gain: float32 [1280], P('col'), may hold values from 1 to 1.8
- up_gain: float32 [5120], P('col'), may hold values from 0.5 to 2
- gate_gain: float32 [5120], P('col'), may hold values from 0.5 to 2
Outputs:
- loss: float32 [], replicated
- output: bfloat16 [16384, 1280], P(('dp', 'row'), 'col')
- hidden_grad: float32 [16384, 1280], P(('dp', 'row'), 'col')
- query_weight_grad: float32 [1280, 1280], P(('dp', 'row'), 'col')
- key_weight_grad: float32 [1280, 1280], P(('dp', 'row'), 'col')
- value_weight_grad: float32 [1280, 1280], P(('dp', 'row'), 'col')
- out_weight_grad: float32 [1280, 1280], P('col', ('dp', 'row'))
- gate_weight_grad: float32 [1280, 5120], P(('dp', 'row'), 'col')
- up_weight_grad: float32 [1280, 5120], P(('dp', 'row'), 'col')
- down_weight_grad: float32 [5120, 1280], P('col', ('dp', 'row'))
- attention_rate_grad: float32 [1280], P('col')
- feedforward_rate_grad: float32 [1280], P('col')
- score_gain_grad: float32 [1280], P('col')
- up_gain_grad: float32 [5120], P('col')
- gate_gain_grad: float32 [5120], P('col')
The draws below stay inside these ranges and needn't reach their ends.
Inputs may be any that keep to these rules, and one draw needn't show every extreme that they name: `segments`: in each group, document numbers never fall along the tokens; each document has 1 to 2048 tokens, and one has exactly 2048.
All inputs are finite; a program needn't handle non-finite values.
Results may differ from the reference program's by a relative error of at most 0.025.
Values may be sent and summed in bfloat16 or wider, within the bound.
A program may use at most 128 MiB of HBM per device.

```python
import math
import jax
import jax.numpy as jnp
import numpy as np
from jax import lax

D = 1280
HEAD_DIM = 64
FF = 5120
GROUP_TOK = 4096
SEG_MOST = 2048
SEG_COUNT = 3
GROUPS = 4
TOKENS = 16384


def draw_valid_mask(key, part):
    positions = jnp.arange(TOKENS, dtype=jnp.int32)
    limits = 300 + 700 * positions // max(TOKENS - 1, 1)
    rolls = jax.random.randint(key, (TOKENS,), 0, 1000, dtype=jnp.int32)
    return (rolls < limits).astype(jnp.int32)


def shard_levels(rng, extent, shards, least, top_value):
    factor_of = 1.0
    for axis_at, blocks in shards:
        steps = jax.random.uniform(jax.random.fold_in(jax.random.fold_in(rng, 6), axis_at), (blocks,), jnp.float32, least / len(shards), top_value / len(shards))
        factor_of = factor_of * jnp.repeat(jnp.exp(steps), extent[axis_at] // blocks).reshape((-1,) + (1,) * (len(extent) - 1 - axis_at))
    return factor_of


def length_profile(count, total, most, slope):
    portions = [(1 << 20) // math.isqrt(standing ** slope) + 1 for standing in range(2, count + 1)]
    surplus, holding = total - most - (count - 1), [1] * (count - 1)
    while surplus > 0:
        candidates = [i for i in range(count - 1) if holding[i] < most]
        mass, budget = sum([portions[i] for i in candidates]), surplus
        for i in candidates:
            more = min(most - holding[i], max(1, budget * portions[i] // mass), surplus)
            holding[i] = holding[i] + more
            surplus = surplus - more
    return np.array([most] + holding)


def uneven(stream_key, amount, total, bound, skew):
    if amount == 2:
        one = jax.random.randint(stream_key, (), max(1, total - bound), min(bound, total - 1) + 1)
        return jnp.stack([one, total - one])
    lengths = jnp.asarray(length_profile(amount, total, bound, skew), jnp.int32)
    couples = (amount - 1) // 2
    giver, receiver = lengths[1:1 + 2 * couples:2], lengths[2:2 + 2 * couples:2]
    slack = jnp.minimum(giver - 1, bound - receiver)
    moved = jax.random.randint(jax.random.fold_in(stream_key, 1), (couples,), 0, 1 << 20) % (slack + 1)
    lengths = lengths.at[1:1 + 2 * couples:2].set(giver - moved).at[2:2 + 2 * couples:2].set(receiver + moved)
    return lengths[jax.random.permutation(jax.random.fold_in(stream_key, 2), amount)]


def gaussian(own_key, extent, spread, limit, cuts=(), kind=jnp.bfloat16):
    entries = spread * jax.random.normal(own_key, extent, jnp.float32)
    if cuts:
        entries = entries * shard_levels(own_key, extent, cuts, -0.22, 0.18)
    return jnp.clip(entries, -limit, limit).astype(kind)


def setup_inputs(seed: int = 0) -> dict:
    streams_of = jax.random.split(jax.random.key(seed), 17)
    hidden = gaussian(streams_of[0], (TOKENS, D), 0.028, 0.15625, ((0, 32), (1, 4)))
    teacher = gaussian(streams_of[1], (TOKENS, D), 0.028, 0.15625, ((0, 32), (1, 4)))
    valid_mask = draw_valid_mask(jax.random.fold_in(streams_of[16], 71), 0)
    segments = jax.vmap(lambda own: jnp.searchsorted(jnp.cumsum(uneven(own, SEG_COUNT, GROUP_TOK, SEG_MOST, 1)), jnp.arange(GROUP_TOK), side="right"))(jax.random.split(streams_of[3], GROUPS)).reshape((GROUPS, GROUP_TOK)).astype(jnp.int32)
    query_weight = gaussian(streams_of[4], (D, D), D ** -0.5, 0.15625, ((0, 32), (1, 4)))
    key_weight = gaussian(streams_of[5], (D, D), D ** -0.5, 0.15625, ((0, 32), (1, 4)))
    value_weight = gaussian(streams_of[6], (D, D), D ** -0.5, 0.15625, ((0, 32), (1, 4)))
    out_weight = gaussian(streams_of[7], (D, D), 16 ** -0.5, 1.5, ((0, 4), (1, 32)))
    gate_weight = gaussian(streams_of[8], (D, FF), D ** -0.5, 0.15625, ((0, 32), (1, 4)))
    up_weight = gaussian(streams_of[9], (D, FF), D ** -0.5, 0.15625, ((0, 32), (1, 4)))
    down_weight = gaussian(streams_of[10], (FF, D), FF ** -0.5, 0.078125, ((0, 4), (1, 32)))
    attention_rate = jnp.clip(jnp.exp(math.log(0.6) - 1.7917595 * jax.random.uniform(streams_of[11], (D,), jnp.float32) ** shard_levels(streams_of[11], (D,), ((0, 4),), -0.2, 0.2)), 0.1, 0.6)
    feedforward_rate = jnp.clip(jnp.exp(math.log(0.6) - 1.7917595 * jax.random.uniform(streams_of[12], (D,), jnp.float32) ** shard_levels(streams_of[12], (D,), ((0, 4),), -0.2, 0.2)), 0.1, 0.6)
    score_gain = jnp.clip(jnp.exp(math.log(1.8) - 0.5877866 * jax.random.uniform(streams_of[13], (D,), jnp.float32) ** shard_levels(streams_of[13], (D,), ((0, 4),), -0.2, 0.2)), 1.0, 1.8)
    up_gain = jnp.clip(jnp.exp(math.log(2.0) - 1.3862944 * jax.random.uniform(streams_of[14], (FF,), jnp.float32) ** shard_levels(streams_of[14], (FF,), ((0, 4),), -0.2, 0.2)), 0.5, 2.0)
    gate_gain = jnp.clip(jnp.exp(math.log(2.0) - 1.3862944 * jax.random.uniform(streams_of[15], (FF,), jnp.float32) ** shard_levels(streams_of[15], (FF,), ((0, 4),), -0.2, 0.2)), 0.5, 2.0)
    return {"hidden": hidden, "teacher": teacher, "valid_mask": valid_mask, "segments": segments, "query_weight": query_weight, "key_weight": key_weight, "value_weight": value_weight, "out_weight": out_weight, "gate_weight": gate_weight, "up_weight": up_weight, "down_weight": down_weight, "attention_rate": attention_rate, "feedforward_rate": feedforward_rate, "score_gain": score_gain, "up_gain": up_gain, "gate_gain": gate_gain}


EPS = 1e-06

@jax.custom_vjp
def low(v):
    return lax.optimization_barrier(v.astype(jnp.bfloat16)).astype(jnp.float32)

@jax.custom_vjp
def low_back(v):
    return v

def low_keep(v):
    return (low(v), None)

def low_pass(kept, grad):
    return (grad,)

def back_keep(v):
    return (v, None)

def back_low(kept, grad):
    return (low(grad),)
low.defvjp(low_keep, low_pass)
low_back.defvjp(back_keep, back_low)

def matmul(left_arr, right_arr):
    return jnp.dot(left_arr, right_arr, precision=lax.Precision.HIGHEST, preferred_element_type=jnp.float32)

def rope_tables(positions, head_dim):
    half_dim = head_dim // 2
    indices = jnp.arange(half_dim, dtype=jnp.float32)
    inverse = jnp.exp(indices * (-2.0 * math.log(10000.0) / head_dim))
    angles = positions[:, None] * inverse[None, :]
    return (jnp.cos(angles), jnp.sin(angles))

def rotate(head_vals, cosine, sine_table):
    half_dim = head_vals.shape[-1] // 2
    first_half = head_vals[..., :half_dim]
    second_half = head_vals[..., half_dim:]
    cos_wide = cosine[:, None, :]
    sin_wide = sine_table[:, None, :]
    return jnp.concatenate([first_half * cos_wide - second_half * sin_wide, second_half * cos_wide + first_half * sin_wide], axis=-1)

def head_map(raw_proj, gains, cosine, sine_table, head_dim):
    row_count = raw_proj.shape[0]
    head_vals = rotate(raw_proj.reshape(row_count, -1, head_dim), cosine, sine_table)
    normed = head_vals * lax.rsqrt(lax.optimization_barrier(jnp.sum(head_vals * head_vals, axis=-1, keepdims=True)) + EPS)
    return normed.reshape(row_count, -1) * gains

def mix_state(states, branch, alphas):
    normed = branch * lax.rsqrt(lax.optimization_barrier(jnp.sum(branch * branch, axis=-1, keepdims=True)) + EPS)
    mixed_vals = states + alphas * (normed - states)
    return mixed_vals * lax.rsqrt(lax.optimization_barrier(jnp.sum(mixed_vals * mixed_vals, axis=-1, keepdims=True)) + EPS)

def swiglu(gate_proj, up_proj, gate_scale, up_scale, width_root):
    return up_scale * up_proj * jax.nn.silu(gate_scale * gate_proj * width_root)

def attention(queries, key_rows, value_rows, seg_ids, head_dim):
    total_rows = queries.shape[0]
    head_count = queries.shape[1] // head_dim
    block_rows = min(512, total_rows)
    score_scale = math.sqrt(head_dim)
    queries3 = queries.reshape(total_rows, head_count, head_dim)
    keys3 = key_rows.reshape(total_rows, head_count, head_dim)
    values3 = value_rows.reshape(total_rows, head_count, head_dim)
    key_pos = jnp.arange(total_rows, dtype=jnp.int32)

    @jax.checkpoint
    def one_block(offset):
        query_block = lax.dynamic_slice_in_dim(queries3, offset, block_rows, 0)
        query_pos = offset + jnp.arange(block_rows, dtype=jnp.int32)
        query_seg = lax.dynamic_slice_in_dim(seg_ids, offset, block_rows, 0)
        scores = low_back(score_scale * jnp.einsum('qhd,khd->hqk', query_block, keys3, precision=lax.Precision.HIGHEST))
        allowed = (query_seg[:, None] == seg_ids[None, :]) & (key_pos[None, :] <= query_pos[:, None])
        scores = jnp.where(allowed[None, :, :], scores, -jnp.inf)
        probs = jnp.exp(scores - jax.nn.logsumexp(scores, axis=-1, keepdims=True))
        return jnp.einsum('hqk,khd->qhd', low(probs), values3, precision=lax.Precision.HIGHEST)
    offsets = jnp.arange(total_rows // block_rows, dtype=jnp.int32) * block_rows
    blocks_out = lax.map(one_block, offsets)
    return blocks_out.reshape(total_rows, head_count * head_dim)

def block_group(hidden_in, weight_set, teacher_g, mask_g, seg_g):
    query_weight, key_weight, value_weight, out_weight, gate_weight, up_weight, down_weight, attention_rate, feedforward_rate, score_gain, up_gain, gate_gain = weight_set
    group_rows = hidden_in.shape[0]
    cosine, sine_table = rope_tables(jnp.arange(group_rows, dtype=jnp.float32), HEAD_DIM)
    query_raw = low_back(matmul(hidden_in, query_weight))
    key_raw = low_back(matmul(hidden_in, key_weight))
    value_raw = low_back(matmul(hidden_in, value_weight))
    queries = low(head_map(query_raw, score_gain, cosine, sine_table, HEAD_DIM))
    key_rows = low(head_map(key_raw, score_gain, cosine, sine_table, HEAD_DIM))
    value_rows = low(value_raw)
    attended = low(low_back(attention(queries, key_rows, value_rows, seg_g, HEAD_DIM)))
    attn_branch = low_back(matmul(attended, out_weight))
    state_one = mix_state(hidden_in, attn_branch, attention_rate)
    inputs_one = low(state_one)
    gate_raw = low_back(matmul(inputs_one, gate_weight))
    up_raw = low_back(matmul(inputs_one, up_weight))
    product = low(swiglu(gate_raw, up_raw, gate_gain, up_gain, math.sqrt(D)))
    mlp_branch = low_back(matmul(product, down_weight))
    state_two = mix_state(state_one, mlp_branch, feedforward_rate)
    errors = state_two - teacher_g
    return (jnp.sum(mask_g[:, None] * errors * errors), state_two)

def reference(hidden, teacher, valid_mask, segments, query_weight, key_weight, value_weight, out_weight, gate_weight, up_weight, down_weight, attention_rate, feedforward_rate, score_gain, up_gain, gate_gain):
    params = (query_weight.astype(jnp.float32), key_weight.astype(jnp.float32), value_weight.astype(jnp.float32), out_weight.astype(jnp.float32), gate_weight.astype(jnp.float32), up_weight.astype(jnp.float32), down_weight.astype(jnp.float32), attention_rate.astype(jnp.float32), feedforward_rate.astype(jnp.float32), score_gain.astype(jnp.float32), up_gain.astype(jnp.float32), gate_gain.astype(jnp.float32))
    token_mask = valid_mask.astype(jnp.float32)
    valid_count = jnp.sum(token_mask)
    loss_scale = TOKENS * math.sqrt(D) / 2.0
    hidden_groups = hidden.astype(jnp.float32).reshape(GROUPS, GROUP_TOK, D)
    teacher_groups = teacher.astype(jnp.float32).reshape(GROUPS, GROUP_TOK, D)
    mask_groups = token_mask.reshape(GROUPS, GROUP_TOK)

    def group_step(carried, group_inputs):
        hidden_g, teacher_g, mask_g, seg_g = group_inputs

        def forward(hidden_in, weight_set):
            return block_group(hidden_in, weight_set, teacher_g, mask_g, seg_g)
        (squared, state_two), back_fn = jax.vjp(forward, hidden_g, params)
        hidden_grad_g, param_grads = back_fn((loss_scale / valid_count, jnp.zeros_like(state_two)))
        carried = jax.tree.map(lambda summed_grad, new_grad: summed_grad + new_grad, carried, param_grads)
        return (carried, (squared, state_two, hidden_grad_g))
    zero_grads = jax.tree.map(jnp.zeros_like, params)
    grads, (squared_all, states_all, hidden_grads) = lax.scan(group_step, zero_grads, (hidden_groups, teacher_groups, mask_groups, segments))
    loss_value = jnp.sum(squared_all) / valid_count
    output = states_all.reshape(TOKENS, D).astype(jnp.bfloat16)
    hidden_grad = hidden_grads.reshape(TOKENS, D)
    return (loss_value, output, hidden_grad, grads[0], grads[1], grads[2], grads[3], grads[4], grads[5], grads[6], grads[7], grads[8], grads[9], grads[10], grads[11])
```

```python
import functools
import math

import jax
import jax.numpy as jnp
from jax import lax
from jax.experimental import pallas as pl
from jax.experimental.pallas import tpu as pltpu
from jax.sharding import PartitionSpec as P

D = 1280
HEAD_DIM = 64
EPS = 1e-06
HEADS = 5
ROWS = 512
TOK = 128
COLS = 320
TILE = 256
F32 = jnp.float32
BF16 = jnp.bfloat16
MESH = pl.DeviceIdType.MESH
DMA = pltpu.SemaphoreType.DMA
VMEM = pltpu.VMEM
IN_VMEM = pl.BlockSpec(memory_space=pltpu.VMEM)
IN_SMEM = pl.BlockSpec(memory_space=pltpu.SMEM)
IN_PLACE = pl.BlockSpec(memory_space=pl.ANY)
LIMIT = 60 << 20


def params(collective=None):
    if collective is None:
        return pltpu.CompilerParams(vmem_limit_bytes=LIMIT)
    return pltpu.CompilerParams(
        collective_id=collective, has_side_effects=True, vmem_limit_bytes=LIMIT
    )


def spot():
    row = lax.axis_index("row")
    return lax.axis_index("dp"), lax.div(row, 2), lax.rem(row, 2), lax.axis_index("col")


def wrap(i):
    return lax.rem(i + 8, 4)


def device(z, x, c, y):
    return (z, 2 * x + c, y)


def meet(others):
    barrier = pltpu.get_barrier_semaphore()
    for other in others:
        pl.semaphore_signal(barrier, inc=1, device_id=other, device_id_type=MESH)
    pl.semaphore_wait(barrier, len(others))


def remote(src, dst, send_sem, recv_sem, to):
    return pltpu.make_async_remote_copy(
        src_ref=src,
        dst_ref=dst,
        send_sem=send_sem,
        recv_sem=recv_sem,
        device_id=to,
        device_id_type=MESH,
    )


def dot_nn(a, b):
    return lax.dot_general(a, b, (((1,), (0,)), ((), ())), preferred_element_type=F32)


def dot_nt(a, b):
    return lax.dot_general(a, b, (((1,), (1,)), ((), ())), preferred_element_type=F32)


def dot_tn(a, b):
    return lax.dot_general(a, b, (((0,), (0,)), ((), ())), preferred_element_type=F32)


class Tally:
    def __init__(self, src, accs, parts, send, recv):
        z, x, c, y = spot()
        self.src, self.accs, self.parts, self.send, self.recv = src, accs, parts, send, recv
        self.peers = [
            [device(z, wrap(x + d), c, y) for d in (1, 2, 3)],
            [device(wrap(z + d), x, c, y) for d in (1, 2, 3)],
            [device(z, x, 1 - c, y)],
        ]
        self.copies = []

    def start(self, stage):
        src = self.src if stage == 0 else self.accs.at[stage - 1]
        for d, peer in enumerate(self.peers[stage]):
            at = 3 * stage + d
            copy = remote(src, self.parts.at[at], self.send.at[at], self.recv.at[at], peer)
            copy.start()
            self.copies.append(copy)

    def finish(self, stage):
        src = self.src if stage == 0 else self.accs.at[stage - 1]
        total = src[...]
        for d in range(len(self.peers[stage])):
            self.copies[3 * stage + d].wait_recv()
            total = total + self.parts[3 * stage + d]
        self.accs[stage] = total

    def close(self):
        for copy in self.copies:
            copy.wait_send()


TALLY_PEERS = 7


def tally_scratch(shape):
    return [
        VMEM((3,) + shape, F32),
        VMEM((7,) + shape, F32),
        DMA((7,)),
        DMA((7,)),
    ]


def torus(z, x, c, y):
    def first(d):
        return device(wrap(z + c * d), wrap(x + (1 - c) * d), c, y)

    def second(d):
        return device(wrap(z + (1 - c) * d), wrap(x + c * d), c, y)

    at_first = x * (1 - c) + z * c
    at_second = z * (1 - c) + x * c

    def block(d1, d2):
        a1, a2 = wrap(at_first + d1), wrap(at_second + d2)
        return (1 - c) * (a2 * 4 + a1) + c * (a1 * 4 + a2)

    return first, second, block


def gather_kernel(
    hid,
    tea,
    rates,
    count,
    shard,
    hid_out,
    tea_out,
    rates_out,
    count_out,
    weights,
    hid_buf,
    tea_buf,
    rate_buf,
    shard_sib,
    own_block,
    y_send,
    y_recv,
    w_send,
    w_recv,
    s_send,
    s_recv,
    local_sem,
    t_accs,
    t_parts,
    t_send,
    t_recv,
):
    z, x, c, y = spot()
    first, second, block = torus(z, x, c, y)
    sibling = device(z, x, 1 - c, y)
    mine = pl.ds(2 * c, 2)
    across = [device(z, x, c, wrap(y + d)) for d in (1, 2, 3)]
    tally = Tally(count, t_accs, t_parts, t_send, t_recv)
    meet(across + tally.peers[0] + tally.peers[1] + tally.peers[2])

    head = remote(shard.at[pl.ds(2 * (1 - c), 2)], shard_sib, w_send.at[0], w_recv.at[0], sibling)
    head.start()
    tally.start(0)
    hid_r = remote(hid, hid_buf.at[y], y_send.at[0], y_recv.at[0], across[0])
    hid_l = remote(hid, hid_buf.at[y], y_send.at[1], y_recv.at[1], across[2])
    hid_r.start()
    hid_l.start()
    small = []
    for d in (1, 2, 3):
        rows = pl.ds(pl.multiple_of(TOK * wrap(y + d), TOK), TOK)
        for k, (src, dst) in enumerate(
            ((tea.at[rows], tea_buf.at[y]), (rates, rate_buf.at[y]))
        ):
            at = 4 + 2 * (d - 1) + k
            copy = remote(src, dst, y_send.at[at], y_recv.at[at], across[d - 1])
            copy.start()
            small.append(copy)
    hid_buf[y] = hid[...]
    tea_buf[y] = tea[pl.ds(pl.multiple_of(TOK * y, TOK), TOK), :]
    rate_buf[y] = rates[...]

    head.wait()
    for j in range(2):
        near = shard[2 * c + j].astype(F32)
        far = shard_sib[j].astype(F32)
        upper = jnp.where(c == 0, near, far)
        lower = jnp.where(c == 0, far, near)
        own_block[j] = jnp.concatenate([upper, lower], axis=0).astype(BF16)

    sends, hands = [], []

    def slab(at):
        return weights.at[mine, at]

    def ship(src, dst, at, to):
        copy = remote(src, dst, w_send.at[at], w_recv.at[at], to)
        copy.start()
        sends.append(copy)
        return copy

    def hand(src, at, sem_at):
        copy = remote(src, slab(at), s_send.at[sem_at], s_recv.at[sem_at], sibling)
        copy.start()
        hands.append(copy)

    own = block(0, 0)
    local = pltpu.make_async_copy(own_block, slab(own), local_sem)
    local.start()
    one_r = ship(own_block, slab(own), 1, first(1))
    one_l = ship(own_block, slab(own), 2, first(-1))
    two_r, two_l, two_f, two_g = {}, {}, {}, {}

    def second_start(d1):
        at = block(d1, 0)
        src = own_block if d1 == 0 else slab(at)
        two_r[d1] = ship(src, slab(at), 5 + 4 * d1, second(1))
        two_l[d1] = ship(src, slab(at), 6 + 4 * d1, second(-1))
        hand(src, at, 4 * d1)

    def second_pass(d1):
        two_r[d1].wait_recv()
        at = block(d1, -1)
        piece = weights.at[2 * c, at]
        two_f[d1] = ship(piece, piece, 7 + 4 * d1, second(1))
        hand(slab(at), at, 4 * d1 + 3)
        two_l[d1].wait_recv()
        at = block(d1, 1)
        piece = weights.at[2 * c + 1, at]
        two_g[d1] = ship(piece, piece, 8 + 4 * d1, second(-1))
        hand(slab(at), at, 4 * d1 + 1)

    def second_end(d1):
        two_f[d1].wait_recv()
        two_g[d1].wait_recv()
        at = block(d1, 2)
        hand(slab(at), at, 4 * d1 + 2)

    second_start(0)
    one_r.wait_recv()
    piece = weights.at[2 * c, block(-1, 0)]
    one_f = ship(piece, piece, 3, first(1))
    second_start(3)
    one_l.wait_recv()
    piece = weights.at[2 * c + 1, block(1, 0)]
    one_g = ship(piece, piece, 4, first(-1))
    second_start(1)
    hid_r.wait_recv()
    piece = hid_buf.at[wrap(y - 1), pl.ds(0, ROWS // 2)]
    hid_f = remote(piece, piece, y_send.at[2], y_recv.at[2], across[0])
    hid_f.start()
    hid_l.wait_recv()
    piece = hid_buf.at[wrap(y + 1), pl.ds(ROWS // 2, ROWS // 2)]
    hid_g = remote(piece, piece, y_send.at[3], y_recv.at[3], across[2])
    hid_g.start()
    tally.finish(0)
    tally.start(1)
    second_pass(0)
    one_f.wait_recv()
    one_g.wait_recv()
    second_start(2)
    for copy in small:
        copy.wait_recv()
    tea_out[...] = jnp.concatenate([tea_buf[k] for k in range(4)], axis=1)
    rates_out[...] = jnp.concatenate([rate_buf[k] for k in range(4)], axis=1)
    hid_f.wait_recv()
    hid_g.wait_recv()
    hid_out[...] = jnp.concatenate([hid_buf[k] for k in range(4)], axis=1)
    tally.finish(1)
    tally.start(2)
    second_pass(3)
    second_pass(1)
    second_end(0)
    second_pass(2)
    second_end(3)
    second_end(1)
    second_end(2)
    tally.finish(2)
    count_out[...] = t_accs[2]
    for copy in hands:
        copy.wait_recv()
    local.wait()
    for copy in sends + hands + small + [hid_r, hid_l, hid_f, hid_g]:
        copy.wait_send()
    tally.close()


def gather_all(hidden, teacher, rates, count, shard):
    return pl.pallas_call(
        gather_kernel,
        out_shape=(
            jax.ShapeDtypeStruct((ROWS, D), BF16),
            jax.ShapeDtypeStruct((TOK, D), BF16),
            jax.ShapeDtypeStruct((2, D), F32),
            jax.ShapeDtypeStruct((8, 128), F32),
            jax.ShapeDtypeStruct((4, 16, 80, D), BF16),
        ),
        in_specs=[IN_VMEM] * 5,
        out_specs=(IN_VMEM,) * 4 + (IN_PLACE,),
        scratch_shapes=[
            VMEM((4, ROWS, COLS), BF16),
            VMEM((4, TOK, COLS), BF16),
            VMEM((4, 2, COLS), F32),
            VMEM((2, 40, D), BF16),
            VMEM((2, 80, D), BF16),
            DMA((10,)),
            DMA((10,)),
            DMA((21,)),
            DMA((21,)),
            DMA((16,)),
            DMA((16,)),
            DMA,
        ]
        + tally_scratch((8, 128)),
        compiler_params=params(0),
        name="gather_all",
    )(hidden, teacher, rates, count, shard)


def window_kernel(kv, win, send, recv, s_send, s_recv, local_sem):
    z, x, c, y = spot()
    sibling = device(z, x, 1 - c, y)
    meet([device(z, wrap(x + d), c, y) for d in (1, 2, 3)] + [sibling])
    one = remote(kv, win.at[2], send.at[0], recv.at[0], device(z, wrap(x + 1), c, y))
    two = remote(kv, win.at[0], send.at[1], recv.at[1], device(z, wrap(x + 2), c, y))
    own = remote(kv, win.at[3], s_send.at[0], s_recv.at[0], sibling)
    one_on = remote(win.at[2], win.at[1 + 2 * c], s_send.at[1], s_recv.at[1], sibling)
    two_on = remote(win.at[0], win.at[1], s_send.at[2], s_recv.at[2], sibling)
    local = pltpu.make_async_copy(kv, win.at[4], local_sem)

    @pl.when(x < 2)
    def _():
        two.start()

    @pl.when(x < 3)
    def _():
        one.start()

    @pl.when(c == 0)
    def _():
        own.start()

    local.start()

    @pl.when(x > 0)
    def _():
        one.wait_recv()
        one_on.start()

    @pl.when(x > 1)
    def _():
        two.wait_recv()

        @pl.when(c == 1)
        def _():
            two_on.start()
            two_on.wait_send()

        @pl.when(c == 0)
        def _():
            two_on.wait_recv()

    @pl.when(x > 0)
    def _():
        one_on.wait_recv()
        one_on.wait_send()

    @pl.when(c == 1)
    def _():
        own.wait_recv()

    @pl.when(c == 0)
    def _():
        own.wait_send()

    @pl.when(x < 2)
    def _():
        two.wait_send()

    @pl.when(x < 3)
    def _():
        one.wait_send()

    local.wait()


def gather_window(kv):
    return pl.pallas_call(
        window_kernel,
        out_shape=jax.ShapeDtypeStruct((5, ROWS, 2 * COLS), BF16),
        in_specs=[IN_VMEM],
        out_specs=IN_PLACE,
        scratch_shapes=[DMA((2,)), DMA((2,)), DMA((3,)), DMA((3,)), DMA],
        compiler_params=params(1),
        name="gather_window",
    )(kv)


def half_mask(half):
    lane = lax.broadcasted_iota(jnp.int32, (1, 128), 1)
    return (lane < 64) if half == 0 else (lane >= 64)


def key_place(h):
    return h // 2, h % 2


def value_place(h):
    return (HEADS + h) // 2, (HEADS + h) % 2


def pad_head(wide, at, half):
    group = wide[:, 128 * at : 128 * at + 128]
    return jnp.where(half_mask(half), group, jnp.zeros_like(group))


def attend_kernel(first_tile, starts, q8, win, out, lse, q_pad, o_acc, l_acc):
    for h in range(HEADS):
        q_pad[h] = pad_head(q8, h // 2, h % 2)
    o_acc[...] = jnp.zeros_like(o_acc)
    l_acc[...] = jnp.zeros_like(l_acc)

    def tile(t, diagonal):
        rows = pl.ds(pl.multiple_of(t * TILE, TILE), TILE)
        key_at = t * TILE + lax.broadcasted_iota(jnp.int32, (TILE, ROWS), 0)
        allowed = key_at >= starts[...]
        if diagonal:
            query_at = 4 * ROWS + lax.broadcasted_iota(jnp.int32, (TILE, ROWS), 1)
            allowed = allowed & (key_at <= query_at)
        for h in range(HEADS):
            kg, _ = key_place(h)
            vg, vh = value_place(h)
            keys = win[rows, 128 * kg : 128 * kg + 128]
            values = win[rows, 128 * vg : 128 * vg + 128]
            scores = dot_nt(keys, q_pad[h])
            weights = jnp.where(allowed, jnp.exp(scores), 0.0)
            l_acc[h] += jnp.sum(weights.reshape(TILE // 8, 8, ROWS), axis=0)
            both = dot_tn(values, weights.astype(BF16))
            o_acc[h] += both[64 * vh : 64 * vh + 64, :]

    def step(t, carry):
        tile(t, False)
        return carry

    lax.fori_loop(first_tile[0], 8, step, 0)
    for t in (8, 9):
        tile(t, True)
    out[:, 0:128] = jnp.zeros((ROWS, 128), F32)
    for h in range(HEADS):
        total = jnp.sum(l_acc[h], axis=0, keepdims=True)
        lse[h] = jnp.broadcast_to(jnp.log(total), (8, ROWS))
        o_acc[h] = o_acc[h] / total
    turned = [o_acc[h] for h in range(HEADS)]
    wide = jnp.concatenate([jnp.zeros((64, ROWS), F32)] + turned, axis=0)
    out[...] = wide.T


def attend(first_tile, starts, q8, win):
    return pl.pallas_call(
        attend_kernel,
        out_shape=(
            jax.ShapeDtypeStruct((ROWS, 384), F32),
            jax.ShapeDtypeStruct((HEADS, 8, ROWS), F32),
        ),
        in_specs=[IN_SMEM] + [IN_VMEM] * 3,
        out_specs=(IN_VMEM,) * 2,
        scratch_shapes=[
            VMEM((HEADS, ROWS, 128), BF16),
            VMEM((HEADS, 64, ROWS), F32),
            VMEM((HEADS, 8, ROWS), F32),
        ],
        compiler_params=params(),
        name="attend",
    )(first_tile, starts, q8, win)


def attend_back_kernel(
    first_tile, starts, q8, win, out, lse, d_out, dq, d_win, q_pad, d_pad, delta, q_acc
):
    for h in range(HEADS):
        q_pad[h] = pad_head(q8, h // 2, h % 2)
        d_pad[h] = pad_head(d_out, (h + 1) // 2, (h + 1) % 2)
    wide = (d_out[...].astype(F32) * out[...]).T
    for h in range(HEADS):
        delta[h] = jnp.broadcast_to(
            jnp.sum(wide[64 * (h + 1) : 64 * (h + 2), :], axis=0, keepdims=True), (8, ROWS)
        )
    q_acc[...] = jnp.zeros_like(q_acc)

    def clear(t, carry):
        d_win[pl.ds(pl.multiple_of(t * TILE, TILE), TILE), :] = jnp.zeros((TILE, 2 * COLS), BF16)
        return carry

    lax.fori_loop(0, first_tile[0], clear, 0)

    def tile(t, diagonal):
        rows = pl.ds(pl.multiple_of(t * TILE, TILE), TILE)
        key_at = t * TILE + lax.broadcasted_iota(jnp.int32, (TILE, ROWS), 0)
        allowed = key_at >= starts[...]
        if diagonal:
            query_at = 4 * ROWS + lax.broadcasted_iota(jnp.int32, (TILE, ROWS), 1)
            allowed = allowed & (key_at <= query_at)
        sums = [None] * 5
        for h in range(HEADS):
            kg, kh = key_place(h)
            vg, _ = value_place(h)
            keys = win[rows, 128 * kg : 128 * kg + 128]
            values = win[rows, 128 * vg : 128 * vg + 128]
            scores = dot_nt(keys, q_pad[h])
            probs = jnp.where(allowed, jnp.exp(scores - lse[h, 0:1, :]), 0.0)
            prob_grad = dot_nt(values, d_pad[h])
            score_grad = (probs * (prob_grad - delta[h, 0:1, :])).astype(BF16)
            v_term = dot_nn(probs.astype(BF16), d_pad[h])
            k_term = dot_nn(score_grad, q_pad[h])
            for at, term in ((kg, k_term), (vg, v_term)):
                sums[at] = term if sums[at] is None else sums[at] + term
            both = dot_tn(keys, score_grad)
            q_acc[h] += both[64 * kh : 64 * kh + 64, :]
        for g in range(5):
            d_win[rows, 128 * g : 128 * g + 128] = sums[g].astype(BF16)

    def step(t, carry):
        tile(t, False)
        return carry

    lax.fori_loop(first_tile[0], 8, step, 0)
    for t in (8, 9):
        tile(t, True)
    wide = jnp.concatenate(
        [q_acc[h] for h in range(HEADS)] + [jnp.zeros((64, ROWS), F32)], axis=0
    )
    dq[...] = wide.T * math.sqrt(HEAD_DIM)


def attend_back(first_tile, starts, q8, win, out, lse, d_out):
    return pl.pallas_call(
        attend_back_kernel,
        out_shape=(
            jax.ShapeDtypeStruct((ROWS, 384), F32),
            jax.ShapeDtypeStruct((5 * ROWS, 2 * COLS), BF16),
        ),
        in_specs=[IN_SMEM] + [IN_VMEM] * 6,
        out_specs=(IN_VMEM,) * 2,
        scratch_shapes=[
            VMEM((HEADS, ROWS, 128), BF16),
            VMEM((HEADS, ROWS, 128), BF16),
            VMEM((HEADS, 8, ROWS), F32),
            VMEM((HEADS, 64, ROWS), F32),
        ],
        compiler_params=params(),
        name="attend_back",
    )(first_tile, starts, q8, win, out, lse, d_out)


def window_back_kernel(d_win, total, sib_one, sib_two, sib_own, one_buf, two_buf, got_one, got_two, send, recv):
    z, x, c, y = spot()
    sibling = device(z, x, 1 - c, y)
    meet([device(z, wrap(x + d), c, y) for d in (1, 2, 3)] + [sibling])
    hand_one = remote(d_win.at[3 - 2 * c], sib_one, send.at[0], recv.at[0], sibling)
    hand_two = remote(d_win.at[1], sib_two, send.at[1], recv.at[1], sibling)
    hand_own = remote(d_win.at[3], sib_own, send.at[2], recv.at[2], sibling)
    one = remote(one_buf, got_one, send.at[3], recv.at[3], device(z, wrap(x + 3), c, y))
    two = remote(two_buf, got_two, send.at[4], recv.at[4], device(z, wrap(x + 2), c, y))

    @pl.when((x > 1) & (c == 0))
    def _():
        hand_two.start()

    @pl.when(x > 0)
    def _():
        hand_one.start()

    @pl.when(c == 1)
    def _():
        hand_own.start()

    @pl.when(x > 1)
    def _():
        @pl.when(c == 1)
        def _():
            hand_two.wait_recv()
            two_buf[...] = (d_win[0].astype(F32) + sib_two[...].astype(F32)).astype(BF16)

        @pl.when(c == 0)
        def _():
            two_buf[...] = d_win[0]

        two.start()

    @pl.when(x > 0)
    def _():
        hand_one.wait_recv()
        one_buf[...] = (d_win[2].astype(F32) + sib_one[...].astype(F32)).astype(BF16)
        one.start()

    total[...] = d_win[4].astype(F32)

    @pl.when(c == 0)
    def _():
        hand_own.wait_recv()
        total[...] += sib_own[...].astype(F32)

    @pl.when(x < 3)
    def _():
        one.wait_recv()
        total[...] += got_one[...].astype(F32)

    @pl.when(x < 2)
    def _():
        two.wait_recv()
        total[...] += got_two[...].astype(F32)

    @pl.when(x > 1)
    def _():
        two.wait_send()

    @pl.when(x > 0)
    def _():
        one.wait_send()
        hand_one.wait_send()

    @pl.when((x > 1) & (c == 0))
    def _():
        hand_two.wait_send()

    @pl.when(c == 1)
    def _():
        hand_own.wait_send()


def window_back(d_win):
    one = (ROWS, 2 * COLS)
    return pl.pallas_call(
        window_back_kernel,
        out_shape=jax.ShapeDtypeStruct(one, F32),
        in_specs=[IN_VMEM],
        out_specs=IN_VMEM,
        scratch_shapes=[VMEM(one, BF16)] * 7 + [DMA((5,)), DMA((5,))],
        compiler_params=params(2),
        name="window_back",
    )(d_win)


def mix_forward(states, branch, alphas):
    branch_scale = lax.rsqrt(jnp.sum(branch * branch, axis=1, keepdims=True) + EPS)
    normed = branch * branch_scale
    mixed = states + alphas * (normed - states)
    mixed_scale = lax.rsqrt(jnp.sum(mixed * mixed, axis=1, keepdims=True) + EPS)
    return mixed * mixed_scale, normed, branch_scale, mixed_scale


def mix_backward(gradient, states, normed, branch_scale, mixed_out, mixed_scale, alphas):
    along = jnp.sum(mixed_out * gradient, axis=1, keepdims=True)
    mixed_grad = mixed_scale * (gradient - mixed_out * along)
    normed_grad = alphas * mixed_grad
    toward = jnp.sum(normed * normed_grad, axis=1, keepdims=True)
    branch_grad = branch_scale * (normed_grad - normed * toward)
    rate_grad = jnp.sum(mixed_grad * (normed - states), axis=0, keepdims=True)
    return (1.0 - alphas) * mixed_grad, branch_grad, rate_grad


def swiglu_parts(gate_raw, up_raw, gate_gain, up_gain):
    root = math.sqrt(D)
    g = gate_gain * gate_raw * root
    q = jax.nn.sigmoid(g)
    return g, q


def middle_kernel(
    att,
    hid_full,
    tea,
    mask,
    count,
    rates,
    up_gain,
    gate_gain,
    weights,
    output,
    in_one,
    product,
    mlp_grad,
    gate_low,
    up_low,
    attn_grad,
    d_att,
    res_zero,
    small,
    w_out,
    w_gate,
    w_up,
    w_down,
    raw_gate,
    raw_up,
    send_buf,
    got_buf,
    own_part,
    out_buf,
    state,
    normed,
    scales,
    w_sem,
    ag_send,
    ag_recv,
    rs_send,
    rs_recv,
    o_send,
    o_recv,
):
    z, x, c, y = spot()
    peers = [device(z, x, c, wrap(y + d)) for d in range(4)]
    loads = [
        pltpu.make_async_copy(weights.at[0, :, pl.ds(0, 384)], w_out, w_sem.at[0]),
        pltpu.make_async_copy(weights.at[1], w_gate, w_sem.at[1]),
        pltpu.make_async_copy(weights.at[2], w_up, w_sem.at[2]),
        pltpu.make_async_copy(weights.at[3], w_down, w_sem.at[3]),
    ]
    for load in loads:
        load.start()
    meet(peers[1:])
    my_rows = pl.ds(pl.multiple_of(TOK * y, TOK), TOK)

    def rows_of(k):
        return pl.ds(pl.multiple_of(TOK * wrap(y - k), TOK), TOK)

    def back_to(k):
        return device(z, x, c, wrap(y - k))

    def scatter(stage, k):
        return remote(
            send_buf.at[stage, k],
            got_buf.at[stage, k],
            rs_send.at[stage, k],
            rs_recv.at[stage, k],
            back_to(k),
        )

    def spread(stage, src, k):
        return remote(
            src.at[my_rows],
            src.at[my_rows],
            ag_send.at[stage, k],
            ag_recv.at[stage, k],
            device(z, x, c, wrap(y + k)),
        )

    def give(stage, k, part):
        @pl.when(k == 0)
        def _():
            own_part[...] = part

        @pl.when(k > 0)
        def _():
            send_buf[stage, k] = part.astype(BF16)
            scatter(stage, k).start()

    def collect(stage):
        total = own_part[...]
        for k in (1, 2, 3):
            scatter(stage, k).wait_recv()
            total = total + got_buf[stage, k].astype(F32)
        return total

    def announce(stage, ref, value):
        ref[my_rows, :] = value.astype(BF16)
        for k in (2, 1, 3):
            spread(stage, ref, k).start()

    def each(body, stage=None, ref=None):
        def step(k, carry):
            if ref is not None:

                @pl.when(k > 0)
                def _():
                    spread(stage, ref, k).wait_recv()

            body(k)
            return carry

        lax.fori_loop(0, 4, step, 0)

    loads[0].wait()

    def project(k):
        give(0, k, dot_nt(att[rows_of(k), :], w_out[...]))

    each(project)
    attn = collect(0)
    states = hid_full[my_rows, :].astype(F32)
    one, normed_one, branch_one, scale_one = mix_forward(states, attn, rates[0:1, :])
    announce(0, in_one, one)
    state[0] = one
    normed[0] = normed_one
    scales[0] = jnp.broadcast_to(branch_one, (TOK, 128))
    scales[1] = jnp.broadcast_to(scale_one, (TOK, 128))
    for load in loads[1:]:
        load.wait()

    def feed(k):
        rows = rows_of(k)
        block = in_one[rows, :]
        gate_raw = dot_nn(block, w_gate[...])
        raw_gate[rows, :] = gate_raw
        up_raw = dot_nn(block, w_up[...])
        raw_up[rows, :] = up_raw
        g, q = swiglu_parts(gate_raw, up_raw, gate_gain[...], up_gain[...])
        low = (up_gain[...] * up_raw * (g * q)).astype(BF16)
        product[rows, :] = low
        give(1, k, dot_nt(low, w_down[...]))

    each(feed, 0, in_one)
    mlp = collect(1)
    one = state[0]
    two, normed_two, branch_two, scale_two = mix_forward(one, mlp, rates[1:2, :])
    for k in range(4):
        out_buf[k] = two[:, COLS * k : COLS * (k + 1)].astype(BF16)
    out_copies = []
    for k in (1, 2, 3):
        copy = remote(
            out_buf.at[wrap(y + k)],
            output.at[my_rows],
            o_send.at[k],
            o_recv.at[k],
            device(z, x, c, wrap(y + k)),
        )
        out_copies.append(copy)
    errors = two - tea[...].astype(F32)
    weight = mask[...]
    loss = jnp.sum(weight * errors * errors)
    factor = 16384 * math.sqrt(D) / count[0:1, 0:1]
    seed = factor * (weight * errors)
    res_one, mlp_back, rate_two = mix_backward(
        seed, one, normed_two, branch_two, two, scale_two, rates[1:2, :]
    )
    announce(1, mlp_grad, mlp_back)
    for copy in out_copies:
        copy.start()
    output[my_rows, :] = out_buf[y]
    small[...] = jnp.zeros_like(small)
    small[1:2, :] = rate_two
    small[4:5, :] = jnp.broadcast_to(loss, (1, D))
    state[1] = res_one

    def unfeed(k):
        rows = rows_of(k)
        grad = dot_nn(mlp_grad[rows, :], w_down[...])
        gate_raw = raw_gate[rows, :]
        up_raw = raw_up[rows, :]
        g, q = swiglu_parts(gate_raw, up_raw, gate_gain[...], up_gain[...])
        silu = g * q
        up_term = grad * silu
        slope = grad * up_gain[...] * up_raw * (q * (1.0 + g * (1.0 - q))) * math.sqrt(D)
        small[2:3, :] += jnp.sum(up_term * up_raw, axis=0, keepdims=True)
        small[3:4, :] += jnp.sum(slope * gate_raw, axis=0, keepdims=True)
        up_back = (up_term * up_gain[...]).astype(BF16)
        gate_back = (slope * gate_gain[...]).astype(BF16)
        up_low[rows, :] = up_back
        gate_low[rows, :] = gate_back
        give(2, k, dot_nt(gate_back, w_gate[...]) + dot_nt(up_back, w_up[...]))

    each(unfeed, 1, mlp_grad)
    grad_one = state[1] + collect(2)
    states = hid_full[my_rows, :].astype(F32)
    res, attn_back, rate_one = mix_backward(
        grad_one,
        states,
        normed[0],
        scales[0, :, 0:1],
        state[0],
        scales[1, :, 0:1],
        rates[0:1, :],
    )
    announce(2, attn_grad, attn_back)
    small[0:1, :] = rate_one
    for k in range(4):
        res_zero[k] = res[:, COLS * k : COLS * (k + 1)]

    def unproject(k):
        rows = rows_of(k)
        d_att[rows, :] = dot_nn(attn_grad[rows, :], w_out[...]).astype(BF16)

    each(unproject, 2, attn_grad)
    for k in (1, 2, 3):
        for stage in range(3):
            scatter(stage, k).wait_send()
        spread(0, in_one, k).wait_send()
        spread(1, mlp_grad, k).wait_send()
        spread(2, attn_grad, k).wait_send()
    for copy in out_copies:
        copy.wait()


def middle(att, hid_full, tea, mask, count, rates, up_gain, gate_gain, weights):
    wide = jax.ShapeDtypeStruct((ROWS, D), BF16)
    return pl.pallas_call(
        middle_kernel,
        out_shape=(
            jax.ShapeDtypeStruct((ROWS, COLS), BF16),
            wide,
            wide,
            wide,
            wide,
            wide,
            wide,
            jax.ShapeDtypeStruct((ROWS, 384), BF16),
            jax.ShapeDtypeStruct((4, TOK, COLS), F32),
            jax.ShapeDtypeStruct((8, D), F32),
        ),
        in_specs=[IN_VMEM] * 8 + [IN_PLACE],
        out_specs=(IN_VMEM,) * 10,
        scratch_shapes=[
            VMEM((D, 384), BF16),
            VMEM((D, D), BF16),
            VMEM((D, D), BF16),
            VMEM((D, D), BF16),
            VMEM((ROWS, D), F32),
            VMEM((ROWS, D), F32),
            VMEM((3, 4, TOK, D), BF16),
            VMEM((3, 4, TOK, D), BF16),
            VMEM((TOK, D), F32),
            VMEM((4, TOK, COLS), BF16),
            VMEM((2, TOK, D), F32),
            VMEM((1, TOK, D), F32),
            VMEM((2, TOK, 128), F32),
            DMA((4,)),
            DMA((3, 4)),
            DMA((3, 4)),
            DMA((3, 4)),
            DMA((3, 4)),
            DMA((4,)),
            DMA((4,)),
        ],
        compiler_params=params(3),
        name="middle",
    )(att, hid_full, tea, mask, count, rates, up_gain, gate_gain, weights)


def back_kernel(pack, res, side, weights, grad, side_out, w_buf, send_buf, got_buf, side_buf, w_sem, send, recv, s_send, s_recv):
    z, x, c, y = spot()
    load = pltpu.make_async_copy(weights.at[0], w_buf, w_sem)
    load.start()
    meet([device(z, x, c, wrap(y + d)) for d in (1, 2, 3)])
    my_rows = pl.ds(pl.multiple_of(TOK * y, TOK), TOK)

    def part(k):
        to = wrap(y + k)
        rows = pl.ds(pl.multiple_of(COLS * to, 64), COLS)
        return to, dot_nt(pack[...], w_buf[rows, :])

    load.wait()
    copies = []
    for k in (2, 1, 3):
        to, term = part(k)
        peer = device(z, x, c, to)
        small = remote(side.at[to], side_buf.at[k], s_send.at[k], s_recv.at[k], peer)
        small.start()
        grad[...] = term
        grad[my_rows, :] += res[to]
        send_buf[k] = grad[...].astype(BF16)
        copy = remote(send_buf.at[k], got_buf.at[k], send.at[k], recv.at[k], peer)
        copy.start()
        copies += [small, copy]
    _, term = part(0)
    grad[...] = term
    grad[my_rows, :] += res[y]
    for copy in copies:
        copy.wait_recv()
    total = grad[...]
    extra = side[y]
    for k in (1, 2, 3):
        total = total + got_buf[k].astype(F32)
        extra = extra + side_buf[k]
    grad[...] = total
    side_out[...] = extra
    for copy in copies:
        copy.wait_send()


def back_project(pack, res, side, weights):
    return pl.pallas_call(
        back_kernel,
        out_shape=(
            jax.ShapeDtypeStruct((ROWS, COLS), F32),
            jax.ShapeDtypeStruct((8, COLS), F32),
        ),
        in_specs=[IN_VMEM] * 3 + [IN_PLACE],
        out_specs=(IN_VMEM,) * 2,
        scratch_shapes=[
            VMEM((D, D), BF16),
            VMEM((4, ROWS, COLS), BF16),
            VMEM((4, ROWS, COLS), BF16),
            VMEM((4, 8, COLS), F32),
            DMA,
            DMA((4,)),
            DMA((4,)),
            DMA((4,)),
            DMA((4,)),
        ],
        compiler_params=params(4),
        name="back_project",
    )(pack, res, side, weights)


def reduce_kernel(
    g0,
    g1,
    g2,
    g3,
    side,
    out,
    side_out,
    own,
    sib,
    got_two,
    mid,
    got_one,
    fin,
    l_sem,
    h_send,
    h_recv,
    b_send,
    b_recv,
    a_send,
    a_recv,
    f_send,
    f_recv,
    t_accs,
    t_parts,
    t_send,
    t_recv,
):
    z, x, c, y = spot()
    first, second, _ = torus(z, x, c, y)
    at_first = x * (1 - c) + z * c
    sibling = device(z, x, 1 - c, y)
    tally = Tally(side, t_accs, t_parts, t_send, t_recv)
    meet(tally.peers[0] + tally.peers[1] + tally.peers[2])
    tally.start(0)
    order = (2, 1, 3, 0)

    @pl.when(c == 0)
    def _():
        for d in order:
            for j, (near, far) in enumerate(((g0, g2), (g1, g3))):
                remote(
                    far.at[:, wrap(x + d)], sib.at[j, d], h_send.at[j, d], h_recv.at[j, d], sibling
                ).start()
                pltpu.make_async_copy(near.at[wrap(z + d)], own.at[j, d], l_sem.at[j, d]).start()

    @pl.when(c == 1)
    def _():
        for d in order:
            for j, (near, far) in enumerate(((g2, g0), (g3, g1))):
                remote(
                    far.at[wrap(z + d)], sib.at[j, d], h_send.at[j, d], h_recv.at[j, d], sibling
                ).start()
                pltpu.make_async_copy(near.at[:, wrap(x + d)], own.at[j, d], l_sem.at[j, d]).start()

    def handed(j, d):
        return remote(g0.at[0], sib.at[j, d], h_send.at[j, d], h_recv.at[j, d], sibling)

    def fetched(j, d):
        return pltpu.make_async_copy(g0.at[0], own.at[j, d], l_sem.at[j, d])

    pairs = []
    for d in order:
        for j in range(2):
            fetched(j, d).wait()
            handed(j, d).wait_recv()

            def add(i, carry, j=j, d=d):
                own[j, d, i] = (own[j, d, i].astype(F32) + sib[j, d, i].astype(F32)).astype(BF16)
                return carry

            lax.fori_loop(0, 4, add, 0)
            if d:
                copy = remote(
                    own.at[j, d], got_two.at[j, d], b_send.at[j, d], b_recv.at[j, d], second(d)
                )
                copy.start()
                pairs.append(copy)
    tally.finish(0)
    tally.start(1)
    for copy in pairs:
        copy.wait_recv()

    def whole(j, at):
        total = own[j, 0, at].astype(F32)
        for d in (1, 2, 3):
            total = total + got_two[j, d, at].astype(F32)
        return total

    lasts = []
    for e in (2, 1, 3):
        for j in range(2):
            mid[j, e] = whole(j, wrap(at_first + e)).astype(BF16)
            copy = remote(
                mid.at[j, e], got_one.at[j, e], a_send.at[j, e], a_recv.at[j, e], first(e)
            )
            copy.start()
            lasts.append(copy)
    tally.finish(1)
    tally.start(2)
    for j in range(2):
        fin[j] = whole(j, at_first)
    for copy in lasts:
        copy.wait_recv()
    for j in range(2):
        total = fin[j]
        for e in (1, 2, 3):
            total = total + got_one[j, e].astype(F32)
        fin[j] = total
    theirs = pl.ds(pl.multiple_of(40 * (1 - c), 8), 40)
    ours = pl.ds(pl.multiple_of(40 * c, 8), 40)
    give = remote(fin.at[:, theirs], out.at[pl.ds(2 * c, 2)], f_send, f_recv, sibling)
    give.start()
    for j in range(2):
        out[2 * c + j] = fin[j, ours, :]
    tally.finish(2)
    side_out[...] = t_accs[2]
    give.wait()
    for copy in pairs + lasts:
        copy.wait_send()
    for j in range(2):
        for d in range(4):
            handed(j, d).wait_send()
    tally.close()


def reduce_all(grads, side):
    block = (80, D)
    return pl.pallas_call(
        reduce_kernel,
        out_shape=(
            jax.ShapeDtypeStruct((4, 40, D), F32),
            jax.ShapeDtypeStruct((8, D), F32),
        ),
        in_specs=[IN_PLACE] * 4 + [IN_VMEM],
        out_specs=(IN_VMEM,) * 2,
        scratch_shapes=[
            VMEM((2, 4, 4) + block, BF16),
            VMEM((2, 4, 4) + block, BF16),
            VMEM((2, 4, 4) + block, BF16),
            VMEM((2, 4) + block, BF16),
            VMEM((2, 4) + block, BF16),
            VMEM((2,) + block, F32),
            DMA((2, 4)),
            DMA((2, 4)),
            DMA((2, 4)),
            DMA((2, 4)),
            DMA((2, 4)),
            DMA((2, 4)),
            DMA((2, 4)),
            DMA,
            DMA,
        ]
        + tally_scratch((8, D)),
        compiler_params=params(5),
        name="reduce_all",
    )(*[g.reshape(4, 4, 80, D) for g in grads], side)


def rope_tables(positions, head_dim):
    half_dim = head_dim // 2
    indices = jnp.arange(half_dim, dtype=F32)
    inverse = jnp.exp(indices * (-2.0 * math.log(10000.0) / head_dim))
    angles = positions[:, None] * inverse[None, :]
    return (jnp.cos(angles), jnp.sin(angles))


def rotate(head_vals, cosine, sine_table):
    half_dim = head_vals.shape[-1] // 2
    first_half = head_vals[..., :half_dim]
    second_half = head_vals[..., half_dim:]
    cos_wide = cosine[:, None, :]
    sin_wide = sine_table[:, None, :]
    return jnp.concatenate(
        [
            first_half * cos_wide - second_half * sin_wide,
            second_half * cos_wide + first_half * sin_wide,
        ],
        axis=-1,
    )


def head_map(raw_proj, gains, cosine, sine_table, head_dim):
    row_count = raw_proj.shape[0]
    head_vals = rotate(raw_proj.reshape(row_count, -1, head_dim), cosine, sine_table)
    normed = head_vals * lax.rsqrt(jnp.sum(head_vals * head_vals, axis=-1, keepdims=True) + EPS)
    return normed.reshape(row_count, -1) * gains


def weight_dot(inputs_low, gradient):
    return lax.dot_general(
        inputs_low, gradient, (((0,), (0,)), ((), ())), preferred_element_type=F32
    ).astype(BF16)


def shards(
    hidden,
    teacher,
    valid_mask,
    segments,
    query_weight,
    key_weight,
    value_weight,
    out_weight,
    gate_weight,
    up_weight,
    down_weight,
    attention_rate,
    feedforward_rate,
    score_gain,
    up_gain,
    gate_gain,
):
    place = lax.axis_index("row")
    col = lax.axis_index("col")
    token_mask = valid_mask.astype(F32)
    count = jnp.broadcast_to(jnp.sum(token_mask), (8, 128))
    rates = jnp.stack([attention_rate, feedforward_rate])
    first = jnp.concatenate(
        [query_weight[:, 256:], out_weight.T, query_weight[:, :256], key_weight, value_weight],
        axis=1,
    )
    shard = jnp.stack([first, gate_weight, up_weight, down_weight.T])
    hid_full, tea_tok, rates_full, count_all, weights = gather_all(
        hidden, teacher, rates, count, shard
    )
    weights = weights.reshape(4, D, D)

    offset = place * ROWS
    query_pos = offset + jnp.arange(ROWS, dtype=jnp.int32)
    cosine, sine_table = rope_tables(query_pos.astype(F32), HEAD_DIM)
    key_seg = segments[0]
    query_seg = lax.dynamic_slice_in_dim(key_seg, offset, ROWS)
    starts = jnp.sum((key_seg[None, :] < query_seg[:, None]).astype(jnp.int32), axis=1)
    starts = starts - (offset - 4 * ROWS)
    first_tile = (starts[0] // TILE).reshape(1)
    starts = starts.reshape(1, ROWS)

    raw = jnp.dot(hid_full, weights[0], preferred_element_type=F32)
    query_raw = jnp.concatenate([raw[:, 384:640], raw[:, :64]], axis=1)
    key_raw = raw[:, 640:960]
    queries = head_map(query_raw, score_gain, cosine, sine_table, HEAD_DIM).astype(BF16)
    keys = head_map(key_raw, score_gain, cosine, sine_table, HEAD_DIM).astype(BF16)
    q8 = jnp.pad(queries * jnp.asarray(math.sqrt(HEAD_DIM), BF16), ((0, 0), (0, 64)))
    kv = jnp.concatenate([keys, raw[:, 960:].astype(BF16)], axis=1)
    win = gather_window(kv).reshape(5 * ROWS, 2 * COLS)
    attended, lse = attend(first_tile, starts, q8, win)
    att = attended.astype(BF16)

    mask_tok = lax.dynamic_slice_in_dim(token_mask, col * TOK, TOK).reshape(TOK, 1)
    (
        output,
        in_one,
        product,
        mlp_grad,
        gate_low,
        up_low,
        attn_grad,
        d_att,
        res_zero,
        small,
    ) = middle(
        att,
        hid_full,
        tea_tok,
        mask_tok,
        count_all,
        rates_full,
        up_gain.reshape(1, -1),
        gate_gain.reshape(1, -1),
        weights,
    )
    gate_grad = weight_dot(in_one, gate_low)
    up_grad = weight_dot(in_one, up_low)
    down_grad = weight_dot(mlp_grad, product)

    dq, d_win = attend_back(first_tile, starts, q8, win, attended, lse, d_att)
    d_kv = window_back(d_win.reshape(5, ROWS, 2 * COLS))

    def head_local(raw_proj, gains):
        return head_map(raw_proj, gains, cosine, sine_table, HEAD_DIM)

    _, query_back = jax.vjp(head_local, query_raw, score_gain)
    query_raw_grad, gain_from_query = query_back(dq[:, :COLS])
    _, key_back = jax.vjp(head_local, key_raw, score_gain)
    key_raw_grad, gain_from_key = key_back(d_kv[:, :COLS])
    query_low = query_raw_grad.astype(BF16)
    pack = jnp.concatenate(
        [
            query_low[:, 256:],
            jnp.zeros((ROWS, COLS), BF16),
            query_low[:, :256],
            key_raw_grad.astype(BF16),
            d_kv[:, COLS:].astype(BF16),
        ],
        axis=1,
    )
    side = jnp.concatenate([small[0:2], small[4:5], jnp.zeros((5, D), F32)], axis=0)
    side = side.reshape(8, 4, COLS).transpose(1, 0, 2)
    hidden_grad, side = back_project(pack, res_zero, side, weights)
    first_grad = (
        lax.dot_general(hid_full, pack, (((0,), (0,)), ((), ())), preferred_element_type=F32)
        + jnp.pad(
            lax.dot_general(attn_grad, att, (((0,), (0,)), ((), ())), preferred_element_type=F32),
            ((0, 0), (0, D - 384)),
        )
    ).astype(BF16)
    sums = jnp.concatenate(
        [
            small[2:4],
            jnp.concatenate(
                [gain_from_query + gain_from_key, side[0], side[1], side[2]], axis=0
            ).reshape(1, D),
            jnp.zeros((5, D), F32),
        ],
        axis=0,
    )
    grads, sums = reduce_all((first_grad, gate_grad, up_grad, down_grad), sums)
    head = grads[0]
    return (
        sums[2, 960] / count_all[0, 0],
        output,
        hidden_grad,
        jnp.concatenate([head[:, 384:640], head[:, :64]], axis=1),
        head[:, 640:960],
        head[:, 960:],
        head[:, 64:384].T,
        grads[1],
        grads[2],
        grads[3].T,
        sums[2, 320:640],
        sums[2, 640:960],
        sums[2, :320],
        sums[0],
        sums[1],
    )


def solution(mesh):
    both = P(("dp", "row"), "col")
    turned = P("col", ("dp", "row"))
    vector = P("col")
    in_specs = (both, both, P(("dp", "row")), P("dp", None), both, both, both, turned, both, both)
    in_specs += (turned,) + (vector,) * 5
    out_specs = (P(), both, both, both, both, both, turned, both, both, turned) + (vector,) * 5
    return jax.shard_map(shards, mesh=mesh, in_specs=in_specs, out_specs=out_specs, check_vma=False)
```

```python
import math

import jax
import jax.numpy as jnp
import numpy as np
from jax import lax
from jax.experimental import pallas as pl
from jax.experimental.pallas import tpu as pltpu
from jax.sharding import PartitionSpec as P

D = 1280
HEAD_DIM = 64
EPS = 1e-06
HEADS = 5
ROWS = 512
TOK = 128
COLS = 320
TILE = 256
F32 = jnp.float32
BF16 = jnp.bfloat16
MESH = pl.DeviceIdType.MESH
DMA = pltpu.SemaphoreType.DMA
VMEM = pltpu.VMEM
IN_VMEM = pl.BlockSpec(memory_space=pltpu.VMEM)
IN_SMEM = pl.BlockSpec(memory_space=pltpu.SMEM)
IN_PLACE = pl.BlockSpec(memory_space=pl.ANY)
LIMIT = 60 << 20


def params(collective=None):
    if collective is None:
        return pltpu.CompilerParams(vmem_limit_bytes=LIMIT)
    return pltpu.CompilerParams(
        collective_id=collective, has_side_effects=True, vmem_limit_bytes=LIMIT
    )


def spot():
    row = lax.axis_index("row")
    return lax.axis_index("dp"), lax.div(row, 2), lax.rem(row, 2), lax.axis_index("col")


def wrap(i):
    return lax.rem(i + 8, 4)


def device(z, x, c, y):
    return (z, 2 * x + c, y)


def meet(others):
    barrier = pltpu.get_barrier_semaphore()
    for other in others:
        pl.semaphore_signal(barrier, inc=1, device_id=other, device_id_type=MESH)
    pl.semaphore_wait(barrier, len(others))


def remote(src, dst, send_sem, recv_sem, to):
    return pltpu.make_async_remote_copy(
        src_ref=src,
        dst_ref=dst,
        send_sem=send_sem,
        recv_sem=recv_sem,
        device_id=to,
        device_id_type=MESH,
    )


def dot_nn(a, b):
    return lax.dot_general(a, b, (((1,), (0,)), ((), ())), preferred_element_type=F32)


def dot_nt(a, b):
    return lax.dot_general(a, b, (((1,), (1,)), ((), ())), preferred_element_type=F32)


def dot_tn(a, b):
    return lax.dot_general(a, b, (((0,), (0,)), ((), ())), preferred_element_type=F32)


class Tally:
    def __init__(self, src, accs, parts, send, recv):
        z, x, c, y = spot()
        self.src, self.accs, self.parts, self.send, self.recv = src, accs, parts, send, recv
        self.peers = [
            [device(z, wrap(x + d), c, y) for d in (1, 2, 3)],
            [device(wrap(z + d), x, c, y) for d in (1, 2, 3)],
            [device(z, x, 1 - c, y)],
        ]
        self.copies = []

    def start(self, stage):
        src = self.src if stage == 0 else self.accs.at[stage - 1]
        for d, peer in enumerate(self.peers[stage]):
            at = 3 * stage + d
            copy = remote(src, self.parts.at[at], self.send.at[at], self.recv.at[at], peer)
            copy.start()
            self.copies.append(copy)

    def finish(self, stage):
        src = self.src if stage == 0 else self.accs.at[stage - 1]
        total = src[...]
        for d in range(len(self.peers[stage])):
            self.copies[3 * stage + d].wait_recv()
            total = total + self.parts[3 * stage + d]
        self.accs[stage] = total

    def close(self):
        for copy in self.copies:
            copy.wait_send()


TALLY_PEERS = 7


def tally_scratch(shape):
    return [
        VMEM((3,) + shape, F32),
        VMEM((7,) + shape, F32),
        DMA((7,)),
        DMA((7,)),
    ]


def torus(z, x, c, y):
    def first(d):
        return device(wrap(z + c * d), wrap(x + (1 - c) * d), c, y)

    def second(d):
        return device(wrap(z + (1 - c) * d), wrap(x + c * d), c, y)

    at_first = x * (1 - c) + z * c
    at_second = z * (1 - c) + x * c

    def block(d1, d2):
        a1, a2 = wrap(at_first + d1), wrap(at_second + d2)
        return (1 - c) * (a2 * 4 + a1) + c * (a1 * 4 + a2)

    return first, second, block


def half_mask(half):
    lane = lax.broadcasted_iota(jnp.int32, (1, 128), 1)
    return (lane < 64) if half == 0 else (lane >= 64)


def key_place(h):
    return h // 2, h % 2


def value_place(h):
    return (HEADS + h) // 2, (HEADS + h) % 2


def pad_head(wide, at, half):
    group = wide[:, 128 * at : 128 * at + 128]
    return jnp.where(half_mask(half), group, jnp.zeros_like(group))


LOW_ROWS = 48


class Ring:
    def __init__(self, own, slab, part, send, recv, h_send, h_recv):
        z, x, c, y = spot()
        self.first, self.second, self.block = torus(z, x, c, y)
        self.sibling = device(z, x, 1 - c, y)
        self.own, self.slab, self.part = own, slab, part
        self.send, self.recv, self.h_send, self.h_recv = send, recv, h_send, h_recv

    def ship(self, src, dst, at, to):
        return remote(src, dst, self.send.at[at], self.recv.at[at], to)

    def one(self, way):
        at = self.block(0, 0)
        return self.ship(self.own, self.slab(at), 0 if way > 0 else 1, self.first(way))

    def one_on(self, way):
        piece = self.part(self.block(-way, 0), way)
        return self.ship(piece, piece, 2 if way > 0 else 3, self.first(way))

    def two(self, d1, way):
        at = self.block(d1, 0)
        src = self.own if d1 == 0 else self.slab(at)
        return self.ship(src, self.slab(at), 4 + 4 * d1 + (0 if way > 0 else 1), self.second(way))

    def two_on(self, d1, way):
        piece = self.part(self.block(d1, -way), way)
        return self.ship(piece, piece, 6 + 4 * d1 + (0 if way > 0 else 1), self.second(way))

    def hand(self, d1, d2):
        at = self.block(d1, d2)
        src = self.own if d1 == 0 and d2 == 0 else self.slab(at)
        k = 4 * d1 + d2
        return remote(src, self.slab(at), self.h_send.at[k], self.h_recv.at[k], self.sibling)

    def open(self):
        self.one(1).start()
        self.one(-1).start()
        self.spread(0)

    def spread(self, d1):
        self.two(d1, 1).start()
        self.two(d1, -1).start()
        self.hand(d1, 0).start()

    def near(self):
        self.one(1).wait_recv()
        self.one_on(1).start()
        self.spread(3)
        self.one(-1).wait_recv()
        self.one_on(-1).start()
        self.spread(1)

    def far(self):
        self.one_on(1).wait_recv()
        self.one_on(-1).wait_recv()
        self.spread(2)

    def turn(self, d1):
        self.two(d1, 1).wait_recv()
        self.two_on(d1, 1).start()
        self.hand(d1, 3).start()
        self.two(d1, -1).wait_recv()
        self.two_on(d1, -1).start()
        self.hand(d1, 1).start()

    def end(self, d1):
        self.two_on(d1, 1).wait_recv()
        self.two_on(d1, -1).wait_recv()
        self.hand(d1, 2).start()

    def arrive(self):
        for d1 in range(4):
            for d2 in range(4):
                self.hand(d1, d2).wait_recv()

    def close(self):
        for way in (1, -1):
            self.one(way).wait_send()
            self.one_on(way).wait_send()
            for d1 in range(4):
                self.two(d1, way).wait_send()
                self.two_on(d1, way).wait_send()
        for d1 in range(4):
            for d2 in range(4):
                self.hand(d1, d2).wait_send()

    def steps(self):
        return [
            self.near,
            lambda: self.turn(0),
            self.far,
            lambda: self.turn(3),
            lambda: self.turn(1),
            lambda: self.end(0),
            lambda: self.turn(2),
            lambda: self.end(3),
            lambda: self.end(1),
            lambda: self.end(2),
        ]


def ring_scratch():
    return [DMA((20,)), DMA((20,)), DMA((16,)), DMA((16,))]


def rope_wide(cos_block, sin_block, turn):
    place = lax.axis_index("row")
    cos_at = turn[place, 0:1, :]
    sin_at = turn[place, 1:2, :]
    cosine = cos_block[...] * cos_at - sin_block[...] * sin_at
    sine = sin_block[...] * cos_at + cos_block[...] * sin_at
    lane = lax.broadcasted_iota(jnp.int32, sine.shape, 1)
    return cosine, jnp.where(lax.rem(lane, 64) < 32, -sine, sine)


def swap_halves(v):
    lane = lax.broadcasted_iota(jnp.int32, v.shape, 1)
    return jnp.where(lax.rem(lane, 64) < 32, pltpu.roll(v, 96, 1), pltpu.roll(v, 32, 1))


def over_heads(v):
    low = half_mask(0)
    left = jnp.sum(jnp.where(low, v, 0.0), axis=1, keepdims=True)
    right = jnp.sum(jnp.where(low, 0.0, v), axis=1, keepdims=True)
    return jnp.where(low, left, right)


def head_norm(raw, cosine, sine):
    scale = lax.rsqrt(over_heads(raw * raw) + EPS)
    return (raw * cosine + swap_halves(raw) * sine) * scale, scale


def front_kernel(
    hid,
    tea,
    query_w,
    key_w,
    value_w,
    out_w,
    gate_w,
    up_w,
    down_w,
    rates,
    count,
    seg,
    gains,
    cos_block,
    sin_block,
    turn,
    hid_out,
    hid_tok,
    tea_tok,
    rates_out,
    count_out,
    weights,
    raw_out,
    q_pad,
    win_out,
    att,
    out_t,
    lse,
    starts_out,
    hid_t,
    hid_n,
    tea_t,
    rate_buf,
    shard,
    shard_sib,
    own_block,
    w_first,
    win,
    o_acc,
    l_acc,
    y_send,
    y_recv,
    s_send,
    s_recv,
    local_sem,
    k_send,
    k_recv,
    a_send,
    a_recv,
    a_hsend,
    a_hrecv,
    b_send,
    b_recv,
    b_hsend,
    b_hrecv,
    t_accs,
    t_parts,
    t_send,
    t_recv,
):
    z, x, c, y = spot()
    place = 2 * x + c
    sibling = device(z, x, 1 - c, y)
    across = [device(z, x, c, wrap(y + d)) for d in (1, 2, 3)]
    tally = Tally(count, t_accs, t_parts, t_send, t_recv)

    shard[0] = jnp.concatenate(
        [query_w[:, 256:], out_w[...], query_w[:, :256], key_w[...], value_w[...]], axis=1
    )
    shard[1] = gate_w[...]
    shard[2] = up_w[...]
    shard[3] = down_w[...]
    meet(across + tally.peers[0] + tally.peers[1] + tally.peers[2])

    ours = pl.ds(pl.multiple_of(640 * c, 128), 640)
    theirs = pl.ds(pl.multiple_of(640 * (1 - c), 128), 640)

    def rows_at(at):
        return pl.multiple_of(80 * at, 16)

    ring_a = Ring(
        own_block.at[0],
        lambda at: w_first.at[pl.ds(rows_at(at), 80), ours],
        lambda at, way: w_first.at[
            pl.ds(rows_at(at), LOW_ROWS) if way > 0 else pl.ds(pl.multiple_of(80 * at + LOW_ROWS, 16), 80 - LOW_ROWS),
            ours,
        ],
        a_send,
        a_recv,
        a_hsend,
        a_hrecv,
    )
    ring_b = Ring(
        own_block.at[pl.ds(1, 3)],
        lambda at: weights.at[pl.ds(1, 3), pl.ds(rows_at(at), 80), ours],
        lambda at, way: weights.at[
            pl.ds(1, 3),
            pl.ds(rows_at(at), LOW_ROWS) if way > 0 else pl.ds(pl.multiple_of(80 * at + LOW_ROWS, 16), 80 - LOW_ROWS),
            ours,
        ],
        b_send,
        b_recv,
        b_hsend,
        b_hrecv,
    )
    head = remote(shard.at[:, :, theirs], shard_sib, s_send, s_recv, sibling)
    head.start()
    my_feats = pl.ds(pl.multiple_of(COLS * y, 64), COLS)
    hid_r = remote(hid, hid_t.at[my_feats], y_send.at[0], y_recv.at[0], across[0])
    hid_l = remote(hid, hid_t.at[my_feats], y_send.at[1], y_recv.at[1], across[2])
    hid_r.start()
    hid_l.start()
    hid_own = pltpu.make_async_copy(hid, hid_t.at[my_feats], local_sem.at[0])
    hid_own.start()
    tea_own = pltpu.make_async_copy(
        tea.at[:, pl.ds(pl.multiple_of(TOK * y, TOK), TOK)], tea_t.at[my_feats], local_sem.at[1]
    )
    tea_own.start()

    head.wait()
    for j in range(4):
        near = shard[j, :, ours].astype(F32)
        far = shard_sib[j].astype(F32)
        upper = jnp.where(c == 0, near, far)
        lower = jnp.where(c == 0, far, near)
        own_block[j] = jnp.concatenate([upper, lower], axis=0).astype(BF16)
    ring_a.open()
    own_at = ring_a.block(0, 0)
    own_a = pltpu.make_async_copy(own_block.at[0], ring_a.slab(own_at), local_sem.at[2])
    own_b = pltpu.make_async_copy(own_block.at[pl.ds(1, 3)], ring_b.slab(own_at), local_sem.at[3])
    own_a.start()
    own_b.start()
    tally.start(0)
    small = []
    for d in (1, 2, 3):
        rows = pl.ds(pl.multiple_of(TOK * wrap(y + d), TOK), TOK)
        pieces = ((tea.at[:, rows], tea_t.at[my_feats]), (rates, rate_buf.at[y]))
        for k, (src, dst) in enumerate(pieces):
            at = 4 + 2 * (d - 1) + k
            copy = remote(src, dst, y_send.at[at], y_recv.at[at], across[d - 1])
            copy.start()
            small.append(copy)
    rate_buf[y] = rates[...]

    first = jnp.sum((seg[...] < 1).astype(jnp.int32), axis=1, keepdims=True)
    second = jnp.sum((seg[...] < 2).astype(jnp.int32), axis=1, keepdims=True)
    query_seg = seg[:, pl.ds(pl.multiple_of(ROWS * place, ROWS), ROWS)]
    starts = jnp.where(query_seg == 0, 0, jnp.where(query_seg == 1, first, second))
    starts_out[...] = starts - (place - 4) * ROWS
    o_acc[...] = jnp.zeros_like(o_acc)
    l_acc[...] = jnp.zeros_like(l_acc)

    ring_a.near()
    ring_a.turn(0)
    ring_a.far()
    hid_r.wait_recv()
    hid_f_ref = hid_t.at[pl.ds(pl.multiple_of(COLS * wrap(y - 1), 64), 160)]
    hid_f = remote(hid_f_ref, hid_f_ref, y_send.at[2], y_recv.at[2], across[0])
    hid_f.start()
    hid_l.wait_recv()
    hid_g_ref = hid_t.at[pl.ds(pl.multiple_of(COLS * wrap(y + 1) + 160, 32), 160)]
    hid_g = remote(hid_g_ref, hid_g_ref, y_send.at[3], y_recv.at[3], across[2])
    hid_g.start()
    ring_a.turn(3)
    ring_a.turn(1)
    tally.finish(0)
    tally.start(1)
    ring_a.end(0)
    ring_a.turn(2)
    ring_a.end(3)
    ring_a.end(1)
    ring_a.end(2)
    tally.finish(1)
    tally.start(2)
    hid_own.wait()
    hid_f.wait_recv()
    hid_g.wait_recv()
    hid_save = pltpu.make_async_copy(hid_t, hid_out, local_sem.at[4])
    hid_save.start()
    for g in range(10):
        hid_n[:, 128 * g : 128 * g + 128] = hid_t[128 * g : 128 * g + 128, :].T
    own_a.wait()
    own_b.wait()
    ring_a.arrive()
    ring_b.open()
    w_save = pltpu.make_async_copy(w_first, weights.at[0], local_sem.at[5])
    w_save.start()

    cosine, sine = rope_wide(cos_block, sin_block, turn)
    raw = dot_nn(hid_n[...], w_first[:, 640:1280])
    for g in range(3):
        group = raw[:, 128 * g : 128 * g + 128]
        raw_out[3 + g] = group
        normed, _ = head_norm(group, cosine, sine)
        keys = normed * gains[:, 128 * g : 128 * g + 128]
        if g == 2:
            keys = jnp.where(half_mask(0), keys, group)
        win[4 * ROWS :, 128 * g : 128 * g + 128] = keys.astype(BF16)
    win[4 * ROWS :, 384:640] = raw[:, 384:640].astype(BF16)

    def slot(s):
        return win.at[pl.ds(pl.multiple_of(ROWS * s, ROWS), ROWS)]

    one = remote(slot(4), slot(2), k_send.at[0], k_recv.at[0], device(z, wrap(x + 1), c, y))
    two = remote(slot(4), slot(0), k_send.at[1], k_recv.at[1], device(z, wrap(x + 2), c, y))
    own = remote(slot(4), slot(3), k_send.at[2], k_recv.at[2], sibling)
    one_on = remote(slot(2), slot(1 + 2 * c), k_send.at[3], k_recv.at[3], sibling)
    two_on = remote(slot(0), slot(1), k_send.at[4], k_recv.at[4], sibling)

    @pl.when(x < 3)
    def _():
        one.start()

    @pl.when(x < 2)
    def _():
        two.start()

    @pl.when(c == 0)
    def _():
        own.start()

    root = math.sqrt(HEAD_DIM)
    for g, at in enumerate((384, 512, 0)):
        group = dot_nn(hid_n[...], w_first[:, at : at + 128])
        raw_out[g] = group
        normed, _ = head_norm(group, cosine, sine)
        scaled = (normed * gains[:, 128 * g : 128 * g + 128]).astype(BF16) * jnp.asarray(root, BF16)
        for half in range(2 if g < 2 else 1):
            q_pad[2 * g + half] = jnp.where(half_mask(half), scaled, jnp.zeros_like(scaled))
    hid_tok[...] = hid_n[pl.ds(pl.multiple_of(TOK * y, TOK), TOK), :]

    def tile(t):
        rows = pl.ds(pl.multiple_of(t * TILE, TILE), TILE)
        key_at = t * TILE + lax.broadcasted_iota(jnp.int32, (TILE, ROWS), 0)
        query_at = 4 * ROWS + lax.broadcasted_iota(jnp.int32, (TILE, ROWS), 1)
        allowed = (key_at >= starts_out[...]) & (key_at <= query_at)
        for h in range(HEADS):
            kg, _ = key_place(h)
            vg, vh = value_place(h)
            keys = win[rows, 128 * kg : 128 * kg + 128]
            values = win[rows, 128 * vg : 128 * vg + 128]
            scores = dot_nt(keys, q_pad[h])
            probs = jnp.where(allowed, jnp.exp(scores), 0.0)
            l_acc[h] += jnp.sum(probs.reshape(TILE // 8, 8, ROWS), axis=0)
            both = dot_tn(values, probs.astype(BF16))
            o_acc[h] += both[64 * vh : 64 * vh + 64, :]

    events = ring_b.steps()

    def step(i, carry):
        k = lax.div(i, 2)
        turned = k - 1 + 2 * lax.rem(k, 2)
        s = jnp.where(k == 0, 4, jnp.where(c == 1, 4 - k, 4 - turned))

        @pl.when((i == 2) & (c == 1))
        def _():
            own.wait_recv()

        @pl.when((x > 0) & (((i == 4) & (c == 1)) | ((i == 2) & (c == 0))))
        def _():
            one.wait_recv()
            one_on.start()

        @pl.when((x > 0) & (((i == 6) & (c == 1)) | ((i == 4) & (c == 0))))
        def _():
            one_on.wait_recv()

        @pl.when((x > 1) & (((i == 8) & (c == 1)) | ((i == 6) & (c == 0))))
        def _():
            two.wait_recv()

            @pl.when(c == 1)
            def _():
                two_on.start()

        @pl.when((x > 1) & (i == 8) & (c == 0))
        def _():
            two_on.wait_recv()

        for n, event in enumerate(events):

            @pl.when(i == n)
            def _(event=event):
                event()

        @pl.when(place + s >= 4)
        def _():
            tile(2 * s + lax.rem(i, 2))

        return carry

    lax.fori_loop(0, 10, step, 0)
    win_save = pltpu.make_async_copy(win, win_out, local_sem.at[6])
    win_save.start()
    for copy in small:
        copy.wait_recv()
    tea_own.wait()
    for g in range(10):
        tea_tok[:, 128 * g : 128 * g + 128] = tea_t[128 * g : 128 * g + 128, :].T
    rates_out[...] = jnp.concatenate([rate_buf[k] for k in range(4)], axis=1)
    tally.finish(2)
    count_out[...] = t_accs[2]
    for h in range(HEADS):
        total = jnp.sum(l_acc[h], axis=0, keepdims=True)
        lse[h] = jnp.broadcast_to(jnp.log(total), (8, ROWS))
        out_t[64 * h : 64 * h + 64, :] = o_acc[h] / total
    wide = jnp.concatenate([jnp.zeros((64, ROWS), F32), out_t[...]], axis=0)
    att[...] = wide.T.astype(BF16)
    ring_b.arrive()
    ring_a.close()
    ring_b.close()
    hid_save.wait()
    w_save.wait()
    win_save.wait()
    for copy in small + [hid_r, hid_l, hid_f, hid_g]:
        copy.wait_send()

    @pl.when(x < 3)
    def _():
        one.wait_send()

    @pl.when(x < 2)
    def _():
        two.wait_send()

    @pl.when(c == 0)
    def _():
        own.wait_send()

    @pl.when(x > 0)
    def _():
        one_on.wait_send()

    @pl.when((x > 1) & (c == 1))
    def _():
        two_on.wait_send()

    tally.close()


def rope_constants():
    inverse = np.exp(np.arange(32) * (-2.0 * math.log(10000.0) / HEAD_DIM))
    inverse = np.tile(inverse, 4)
    inside = np.arange(ROWS)[:, None] * inverse[None, :]
    at = (ROWS * np.arange(8))[:, None] * inverse[None, :]
    turn = np.stack([np.cos(at), np.sin(at)], axis=1)
    return [jnp.asarray(v, F32) for v in (np.cos(inside), np.sin(inside), turn)]


def front(hidden, teacher, shards, rates, count, segments, gains, ropes):
    sds = jax.ShapeDtypeStruct
    outs = [
        (sds((D, ROWS), BF16), IN_PLACE),
        (sds((TOK, D), BF16), IN_VMEM),
        (sds((TOK, D), BF16), IN_VMEM),
        (sds((2, D), F32), IN_VMEM),
        (sds((8, 128), F32), IN_VMEM),
        (sds((4, D, D), BF16), IN_PLACE),
        (sds((6, ROWS, 128), F32), IN_VMEM),
        (sds((HEADS, ROWS, 128), BF16), IN_VMEM),
        (sds((5 * ROWS, 2 * COLS), BF16), IN_PLACE),
        (sds((ROWS, 384), BF16), IN_VMEM),
        (sds((COLS, ROWS), F32), IN_VMEM),
        (sds((HEADS, 8, ROWS), F32), IN_VMEM),
        (sds((1, ROWS), jnp.int32), IN_VMEM),
    ]
    return pl.pallas_call(
        front_kernel,
        out_shape=tuple(o[0] for o in outs),
        in_specs=[IN_PLACE] * 2 + [IN_VMEM] * 14,
        out_specs=tuple(o[1] for o in outs),
        scratch_shapes=[
            VMEM((D, ROWS), BF16),
            VMEM((ROWS, D), BF16),
            VMEM((D, TOK), BF16),
            VMEM((4, 2, COLS), F32),
            VMEM((4, 40, D), BF16),
            VMEM((4, 40, 640), BF16),
            VMEM((4, 80, 640), BF16),
            VMEM((D, D), BF16),
            VMEM((5 * ROWS, 2 * COLS), BF16),
            VMEM((HEADS, 64, ROWS), F32),
            VMEM((HEADS, 8, ROWS), F32),
            DMA((10,)),
            DMA((10,)),
            DMA,
            DMA,
            DMA((7,)),
            DMA((5,)),
            DMA((5,)),
        ]
        + ring_scratch()
        + ring_scratch()
        + tally_scratch((8, 128)),
        compiler_params=params(0),
        name="front",
    )(hidden, teacher, *shards, rates, count, segments, gains, *ropes)


def attend_back_kernel(
    first_tile, starts, q_pad, win, out_t, lse, d_out, dq, d_win, d_pad, delta, q_acc
):
    for h in range(HEADS):
        d_pad[h] = pad_head(d_out, (h + 1) // 2, (h + 1) % 2)
    wide = d_out[...].astype(F32).T[64:, :] * out_t[...]
    for h in range(HEADS):
        delta[h] = jnp.broadcast_to(
            jnp.sum(wide[64 * h : 64 * (h + 1), :], axis=0, keepdims=True), (8, ROWS)
        )
    q_acc[...] = jnp.zeros_like(q_acc)

    def clear(t, carry):
        d_win[pl.ds(pl.multiple_of(t * TILE, TILE), TILE), :] = jnp.zeros((TILE, 2 * COLS), BF16)
        return carry

    lax.fori_loop(0, first_tile[0], clear, 0)

    def tile(t, diagonal):
        rows = pl.ds(pl.multiple_of(t * TILE, TILE), TILE)
        key_at = t * TILE + lax.broadcasted_iota(jnp.int32, (TILE, ROWS), 0)
        allowed = key_at >= starts[...]
        if diagonal:
            query_at = 4 * ROWS + lax.broadcasted_iota(jnp.int32, (TILE, ROWS), 1)
            allowed = allowed & (key_at <= query_at)
        sums = [None] * 5
        for h in range(HEADS):
            kg, kh = key_place(h)
            vg, _ = value_place(h)
            keys = win[rows, 128 * kg : 128 * kg + 128]
            values = win[rows, 128 * vg : 128 * vg + 128]
            scores = dot_nt(keys, q_pad[h])
            probs = jnp.where(allowed, jnp.exp(scores - lse[h, 0:1, :]), 0.0)
            prob_grad = dot_nt(values, d_pad[h])
            score_grad = (probs * (prob_grad - delta[h, 0:1, :])).astype(BF16)
            v_term = dot_nn(probs.astype(BF16), d_pad[h])
            k_term = dot_nn(score_grad, q_pad[h])
            for at, term in ((kg, k_term), (vg, v_term)):
                sums[at] = term if sums[at] is None else sums[at] + term
            both = dot_tn(keys, score_grad)
            q_acc[h] += both[64 * kh : 64 * kh + 64, :]
        for g in range(5):
            d_win[rows, 128 * g : 128 * g + 128] = sums[g].astype(BF16)

    def step(t, carry):
        tile(t, False)
        return carry

    lax.fori_loop(first_tile[0], 8, step, 0)
    for t in (8, 9):
        tile(t, True)
    wide = jnp.concatenate(
        [q_acc[h] for h in range(HEADS)] + [jnp.zeros((64, ROWS), F32)], axis=0
    )
    dq[...] = wide.T * math.sqrt(HEAD_DIM)


def attend_back(first_tile, starts, q_pad, win, out_t, lse, d_out):
    return pl.pallas_call(
        attend_back_kernel,
        out_shape=(
            jax.ShapeDtypeStruct((ROWS, 384), F32),
            jax.ShapeDtypeStruct((5 * ROWS, 2 * COLS), BF16),
        ),
        in_specs=[IN_SMEM] + [IN_VMEM] * 6,
        out_specs=(IN_VMEM,) * 2,
        scratch_shapes=[
            VMEM((HEADS, ROWS, 128), BF16),
            VMEM((HEADS, 8, ROWS), F32),
            VMEM((HEADS, 64, ROWS), F32),
        ],
        compiler_params=params(),
        name="attend_back",
    )(first_tile, starts, q_pad, win, out_t, lse, d_out)


def window_back_kernel(d_win, total, sib_one, sib_two, sib_own, one_buf, two_buf, got_one, got_two, send, recv):
    z, x, c, y = spot()
    sibling = device(z, x, 1 - c, y)
    meet([device(z, wrap(x + d), c, y) for d in (1, 2, 3)] + [sibling])
    hand_one = remote(d_win.at[3 - 2 * c], sib_one, send.at[0], recv.at[0], sibling)
    hand_two = remote(d_win.at[1], sib_two, send.at[1], recv.at[1], sibling)
    hand_own = remote(d_win.at[3], sib_own, send.at[2], recv.at[2], sibling)
    one = remote(one_buf, got_one, send.at[3], recv.at[3], device(z, wrap(x + 3), c, y))
    two = remote(two_buf, got_two, send.at[4], recv.at[4], device(z, wrap(x + 2), c, y))

    @pl.when((x > 1) & (c == 0))
    def _():
        hand_two.start()

    @pl.when(x > 0)
    def _():
        hand_one.start()

    @pl.when(c == 1)
    def _():
        hand_own.start()

    @pl.when(x > 1)
    def _():
        @pl.when(c == 1)
        def _():
            hand_two.wait_recv()
            two_buf[...] = (d_win[0].astype(F32) + sib_two[...].astype(F32)).astype(BF16)

        @pl.when(c == 0)
        def _():
            two_buf[...] = d_win[0]

        two.start()

    @pl.when(x > 0)
    def _():
        hand_one.wait_recv()
        one_buf[...] = (d_win[2].astype(F32) + sib_one[...].astype(F32)).astype(BF16)
        one.start()

    total[...] = d_win[4].astype(F32)

    @pl.when(c == 0)
    def _():
        hand_own.wait_recv()
        total[...] += sib_own[...].astype(F32)

    @pl.when(x < 3)
    def _():
        one.wait_recv()
        total[...] += got_one[...].astype(F32)

    @pl.when(x < 2)
    def _():
        two.wait_recv()
        total[...] += got_two[...].astype(F32)

    @pl.when(x > 1)
    def _():
        two.wait_send()

    @pl.when(x > 0)
    def _():
        one.wait_send()
        hand_one.wait_send()

    @pl.when((x > 1) & (c == 0))
    def _():
        hand_two.wait_send()

    @pl.when(c == 1)
    def _():
        hand_own.wait_send()


def window_back(d_win):
    one = (ROWS, 2 * COLS)
    return pl.pallas_call(
        window_back_kernel,
        out_shape=jax.ShapeDtypeStruct(one, F32),
        in_specs=[IN_VMEM],
        out_specs=IN_VMEM,
        scratch_shapes=[VMEM(one, BF16)] * 7 + [DMA((5,)), DMA((5,))],
        compiler_params=params(2),
        name="window_back",
    )(d_win)


def mix_forward(states, branch, alphas):
    branch_scale = lax.rsqrt(jnp.sum(branch * branch, axis=1, keepdims=True) + EPS)
    normed = branch * branch_scale
    mixed = states + alphas * (normed - states)
    mixed_scale = lax.rsqrt(jnp.sum(mixed * mixed, axis=1, keepdims=True) + EPS)
    return mixed * mixed_scale, normed, branch_scale, mixed_scale


def mix_backward(gradient, states, normed, branch_scale, mixed_out, mixed_scale, alphas):
    along = jnp.sum(mixed_out * gradient, axis=1, keepdims=True)
    mixed_grad = mixed_scale * (gradient - mixed_out * along)
    normed_grad = alphas * mixed_grad
    toward = jnp.sum(normed * normed_grad, axis=1, keepdims=True)
    branch_grad = branch_scale * (normed_grad - normed * toward)
    rate_grad = jnp.sum(mixed_grad * (normed - states), axis=0, keepdims=True)
    return (1.0 - alphas) * mixed_grad, branch_grad, rate_grad


def swiglu_parts(gate_raw, up_raw, gate_gain, up_gain):
    root = math.sqrt(D)
    g = gate_gain * gate_raw * root
    q = jax.nn.sigmoid(g)
    return g, q


def middle_kernel(
    att,
    hid_tok,
    tea,
    mask,
    count,
    rates,
    up_gain,
    gate_gain,
    weights,
    output,
    in_one,
    product,
    mlp_grad,
    gate_low,
    up_low,
    attn_grad,
    d_att,
    res_zero,
    small,
    w_out,
    w_gate,
    w_up,
    w_down,
    raw_gate,
    raw_up,
    send_buf,
    got_buf,
    own_part,
    out_buf,
    state,
    normed,
    scales,
    w_sem,
    ag_send,
    ag_recv,
    rs_send,
    rs_recv,
    o_send,
    o_recv,
):
    z, x, c, y = spot()
    peers = [device(z, x, c, wrap(y + d)) for d in range(4)]
    loads = [
        pltpu.make_async_copy(weights.at[0, :, pl.ds(0, 384)], w_out, w_sem.at[0]),
        pltpu.make_async_copy(weights.at[1], w_gate, w_sem.at[1]),
        pltpu.make_async_copy(weights.at[2], w_up, w_sem.at[2]),
        pltpu.make_async_copy(weights.at[3], w_down, w_sem.at[3]),
    ]
    for load in loads:
        load.start()
    meet(peers[1:])
    my_rows = pl.ds(pl.multiple_of(TOK * y, TOK), TOK)

    def rows_of(k):
        return pl.ds(pl.multiple_of(TOK * wrap(y - k), TOK), TOK)

    def back_to(k):
        return device(z, x, c, wrap(y - k))

    def scatter(stage, k):
        return remote(
            send_buf.at[stage, k],
            got_buf.at[stage, k],
            rs_send.at[stage, k],
            rs_recv.at[stage, k],
            back_to(k),
        )

    def spread(stage, src, k):
        return remote(
            src.at[my_rows],
            src.at[my_rows],
            ag_send.at[stage, k],
            ag_recv.at[stage, k],
            device(z, x, c, wrap(y + k)),
        )

    def give(stage, k, part):
        @pl.when(k == 0)
        def _():
            own_part[...] = part

        @pl.when(k > 0)
        def _():
            send_buf[stage, k] = part.astype(BF16)
            scatter(stage, k).start()

    def collect(stage):
        total = own_part[...]
        for k in (1, 2, 3):
            scatter(stage, k).wait_recv()
            total = total + got_buf[stage, k].astype(F32)
        return total

    def announce(stage, ref, value):
        ref[my_rows, :] = value.astype(BF16)
        for k in (2, 1, 3):
            spread(stage, ref, k).start()

    def each(body, stage=None, ref=None):
        def step(k, carry):
            if ref is not None:

                @pl.when(k > 0)
                def _():
                    spread(stage, ref, k).wait_recv()

            body(k)
            return carry

        lax.fori_loop(0, 4, step, 0)

    loads[0].wait()

    def project(k):
        give(0, k, dot_nt(att[rows_of(k), :], w_out[...]))

    each(project)
    attn = collect(0)
    states = hid_tok[...].astype(F32)
    one, normed_one, branch_one, scale_one = mix_forward(states, attn, rates[0:1, :])
    announce(0, in_one, one)
    state[0] = one
    normed[0] = normed_one
    scales[0] = jnp.broadcast_to(branch_one, (TOK, 128))
    scales[1] = jnp.broadcast_to(scale_one, (TOK, 128))
    for load in loads[1:]:
        load.wait()

    def feed(k):
        rows = rows_of(k)
        block = in_one[rows, :]
        gate_raw = dot_nn(block, w_gate[...])
        raw_gate[rows, :] = gate_raw
        up_raw = dot_nn(block, w_up[...])
        raw_up[rows, :] = up_raw
        g, q = swiglu_parts(gate_raw, up_raw, gate_gain[...], up_gain[...])
        low = (up_gain[...] * up_raw * (g * q)).astype(BF16)
        product[rows, :] = low
        give(1, k, dot_nt(low, w_down[...]))

    each(feed, 0, in_one)
    mlp = collect(1)
    one = state[0]
    two, normed_two, branch_two, scale_two = mix_forward(one, mlp, rates[1:2, :])
    for k in range(4):
        out_buf[k] = two[:, COLS * k : COLS * (k + 1)].astype(BF16)
    out_copies = []
    for k in (1, 2, 3):
        copy = remote(
            out_buf.at[wrap(y + k)],
            output.at[my_rows],
            o_send.at[k],
            o_recv.at[k],
            device(z, x, c, wrap(y + k)),
        )
        out_copies.append(copy)
    errors = two - tea[...].astype(F32)
    weight = mask[...]
    loss = jnp.sum(weight * errors * errors)
    factor = 16384 * math.sqrt(D) / count[0:1, 0:1]
    seed = factor * (weight * errors)
    res_one, mlp_back, rate_two = mix_backward(
        seed, one, normed_two, branch_two, two, scale_two, rates[1:2, :]
    )
    announce(1, mlp_grad, mlp_back)
    for copy in out_copies:
        copy.start()
    output[my_rows, :] = out_buf[y]
    small[...] = jnp.zeros_like(small)
    small[1:2, :] = rate_two
    small[4:5, :] = jnp.broadcast_to(loss, (1, D))
    state[1] = res_one

    def unfeed(k):
        rows = rows_of(k)
        grad = dot_nn(mlp_grad[rows, :], w_down[...])
        gate_raw = raw_gate[rows, :]
        up_raw = raw_up[rows, :]
        g, q = swiglu_parts(gate_raw, up_raw, gate_gain[...], up_gain[...])
        silu = g * q
        up_term = grad * silu
        slope = grad * up_gain[...] * up_raw * (q * (1.0 + g * (1.0 - q))) * math.sqrt(D)
        small[2:3, :] += jnp.sum(up_term * up_raw, axis=0, keepdims=True)
        small[3:4, :] += jnp.sum(slope * gate_raw, axis=0, keepdims=True)
        up_back = (up_term * up_gain[...]).astype(BF16)
        gate_back = (slope * gate_gain[...]).astype(BF16)
        up_low[rows, :] = up_back
        gate_low[rows, :] = gate_back
        give(2, k, dot_nt(gate_back, w_gate[...]) + dot_nt(up_back, w_up[...]))

    each(unfeed, 1, mlp_grad)
    grad_one = state[1] + collect(2)
    states = hid_tok[...].astype(F32)
    res, attn_back, rate_one = mix_backward(
        grad_one,
        states,
        normed[0],
        scales[0, :, 0:1],
        state[0],
        scales[1, :, 0:1],
        rates[0:1, :],
    )
    announce(2, attn_grad, attn_back)
    small[0:1, :] = rate_one
    for k in range(4):
        res_zero[k] = res[:, COLS * k : COLS * (k + 1)]

    def unproject(k):
        rows = rows_of(k)
        d_att[rows, :] = dot_nn(attn_grad[rows, :], w_out[...]).astype(BF16)

    each(unproject, 2, attn_grad)
    for k in (1, 2, 3):
        for stage in range(3):
            scatter(stage, k).wait_send()
        spread(0, in_one, k).wait_send()
        spread(1, mlp_grad, k).wait_send()
        spread(2, attn_grad, k).wait_send()
    for copy in out_copies:
        copy.wait()


def middle(att, hid_tok, tea, mask, count, rates, up_gain, gate_gain, weights):
    wide = jax.ShapeDtypeStruct((ROWS, D), BF16)
    return pl.pallas_call(
        middle_kernel,
        out_shape=(
            jax.ShapeDtypeStruct((ROWS, COLS), BF16),
            wide,
            wide,
            wide,
            wide,
            wide,
            wide,
            jax.ShapeDtypeStruct((ROWS, 384), BF16),
            jax.ShapeDtypeStruct((4, TOK, COLS), F32),
            jax.ShapeDtypeStruct((8, D), F32),
        ),
        in_specs=[IN_VMEM] * 8 + [IN_PLACE],
        out_specs=(IN_VMEM,) * 10,
        scratch_shapes=[
            VMEM((D, 384), BF16),
            VMEM((D, D), BF16),
            VMEM((D, D), BF16),
            VMEM((D, D), BF16),
            VMEM((ROWS, D), F32),
            VMEM((ROWS, D), F32),
            VMEM((3, 4, TOK, D), BF16),
            VMEM((3, 4, TOK, D), BF16),
            VMEM((TOK, D), F32),
            VMEM((4, TOK, COLS), BF16),
            VMEM((2, TOK, D), F32),
            VMEM((1, TOK, D), F32),
            VMEM((2, TOK, 128), F32),
            DMA((4,)),
            DMA((3, 4)),
            DMA((3, 4)),
            DMA((3, 4)),
            DMA((3, 4)),
            DMA((4,)),
            DMA((4,)),
        ],
        compiler_params=params(3),
        name="middle",
    )(att, hid_tok, tea, mask, count, rates, up_gain, gate_gain, weights)


def back_kernel(pack, res, side, weights, grad, side_out, w_buf, send_buf, got_buf, side_buf, w_sem, send, recv, s_send, s_recv):
    z, x, c, y = spot()
    load = pltpu.make_async_copy(weights.at[0], w_buf, w_sem)
    load.start()
    meet([device(z, x, c, wrap(y + d)) for d in (1, 2, 3)])
    my_rows = pl.ds(pl.multiple_of(TOK * y, TOK), TOK)

    def part(k):
        to = wrap(y + k)
        rows = pl.ds(pl.multiple_of(COLS * to, 64), COLS)
        return to, dot_nt(pack[...], w_buf[rows, :])

    load.wait()
    copies = []
    for k in (2, 1, 3):
        to, term = part(k)
        peer = device(z, x, c, to)
        small = remote(side.at[to], side_buf.at[k], s_send.at[k], s_recv.at[k], peer)
        small.start()
        grad[...] = term
        grad[my_rows, :] += res[to]
        send_buf[k] = grad[...].astype(BF16)
        copy = remote(send_buf.at[k], got_buf.at[k], send.at[k], recv.at[k], peer)
        copy.start()
        copies += [small, copy]
    _, term = part(0)
    grad[...] = term
    grad[my_rows, :] += res[y]
    for copy in copies:
        copy.wait_recv()
    total = grad[...]
    extra = side[y]
    for k in (1, 2, 3):
        total = total + got_buf[k].astype(F32)
        extra = extra + side_buf[k]
    grad[...] = total
    side_out[...] = extra
    for copy in copies:
        copy.wait_send()


def back_project(pack, res, side, weights):
    return pl.pallas_call(
        back_kernel,
        out_shape=(
            jax.ShapeDtypeStruct((ROWS, COLS), F32),
            jax.ShapeDtypeStruct((8, COLS), F32),
        ),
        in_specs=[IN_VMEM] * 3 + [IN_PLACE],
        out_specs=(IN_VMEM,) * 2,
        scratch_shapes=[
            VMEM((D, D), BF16),
            VMEM((4, ROWS, COLS), BF16),
            VMEM((4, ROWS, COLS), BF16),
            VMEM((4, 8, COLS), F32),
            DMA,
            DMA((4,)),
            DMA((4,)),
            DMA((4,)),
            DMA((4,)),
        ],
        compiler_params=params(4),
        name="back_project",
    )(pack, res, side, weights)


def reduce_kernel(
    g0,
    g1,
    g2,
    g3,
    side,
    out,
    side_out,
    own,
    sib,
    got_two,
    mid,
    got_one,
    fin,
    l_sem,
    h_send,
    h_recv,
    b_send,
    b_recv,
    a_send,
    a_recv,
    f_send,
    f_recv,
    t_accs,
    t_parts,
    t_send,
    t_recv,
):
    z, x, c, y = spot()
    first, second, _ = torus(z, x, c, y)
    at_first = x * (1 - c) + z * c
    sibling = device(z, x, 1 - c, y)
    tally = Tally(side, t_accs, t_parts, t_send, t_recv)
    meet(tally.peers[0] + tally.peers[1] + tally.peers[2])
    tally.start(0)
    order = (2, 1, 3, 0)

    @pl.when(c == 0)
    def _():
        for d in order:
            for j, (near, far) in enumerate(((g0, g2), (g1, g3))):
                remote(
                    far.at[:, wrap(x + d)], sib.at[j, d], h_send.at[j, d], h_recv.at[j, d], sibling
                ).start()
                pltpu.make_async_copy(near.at[wrap(z + d)], own.at[j, d], l_sem.at[j, d]).start()

    @pl.when(c == 1)
    def _():
        for d in order:
            for j, (near, far) in enumerate(((g2, g0), (g3, g1))):
                remote(
                    far.at[wrap(z + d)], sib.at[j, d], h_send.at[j, d], h_recv.at[j, d], sibling
                ).start()
                pltpu.make_async_copy(near.at[:, wrap(x + d)], own.at[j, d], l_sem.at[j, d]).start()

    def handed(j, d):
        return remote(g0.at[0], sib.at[j, d], h_send.at[j, d], h_recv.at[j, d], sibling)

    def fetched(j, d):
        return pltpu.make_async_copy(g0.at[0], own.at[j, d], l_sem.at[j, d])

    pairs = []
    for d in order:
        for j in range(2):
            fetched(j, d).wait()
            handed(j, d).wait_recv()

            def add(i, carry, j=j, d=d):
                own[j, d, i] = (own[j, d, i].astype(F32) + sib[j, d, i].astype(F32)).astype(BF16)
                return carry

            lax.fori_loop(0, 4, add, 0)
            if d:
                copy = remote(
                    own.at[j, d], got_two.at[j, d], b_send.at[j, d], b_recv.at[j, d], second(d)
                )
                copy.start()
                pairs.append(copy)
    tally.finish(0)
    tally.start(1)
    for copy in pairs:
        copy.wait_recv()

    def whole(j, at):
        total = own[j, 0, at].astype(F32)
        for d in (1, 2, 3):
            total = total + got_two[j, d, at].astype(F32)
        return total

    lasts = []
    for e in (2, 1, 3):
        for j in range(2):
            mid[j, e] = whole(j, wrap(at_first + e)).astype(BF16)
            copy = remote(
                mid.at[j, e], got_one.at[j, e], a_send.at[j, e], a_recv.at[j, e], first(e)
            )
            copy.start()
            lasts.append(copy)
    tally.finish(1)
    tally.start(2)
    for j in range(2):
        fin[j] = whole(j, at_first)
    for copy in lasts:
        copy.wait_recv()
    for j in range(2):
        total = fin[j]
        for e in (1, 2, 3):
            total = total + got_one[j, e].astype(F32)
        fin[j] = total
    theirs = pl.ds(pl.multiple_of(40 * (1 - c), 8), 40)
    ours = pl.ds(pl.multiple_of(40 * c, 8), 40)
    give = remote(fin.at[:, theirs], out.at[pl.ds(2 * c, 2)], f_send, f_recv, sibling)
    give.start()
    for j in range(2):
        out[2 * c + j] = fin[j, ours, :]
    tally.finish(2)
    side_out[...] = t_accs[2]
    give.wait()
    for copy in pairs + lasts:
        copy.wait_send()
    for j in range(2):
        for d in range(4):
            handed(j, d).wait_send()
    tally.close()


def reduce_all(grads, side):
    block = (80, D)
    return pl.pallas_call(
        reduce_kernel,
        out_shape=(
            jax.ShapeDtypeStruct((4, 40, D), F32),
            jax.ShapeDtypeStruct((8, D), F32),
        ),
        in_specs=[IN_PLACE] * 4 + [IN_VMEM],
        out_specs=(IN_VMEM,) * 2,
        scratch_shapes=[
            VMEM((2, 4, 4) + block, BF16),
            VMEM((2, 4, 4) + block, BF16),
            VMEM((2, 4, 4) + block, BF16),
            VMEM((2, 4) + block, BF16),
            VMEM((2, 4) + block, BF16),
            VMEM((2,) + block, F32),
            DMA((2, 4)),
            DMA((2, 4)),
            DMA((2, 4)),
            DMA((2, 4)),
            DMA((2, 4)),
            DMA((2, 4)),
            DMA((2, 4)),
            DMA,
            DMA,
        ]
        + tally_scratch((8, D)),
        compiler_params=params(5),
        name="reduce_all",
    )(*[g.reshape(4, 4, 80, D) for g in grads], side)


def rope_tables(positions, head_dim):
    half_dim = head_dim // 2
    indices = jnp.arange(half_dim, dtype=F32)
    inverse = jnp.exp(indices * (-2.0 * math.log(10000.0) / head_dim))
    angles = positions[:, None] * inverse[None, :]
    return (jnp.cos(angles), jnp.sin(angles))


def rotate(head_vals, cosine, sine_table):
    half_dim = head_vals.shape[-1] // 2
    first_half = head_vals[..., :half_dim]
    second_half = head_vals[..., half_dim:]
    cos_wide = cosine[:, None, :]
    sin_wide = sine_table[:, None, :]
    return jnp.concatenate(
        [
            first_half * cos_wide - second_half * sin_wide,
            second_half * cos_wide + first_half * sin_wide,
        ],
        axis=-1,
    )


def head_map(raw_proj, gains, cosine, sine_table, head_dim):
    row_count = raw_proj.shape[0]
    head_vals = rotate(raw_proj.reshape(row_count, -1, head_dim), cosine, sine_table)
    normed = head_vals * lax.rsqrt(jnp.sum(head_vals * head_vals, axis=-1, keepdims=True) + EPS)
    return normed.reshape(row_count, -1) * gains


def weight_dot(inputs_low, gradient):
    return lax.dot_general(
        inputs_low, gradient, (((0,), (0,)), ((), ())), preferred_element_type=F32
    ).astype(BF16)


def shards(
    hidden,
    teacher,
    valid_mask,
    segments,
    query_weight,
    key_weight,
    value_weight,
    out_weight,
    gate_weight,
    up_weight,
    down_weight,
    attention_rate,
    feedforward_rate,
    score_gain,
    up_gain,
    gate_gain,
):
    place = lax.axis_index("row")
    col = lax.axis_index("col")
    token_mask = valid_mask.astype(F32)
    count = jnp.broadcast_to(jnp.sum(token_mask), (8, 128))
    rates = jnp.stack([attention_rate, feedforward_rate])
    gains = jnp.pad(score_gain, (0, 64)).reshape(1, 384)
    ropes = rope_constants()
    projections = (query_weight, key_weight, value_weight, out_weight.T)
    projections += (gate_weight, up_weight, down_weight.T)
    (
        hid_t,
        hid_tok,
        tea_tok,
        rates_full,
        count_all,
        weights,
        raw,
        q_pad,
        win,
        att,
        out_t,
        lse,
        starts,
    ) = front(hidden.T, teacher.T, projections, rates, count, segments, gains, ropes)
    first_tile = (starts[0, 0] // TILE).reshape(1)
    query_raw = jnp.concatenate([raw[0], raw[1], raw[2, :, :64]], axis=1)
    key_raw = jnp.concatenate([raw[3], raw[4], raw[5, :, :64]], axis=1)
    offset = place * ROWS
    query_pos = offset + jnp.arange(ROWS, dtype=jnp.int32)
    cosine, sine_table = rope_tables(query_pos.astype(F32), HEAD_DIM)

    mask_tok = lax.dynamic_slice_in_dim(token_mask, col * TOK, TOK).reshape(TOK, 1)
    (
        output,
        in_one,
        product,
        mlp_grad,
        gate_low,
        up_low,
        attn_grad,
        d_att,
        res_zero,
        small,
    ) = middle(
        att,
        hid_tok,
        tea_tok,
        mask_tok,
        count_all,
        rates_full,
        up_gain.reshape(1, -1),
        gate_gain.reshape(1, -1),
        weights,
    )
    gate_grad = weight_dot(in_one, gate_low)
    up_grad = weight_dot(in_one, up_low)
    down_grad = weight_dot(mlp_grad, product)

    dq, d_win = attend_back(first_tile, starts, q_pad, win, out_t, lse, d_att)
    d_kv = window_back(d_win.reshape(5, ROWS, 2 * COLS))

    def head_local(raw_proj, gains):
        return head_map(raw_proj, gains, cosine, sine_table, HEAD_DIM)

    _, query_back = jax.vjp(head_local, query_raw, score_gain)
    query_raw_grad, gain_from_query = query_back(dq[:, :COLS])
    _, key_back = jax.vjp(head_local, key_raw, score_gain)
    key_raw_grad, gain_from_key = key_back(d_kv[:, :COLS])
    query_low = query_raw_grad.astype(BF16)
    pack = jnp.concatenate(
        [
            query_low[:, 256:],
            jnp.zeros((ROWS, COLS), BF16),
            query_low[:, :256],
            key_raw_grad.astype(BF16),
            d_kv[:, COLS:].astype(BF16),
        ],
        axis=1,
    )
    side = jnp.concatenate([small[0:2], small[4:5], jnp.zeros((5, D), F32)], axis=0)
    side = side.reshape(8, 4, COLS).transpose(1, 0, 2)
    hidden_grad, side = back_project(pack, res_zero, side, weights)
    first_grad = (
        lax.dot_general(hid_t, pack, (((1,), (0,)), ((), ())), preferred_element_type=F32)
        + jnp.pad(
            lax.dot_general(attn_grad, att, (((0,), (0,)), ((), ())), preferred_element_type=F32),
            ((0, 0), (0, D - 384)),
        )
    ).astype(BF16)
    sums = jnp.concatenate(
        [
            small[2:4],
            jnp.concatenate(
                [gain_from_query + gain_from_key, side[0], side[1], side[2]], axis=0
            ).reshape(1, D),
            jnp.zeros((5, D), F32),
        ],
        axis=0,
    )
    grads, sums = reduce_all((first_grad, gate_grad, up_grad, down_grad), sums)
    head = grads[0]
    return (
        sums[2, 960] / count_all[0, 0],
        output,
        hidden_grad,
        jnp.concatenate([head[:, 384:640], head[:, :64]], axis=1),
        head[:, 640:960],
        head[:, 960:],
        head[:, 64:384].T,
        grads[1],
        grads[2],
        grads[3].T,
        sums[2, 320:640],
        sums[2, 640:960],
        sums[2, :320],
        sums[0],
        sums[1],
    )


def solution(mesh):
    both = P(("dp", "row"), "col")
    turned = P("col", ("dp", "row"))
    vector = P("col")
    in_specs = (both, both, P(("dp", "row")), P("dp", None), both, both, both, turned, both, both)
    in_specs += (turned,) + (vector,) * 5
    out_specs = (P(), both, both, both, both, both, turned, both, both, turned) + (vector,) * 5
    return jax.shard_map(shards, mesh=mesh, in_specs=in_specs, out_specs=out_specs, check_vma=False)
```

```python
import math

import jax
import jax.numpy as jnp
import numpy as np
from jax import lax
from jax.experimental import pallas as pl
from jax.experimental.pallas import tpu as pltpu
from jax.sharding import PartitionSpec as P

D = 1280
HEAD_DIM = 64
EPS = 1e-06
HEADS = 5
ROWS = 512
TOK = 128
COLS = 320
TILE = 256
F32 = jnp.float32
BF16 = jnp.bfloat16
MESH = pl.DeviceIdType.MESH
DMA = pltpu.SemaphoreType.DMA
VMEM = pltpu.VMEM
IN_VMEM = pl.BlockSpec(memory_space=pltpu.VMEM)
IN_SMEM = pl.BlockSpec(memory_space=pltpu.SMEM)
IN_PLACE = pl.BlockSpec(memory_space=pl.ANY)
LIMIT = 60 << 20


def params(collective=None):
    if collective is None:
        return pltpu.CompilerParams(vmem_limit_bytes=LIMIT)
    return pltpu.CompilerParams(
        collective_id=collective, has_side_effects=True, vmem_limit_bytes=LIMIT
    )


def spot():
    row = lax.axis_index("row")
    return lax.axis_index("dp"), lax.div(row, 2), lax.rem(row, 2), lax.axis_index("col")


def wrap(i):
    return lax.rem(i + 8, 4)


def device(z, x, c, y):
    return (z, 2 * x + c, y)


def meet(others):
    barrier = pltpu.get_barrier_semaphore()
    for other in others:
        pl.semaphore_signal(barrier, inc=1, device_id=other, device_id_type=MESH)
    pl.semaphore_wait(barrier, len(others))


def remote(src, dst, send_sem, recv_sem, to):
    return pltpu.make_async_remote_copy(
        src_ref=src,
        dst_ref=dst,
        send_sem=send_sem,
        recv_sem=recv_sem,
        device_id=to,
        device_id_type=MESH,
    )


def dot_nn(a, b):
    return lax.dot_general(a, b, (((1,), (0,)), ((), ())), preferred_element_type=F32)


def dot_nt(a, b):
    return lax.dot_general(a, b, (((1,), (1,)), ((), ())), preferred_element_type=F32)


def dot_tn(a, b):
    return lax.dot_general(a, b, (((0,), (0,)), ((), ())), preferred_element_type=F32)


class Tally:
    def __init__(self, src, accs, parts, send, recv):
        z, x, c, y = spot()
        self.src, self.accs, self.parts, self.send, self.recv = src, accs, parts, send, recv
        self.peers = [
            [device(z, wrap(x + d), c, y) for d in (1, 2, 3)],
            [device(wrap(z + d), x, c, y) for d in (1, 2, 3)],
            [device(z, x, 1 - c, y)],
        ]
        self.copies = []

    def start(self, stage):
        src = self.src if stage == 0 else self.accs.at[stage - 1]
        for d, peer in enumerate(self.peers[stage]):
            at = 3 * stage + d
            copy = remote(src, self.parts.at[at], self.send.at[at], self.recv.at[at], peer)
            copy.start()
            self.copies.append(copy)

    def finish(self, stage):
        src = self.src if stage == 0 else self.accs.at[stage - 1]
        total = src[...]
        for d in range(len(self.peers[stage])):
            self.copies[3 * stage + d].wait_recv()
            total = total + self.parts[3 * stage + d]
        self.accs[stage] = total

    def close(self):
        for copy in self.copies:
            copy.wait_send()


TALLY_PEERS = 7


def tally_scratch(shape):
    return [
        VMEM((3,) + shape, F32),
        VMEM((7,) + shape, F32),
        DMA((7,)),
        DMA((7,)),
    ]


def torus(z, x, c, y):
    def first(d):
        return device(wrap(z + c * d), wrap(x + (1 - c) * d), c, y)

    def second(d):
        return device(wrap(z + (1 - c) * d), wrap(x + c * d), c, y)

    at_first = x * (1 - c) + z * c
    at_second = z * (1 - c) + x * c

    def block(d1, d2):
        a1, a2 = wrap(at_first + d1), wrap(at_second + d2)
        return (1 - c) * (a2 * 4 + a1) + c * (a1 * 4 + a2)

    return first, second, block


def half_mask(half):
    lane = lax.broadcasted_iota(jnp.int32, (1, 128), 1)
    return (lane < 64) if half == 0 else (lane >= 64)


def key_place(h):
    return h // 2, h % 2


def value_place(h):
    return (HEADS + h) // 2, (HEADS + h) % 2


def pad_head(wide, at, half):
    group = wide[:, 128 * at : 128 * at + 128]
    return jnp.where(half_mask(half), group, jnp.zeros_like(group))


LOW_ROWS = 48


class Ring:
    def __init__(self, own, slab, part, send, recv, h_send, h_recv):
        z, x, c, y = spot()
        self.first, self.second, self.block = torus(z, x, c, y)
        self.sibling = device(z, x, 1 - c, y)
        self.own, self.slab, self.part = own, slab, part
        self.send, self.recv, self.h_send, self.h_recv = send, recv, h_send, h_recv

    def ship(self, src, dst, at, to):
        return remote(src, dst, self.send.at[at], self.recv.at[at], to)

    def one(self, way):
        at = self.block(0, 0)
        return self.ship(self.own, self.slab(at), 0 if way > 0 else 1, self.first(way))

    def one_on(self, way):
        piece = self.part(self.block(-way, 0), way)
        return self.ship(piece, piece, 2 if way > 0 else 3, self.first(way))

    def two(self, d1, way):
        at = self.block(d1, 0)
        src = self.own if d1 == 0 else self.slab(at)
        return self.ship(src, self.slab(at), 4 + 4 * d1 + (0 if way > 0 else 1), self.second(way))

    def two_on(self, d1, way):
        piece = self.part(self.block(d1, -way), way)
        return self.ship(piece, piece, 6 + 4 * d1 + (0 if way > 0 else 1), self.second(way))

    def hand(self, d1, d2):
        at = self.block(d1, d2)
        src = self.own if d1 == 0 and d2 == 0 else self.slab(at)
        k = 4 * d1 + d2
        return remote(src, self.slab(at), self.h_send.at[k], self.h_recv.at[k], self.sibling)

    def open(self):
        self.one(1).start()
        self.one(-1).start()
        self.spread(0)

    def spread(self, d1):
        self.two(d1, 1).start()
        self.two(d1, -1).start()
        self.hand(d1, 0).start()

    def near(self):
        self.one(1).wait_recv()
        self.one_on(1).start()
        self.spread(3)
        self.one(-1).wait_recv()
        self.one_on(-1).start()
        self.spread(1)

    def far(self):
        self.one_on(1).wait_recv()
        self.one_on(-1).wait_recv()
        self.spread(2)

    def turn(self, d1):
        self.two(d1, 1).wait_recv()
        self.two_on(d1, 1).start()
        self.hand(d1, 3).start()
        self.two(d1, -1).wait_recv()
        self.two_on(d1, -1).start()
        self.hand(d1, 1).start()

    def end(self, d1):
        self.two_on(d1, 1).wait_recv()
        self.two_on(d1, -1).wait_recv()
        self.hand(d1, 2).start()

    def arrive(self):
        for d1 in range(4):
            for d2 in range(4):
                self.hand(d1, d2).wait_recv()

    def close(self):
        for way in (1, -1):
            self.one(way).wait_send()
            self.one_on(way).wait_send()
            for d1 in range(4):
                self.two(d1, way).wait_send()
                self.two_on(d1, way).wait_send()
        for d1 in range(4):
            for d2 in range(4):
                self.hand(d1, d2).wait_send()

    def steps(self):
        return [
            self.near,
            lambda: self.turn(0),
            self.far,
            lambda: self.turn(3),
            lambda: self.turn(1),
            lambda: self.end(0),
            lambda: self.turn(2),
            lambda: self.end(3),
            lambda: self.end(1),
            lambda: self.end(2),
        ]


def ring_scratch():
    return [DMA((20,)), DMA((20,)), DMA((16,)), DMA((16,))]


def rope_wide(cos_block, sin_block, turn):
    place = lax.axis_index("row")
    cos_at = turn[place, 0:1, :]
    sin_at = turn[place, 1:2, :]
    cosine = cos_block[...] * cos_at - sin_block[...] * sin_at
    sine = sin_block[...] * cos_at + cos_block[...] * sin_at
    lane = lax.broadcasted_iota(jnp.int32, sine.shape, 1)
    return cosine, jnp.where(lax.rem(lane, 64) < 32, -sine, sine)


def swap_halves(v):
    lane = lax.broadcasted_iota(jnp.int32, v.shape, 1)
    return jnp.where(lax.rem(lane, 64) < 32, pltpu.roll(v, 96, 1), pltpu.roll(v, 32, 1))


def over_heads(v):
    low = half_mask(0)
    left = jnp.sum(jnp.where(low, v, 0.0), axis=1, keepdims=True)
    right = jnp.sum(jnp.where(low, 0.0, v), axis=1, keepdims=True)
    return jnp.where(low, left, right)


def head_norm(raw, cosine, sine):
    scale = lax.rsqrt(over_heads(raw * raw) + EPS)
    return (raw * cosine + swap_halves(raw) * sine) * scale, scale


def front_kernel(
    hid,
    tea,
    query_w,
    key_w,
    value_w,
    out_w,
    gate_w,
    up_w,
    down_w,
    rates,
    count,
    seg,
    gains,
    cos_block,
    sin_block,
    turn,
    hid_out,
    hid_tok,
    tea_tok,
    rates_out,
    count_out,
    weights,
    raw_out,
    q_pad,
    win_out,
    att,
    out_t,
    lse,
    starts_out,
    hid_t,
    hid_n,
    tea_t,
    rate_buf,
    shard,
    shard_sib,
    own_block,
    w_first,
    win,
    o_acc,
    l_acc,
    y_send,
    y_recv,
    s_send,
    s_recv,
    local_sem,
    k_send,
    k_recv,
    a_send,
    a_recv,
    a_hsend,
    a_hrecv,
    b_send,
    b_recv,
    b_hsend,
    b_hrecv,
    t_accs,
    t_parts,
    t_send,
    t_recv,
):
    z, x, c, y = spot()
    place = 2 * x + c
    sibling = device(z, x, 1 - c, y)
    across = [device(z, x, c, wrap(y + d)) for d in (1, 2, 3)]
    tally = Tally(count, t_accs, t_parts, t_send, t_recv)

    shard[0] = jnp.concatenate(
        [query_w[:, 256:], out_w[...], query_w[:, :256], key_w[...], value_w[...]], axis=1
    )
    shard[1] = gate_w[...]
    shard[2] = up_w[...]
    shard[3] = down_w[...]
    meet(across + tally.peers[0] + tally.peers[1] + tally.peers[2])

    ours = pl.ds(pl.multiple_of(640 * c, 128), 640)
    theirs = pl.ds(pl.multiple_of(640 * (1 - c), 128), 640)

    def rows_at(at):
        return pl.multiple_of(80 * at, 16)

    ring_a = Ring(
        own_block.at[0],
        lambda at: w_first.at[pl.ds(rows_at(at), 80), ours],
        lambda at, way: w_first.at[
            pl.ds(rows_at(at), LOW_ROWS) if way > 0 else pl.ds(pl.multiple_of(80 * at + LOW_ROWS, 16), 80 - LOW_ROWS),
            ours,
        ],
        a_send,
        a_recv,
        a_hsend,
        a_hrecv,
    )
    ring_b = Ring(
        own_block.at[pl.ds(1, 3)],
        lambda at: weights.at[pl.ds(1, 3), pl.ds(rows_at(at), 80), ours],
        lambda at, way: weights.at[
            pl.ds(1, 3),
            pl.ds(rows_at(at), LOW_ROWS) if way > 0 else pl.ds(pl.multiple_of(80 * at + LOW_ROWS, 16), 80 - LOW_ROWS),
            ours,
        ],
        b_send,
        b_recv,
        b_hsend,
        b_hrecv,
    )
    head = remote(shard.at[:, :, theirs], shard_sib, s_send, s_recv, sibling)
    head.start()
    my_feats = pl.ds(pl.multiple_of(COLS * y, 64), COLS)
    hid_r = remote(hid, hid_t.at[my_feats], y_send.at[0], y_recv.at[0], across[0])
    hid_l = remote(hid, hid_t.at[my_feats], y_send.at[1], y_recv.at[1], across[2])
    hid_r.start()
    hid_l.start()
    hid_own = pltpu.make_async_copy(hid, hid_t.at[my_feats], local_sem.at[0])
    hid_own.start()
    tea_own = pltpu.make_async_copy(
        tea.at[:, pl.ds(pl.multiple_of(TOK * y, TOK), TOK)], tea_t.at[my_feats], local_sem.at[1]
    )
    tea_own.start()

    head.wait()
    for j in range(4):
        near = shard[j, :, ours].astype(F32)
        far = shard_sib[j].astype(F32)
        upper = jnp.where(c == 0, near, far)
        lower = jnp.where(c == 0, far, near)
        own_block[j] = jnp.concatenate([upper, lower], axis=0).astype(BF16)
    ring_a.open()
    own_at = ring_a.block(0, 0)
    own_a = pltpu.make_async_copy(own_block.at[0], ring_a.slab(own_at), local_sem.at[2])
    own_b = pltpu.make_async_copy(own_block.at[pl.ds(1, 3)], ring_b.slab(own_at), local_sem.at[3])
    own_a.start()
    own_b.start()
    tally.start(0)
    small = []
    for d in (1, 2, 3):
        rows = pl.ds(pl.multiple_of(TOK * wrap(y + d), TOK), TOK)
        pieces = ((tea.at[:, rows], tea_t.at[my_feats]), (rates, rate_buf.at[y]))
        for k, (src, dst) in enumerate(pieces):
            at = 4 + 2 * (d - 1) + k
            copy = remote(src, dst, y_send.at[at], y_recv.at[at], across[d - 1])
            copy.start()
            small.append(copy)
    rate_buf[y] = rates[...]

    first = jnp.sum((seg[...] < 1).astype(jnp.int32), axis=1, keepdims=True)
    second = jnp.sum((seg[...] < 2).astype(jnp.int32), axis=1, keepdims=True)
    query_seg = seg[:, pl.ds(pl.multiple_of(ROWS * place, ROWS), ROWS)]
    starts = jnp.where(query_seg == 0, 0, jnp.where(query_seg == 1, first, second))
    starts_out[...] = starts - (place - 4) * ROWS
    o_acc[...] = jnp.zeros_like(o_acc)
    l_acc[...] = jnp.zeros_like(l_acc)

    ring_a.near()
    ring_a.turn(0)
    ring_a.far()
    hid_r.wait_recv()
    hid_f_ref = hid_t.at[pl.ds(pl.multiple_of(COLS * wrap(y - 1), 64), 160)]
    hid_f = remote(hid_f_ref, hid_f_ref, y_send.at[2], y_recv.at[2], across[0])
    hid_f.start()
    hid_l.wait_recv()
    hid_g_ref = hid_t.at[pl.ds(pl.multiple_of(COLS * wrap(y + 1) + 160, 32), 160)]
    hid_g = remote(hid_g_ref, hid_g_ref, y_send.at[3], y_recv.at[3], across[2])
    hid_g.start()
    ring_a.turn(3)
    ring_a.turn(1)
    tally.finish(0)
    tally.start(1)
    ring_a.end(0)
    ring_a.turn(2)
    ring_a.end(3)
    ring_a.end(1)
    ring_a.end(2)
    tally.finish(1)
    tally.start(2)
    hid_own.wait()
    hid_f.wait_recv()
    hid_g.wait_recv()
    hid_save = pltpu.make_async_copy(hid_t, hid_out, local_sem.at[4])
    hid_save.start()
    for g in range(10):
        hid_n[:, 128 * g : 128 * g + 128] = hid_t[128 * g : 128 * g + 128, :].T
    own_a.wait()
    own_b.wait()
    ring_a.arrive()
    ring_b.open()
    w_save = pltpu.make_async_copy(w_first, weights.at[0], local_sem.at[5])
    w_save.start()

    cosine, sine = rope_wide(cos_block, sin_block, turn)
    raw = dot_nn(hid_n[...], w_first[:, 640:1280])
    for g in range(3):
        group = raw[:, 128 * g : 128 * g + 128]
        raw_out[3 + g] = group
        normed, _ = head_norm(group, cosine, sine)
        keys = normed * gains[:, 128 * g : 128 * g + 128]
        if g == 2:
            keys = jnp.where(half_mask(0), keys, group)
        win[4 * ROWS :, 128 * g : 128 * g + 128] = keys.astype(BF16)
    win[4 * ROWS :, 384:640] = raw[:, 384:640].astype(BF16)

    def slot(s):
        return win.at[pl.ds(pl.multiple_of(ROWS * s, ROWS), ROWS)]

    one = remote(slot(4), slot(2), k_send.at[0], k_recv.at[0], device(z, wrap(x + 1), c, y))
    two = remote(slot(4), slot(0), k_send.at[1], k_recv.at[1], device(z, wrap(x + 2), c, y))
    own = remote(slot(4), slot(3), k_send.at[2], k_recv.at[2], sibling)
    one_on = remote(slot(2), slot(1 + 2 * c), k_send.at[3], k_recv.at[3], sibling)
    two_on = remote(slot(0), slot(1), k_send.at[4], k_recv.at[4], sibling)

    @pl.when(x < 3)
    def _():
        one.start()

    @pl.when(x < 2)
    def _():
        two.start()

    @pl.when(c == 0)
    def _():
        own.start()

    root = math.sqrt(HEAD_DIM)
    for g, at in enumerate((384, 512, 0)):
        group = dot_nn(hid_n[...], w_first[:, at : at + 128])
        raw_out[g] = group
        normed, _ = head_norm(group, cosine, sine)
        scaled = (normed * gains[:, 128 * g : 128 * g + 128]).astype(BF16) * jnp.asarray(root, BF16)
        for half in range(2 if g < 2 else 1):
            q_pad[2 * g + half] = jnp.where(half_mask(half), scaled, jnp.zeros_like(scaled))
    hid_tok[...] = hid_n[pl.ds(pl.multiple_of(TOK * y, TOK), TOK), :]

    def tile(t):
        rows = pl.ds(pl.multiple_of(t * TILE, TILE), TILE)
        key_at = t * TILE + lax.broadcasted_iota(jnp.int32, (TILE, ROWS), 0)
        query_at = 4 * ROWS + lax.broadcasted_iota(jnp.int32, (TILE, ROWS), 1)
        allowed = (key_at >= starts_out[...]) & (key_at <= query_at)
        for h in range(HEADS):
            kg, _ = key_place(h)
            vg, vh = value_place(h)
            keys = win[rows, 128 * kg : 128 * kg + 128]
            values = win[rows, 128 * vg : 128 * vg + 128]
            scores = dot_nt(keys, q_pad[h])
            probs = jnp.where(allowed, jnp.exp(scores), 0.0)
            l_acc[h] += jnp.sum(probs.reshape(TILE // 8, 8, ROWS), axis=0)
            both = dot_tn(values, probs.astype(BF16))
            o_acc[h] += both[64 * vh : 64 * vh + 64, :]

    events = ring_b.steps()

    def step(i, carry):
        k = lax.div(i, 2)
        turned = k - 1 + 2 * lax.rem(k, 2)
        s = jnp.where(k == 0, 4, jnp.where(c == 1, 4 - k, 4 - turned))

        @pl.when((i == 2) & (c == 1))
        def _():
            own.wait_recv()

        @pl.when((x > 0) & (((i == 4) & (c == 1)) | ((i == 2) & (c == 0))))
        def _():
            one.wait_recv()
            one_on.start()

        @pl.when((x > 0) & (((i == 6) & (c == 1)) | ((i == 4) & (c == 0))))
        def _():
            one_on.wait_recv()

        @pl.when((x > 1) & (((i == 8) & (c == 1)) | ((i == 6) & (c == 0))))
        def _():
            two.wait_recv()

            @pl.when(c == 1)
            def _():
                two_on.start()

        @pl.when((x > 1) & (i == 8) & (c == 0))
        def _():
            two_on.wait_recv()

        for n, event in enumerate(events):

            @pl.when(i == n)
            def _(event=event):
                event()

        @pl.when(place + s >= 4)
        def _():
            tile(2 * s + lax.rem(i, 2))

        return carry

    lax.fori_loop(0, 10, step, 0)
    win_save = pltpu.make_async_copy(win, win_out, local_sem.at[6])
    win_save.start()
    for copy in small:
        copy.wait_recv()
    tea_own.wait()
    for g in range(10):
        tea_tok[:, 128 * g : 128 * g + 128] = tea_t[128 * g : 128 * g + 128, :].T
    rates_out[...] = jnp.concatenate([rate_buf[k] for k in range(4)], axis=1)
    tally.finish(2)
    count_out[...] = t_accs[2]
    for h in range(HEADS):
        total = jnp.sum(l_acc[h], axis=0, keepdims=True)
        lse[h] = jnp.broadcast_to(jnp.log(total), (8, ROWS))
        out_t[64 * h : 64 * h + 64, :] = o_acc[h] / total
    wide = jnp.concatenate([jnp.zeros((64, ROWS), F32), out_t[...]], axis=0)
    att[...] = wide.T.astype(BF16)
    ring_b.arrive()
    ring_a.close()
    ring_b.close()
    hid_save.wait()
    w_save.wait()
    win_save.wait()
    for copy in small + [hid_r, hid_l, hid_f, hid_g]:
        copy.wait_send()

    @pl.when(x < 3)
    def _():
        one.wait_send()

    @pl.when(x < 2)
    def _():
        two.wait_send()

    @pl.when(c == 0)
    def _():
        own.wait_send()

    @pl.when(x > 0)
    def _():
        one_on.wait_send()

    @pl.when((x > 1) & (c == 1))
    def _():
        two_on.wait_send()

    tally.close()


def rope_constants():
    inverse = np.exp(np.arange(32) * (-2.0 * math.log(10000.0) / HEAD_DIM))
    inverse = np.tile(inverse, 4)
    inside = np.arange(ROWS)[:, None] * inverse[None, :]
    at = (ROWS * np.arange(8))[:, None] * inverse[None, :]
    turn = np.stack([np.cos(at), np.sin(at)], axis=1)
    return [jnp.asarray(v, F32) for v in (np.cos(inside), np.sin(inside), turn)]


def front(hidden, teacher, shards, rates, count, segments, gains, ropes):
    sds = jax.ShapeDtypeStruct
    outs = [
        (sds((D, ROWS), BF16), IN_PLACE),
        (sds((TOK, D), BF16), IN_VMEM),
        (sds((TOK, D), BF16), IN_VMEM),
        (sds((2, D), F32), IN_VMEM),
        (sds((8, 128), F32), IN_VMEM),
        (sds((4, D, D), BF16), IN_PLACE),
        (sds((6, ROWS, 128), F32), IN_VMEM),
        (sds((HEADS, ROWS, 128), BF16), IN_VMEM),
        (sds((5 * ROWS, 2 * COLS), BF16), IN_PLACE),
        (sds((ROWS, 384), BF16), IN_VMEM),
        (sds((COLS, ROWS), F32), IN_VMEM),
        (sds((HEADS, 8, ROWS), F32), IN_VMEM),
        (sds((1, ROWS), jnp.int32), IN_VMEM),
    ]
    return pl.pallas_call(
        front_kernel,
        out_shape=tuple(o[0] for o in outs),
        in_specs=[IN_PLACE] * 2 + [IN_VMEM] * 14,
        out_specs=tuple(o[1] for o in outs),
        scratch_shapes=[
            VMEM((D, ROWS), BF16),
            VMEM((ROWS, D), BF16),
            VMEM((D, TOK), BF16),
            VMEM((4, 2, COLS), F32),
            VMEM((4, 40, D), BF16),
            VMEM((4, 40, 640), BF16),
            VMEM((4, 80, 640), BF16),
            VMEM((D, D), BF16),
            VMEM((5 * ROWS, 2 * COLS), BF16),
            VMEM((HEADS, 64, ROWS), F32),
            VMEM((HEADS, 8, ROWS), F32),
            DMA((10,)),
            DMA((10,)),
            DMA,
            DMA,
            DMA((7,)),
            DMA((5,)),
            DMA((5,)),
        ]
        + ring_scratch()
        + ring_scratch()
        + tally_scratch((8, 128)),
        compiler_params=params(0),
        name="front",
    )(hidden, teacher, *shards, rates, count, segments, gains, *ropes)


def mix_forward(states, branch, alphas):
    branch_scale = lax.rsqrt(jnp.sum(branch * branch, axis=1, keepdims=True) + EPS)
    normed = branch * branch_scale
    mixed = states + alphas * (normed - states)
    mixed_scale = lax.rsqrt(jnp.sum(mixed * mixed, axis=1, keepdims=True) + EPS)
    return mixed * mixed_scale, normed, branch_scale, mixed_scale


def mix_backward(gradient, states, normed, branch_scale, mixed_out, mixed_scale, alphas):
    along = jnp.sum(mixed_out * gradient, axis=1, keepdims=True)
    mixed_grad = mixed_scale * (gradient - mixed_out * along)
    normed_grad = alphas * mixed_grad
    toward = jnp.sum(normed * normed_grad, axis=1, keepdims=True)
    branch_grad = branch_scale * (normed_grad - normed * toward)
    rate_grad = jnp.sum(mixed_grad * (normed - states), axis=0, keepdims=True)
    return (1.0 - alphas) * mixed_grad, branch_grad, rate_grad


def swiglu_parts(gate_raw, up_raw, gate_gain, up_gain):
    root = math.sqrt(D)
    g = gate_gain * gate_raw * root
    q = jax.nn.sigmoid(g)
    return g, q


def middle_kernel(
    att,
    hid_tok,
    tea,
    mask,
    count,
    rates,
    up_gain,
    gate_gain,
    weights,
    output,
    in_one,
    product,
    mlp_grad,
    gate_low,
    up_low,
    attn_grad,
    d_att,
    res_zero,
    small,
    w_out,
    w_gate,
    w_up,
    w_down,
    raw_gate,
    raw_up,
    send_buf,
    got_buf,
    own_part,
    out_buf,
    state,
    normed,
    scales,
    w_sem,
    ag_send,
    ag_recv,
    rs_send,
    rs_recv,
    o_send,
    o_recv,
):
    z, x, c, y = spot()
    peers = [device(z, x, c, wrap(y + d)) for d in range(4)]
    loads = [
        pltpu.make_async_copy(weights.at[0, :, pl.ds(0, 384)], w_out, w_sem.at[0]),
        pltpu.make_async_copy(weights.at[1], w_gate, w_sem.at[1]),
        pltpu.make_async_copy(weights.at[2], w_up, w_sem.at[2]),
        pltpu.make_async_copy(weights.at[3], w_down, w_sem.at[3]),
    ]
    for load in loads:
        load.start()
    meet(peers[1:])
    my_rows = pl.ds(pl.multiple_of(TOK * y, TOK), TOK)

    def rows_of(k):
        return pl.ds(pl.multiple_of(TOK * wrap(y - k), TOK), TOK)

    def feats(k):
        return pl.ds(pl.multiple_of(COLS * k, 64), COLS)

    def back_to(k):
        return device(z, x, c, wrap(y - k))

    def scatter(stage, k):
        return remote(
            send_buf.at[stage, k],
            got_buf.at[stage, k],
            rs_send.at[stage, k],
            rs_recv.at[stage, k],
            back_to(k),
        )

    def spread(stage, src, k):
        return remote(
            src.at[my_rows],
            src.at[my_rows],
            ag_send.at[stage, k],
            ag_recv.at[stage, k],
            device(z, x, c, wrap(y + k)),
        )

    def give(stage, k, part):
        @pl.when(k == 0)
        def _():
            own_part[...] = part

        @pl.when(k > 0)
        def _():
            send_buf[stage, k] = part.astype(BF16)
            scatter(stage, k).start()

    def collect(stage):
        total = own_part[...]
        for k in (1, 2, 3):
            scatter(stage, k).wait_recv()
            total = total + got_buf[stage, k].astype(F32)
        return total

    def announce(stage, ref, value):
        ref[my_rows, :] = value.astype(BF16)
        for k in (2, 1, 3):
            spread(stage, ref, k).start()

    def each(body, stage=None, ref=None):
        def step(k, carry):
            if ref is not None:

                @pl.when(k > 0)
                def _():
                    spread(stage, ref, k).wait_recv()

            body(k)
            return carry

        lax.fori_loop(0, 4, step, 0)

    loads[0].wait()

    def project(k):
        give(0, k, dot_nt(att[rows_of(k), :], w_out[...]))

    each(project)
    attn = collect(0)
    states = hid_tok[...].astype(F32)
    one, normed_one, branch_one, scale_one = mix_forward(states, attn, rates[0:1, :])
    announce(0, in_one, one)
    state[0] = one
    normed[0] = normed_one
    scales[0] = jnp.broadcast_to(branch_one, (TOK, 128))
    scales[1] = jnp.broadcast_to(scale_one, (TOK, 128))
    for load in loads[1:]:
        load.wait()

    def feed(k):
        rows = rows_of(k)
        block = in_one[rows, :]
        gate_raw = dot_nn(block, w_gate[...])
        raw_gate[rows, :] = gate_raw
        up_raw = dot_nn(block, w_up[...])
        raw_up[rows, :] = up_raw
        g, q = swiglu_parts(gate_raw, up_raw, gate_gain[...], up_gain[...])
        low = (up_gain[...] * up_raw * (g * q)).astype(BF16)
        product[rows, :] = low
        give(1, k, dot_nt(low, w_down[...]))

    each(feed, 0, in_one)
    mlp = collect(1)
    one = state[0]
    two, normed_two, branch_two, scale_two = mix_forward(one, mlp, rates[1:2, :])
    for g in range(10):
        out_buf[128 * g : 128 * g + 128, :] = two[:, 128 * g : 128 * g + 128].T.astype(BF16)
    out_copies = []
    for k in (1, 2, 3):
        copy = remote(
            out_buf.at[feats(wrap(y + k))],
            output.at[:, my_rows],
            o_send.at[k],
            o_recv.at[k],
            device(z, x, c, wrap(y + k)),
        )
        out_copies.append(copy)
    errors = two - tea[...].astype(F32)
    weight = mask[...]
    loss = jnp.sum(weight * errors * errors)
    factor = 16384 * math.sqrt(D) / count[0:1, 0:1]
    seed = factor * (weight * errors)
    res_one, mlp_back, rate_two = mix_backward(
        seed, one, normed_two, branch_two, two, scale_two, rates[1:2, :]
    )
    announce(1, mlp_grad, mlp_back)
    for copy in out_copies:
        copy.start()
    output[:, my_rows] = out_buf[feats(y), :]
    small[...] = jnp.zeros_like(small)
    small[1:2, :] = rate_two
    small[4:5, :] = jnp.broadcast_to(loss, (1, D))
    state[1] = res_one

    def unfeed(k):
        rows = rows_of(k)
        grad = dot_nn(mlp_grad[rows, :], w_down[...])
        gate_raw = raw_gate[rows, :]
        up_raw = raw_up[rows, :]
        g, q = swiglu_parts(gate_raw, up_raw, gate_gain[...], up_gain[...])
        silu = g * q
        up_term = grad * silu
        slope = grad * up_gain[...] * up_raw * (q * (1.0 + g * (1.0 - q))) * math.sqrt(D)
        small[2:3, :] += jnp.sum(up_term * up_raw, axis=0, keepdims=True)
        small[3:4, :] += jnp.sum(slope * gate_raw, axis=0, keepdims=True)
        up_back = (up_term * up_gain[...]).astype(BF16)
        gate_back = (slope * gate_gain[...]).astype(BF16)
        up_low[rows, :] = up_back
        gate_low[rows, :] = gate_back
        give(2, k, dot_nt(gate_back, w_gate[...]) + dot_nt(up_back, w_up[...]))

    each(unfeed, 1, mlp_grad)
    grad_one = state[1] + collect(2)
    states = hid_tok[...].astype(F32)
    res, attn_back, rate_one = mix_backward(
        grad_one,
        states,
        normed[0],
        scales[0, :, 0:1],
        state[0],
        scales[1, :, 0:1],
        rates[0:1, :],
    )
    announce(2, attn_grad, attn_back)
    small[0:1, :] = rate_one
    for g in range(10):
        res_zero[128 * g : 128 * g + 128, :] = res[:, 128 * g : 128 * g + 128].T

    def unproject(k):
        rows = rows_of(k)
        d_att[rows, :] = dot_nn(attn_grad[rows, :], w_out[...]).astype(BF16)

    each(unproject, 2, attn_grad)
    for k in (1, 2, 3):
        for stage in range(3):
            scatter(stage, k).wait_send()
        spread(0, in_one, k).wait_send()
        spread(1, mlp_grad, k).wait_send()
        spread(2, attn_grad, k).wait_send()
    for copy in out_copies:
        copy.wait()


def middle(att, hid_tok, tea, mask, count, rates, up_gain, gate_gain, weights):
    wide = jax.ShapeDtypeStruct((ROWS, D), BF16)
    return pl.pallas_call(
        middle_kernel,
        out_shape=(
            jax.ShapeDtypeStruct((COLS, ROWS), BF16),
            wide,
            wide,
            wide,
            wide,
            wide,
            wide,
            jax.ShapeDtypeStruct((ROWS, 384), BF16),
            jax.ShapeDtypeStruct((D, TOK), F32),
            jax.ShapeDtypeStruct((8, D), F32),
        ),
        in_specs=[IN_VMEM] * 8 + [IN_PLACE],
        out_specs=(IN_VMEM,) * 10,
        scratch_shapes=[
            VMEM((D, 384), BF16),
            VMEM((D, D), BF16),
            VMEM((D, D), BF16),
            VMEM((D, D), BF16),
            VMEM((ROWS, D), F32),
            VMEM((ROWS, D), F32),
            VMEM((3, 4, TOK, D), BF16),
            VMEM((3, 4, TOK, D), BF16),
            VMEM((TOK, D), F32),
            VMEM((D, TOK), BF16),
            VMEM((2, TOK, D), F32),
            VMEM((1, TOK, D), F32),
            VMEM((2, TOK, 128), F32),
            DMA((4,)),
            DMA((3, 4)),
            DMA((3, 4)),
            DMA((3, 4)),
            DMA((3, 4)),
            DMA((4,)),
            DMA((4,)),
        ],
        compiler_params=params(3),
        name="middle",
    )(att, hid_tok, tea, mask, count, rates, up_gain, gate_gain, weights)


class Fold:
    def __init__(self, bufs, sems):
        z, x, c, y = spot()
        self.z, self.x, self.c = z, x, c
        self.first, self.second, _ = torus(z, x, c, y)
        self.at_first = x * (1 - c) + z * c
        self.sibling = device(z, x, 1 - c, y)
        self.own, self.sib, self.got_two, self.mid, self.got_one, self.fin = bufs
        self.l_sem, self.h_send, self.h_recv, self.b_send, self.b_recv, self.a_send, self.a_recv, self.f_send, self.f_recv = sems
        self.count = self.own.shape[0]
        self.lanes = pl.ds(pl.multiple_of(640 * c, 128), 640)
        self.other = pl.ds(pl.multiple_of(640 * (1 - c), 128), 640)

    def handed(self, j, d, src):
        return remote(src, self.sib.at[j, d], self.h_send.at[j, d], self.h_recv.at[j, d], self.sibling)

    def fetched(self, j, d, src):
        return pltpu.make_async_copy(src, self.own.at[j, d], self.l_sem.at[j, d])

    def open(self, srcs):
        z, x = self.z, self.x

        @pl.when(self.c == 0)
        def _():
            for d in (2, 1, 3, 0):
                for j, src in enumerate(srcs):
                    self.handed(j, d, src.at[:, wrap(x + d), :, self.other]).start()
                    self.fetched(j, d, src.at[wrap(z + d), :, :, self.lanes]).start()

        @pl.when(self.c == 1)
        def _():
            for d in (2, 1, 3, 0):
                for j, src in enumerate(srcs):
                    self.handed(j, d, src.at[wrap(z + d), :, :, self.other]).start()
                    self.fetched(j, d, src.at[:, wrap(x + d), :, self.lanes]).start()

    def pair(self, d):
        return remote(
            self.own.at[:, d], self.got_two.at[:, d - 1], self.b_send.at[d], self.b_recv.at[d], self.second(d)
        )

    def last(self, e):
        return remote(
            self.mid.at[:, e - 1], self.got_one.at[:, e - 1], self.a_send.at[e], self.a_recv.at[e], self.first(e)
        )

    def add(self, d):
        for j in range(self.count):
            blank = self.sib.at[j, d]
            self.fetched(j, d, blank).wait()
            self.handed(j, d, blank).wait_recv()

        def each(i, carry):
            j, a = lax.div(i, 4), lax.rem(i, 4)
            total = self.own[j, d, a].astype(F32) + self.sib[j, d, a].astype(F32)
            self.own[j, d, a] = total.astype(BF16)
            return carry

        lax.fori_loop(0, 4 * self.count, each, 0)
        if d:
            self.pair(d).start()

    def whole(self, j, at):
        total = self.own[j, 0, at].astype(F32)
        for d in (1, 2, 3):
            total = total + self.got_two[j, d - 1, at].astype(F32)
        return total

    def cross(self):
        for d in (1, 2, 3):
            self.pair(d).wait_recv()
        for e in (2, 1, 3):

            def each(j, carry, e=e):
                self.mid[j, e - 1] = self.whole(j, wrap(self.at_first + e)).astype(BF16)
                return carry

            lax.fori_loop(0, self.count, each, 0)
            self.last(e).start()

    def give(self, out):
        rows = pl.ds(pl.multiple_of(40 * (1 - self.c), 8), 40)
        return remote(self.fin.at[:, rows], out.at[:, :, self.lanes], self.f_send, self.f_recv, self.sibling)

    def finish(self, out):
        for e in (1, 2, 3):
            self.last(e).wait_recv()

        def each(j, carry):
            total = self.whole(j, self.at_first)
            for e in (1, 2, 3):
                total = total + self.got_one[j, e - 1].astype(F32)
            self.fin[j] = total
            return carry

        lax.fori_loop(0, self.count, each, 0)
        self.give(out).start()
        rows = pl.ds(pl.multiple_of(40 * self.c, 8), 40)
        for j in range(self.count):
            out[j, :, self.lanes] = self.fin[j, rows, :]

    def close(self, out):
        self.give(out).wait()
        for d in (1, 2, 3):
            self.pair(d).wait_send()
            self.last(d).wait_send()
        for j in range(self.count):
            for d in range(4):
                self.handed(j, d, self.sib.at[j, d]).wait_send()


def fold_scratch(count):
    block = (80, 640)
    return [
        VMEM((count, 4, 4) + block, BF16),
        VMEM((count, 4, 4) + block, BF16),
        VMEM((count, 3, 4) + block, BF16),
        VMEM((count, 3) + block, BF16),
        VMEM((count, 3) + block, BF16),
        VMEM((count,) + block, F32),
        DMA((count, 4)),
        DMA((count, 4)),
        DMA((count, 4)),
        DMA((4,)),
        DMA((4,)),
        DMA((4,)),
        DMA((4,)),
        DMA,
        DMA,
    ]


def head_back(grad, raw, gain, cosine, sine):
    normed, scale = head_norm(raw, cosine, sine)
    gain_grad = jnp.sum(grad * normed, axis=0, keepdims=True)
    pulled = grad * gain
    turned = scale * (pulled - normed * over_heads(normed * pulled))
    return turned * cosine + swap_halves(turned * sine), gain_grad


def tail_kernel(
    starts,
    q_pad,
    out_t,
    lse,
    d_att,
    att,
    gains,
    cos_block,
    sin_block,
    turn,
    res_t,
    small,
    count,
    win_in,
    raw_in,
    hid_in,
    w_in,
    attn_in,
    m0,
    m1,
    m2,
    hidden_grad,
    query_g,
    key_g,
    value_g,
    out_g,
    gate_g,
    up_g,
    down_g,
    loss_out,
    attention_out,
    feedforward_out,
    score_out,
    up_out,
    gate_out,
    win,
    raw,
    hid_t,
    w_first,
    attn,
    d_pad,
    delta,
    q_acc,
    d_win,
    sib_one,
    sib_two,
    sib_own,
    one_buf,
    two_buf,
    got_one,
    got_two,
    kv_sum,
    pack,
    out_part,
    first_g,
    y_send_buf,
    y_got_buf,
    side_src,
    side_got,
    sums,
    m_out,
    f_out,
    in_sem,
    k_send,
    k_recv,
    y_send,
    y_recv,
    v_send,
    v_recv,
    *rest,
):
    m_bufs, m_sems, rest = rest[:6], rest[6:15], rest[15:]
    f_bufs, f_sems, rest = rest[:6], rest[6:15], rest[15:]
    t_accs, t_parts, t_send, t_recv = rest
    z, x, c, y = spot()
    place = 2 * x + c
    sibling = device(z, x, 1 - c, y)
    across = [device(z, x, c, wrap(y + d)) for d in (1, 2, 3)]
    tally = Tally(sums, t_accs, t_parts, t_send, t_recv)

    def slot(ref, s):
        return ref.at[pl.ds(pl.multiple_of(ROWS * s, ROWS), ROWS)]

    win_loads = [
        pltpu.make_async_copy(slot(win_in, s), slot(win, s), in_sem.at[s]) for s in range(5)
    ]
    for s in range(5):
        win_loads[s].start()
    loads = [
        pltpu.make_async_copy(src, dst, in_sem.at[5 + k])
        for k, (src, dst) in enumerate(
            ((raw_in, raw), (attn_in, attn), (w_in.at[0], w_first), (hid_in, hid_t))
        )
    ]
    meet(across + tally.peers[0] + tally.peers[1] + tally.peers[2])
    fold_m = Fold(m_bufs, m_sems)
    fold_f = Fold(f_bufs, f_sems)
    fold_m.open([m0, m1, m2])
    side_src[...] = jnp.zeros_like(side_src)
    for k in range(4):
        lanes = slice(COLS * k, COLS * (k + 1))
        side_src[k, 0:2, 0:COLS] = small[0:2, lanes]
        side_src[k, 2:3, 0:COLS] = small[4:5, lanes]

    def side(k):
        return remote(side_src.at[wrap(y + k)], side_got.at[k], v_send.at[k], v_recv.at[k], across[k - 1])

    for k in (1, 2, 3):
        side(k).start()
    for load in loads:
        load.start()

    for h in range(HEADS):
        d_pad[h] = pad_head(d_att, (h + 1) // 2, (h + 1) % 2)
    wide = d_att[...].astype(F32).T[64:, :] * out_t[...]
    for h in range(HEADS):
        delta[h] = jnp.broadcast_to(
            jnp.sum(wide[64 * h : 64 * (h + 1), :], axis=0, keepdims=True), (8, ROWS)
        )
    q_acc[...] = jnp.zeros_like(q_acc)

    hand_one = remote(slot(d_win, 3 - 2 * c), sib_one, k_send.at[0], k_recv.at[0], sibling)
    hand_two = remote(slot(d_win, 1), sib_two, k_send.at[1], k_recv.at[1], sibling)
    hand_own = remote(slot(d_win, 3), sib_own, k_send.at[2], k_recv.at[2], sibling)
    one = remote(one_buf, got_one, k_send.at[3], k_recv.at[3], device(z, wrap(x + 3), c, y))
    two = remote(two_buf, got_two, k_send.at[4], k_recv.at[4], device(z, wrap(x + 2), c, y))

    def tile(t):
        rows = pl.ds(pl.multiple_of(t * TILE, TILE), TILE)
        key_at = t * TILE + lax.broadcasted_iota(jnp.int32, (TILE, ROWS), 0)
        query_at = 4 * ROWS + lax.broadcasted_iota(jnp.int32, (TILE, ROWS), 1)
        allowed = (key_at >= starts[...]) & (key_at <= query_at)
        terms = [None] * 5
        for h in range(HEADS):
            kg, kh = key_place(h)
            vg, _ = value_place(h)
            keys = win[rows, 128 * kg : 128 * kg + 128]
            values = win[rows, 128 * vg : 128 * vg + 128]
            scores = dot_nt(keys, q_pad[h])
            probs = jnp.where(allowed, jnp.exp(scores - lse[h, 0:1, :]), 0.0)
            prob_grad = dot_nt(values, d_pad[h])
            score_grad = (probs * (prob_grad - delta[h, 0:1, :])).astype(BF16)
            v_term = dot_nn(probs.astype(BF16), d_pad[h])
            k_term = dot_nn(score_grad, q_pad[h])
            for at, term in ((kg, k_term), (vg, v_term)):
                terms[at] = term if terms[at] is None else terms[at] + term
            both = dot_tn(keys, score_grad)
            q_acc[h] += both[64 * kh : 64 * kh + 64, :]
        for g in range(5):
            d_win[rows, 128 * g : 128 * g + 128] = terms[g].astype(BF16)

    def after(k):
        if k == 0:

            @pl.when((c == 0) & (x > 1))
            def _():
                two_buf[...] = d_win[0:ROWS, :]
                two.start()

        if k == 1:

            @pl.when((c == 0) & (x > 1))
            def _():
                hand_two.start()

            @pl.when((c == 1) & (x > 0))
            def _():
                hand_one.start()

        if k == 2:

            @pl.when((c == 0) & (x > 0))
            def _():
                hand_one.start()

            @pl.when((c == 1) & (x > 1))
            def _():
                hand_two.wait_recv()
                two_buf[...] = (
                    d_win[0:ROWS, :].astype(F32) + sib_two[...].astype(F32)
                ).astype(BF16)
                two.start()

        if k == 3:

            @pl.when(x > 0)
            def _():
                hand_one.wait_recv()
                one_buf[...] = (
                    d_win[2 * ROWS : 3 * ROWS, :].astype(F32) + sib_one[...].astype(F32)
                ).astype(BF16)
                one.start()

            @pl.when(c == 1)
            def _():
                hand_own.start()

    for load in win_loads:
        load.wait()
    folds = {2: 2, 3: 1, 5: 3, 7: 0}

    def step(i, carry):
        k = lax.div(i, 2)
        s = jnp.where((c == 0) & (k == 2), 3, jnp.where((c == 0) & (k == 3), 2, k))

        @pl.when(place + s >= 4)
        def _():
            tile(2 * s + lax.rem(i, 2))

        for k in range(4):

            @pl.when(i == 2 * k + 1)
            def _(k=k):
                after(k)

        for n, d in folds.items():

            @pl.when(i == n)
            def _(d=d):
                fold_m.add(d)

        return carry

    lax.fori_loop(0, 10, step, 0)
    for load in loads:
        load.wait()
    cosine, sine = rope_wide(cos_block, sin_block, turn)
    pack[:, 128:384] = jnp.zeros((ROWS, 256), BF16)
    gain_parts = []
    wide = jnp.concatenate([q_acc[h] for h in range(HEADS)] + [jnp.zeros((64, ROWS), F32)], axis=0)
    for g, at in enumerate((384, 512, 0)):
        grad = wide[128 * g : 128 * g + 128, :].T * math.sqrt(HEAD_DIM)
        term, gain_part = head_back(grad, raw[g], gains[:, 128 * g : 128 * g + 128], cosine, sine)
        if g == 2:
            term = jnp.where(half_mask(0), term, 0.0)
        pack[:, at : at + 128] = term.astype(BF16)
        gain_parts.append(gain_part)
    out_part[...] = dot_tn(attn[...], att[...])

    kv_sum[...] = d_win[4 * ROWS :, :].astype(F32)

    @pl.when(c == 0)
    def _():
        hand_own.wait_recv()
        kv_sum[...] += sib_own[...].astype(F32)

    @pl.when(x < 3)
    def _():
        one.wait_recv()
        kv_sum[...] += got_one[...].astype(F32)

    @pl.when(x < 2)
    def _():
        two.wait_recv()
        kv_sum[...] += got_two[...].astype(F32)

    for g in range(3):
        grad = kv_sum[:, 128 * g : 128 * g + 128]
        gain = gains[:, 128 * g : 128 * g + 128]
        term, gain_part = head_back(grad, raw[3 + g], gain, cosine, sine)
        if g == 2:
            term = jnp.where(half_mask(0), term, grad)
        at = 640 + 128 * g
        pack[:, at : at + 128] = term.astype(BF16)
        gain_parts[g] += gain_part
    pack[:, 1024:1280] = kv_sum[:, 384:640].astype(BF16)

    my_cols = pl.ds(pl.multiple_of(TOK * y, TOK), TOK)

    def project(to):
        rows = pl.ds(pl.multiple_of(COLS * to, 64), COLS)
        hidden_grad[...] = dot_nt(w_first[rows, :], pack[...])
        hidden_grad[:, my_cols] += res_t[rows, :]

    def grad_copy(k):
        return remote(y_send_buf.at[k - 1], y_got_buf.at[k - 1], y_send.at[k], y_recv.at[k], across[k - 1])

    for k in (2, 1, 3):
        project(wrap(y + k))
        y_send_buf[k - 1] = hidden_grad[...].astype(BF16)
        grad_copy(k).start()

    extra = side_src[y]
    for k in (1, 2, 3):
        side(k).wait_recv()
        extra = extra + side_got[k]
    sums[...] = jnp.zeros_like(sums)
    sums[0:2, :] = small[2:4, :]
    sums[2:3, 0:384] = jnp.concatenate(gain_parts, axis=1)
    sums[3:6, 0:384] = extra[0:3, :]
    tally.start(0)

    def first_grad(k, carry):
        rows = pl.ds(pl.multiple_of(COLS * k, 64), COLS)
        grad = dot_nn(hid_t[rows, :], pack[...])
        low = grad[:, 0:384] + out_part[rows, :]
        for a in range(4):
            first_g[k, a, :, 0:384] = low[80 * a : 80 * a + 80].astype(BF16)
            first_g[k, a, :, 384:] = grad[80 * a : 80 * a + 80, 384:].astype(BF16)
        return carry

    lax.fori_loop(0, 4, first_grad, 0)
    fold_f.open([first_g])
    fold_m.cross()
    tally.finish(0)
    tally.start(1)
    project(y)
    for d in (2, 1, 3, 0):
        fold_f.add(d)
    for k in (1, 2, 3):
        grad_copy(k).wait_recv()
        hidden_grad[...] += y_got_buf[k - 1].astype(F32)
    tally.finish(1)
    tally.start(2)
    fold_m.finish(m_out)
    fold_f.cross()
    fold_f.finish(f_out)
    tally.finish(2)
    fold_m.close(m_out)
    fold_f.close(f_out)
    gate_g[...] = m_out[0]
    up_g[...] = m_out[1]
    down_g[...] = m_out[2]
    query_g[:, 0:256] = f_out[0, :, 384:640]
    query_g[:, 256:320] = f_out[0, :, 0:64]
    key_g[...] = f_out[0, :, 640:960]
    value_g[...] = f_out[0, :, 960:1280]
    out_g[...] = f_out[0, :, 64:384]
    totals = t_accs[2]
    loss_out[...] = totals[5:6, 0:1] / count[0:1, 0:1]
    attention_out[...] = totals[3:4, 0:COLS]
    feedforward_out[...] = totals[4:5, 0:COLS]
    score_out[...] = totals[2:3, 0:COLS]
    up_out[...] = totals[0:1, :]
    gate_out[...] = totals[1:2, :]
    for k in (1, 2, 3):
        grad_copy(k).wait_send()
        side(k).wait_send()

    @pl.when(x > 0)
    def _():
        hand_one.wait_send()
        one.wait_send()

    @pl.when(x > 1)
    def _():
        two.wait_send()

        @pl.when(c == 0)
        def _():
            hand_two.wait_send()

    @pl.when(c == 1)
    def _():
        hand_own.wait_send()

    tally.close()


def tail(vmem_args, placed_args):
    sds = jax.ShapeDtypeStruct
    block = VMEM((ROWS, 2 * COLS), BF16)
    shapes = [(COLS, ROWS)] + [(40, COLS)] * 4 + [(40, D)] * 3 + [(1, 1)] + [(1, COLS)] * 3 + [(1, D)] * 2
    return pl.pallas_call(
        tail_kernel,
        out_shape=tuple(sds(s, F32) for s in shapes),
        in_specs=[IN_VMEM] * len(vmem_args) + [IN_PLACE] * len(placed_args),
        out_specs=(IN_VMEM,) * len(shapes),
        scratch_shapes=[
            VMEM((5 * ROWS, 2 * COLS), BF16),
            VMEM((6, ROWS, 128), F32),
            VMEM((D, ROWS), BF16),
            VMEM((D, D), BF16),
            VMEM((ROWS, D), BF16),
            VMEM((HEADS, ROWS, 128), BF16),
            VMEM((HEADS, 8, ROWS), F32),
            VMEM((HEADS, 64, ROWS), F32),
            VMEM((5 * ROWS, 2 * COLS), BF16),
        ]
        + [block] * 7
        + [
            VMEM((ROWS, 2 * COLS), F32),
            VMEM((ROWS, D), BF16),
            VMEM((D, 384), F32),
            VMEM((4, 4, 80, D), BF16),
            VMEM((3, COLS, ROWS), BF16),
            VMEM((3, COLS, ROWS), BF16),
            VMEM((4, 8, 384), F32),
            VMEM((4, 8, 384), F32),
            VMEM((8, D), F32),
            VMEM((3, 40, D), F32),
            VMEM((1, 40, D), F32),
            DMA((9,)),
            DMA((5,)),
            DMA((5,)),
            DMA((4,)),
            DMA((4,)),
            DMA((4,)),
            DMA((4,)),
        ]
        + fold_scratch(3)
        + fold_scratch(1)
        + tally_scratch((8, D)),
        compiler_params=params(2),
        name="tail",
    )(*vmem_args, *placed_args)


def weight_dot(inputs_low, gradient):
    return lax.dot_general(
        inputs_low, gradient, (((0,), (0,)), ((), ())), preferred_element_type=F32
    ).astype(BF16)


def shards(
    hidden,
    teacher,
    valid_mask,
    segments,
    query_weight,
    key_weight,
    value_weight,
    out_weight,
    gate_weight,
    up_weight,
    down_weight,
    attention_rate,
    feedforward_rate,
    score_gain,
    up_gain,
    gate_gain,
):
    col = lax.axis_index("col")
    token_mask = valid_mask.astype(F32)
    count = jnp.broadcast_to(jnp.sum(token_mask), (8, 128))
    rates = jnp.stack([attention_rate, feedforward_rate])
    gains = jnp.pad(score_gain, (0, 64)).reshape(1, 384)
    ropes = rope_constants()
    projections = (query_weight, key_weight, value_weight, out_weight.T)
    projections += (gate_weight, up_weight, down_weight.T)
    (
        hid_t,
        hid_tok,
        tea_tok,
        rates_full,
        count_all,
        weights,
        raw,
        q_pad,
        win,
        att,
        out_t,
        lse,
        starts,
    ) = front(hidden.T, teacher.T, projections, rates, count, segments, gains, ropes)

    mask_tok = lax.dynamic_slice_in_dim(token_mask, col * TOK, TOK).reshape(TOK, 1)
    (
        output,
        in_one,
        product,
        mlp_grad,
        gate_low,
        up_low,
        attn_grad,
        d_att,
        res_zero,
        small,
    ) = middle(
        att,
        hid_tok,
        tea_tok,
        mask_tok,
        count_all,
        rates_full,
        up_gain.reshape(1, -1),
        gate_gain.reshape(1, -1),
        weights,
    )
    gate_grad = weight_dot(in_one, gate_low)
    up_grad = weight_dot(in_one, up_low)
    down_grad = weight_dot(mlp_grad, product)

    blocks = (4, 4, 80, D)
    results = tail(
        (starts, q_pad, out_t, lse, d_att, att, gains, *ropes, res_zero, small, count_all),
        (win, raw, hid_t, weights, attn_grad)
        + tuple(g.reshape(blocks) for g in (gate_grad, up_grad, down_grad)),
    )
    hidden_grad, query_g, key_g, value_g, out_g, gate_g, up_g, down_g, loss = results[:9]
    return (
        loss.reshape(()),
        output.T,
        hidden_grad.T,
        query_g,
        key_g,
        value_g,
        out_g.T,
        gate_g,
        up_g,
        down_g.T,
    ) + tuple(v.reshape(-1) for v in results[9:])


def solution(mesh):
    both = P(("dp", "row"), "col")
    turned = P("col", ("dp", "row"))
    vector = P("col")
    in_specs = (both, both, P(("dp", "row")), P("dp", None), both, both, both, turned, both, both)
    in_specs += (turned,) + (vector,) * 5
    out_specs = (P(), both, both, both, both, both, turned, both, both, turned) + (vector,) * 5
    return jax.shard_map(shards, mesh=mesh, in_specs=in_specs, out_specs=out_specs, check_vma=False)
```

```python
import math

import jax
import jax.numpy as jnp
import numpy as np
from jax import lax
from jax.experimental import pallas as pl
from jax.experimental.pallas import tpu as pltpu
from jax.sharding import PartitionSpec as P

D = 1280
HEAD_DIM = 64
EPS = 1e-06
HEADS = 5
ROWS = 512
TOK = 128
COLS = 320
TILE = 256
F32 = jnp.float32
BF16 = jnp.bfloat16
MESH = pl.DeviceIdType.MESH
DMA = pltpu.SemaphoreType.DMA
VMEM = pltpu.VMEM
IN_VMEM = pl.BlockSpec(memory_space=pltpu.VMEM)
IN_SMEM = pl.BlockSpec(memory_space=pltpu.SMEM)
IN_PLACE = pl.BlockSpec(memory_space=pl.ANY)
LIMIT = 60 << 20


def params(collective=None):
    if collective is None:
        return pltpu.CompilerParams(vmem_limit_bytes=LIMIT)
    return pltpu.CompilerParams(
        collective_id=collective, has_side_effects=True, vmem_limit_bytes=LIMIT
    )


def spot():
    row = lax.axis_index("row")
    return lax.axis_index("dp"), lax.div(row, 2), lax.rem(row, 2), lax.axis_index("col")


def wrap(i):
    return lax.rem(i + 8, 4)


def device(z, x, c, y):
    return (z, 2 * x + c, y)


def meet(others):
    barrier = pltpu.get_barrier_semaphore()
    for other in others:
        pl.semaphore_signal(barrier, inc=1, device_id=other, device_id_type=MESH)
    pl.semaphore_wait(barrier, len(others))


def remote(src, dst, send_sem, recv_sem, to):
    return pltpu.make_async_remote_copy(
        src_ref=src,
        dst_ref=dst,
        send_sem=send_sem,
        recv_sem=recv_sem,
        device_id=to,
        device_id_type=MESH,
    )


def dot_nn(a, b):
    return lax.dot_general(a, b, (((1,), (0,)), ((), ())), preferred_element_type=F32)


def dot_nt(a, b):
    return lax.dot_general(a, b, (((1,), (1,)), ((), ())), preferred_element_type=F32)


def dot_tn(a, b):
    return lax.dot_general(a, b, (((0,), (0,)), ((), ())), preferred_element_type=F32)


class Tally:
    def __init__(self, src, accs, parts, send, recv):
        z, x, c, y = spot()
        self.src, self.accs, self.parts, self.send, self.recv = src, accs, parts, send, recv
        self.peers = [
            [device(z, wrap(x + d), c, y) for d in (1, 2, 3)],
            [device(wrap(z + d), x, c, y) for d in (1, 2, 3)],
            [device(z, x, 1 - c, y)],
        ]
        self.copies = []

    def start(self, stage):
        src = self.src if stage == 0 else self.accs.at[stage - 1]
        for d, peer in enumerate(self.peers[stage]):
            at = 3 * stage + d
            copy = remote(src, self.parts.at[at], self.send.at[at], self.recv.at[at], peer)
            copy.start()
            self.copies.append(copy)

    def finish(self, stage):
        src = self.src if stage == 0 else self.accs.at[stage - 1]
        total = src[...]
        for d in range(len(self.peers[stage])):
            self.copies[3 * stage + d].wait_recv()
            total = total + self.parts[3 * stage + d]
        self.accs[stage] = total

    def close(self):
        for copy in self.copies:
            copy.wait_send()


TALLY_PEERS = 7


def tally_scratch(shape):
    return [
        VMEM((3,) + shape, F32),
        VMEM((7,) + shape, F32),
        DMA((7,)),
        DMA((7,)),
    ]


def torus(z, x, c, y):
    def first(d):
        return device(wrap(z + c * d), wrap(x + (1 - c) * d), c, y)

    def second(d):
        return device(wrap(z + (1 - c) * d), wrap(x + c * d), c, y)

    at_first = x * (1 - c) + z * c
    at_second = z * (1 - c) + x * c

    def block(d1, d2):
        a1, a2 = wrap(at_first + d1), wrap(at_second + d2)
        return (1 - c) * (a2 * 4 + a1) + c * (a1 * 4 + a2)

    return first, second, block


def half_mask(half):
    lane = lax.broadcasted_iota(jnp.int32, (1, 128), 1)
    return (lane < 64) if half == 0 else (lane >= 64)


def key_place(h):
    return h // 2, h % 2


def value_place(h):
    return (HEADS + h) // 2, (HEADS + h) % 2


def pad_head(wide, at, half):
    group = wide[:, 128 * at : 128 * at + 128]
    return jnp.where(half_mask(half), group, jnp.zeros_like(group))


LOW_ROWS = 48


def lane_halves(c):
    ours = pl.ds(pl.multiple_of(640 * c, 128), 640)
    theirs = pl.ds(pl.multiple_of(640 * (1 - c), 128), 640)
    return ours, theirs


def lane_slab(ref, lanes):
    return lambda at: ref.at[:, pl.ds(pl.multiple_of(80 * at, 16), 80), lanes]


def lane_part(ref, lanes):
    def part(at, way):
        if way > 0:
            rows = pl.ds(pl.multiple_of(80 * at, 16), LOW_ROWS)
        else:
            rows = pl.ds(pl.multiple_of(80 * at + LOW_ROWS, 16), 80 - LOW_ROWS)
        return ref.at[:, rows, lanes]

    return part


def join_cores(c, shard, shard_sib, own_block, ours):
    for j in range(own_block.shape[0]):
        near = shard[j, :, ours].astype(F32)
        far = shard_sib[j].astype(F32)
        upper = jnp.where(c == 0, near, far)
        lower = jnp.where(c == 0, far, near)
        own_block[j] = jnp.concatenate([upper, lower], axis=0).astype(BF16)


class Ring:
    def __init__(self, own, slab, part, send, recv, h_send, h_recv):
        z, x, c, y = spot()
        self.first, self.second, self.block = torus(z, x, c, y)
        self.sibling = device(z, x, 1 - c, y)
        self.own, self.slab, self.part = own, slab, part
        self.send, self.recv, self.h_send, self.h_recv = send, recv, h_send, h_recv

    def ship(self, src, dst, at, to):
        return remote(src, dst, self.send.at[at], self.recv.at[at], to)

    def one(self, way):
        at = self.block(0, 0)
        return self.ship(self.own, self.slab(at), 0 if way > 0 else 1, self.first(way))

    def one_on(self, way):
        piece = self.part(self.block(-way, 0), way)
        return self.ship(piece, piece, 2 if way > 0 else 3, self.first(way))

    def two(self, d1, way):
        at = self.block(d1, 0)
        src = self.own if d1 == 0 else self.slab(at)
        return self.ship(src, self.slab(at), 4 + 4 * d1 + (0 if way > 0 else 1), self.second(way))

    def two_on(self, d1, way):
        piece = self.part(self.block(d1, -way), way)
        return self.ship(piece, piece, 6 + 4 * d1 + (0 if way > 0 else 1), self.second(way))

    def hand(self, d1, d2):
        at = self.block(d1, d2)
        src = self.own if d1 == 0 and d2 == 0 else self.slab(at)
        k = 4 * d1 + d2
        return remote(src, self.slab(at), self.h_send.at[k], self.h_recv.at[k], self.sibling)

    def open(self):
        self.one(1).start()
        self.one(-1).start()
        self.spread(0)

    def spread(self, d1):
        self.two(d1, 1).start()
        self.two(d1, -1).start()
        self.hand(d1, 0).start()

    def near(self):
        self.one(1).wait_recv()
        self.one_on(1).start()
        self.spread(3)
        self.one(-1).wait_recv()
        self.one_on(-1).start()
        self.spread(1)

    def far(self):
        self.one_on(1).wait_recv()
        self.one_on(-1).wait_recv()
        self.spread(2)

    def turn(self, d1):
        self.two(d1, 1).wait_recv()
        self.two_on(d1, 1).start()
        self.hand(d1, 3).start()
        self.two(d1, -1).wait_recv()
        self.two_on(d1, -1).start()
        self.hand(d1, 1).start()

    def end(self, d1):
        self.two_on(d1, 1).wait_recv()
        self.two_on(d1, -1).wait_recv()
        self.hand(d1, 2).start()

    def arrive(self):
        for d1 in range(4):
            for d2 in range(4):
                self.hand(d1, d2).wait_recv()

    def close(self):
        for way in (1, -1):
            self.one(way).wait_send()
            self.one_on(way).wait_send()
            for d1 in range(4):
                self.two(d1, way).wait_send()
                self.two_on(d1, way).wait_send()
        for d1 in range(4):
            for d2 in range(4):
                self.hand(d1, d2).wait_send()

    def steps(self):
        return [
            self.near,
            lambda: self.turn(0),
            self.far,
            lambda: self.turn(3),
            lambda: self.turn(1),
            lambda: self.end(0),
            lambda: self.turn(2),
            lambda: self.end(3),
            lambda: self.end(1),
            lambda: self.end(2),
        ]


def ring_scratch():
    return [DMA((20,)), DMA((20,)), DMA((16,)), DMA((16,))]


def rope_wide(cos_block, sin_block, turn):
    place = lax.axis_index("row")
    cos_at = turn[place, 0:1, :]
    sin_at = turn[place, 1:2, :]
    cosine = cos_block[...] * cos_at - sin_block[...] * sin_at
    sine = sin_block[...] * cos_at + cos_block[...] * sin_at
    lane = lax.broadcasted_iota(jnp.int32, sine.shape, 1)
    return cosine, jnp.where(lax.rem(lane, 64) < 32, -sine, sine)


def swap_halves(v):
    lane = lax.broadcasted_iota(jnp.int32, v.shape, 1)
    return jnp.where(lax.rem(lane, 64) < 32, pltpu.roll(v, 96, 1), pltpu.roll(v, 32, 1))


def over_heads(v):
    low = half_mask(0)
    left = jnp.sum(jnp.where(low, v, 0.0), axis=1, keepdims=True)
    right = jnp.sum(jnp.where(low, 0.0, v), axis=1, keepdims=True)
    return jnp.where(low, left, right)


def head_norm(raw, cosine, sine):
    scale = lax.rsqrt(over_heads(raw * raw) + EPS)
    return (raw * cosine + swap_halves(raw) * sine) * scale, scale


def front_kernel(
    hid,
    tea,
    query_w,
    key_w,
    value_w,
    out_w,
    rate_one,
    rate_two,
    valid,
    seg,
    score_gain,
    cos_block,
    sin_block,
    turn,
    hid_out,
    hid_tok,
    tea_tok,
    rates_out,
    count_out,
    mask_out,
    gains_out,
    weights,
    raw_out,
    q_pad,
    win_out,
    att,
    out_t,
    lse,
    starts_out,
    hid_t,
    hid_n,
    tea_t,
    rates,
    count,
    count_rows,
    rate_buf,
    shard,
    shard_sib,
    own_block,
    w_first,
    win,
    o_acc,
    l_acc,
    y_send,
    y_recv,
    s_send,
    s_recv,
    local_sem,
    k_send,
    k_recv,
    a_send,
    a_recv,
    a_hsend,
    a_hrecv,
    t_accs,
    t_parts,
    t_send,
    t_recv,
):
    z, x, c, y = spot()
    place = 2 * x + c
    sibling = device(z, x, 1 - c, y)
    across = [device(z, x, c, wrap(y + d)) for d in (1, 2, 3)]
    tally = Tally(count, t_accs, t_parts, t_send, t_recv)

    shard[0] = jnp.concatenate(
        [query_w[:, 256:], out_w[...], query_w[:, :256], key_w[...], value_w[...]], axis=1
    )
    rates[0:1, :] = rate_one[...].reshape(1, COLS)
    rates[1:2, :] = rate_two[...].reshape(1, COLS)
    token_mask = valid[...].reshape(1, ROWS).astype(F32)
    count[...] = jnp.broadcast_to(jnp.sum(token_mask, axis=1, keepdims=True), (8, 128))
    meet(across + tally.peers[0] + tally.peers[1] + tally.peers[2])

    ours, theirs = lane_halves(c)
    ring_a = Ring(own_block, lane_slab(w_first, ours), lane_part(w_first, ours), a_send, a_recv, a_hsend, a_hrecv)
    head = remote(shard.at[:, :, theirs], shard_sib, s_send, s_recv, sibling)
    head.start()
    my_feats = pl.ds(pl.multiple_of(COLS * y, 64), COLS)
    hid_r = remote(hid, hid_t.at[my_feats], y_send.at[0], y_recv.at[0], across[0])
    hid_l = remote(hid, hid_t.at[my_feats], y_send.at[1], y_recv.at[1], across[2])
    hid_r.start()
    hid_l.start()
    hid_own = pltpu.make_async_copy(hid, hid_t.at[my_feats], local_sem.at[0])
    hid_own.start()
    tea_own = pltpu.make_async_copy(
        tea.at[:, pl.ds(pl.multiple_of(TOK * y, TOK), TOK)], tea_t.at[my_feats], local_sem.at[1]
    )
    tea_own.start()

    head.wait()
    join_cores(c, shard, shard_sib, own_block, ours)
    ring_a.open()
    own_at = ring_a.block(0, 0)
    own_a = pltpu.make_async_copy(own_block, ring_a.slab(own_at), local_sem.at[2])
    own_a.start()
    tally.start(0)
    small = []
    for d in (1, 2, 3):
        rows = pl.ds(pl.multiple_of(TOK * wrap(y + d), TOK), TOK)
        pieces = ((tea.at[:, rows], tea_t.at[my_feats]), (rates, rate_buf.at[y]))
        for k, (src, dst) in enumerate(pieces):
            at = 4 + 2 * (d - 1) + k
            copy = remote(src, dst, y_send.at[at], y_recv.at[at], across[d - 1])
            copy.start()
            small.append(copy)
    rate_buf[y] = rates[...]
    gains = jnp.concatenate([score_gain[...].reshape(1, COLS), jnp.zeros((1, 64), F32)], axis=1)
    gains_out[...] = gains
    token = pl.ds(pl.multiple_of(TOK * y, TOK), TOK)
    count_rows[0:1, :] = token_mask
    mask_out[...] = jnp.broadcast_to(count_rows[0:1, token], (TOK, TOK)).T

    first = jnp.sum((seg[...] < 1).astype(jnp.int32), axis=1, keepdims=True)
    second = jnp.sum((seg[...] < 2).astype(jnp.int32), axis=1, keepdims=True)
    query_seg = seg[:, pl.ds(pl.multiple_of(ROWS * place, ROWS), ROWS)]
    starts = jnp.where(query_seg == 0, 0, jnp.where(query_seg == 1, first, second))
    starts_out[...] = starts - (place - 4) * ROWS
    o_acc[...] = jnp.zeros_like(o_acc)
    l_acc[...] = jnp.zeros_like(l_acc)

    ring_a.near()
    ring_a.turn(0)
    ring_a.far()
    hid_r.wait_recv()
    hid_f_ref = hid_t.at[pl.ds(pl.multiple_of(COLS * wrap(y - 1), 64), 160)]
    hid_f = remote(hid_f_ref, hid_f_ref, y_send.at[2], y_recv.at[2], across[0])
    hid_f.start()
    hid_l.wait_recv()
    hid_g_ref = hid_t.at[pl.ds(pl.multiple_of(COLS * wrap(y + 1) + 160, 32), 160)]
    hid_g = remote(hid_g_ref, hid_g_ref, y_send.at[3], y_recv.at[3], across[2])
    hid_g.start()
    ring_a.turn(3)
    ring_a.turn(1)
    tally.finish(0)
    tally.start(1)
    ring_a.end(0)
    ring_a.turn(2)
    ring_a.end(3)
    ring_a.end(1)
    ring_a.end(2)
    tally.finish(1)
    tally.start(2)
    hid_own.wait()
    hid_f.wait_recv()
    hid_g.wait_recv()
    hid_save = pltpu.make_async_copy(hid_t, hid_out, local_sem.at[4])
    hid_save.start()
    for g in range(10):
        hid_n[:, 128 * g : 128 * g + 128] = hid_t[128 * g : 128 * g + 128, :].T
    own_a.wait()
    ring_a.arrive()
    w_save = pltpu.make_async_copy(w_first.at[0], weights, local_sem.at[5])
    w_save.start()

    cosine, sine = rope_wide(cos_block, sin_block, turn)
    raw = dot_nn(hid_n[...], w_first[0, :, 640:1280])
    for g in range(3):
        group = raw[:, 128 * g : 128 * g + 128]
        raw_out[3 + g] = group
        normed, _ = head_norm(group, cosine, sine)
        keys = normed * gains[:, 128 * g : 128 * g + 128]
        if g == 2:
            keys = jnp.where(half_mask(0), keys, group)
        win[4 * ROWS :, 128 * g : 128 * g + 128] = keys.astype(BF16)
    win[4 * ROWS :, 384:640] = raw[:, 384:640].astype(BF16)

    def slot(s):
        return win.at[pl.ds(pl.multiple_of(ROWS * s, ROWS), ROWS)]

    one = remote(slot(4), slot(2), k_send.at[0], k_recv.at[0], device(z, wrap(x + 1), c, y))
    two = remote(slot(4), slot(0), k_send.at[1], k_recv.at[1], device(z, wrap(x + 2), c, y))
    own = remote(slot(4), slot(3), k_send.at[2], k_recv.at[2], sibling)
    one_on = remote(slot(2), slot(1 + 2 * c), k_send.at[3], k_recv.at[3], sibling)
    two_on = remote(slot(0), slot(1), k_send.at[4], k_recv.at[4], sibling)

    @pl.when(x < 3)
    def _():
        one.start()

    @pl.when(x < 2)
    def _():
        two.start()

    @pl.when(c == 0)
    def _():
        own.start()

    root = math.sqrt(HEAD_DIM)
    for g, at in enumerate((384, 512, 0)):
        group = dot_nn(hid_n[...], w_first[0, :, at : at + 128])
        raw_out[g] = group
        normed, _ = head_norm(group, cosine, sine)
        scaled = (normed * gains[:, 128 * g : 128 * g + 128]).astype(BF16) * jnp.asarray(root, BF16)
        for half in range(2 if g < 2 else 1):
            q_pad[2 * g + half] = jnp.where(half_mask(half), scaled, jnp.zeros_like(scaled))
    hid_tok[...] = hid_n[pl.ds(pl.multiple_of(TOK * y, TOK), TOK), :]

    def tile(t):
        rows = pl.ds(pl.multiple_of(t * TILE, TILE), TILE)
        key_at = t * TILE + lax.broadcasted_iota(jnp.int32, (TILE, ROWS), 0)
        query_at = 4 * ROWS + lax.broadcasted_iota(jnp.int32, (TILE, ROWS), 1)
        allowed = (key_at >= starts_out[...]) & (key_at <= query_at)
        for h in range(HEADS):
            kg, _ = key_place(h)
            vg, vh = value_place(h)
            keys = win[rows, 128 * kg : 128 * kg + 128]
            values = win[rows, 128 * vg : 128 * vg + 128]
            scores = dot_nt(keys, q_pad[h])
            probs = jnp.where(allowed, jnp.exp(scores), 0.0)
            l_acc[h] += jnp.sum(probs.reshape(TILE // 8, 8, ROWS), axis=0)
            both = dot_tn(values, probs.astype(BF16))
            o_acc[h] += both[64 * vh : 64 * vh + 64, :]

    def step(i, carry):
        k = lax.div(i, 2)
        turned = k - 1 + 2 * lax.rem(k, 2)
        s = jnp.where(k == 0, 4, jnp.where(c == 1, 4 - k, 4 - turned))

        @pl.when((i == 2) & (c == 1))
        def _():
            own.wait_recv()

        @pl.when((x > 0) & (((i == 4) & (c == 1)) | ((i == 2) & (c == 0))))
        def _():
            one.wait_recv()
            one_on.start()

        @pl.when((x > 0) & (((i == 6) & (c == 1)) | ((i == 4) & (c == 0))))
        def _():
            one_on.wait_recv()

        @pl.when((x > 1) & (((i == 8) & (c == 1)) | ((i == 6) & (c == 0))))
        def _():
            two.wait_recv()

            @pl.when(c == 1)
            def _():
                two_on.start()

        @pl.when((x > 1) & (i == 8) & (c == 0))
        def _():
            two_on.wait_recv()

        @pl.when(place + s >= 4)
        def _():
            tile(2 * s + lax.rem(i, 2))

        return carry

    lax.fori_loop(0, 10, step, 0)
    win_save = pltpu.make_async_copy(win, win_out, local_sem.at[6])
    win_save.start()
    for copy in small:
        copy.wait_recv()
    tea_own.wait()
    for g in range(10):
        tea_tok[:, 128 * g : 128 * g + 128] = tea_t[128 * g : 128 * g + 128, :].T
    rates_out[...] = jnp.concatenate([rate_buf[k] for k in range(4)], axis=1)
    tally.finish(2)
    count_out[...] = t_accs[2]
    for h in range(HEADS):
        total = jnp.sum(l_acc[h], axis=0, keepdims=True)
        lse[h] = jnp.broadcast_to(jnp.log(total), (8, ROWS))
        out_t[64 * h : 64 * h + 64, :] = o_acc[h] / total
    wide = jnp.concatenate([jnp.zeros((64, ROWS), F32), out_t[...]], axis=0)
    att[...] = wide.T.astype(BF16)
    ring_a.close()
    hid_save.wait()
    w_save.wait()
    win_save.wait()
    for copy in small + [hid_r, hid_l, hid_f, hid_g]:
        copy.wait_send()

    @pl.when(x < 3)
    def _():
        one.wait_send()

    @pl.when(x < 2)
    def _():
        two.wait_send()

    @pl.when(c == 0)
    def _():
        own.wait_send()

    @pl.when(x > 0)
    def _():
        one_on.wait_send()

    @pl.when((x > 1) & (c == 1))
    def _():
        two_on.wait_send()

    tally.close()


def rope_constants():
    inverse = np.exp(np.arange(32) * (-2.0 * math.log(10000.0) / HEAD_DIM))
    inverse = np.tile(inverse, 4)
    inside = np.arange(ROWS)[:, None] * inverse[None, :]
    at = (ROWS * np.arange(8))[:, None] * inverse[None, :]
    turn = np.stack([np.cos(at), np.sin(at)], axis=1)
    return [jnp.asarray(v, F32) for v in (np.cos(inside), np.sin(inside), turn)]


def front(hidden, teacher, others):
    sds = jax.ShapeDtypeStruct
    outs = [
        (sds((D, ROWS), BF16), IN_PLACE),
        (sds((TOK, D), BF16), IN_VMEM),
        (sds((TOK, D), BF16), IN_VMEM),
        (sds((2, D), F32), IN_VMEM),
        (sds((8, 128), F32), IN_VMEM),
        (sds((TOK, TOK), F32), IN_VMEM),
        (sds((1, 384), F32), IN_VMEM),
        (sds((D, D), BF16), IN_PLACE),
        (sds((6, ROWS, 128), F32), IN_VMEM),
        (sds((HEADS, ROWS, 128), BF16), IN_VMEM),
        (sds((5 * ROWS, 2 * COLS), BF16), IN_PLACE),
        (sds((ROWS, 384), BF16), IN_VMEM),
        (sds((COLS, ROWS), F32), IN_VMEM),
        (sds((HEADS, 8, ROWS), F32), IN_VMEM),
        (sds((1, ROWS), jnp.int32), IN_VMEM),
    ]
    return pl.pallas_call(
        front_kernel,
        out_shape=tuple(o[0] for o in outs),
        in_specs=[IN_PLACE] * 2 + [IN_VMEM] * len(others),
        out_specs=tuple(o[1] for o in outs),
        scratch_shapes=[
            VMEM((D, ROWS), BF16),
            VMEM((ROWS, D), BF16),
            VMEM((D, TOK), BF16),
            VMEM((2, COLS), F32),
            VMEM((8, 128), F32),
            VMEM((8, ROWS), F32),
            VMEM((4, 2, COLS), F32),
            VMEM((1, 40, D), BF16),
            VMEM((1, 40, 640), BF16),
            VMEM((1, 80, 640), BF16),
            VMEM((1, D, D), BF16),
            VMEM((5 * ROWS, 2 * COLS), BF16),
            VMEM((HEADS, 64, ROWS), F32),
            VMEM((HEADS, 8, ROWS), F32),
            DMA((10,)),
            DMA((10,)),
            DMA,
            DMA,
            DMA((7,)),
            DMA((5,)),
            DMA((5,)),
        ]
        + ring_scratch()
        + tally_scratch((8, 128)),
        compiler_params=params(0),
        name="front",
    )(hidden, teacher, *others)


def mix_forward(states, branch, alphas):
    branch_scale = lax.rsqrt(jnp.sum(branch * branch, axis=1, keepdims=True) + EPS)
    normed = branch * branch_scale
    mixed = states + alphas * (normed - states)
    mixed_scale = lax.rsqrt(jnp.sum(mixed * mixed, axis=1, keepdims=True) + EPS)
    return mixed * mixed_scale, normed, branch_scale, mixed_scale


def mix_backward(gradient, states, normed, branch_scale, mixed_out, mixed_scale, alphas):
    along = jnp.sum(mixed_out * gradient, axis=1, keepdims=True)
    mixed_grad = mixed_scale * (gradient - mixed_out * along)
    normed_grad = alphas * mixed_grad
    toward = jnp.sum(normed * normed_grad, axis=1, keepdims=True)
    branch_grad = branch_scale * (normed_grad - normed * toward)
    rate_grad = jnp.sum(mixed_grad * (normed - states), axis=0, keepdims=True)
    return (1.0 - alphas) * mixed_grad, branch_grad, rate_grad


def swiglu_parts(gate_raw, up_raw, gate_gain, up_gain):
    root = math.sqrt(D)
    g = gate_gain * gate_raw * root
    q = jax.nn.sigmoid(g)
    return g, q


def middle_kernel(
    att,
    hid_tok,
    tea,
    mask,
    count,
    rates,
    up_gain_in,
    gate_gain_in,
    gate_w,
    up_w,
    down_w,
    weights,
    output,
    attn_grad,
    d_att,
    res_zero,
    small,
    gate_out,
    up_out,
    down_out,
    in_one,
    product,
    mlp_grad,
    gate_low,
    up_low,
    w_out,
    w_all,
    grads,
    shard,
    shard_sib,
    own_block,
    raw_gate,
    raw_up,
    send_buf,
    got_buf,
    own_part,
    out_buf,
    state,
    normed,
    scales,
    w_sem,
    g_sem,
    s_send,
    s_recv,
    b_send,
    b_recv,
    b_hsend,
    b_hrecv,
    ag_send,
    ag_recv,
    rs_send,
    rs_recv,
    o_send,
    o_recv,
):
    z, x, c, y = spot()
    peers = [device(z, x, c, wrap(y + d)) for d in range(4)]
    load = pltpu.make_async_copy(weights.at[:, pl.ds(0, 384)], w_out, w_sem.at[0])
    load.start()
    shard[0] = gate_w[...]
    shard[1] = up_w[...]
    shard[2] = down_w[...]
    up_gain = up_gain_in[...].reshape(1, D)
    gate_gain = gate_gain_in[...].reshape(1, D)
    w_gate, w_up, w_down = (w_all.at[k] for k in range(3))
    sibling = device(z, x, 1 - c, y)
    ring_peers = [device(z, wrap(x + d), c, y) for d in (1, 3)]
    ring_peers += [device(wrap(z + d), x, c, y) for d in (1, 3)]
    meet(peers[1:] + ring_peers + [sibling])
    ours, theirs = lane_halves(c)
    ring = Ring(
        own_block, lane_slab(w_all, ours), lane_part(w_all, ours), b_send, b_recv, b_hsend, b_hrecv
    )
    head = remote(shard.at[:, :, theirs], shard_sib, s_send, s_recv, sibling)
    head.start()
    my_rows = pl.ds(pl.multiple_of(TOK * y, TOK), TOK)

    def rows_of(k):
        return pl.ds(pl.multiple_of(TOK * wrap(y - k), TOK), TOK)

    def feats(k):
        return pl.ds(pl.multiple_of(COLS * k, 64), COLS)

    def back_to(k):
        return device(z, x, c, wrap(y - k))

    def scatter(stage, k):
        return remote(
            send_buf.at[stage, k - 1],
            got_buf.at[stage, k - 1],
            rs_send.at[stage, k],
            rs_recv.at[stage, k],
            back_to(k),
        )

    def spread(stage, src, k):
        return remote(
            src.at[my_rows],
            src.at[my_rows],
            ag_send.at[stage, k],
            ag_recv.at[stage, k],
            device(z, x, c, wrap(y + k)),
        )

    def give(stage, k, part):
        @pl.when(k == 0)
        def _():
            own_part[...] = part

        @pl.when(k > 0)
        def _():
            send_buf[stage, k - 1] = part.astype(BF16)
            scatter(stage, k).start()

    def collect(stage):
        total = own_part[...]
        for k in (1, 2, 3):
            scatter(stage, k).wait_recv()
            total = total + got_buf[stage, k - 1].astype(F32)
        return total

    def announce(stage, ref, value):
        ref[my_rows, :] = value.astype(BF16)
        for k in (2, 1, 3):
            spread(stage, ref, k).start()

    def each(body, stage=None, ref=None):
        def step(k, carry):
            if ref is not None:

                @pl.when(k > 0)
                def _():
                    spread(stage, ref, k).wait_recv()

            body(k)
            return carry

        lax.fori_loop(0, 4, step, 0)

    load.wait()
    for k in (2, 1, 3):
        send_buf[0, k - 1] = dot_nt(att[rows_of(k), :], w_out[...]).astype(BF16)
        scatter(0, k).start()
    head.wait()
    join_cores(c, shard, shard_sib, own_block, ours)
    ring.open()
    ring_own = pltpu.make_async_copy(own_block, ring.slab(ring.block(0, 0)), w_sem.at[1])
    ring_own.start()
    own_part[...] = dot_nt(att[my_rows, :], w_out[...])
    ring.near()
    ring.turn(0)
    ring.far()
    attn = collect(0)
    states = hid_tok[...].astype(F32)
    one, normed_one, branch_one, scale_one = mix_forward(states, attn, rates[0:1, :])
    announce(0, in_one, one)
    state[0] = one
    normed[0] = normed_one
    scales[0] = jnp.broadcast_to(branch_one, (TOK, 128))
    scales[1] = jnp.broadcast_to(scale_one, (TOK, 128))
    ring.turn(3)
    ring.turn(1)
    ring.end(0)
    ring.turn(2)
    ring.end(3)
    ring.end(1)
    ring.end(2)
    ring_own.wait()
    ring.arrive()

    def feed(k):
        rows = rows_of(k)
        block = in_one[rows, :]
        gate_raw = dot_nn(block, w_gate[...])
        raw_gate[rows, :] = gate_raw
        up_raw = dot_nn(block, w_up[...])
        raw_up[rows, :] = up_raw
        g, q = swiglu_parts(gate_raw, up_raw, gate_gain, up_gain)
        low = (up_gain * up_raw * (g * q)).astype(BF16)
        product[rows, :] = low
        give(1, k, dot_nt(low, w_down[...]))

    each(feed, 0, in_one)
    mlp = collect(1)
    one = state[0]
    two, normed_two, branch_two, scale_two = mix_forward(one, mlp, rates[1:2, :])
    for g in range(10):
        out_buf[128 * g : 128 * g + 128, :] = two[:, 128 * g : 128 * g + 128].T.astype(BF16)
    out_copies = []
    for k in (1, 2, 3):
        copy = remote(
            out_buf.at[feats(wrap(y + k))],
            output.at[:, my_rows],
            o_send.at[k],
            o_recv.at[k],
            device(z, x, c, wrap(y + k)),
        )
        out_copies.append(copy)
    errors = two - tea[...].astype(F32)
    weight = mask[:, 0:1]
    loss = jnp.sum(weight * errors * errors)
    factor = 16384 * math.sqrt(D) / count[0:1, 0:1]
    seed = factor * (weight * errors)
    res_one, mlp_back, rate_two = mix_backward(
        seed, one, normed_two, branch_two, two, scale_two, rates[1:2, :]
    )
    announce(1, mlp_grad, mlp_back)
    for copy in out_copies:
        copy.start()
    output[:, my_rows] = out_buf[feats(y), :]
    small[...] = jnp.zeros_like(small)
    small[1:2, :] = rate_two
    small[4:5, :] = jnp.broadcast_to(loss, (1, D))
    state[1] = res_one

    def unfeed(k):
        rows = rows_of(k)
        grad = dot_nn(mlp_grad[rows, :], w_down[...])
        gate_raw = raw_gate[rows, :]
        up_raw = raw_up[rows, :]
        g, q = swiglu_parts(gate_raw, up_raw, gate_gain, up_gain)
        silu = g * q
        up_term = grad * silu
        slope = grad * up_gain * up_raw * (q * (1.0 + g * (1.0 - q))) * math.sqrt(D)
        small[2:3, :] += jnp.sum(up_term * up_raw, axis=0, keepdims=True)
        small[3:4, :] += jnp.sum(slope * gate_raw, axis=0, keepdims=True)
        up_back = (up_term * up_gain).astype(BF16)
        gate_back = (slope * gate_gain).astype(BF16)
        up_low[rows, :] = up_back
        gate_low[rows, :] = gate_back
        give(2, k, dot_nt(gate_back, w_gate[...]) + dot_nt(up_back, w_up[...]))

    each(unfeed, 1, mlp_grad)

    def weight_grad(j, left, right, out):
        def step(k, carry):
            rows = pl.ds(pl.multiple_of(256 * k, 256), 256)
            grads[j, rows, :] = dot_tn(left[:, rows], right[...]).astype(BF16)
            return carry

        lax.fori_loop(0, 5, step, 0)
        pltpu.make_async_copy(grads.at[j], out, g_sem.at[j]).start()

    weight_grad(2, mlp_grad, product, down_out)
    grad_one = state[1] + collect(2)
    states = hid_tok[...].astype(F32)
    res, attn_back, rate_one = mix_backward(
        grad_one,
        states,
        normed[0],
        scales[0, :, 0:1],
        state[0],
        scales[1, :, 0:1],
        rates[0:1, :],
    )
    announce(2, attn_grad, attn_back)
    small[0:1, :] = rate_one
    for g in range(10):
        res_zero[128 * g : 128 * g + 128, :] = res[:, 128 * g : 128 * g + 128].T

    def unproject(k):
        rows = rows_of(k)
        d_att[rows, :] = dot_nn(attn_grad[rows, :], w_out[...]).astype(BF16)

    weight_grad(0, in_one, gate_low, gate_out)
    weight_grad(1, in_one, up_low, up_out)
    each(unproject, 2, attn_grad)
    for j, out in enumerate((gate_out, up_out, down_out)):
        pltpu.make_async_copy(grads.at[j], out, g_sem.at[j]).wait()
    ring.close()
    for k in (1, 2, 3):
        for stage in range(3):
            scatter(stage, k).wait_send()
        spread(0, in_one, k).wait_send()
        spread(1, mlp_grad, k).wait_send()
        spread(2, attn_grad, k).wait_send()
    for copy in out_copies:
        copy.wait()


def middle(vmem_args, weights):
    sds = jax.ShapeDtypeStruct
    wide = VMEM((ROWS, D), BF16)
    square = sds((D, D), BF16)
    return pl.pallas_call(
        middle_kernel,
        out_shape=(
            sds((COLS, ROWS), BF16),
            sds((ROWS, D), BF16),
            sds((ROWS, 384), BF16),
            sds((D, TOK), F32),
            sds((8, D), F32),
            square,
            square,
            square,
        ),
        in_specs=[IN_VMEM] * len(vmem_args) + [IN_PLACE],
        out_specs=(IN_VMEM,) * 5 + (IN_PLACE,) * 3,
        scratch_shapes=[
            wide,
            wide,
            wide,
            wide,
            wide,
            VMEM((D, 384), BF16),
            VMEM((3, D, D), BF16),
            VMEM((3, D, D), BF16),
            VMEM((3, 40, D), BF16),
            VMEM((3, 40, 640), BF16),
            VMEM((3, 80, 640), BF16),
            VMEM((ROWS, D), F32),
            VMEM((ROWS, D), F32),
            VMEM((3, 3, TOK, D), BF16),
            VMEM((3, 3, TOK, D), BF16),
            VMEM((TOK, D), F32),
            VMEM((D, TOK), BF16),
            VMEM((2, TOK, D), F32),
            VMEM((1, TOK, D), F32),
            VMEM((2, TOK, 128), F32),
            DMA((2,)),
            DMA((3,)),
            DMA,
            DMA,
        ]
        + ring_scratch()
        + [
            DMA((3, 4)),
            DMA((3, 4)),
            DMA((3, 4)),
            DMA((3, 4)),
            DMA((4,)),
            DMA((4,)),
        ],
        compiler_params=params(1),
        name="middle",
    )(*vmem_args, weights)


class Fold:
    def __init__(self, bufs, sems, z_heavy):
        z, x, c, y = spot()
        self.z, self.x, self.c = z, x, c
        self.z_heavy = z_heavy
        if z_heavy:
            self.first = lambda d: device(z, wrap(x + d), c, y)
            self.second = lambda d: device(wrap(z + d), x, c, y)
            self.at_first = x
        else:
            self.first, self.second, _ = torus(z, x, c, y)
            self.at_first = x * (1 - c) + z * c
        self.sibling = device(z, x, 1 - c, y)
        self.own, self.sib, self.got_two, self.mid, self.got_one, self.fin = bufs
        self.l_sem, self.h_send, self.h_recv, self.b_send, self.b_recv, self.a_send, self.a_recv, self.f_send, self.f_recv = sems
        self.count = self.own.shape[0]
        self.lanes = pl.ds(pl.multiple_of(640 * c, 128), 640)
        self.other = pl.ds(pl.multiple_of(640 * (1 - c), 128), 640)

    def handed(self, j, d, src):
        return remote(src, self.sib.at[j, d], self.h_send.at[j, d], self.h_recv.at[j, d], self.sibling)

    def fetched(self, j, d, src):
        return pltpu.make_async_copy(src, self.own.at[j, d], self.l_sem.at[j, d])

    def open(self, srcs):
        z, x = self.z, self.x
        if self.z_heavy:
            for d in (2, 1, 3, 0):
                for j, src in enumerate(srcs):
                    self.handed(j, d, src.at[wrap(z + d), :, :, self.other]).start()
                    self.fetched(j, d, src.at[wrap(z + d), :, :, self.lanes]).start()
            return

        @pl.when(self.c == 0)
        def _():
            for d in (2, 1, 3, 0):
                for j, src in enumerate(srcs):
                    self.handed(j, d, src.at[:, wrap(x + d), :, self.other]).start()
                    self.fetched(j, d, src.at[wrap(z + d), :, :, self.lanes]).start()

        @pl.when(self.c == 1)
        def _():
            for d in (2, 1, 3, 0):
                for j, src in enumerate(srcs):
                    self.handed(j, d, src.at[wrap(z + d), :, :, self.other]).start()
                    self.fetched(j, d, src.at[:, wrap(x + d), :, self.lanes]).start()

    def pair(self, d):
        return remote(
            self.own.at[:, d], self.got_two.at[:, d - 1], self.b_send.at[d], self.b_recv.at[d], self.second(d)
        )

    def last(self, e):
        return remote(
            self.mid.at[:, e - 1], self.got_one.at[:, e - 1], self.a_send.at[e], self.a_recv.at[e], self.first(e)
        )

    def add(self, d):
        for j in range(self.count):
            blank = self.sib.at[j, d]
            self.fetched(j, d, blank).wait()
            self.handed(j, d, blank).wait_recv()

        def each(i, carry):
            j, a = lax.div(i, 4), lax.rem(i, 4)
            total = self.own[j, d, a].astype(F32) + self.sib[j, d, a].astype(F32)
            self.own[j, d, a] = total.astype(BF16)
            return carry

        lax.fori_loop(0, 4 * self.count, each, 0)
        if d:
            self.pair(d).start()

    def whole(self, j, at):
        total = self.own[j, 0, at].astype(F32)
        for d in (1, 2, 3):
            total = total + self.got_two[j, d - 1, at].astype(F32)
        return total

    def cross(self):
        for d in (1, 2, 3):
            self.pair(d).wait_recv()
        for e in (2, 1, 3):

            def each(j, carry, e=e):
                self.mid[j, e - 1] = self.whole(j, wrap(self.at_first + e)).astype(BF16)
                return carry

            lax.fori_loop(0, self.count, each, 0)
            self.last(e).start()

    def give(self, out):
        rows = pl.ds(pl.multiple_of(40 * (1 - self.c), 8), 40)
        return remote(self.fin.at[:, rows], out.at[:, :, self.lanes], self.f_send, self.f_recv, self.sibling)

    def finish(self, out):
        for e in (1, 2, 3):
            self.last(e).wait_recv()

        def each(j, carry):
            total = self.whole(j, self.at_first)
            for e in (1, 2, 3):
                total = total + self.got_one[j, e - 1].astype(F32)
            self.fin[j] = total
            return carry

        lax.fori_loop(0, self.count, each, 0)
        self.give(out).start()
        rows = pl.ds(pl.multiple_of(40 * self.c, 8), 40)
        for j in range(self.count):
            out[j, :, self.lanes] = self.fin[j, rows, :]

    def close(self, out):
        self.give(out).wait()
        for d in (1, 2, 3):
            self.pair(d).wait_send()
            self.last(d).wait_send()
        for j in range(self.count):
            for d in range(4):
                self.handed(j, d, self.sib.at[j, d]).wait_send()


def fold_scratch(count):
    block = (80, 640)
    return [
        VMEM((count, 4, 4) + block, BF16),
        VMEM((count, 4, 4) + block, BF16),
        VMEM((count, 3, 4) + block, BF16),
        VMEM((count, 3) + block, BF16),
        VMEM((count, 3) + block, BF16),
        VMEM((count,) + block, F32),
        DMA((count, 4)),
        DMA((count, 4)),
        DMA((count, 4)),
        DMA((4,)),
        DMA((4,)),
        DMA((4,)),
        DMA((4,)),
        DMA,
        DMA,
    ]


def head_back(grad, raw, gain, cosine, sine):
    normed, scale = head_norm(raw, cosine, sine)
    gain_grad = jnp.sum(grad * normed, axis=0, keepdims=True)
    pulled = grad * gain
    turned = scale * (pulled - normed * over_heads(normed * pulled))
    return turned * cosine + swap_halves(turned * sine), gain_grad


def tail_kernel(
    starts,
    q_pad,
    out_t,
    lse,
    d_att,
    att,
    gains,
    cos_block,
    sin_block,
    turn,
    res_t,
    small,
    count,
    win_in,
    raw_in,
    hid_in,
    w_in,
    attn_in,
    m0,
    m1,
    m2,
    hidden_grad,
    query_g,
    key_g,
    value_g,
    out_g,
    gate_g,
    up_g,
    down_g,
    sums_out,
    win,
    raw,
    hid_t,
    w_first,
    attn,
    d_pad,
    delta,
    q_acc,
    d_win,
    sib_one,
    sib_two,
    sib_own,
    one_buf,
    two_buf,
    got_one,
    got_two,
    kv_sum,
    pack,
    out_part,
    first_g,
    y_send_buf,
    y_got_buf,
    side_src,
    side_got,
    sums,
    m_out,
    f_out,
    in_sem,
    k_send,
    k_recv,
    y_send,
    y_recv,
    v_send,
    v_recv,
    *rest,
):
    m_bufs, m_sems, rest = rest[:6], rest[6:15], rest[15:]
    f_bufs, f_sems, rest = rest[:6], rest[6:15], rest[15:]
    t_accs, t_parts, t_send, t_recv = rest
    z, x, c, y = spot()
    place = 2 * x + c
    sibling = device(z, x, 1 - c, y)
    across = [device(z, x, c, wrap(y + d)) for d in (1, 2, 3)]
    tally = Tally(sums, t_accs, t_parts, t_send, t_recv)

    def slot(ref, s):
        return ref.at[pl.ds(pl.multiple_of(ROWS * s, ROWS), ROWS)]

    win_loads = [
        pltpu.make_async_copy(slot(win_in, s), slot(win, s), in_sem.at[s]) for s in range(5)
    ]
    for s in range(5):
        win_loads[s].start()
    loads = [
        pltpu.make_async_copy(src, dst, in_sem.at[5 + k])
        for k, (src, dst) in enumerate(
            ((raw_in, raw), (attn_in, attn), (w_in, w_first), (hid_in, hid_t))
        )
    ]
    meet(across + tally.peers[0] + tally.peers[1] + tally.peers[2])
    fold_m = Fold(m_bufs, m_sems, True)
    fold_f = Fold(f_bufs, f_sems, False)
    fold_m.open([m0, m1, m2])
    side_src[...] = jnp.zeros_like(side_src)
    for k in range(4):
        lanes = slice(COLS * k, COLS * (k + 1))
        side_src[k, 0:2, 0:COLS] = small[0:2, lanes]
        side_src[k, 2:3, 0:COLS] = small[4:5, lanes]

    def side(k):
        return remote(side_src.at[wrap(y + k)], side_got.at[k], v_send.at[k], v_recv.at[k], across[k - 1])

    for k in (1, 2, 3):
        side(k).start()
    for load in loads:
        load.start()

    for h in range(HEADS):
        d_pad[h] = pad_head(d_att, (h + 1) // 2, (h + 1) % 2)
    wide = d_att[...].astype(F32).T[64:, :] * out_t[...]
    for h in range(HEADS):
        delta[h] = jnp.broadcast_to(
            jnp.sum(wide[64 * h : 64 * (h + 1), :], axis=0, keepdims=True), (8, ROWS)
        )
    q_acc[...] = jnp.zeros_like(q_acc)

    hand_one = remote(slot(d_win, 3 - 2 * c), sib_one, k_send.at[0], k_recv.at[0], sibling)
    hand_two = remote(slot(d_win, 1), sib_two, k_send.at[1], k_recv.at[1], sibling)
    hand_own = remote(slot(d_win, 3), sib_own, k_send.at[2], k_recv.at[2], sibling)
    one = remote(one_buf, got_one, k_send.at[3], k_recv.at[3], device(z, wrap(x + 3), c, y))
    two = remote(two_buf, got_two, k_send.at[4], k_recv.at[4], device(z, wrap(x + 2), c, y))

    def tile(t):
        rows = pl.ds(pl.multiple_of(t * TILE, TILE), TILE)
        key_at = t * TILE + lax.broadcasted_iota(jnp.int32, (TILE, ROWS), 0)
        query_at = 4 * ROWS + lax.broadcasted_iota(jnp.int32, (TILE, ROWS), 1)
        allowed = (key_at >= starts[...]) & (key_at <= query_at)
        terms = [None] * 5
        for h in range(HEADS):
            kg, kh = key_place(h)
            vg, _ = value_place(h)
            keys = win[rows, 128 * kg : 128 * kg + 128]
            values = win[rows, 128 * vg : 128 * vg + 128]
            scores = dot_nt(keys, q_pad[h])
            probs = jnp.where(allowed, jnp.exp(scores - lse[h, 0:1, :]), 0.0)
            prob_grad = dot_nt(values, d_pad[h])
            score_grad = (probs * (prob_grad - delta[h, 0:1, :])).astype(BF16)
            v_term = dot_nn(probs.astype(BF16), d_pad[h])
            k_term = dot_nn(score_grad, q_pad[h])
            for at, term in ((kg, k_term), (vg, v_term)):
                terms[at] = term if terms[at] is None else terms[at] + term
            both = dot_tn(keys, score_grad)
            q_acc[h] += both[64 * kh : 64 * kh + 64, :]
        for g in range(5):
            d_win[rows, 128 * g : 128 * g + 128] = terms[g].astype(BF16)

    def after(k):
        if k == 0:

            @pl.when((c == 0) & (x > 1))
            def _():
                two_buf[...] = d_win[0:ROWS, :]
                two.start()

        if k == 1:

            @pl.when((c == 0) & (x > 1))
            def _():
                hand_two.start()

            @pl.when((c == 1) & (x > 0))
            def _():
                hand_one.start()

        if k == 2:

            @pl.when((c == 0) & (x > 0))
            def _():
                hand_one.start()

            @pl.when((c == 1) & (x > 1))
            def _():
                hand_two.wait_recv()
                two_buf[...] = (
                    d_win[0:ROWS, :].astype(F32) + sib_two[...].astype(F32)
                ).astype(BF16)
                two.start()

        if k == 3:

            @pl.when(x > 0)
            def _():
                hand_one.wait_recv()
                one_buf[...] = (
                    d_win[2 * ROWS : 3 * ROWS, :].astype(F32) + sib_one[...].astype(F32)
                ).astype(BF16)
                one.start()

            @pl.when(c == 1)
            def _():
                hand_own.start()

    for load in win_loads:
        load.wait()
    folds = {2: 2, 3: 1, 5: 3, 7: 0}

    def step(i, carry):
        k = lax.div(i, 2)
        s = jnp.where((c == 0) & (k == 2), 3, jnp.where((c == 0) & (k == 3), 2, k))

        @pl.when(place + s >= 4)
        def _():
            tile(2 * s + lax.rem(i, 2))

        for k in range(4):

            @pl.when(i == 2 * k + 1)
            def _(k=k):
                after(k)

        for n, d in folds.items():

            @pl.when(i == n)
            def _(d=d):
                fold_m.add(d)

        return carry

    lax.fori_loop(0, 10, step, 0)
    for load in loads:
        load.wait()
    cosine, sine = rope_wide(cos_block, sin_block, turn)
    pack[:, 128:384] = jnp.zeros((ROWS, 256), BF16)
    gain_parts = []
    wide = jnp.concatenate([q_acc[h] for h in range(HEADS)] + [jnp.zeros((64, ROWS), F32)], axis=0)
    for g, at in enumerate((384, 512, 0)):
        grad = wide[128 * g : 128 * g + 128, :].T * math.sqrt(HEAD_DIM)
        term, gain_part = head_back(grad, raw[g], gains[:, 128 * g : 128 * g + 128], cosine, sine)
        if g == 2:
            term = jnp.where(half_mask(0), term, 0.0)
        pack[:, at : at + 128] = term.astype(BF16)
        gain_parts.append(gain_part)
    out_part[...] = dot_tn(attn[...], att[...])

    kv_sum[...] = d_win[4 * ROWS :, :].astype(F32)

    @pl.when(c == 0)
    def _():
        hand_own.wait_recv()
        kv_sum[...] += sib_own[...].astype(F32)

    @pl.when(x < 3)
    def _():
        one.wait_recv()
        kv_sum[...] += got_one[...].astype(F32)

    @pl.when(x < 2)
    def _():
        two.wait_recv()
        kv_sum[...] += got_two[...].astype(F32)

    for g in range(3):
        grad = kv_sum[:, 128 * g : 128 * g + 128]
        gain = gains[:, 128 * g : 128 * g + 128]
        term, gain_part = head_back(grad, raw[3 + g], gain, cosine, sine)
        if g == 2:
            term = jnp.where(half_mask(0), term, grad)
        at = 640 + 128 * g
        pack[:, at : at + 128] = term.astype(BF16)
        gain_parts[g] += gain_part
    pack[:, 1024:1280] = kv_sum[:, 384:640].astype(BF16)

    my_cols = pl.ds(pl.multiple_of(TOK * y, TOK), TOK)

    def project(to):
        rows = pl.ds(pl.multiple_of(COLS * to, 64), COLS)
        hidden_grad[...] = dot_nt(w_first[rows, :], pack[...])
        hidden_grad[:, my_cols] += res_t[rows, :]

    def grad_copy(k):
        return remote(y_send_buf.at[k - 1], y_got_buf.at[k - 1], y_send.at[k], y_recv.at[k], across[k - 1])

    for k in (2, 1, 3):
        project(wrap(y + k))
        y_send_buf[k - 1] = hidden_grad[...].astype(BF16)
        grad_copy(k).start()

    extra = side_src[y]
    for k in (1, 2, 3):
        side(k).wait_recv()
        extra = extra + side_got[k]
    sums[...] = jnp.zeros_like(sums)
    sums[0:2, :] = small[2:4, :]
    sums[2:3, 0:384] = jnp.concatenate(gain_parts, axis=1)
    sums[3:6, 0:384] = extra[0:3, :]
    tally.start(0)

    def first_grad(k, carry):
        rows = pl.ds(pl.multiple_of(COLS * k, 64), COLS)
        grad = dot_nn(hid_t[rows, :], pack[...])
        low = grad[:, 0:384] + out_part[rows, :]
        for a in range(4):
            first_g[k, a, :, 0:384] = low[80 * a : 80 * a + 80].astype(BF16)
            first_g[k, a, :, 384:] = grad[80 * a : 80 * a + 80, 384:].astype(BF16)
        return carry

    lax.fori_loop(0, 4, first_grad, 0)
    fold_f.open([first_g])
    fold_m.cross()
    tally.finish(0)
    tally.start(1)
    project(y)
    for d in (2, 1, 3, 0):
        fold_f.add(d)
    for k in (1, 2, 3):
        grad_copy(k).wait_recv()
        hidden_grad[...] += y_got_buf[k - 1].astype(F32)
    tally.finish(1)
    tally.start(2)
    fold_m.finish(m_out)
    fold_f.cross()
    fold_f.finish(f_out)
    tally.finish(2)
    fold_m.close(m_out)
    fold_f.close(f_out)
    gate_g[...] = m_out[0]
    up_g[...] = m_out[1]
    down_g[...] = m_out[2]
    query_g[:, 0:256] = f_out[0, :, 384:640]
    query_g[:, 256:320] = f_out[0, :, 0:64]
    key_g[...] = f_out[0, :, 640:960]
    value_g[...] = f_out[0, :, 960:1280]
    out_g[...] = f_out[0, :, 64:384]
    sums_out[...] = t_accs[2]
    sums_out[6:7, :] = jnp.broadcast_to(count[0:1, 0:1], (1, D))
    for k in (1, 2, 3):
        grad_copy(k).wait_send()
        side(k).wait_send()

    @pl.when(x > 0)
    def _():
        hand_one.wait_send()
        one.wait_send()

    @pl.when(x > 1)
    def _():
        two.wait_send()

        @pl.when(c == 0)
        def _():
            hand_two.wait_send()

    @pl.when(c == 1)
    def _():
        hand_own.wait_send()

    tally.close()


def tail(vmem_args, placed_args):
    sds = jax.ShapeDtypeStruct
    block = VMEM((ROWS, 2 * COLS), BF16)
    shapes = [(COLS, ROWS)] + [(40, COLS)] * 4 + [(40, D)] * 3 + [(8, D)]
    return pl.pallas_call(
        tail_kernel,
        out_shape=tuple(sds(s, F32) for s in shapes),
        in_specs=[IN_VMEM] * len(vmem_args) + [IN_PLACE] * len(placed_args),
        out_specs=(IN_VMEM,) * len(shapes),
        scratch_shapes=[
            VMEM((5 * ROWS, 2 * COLS), BF16),
            VMEM((6, ROWS, 128), F32),
            VMEM((D, ROWS), BF16),
            VMEM((D, D), BF16),
            VMEM((ROWS, D), BF16),
            VMEM((HEADS, ROWS, 128), BF16),
            VMEM((HEADS, 8, ROWS), F32),
            VMEM((HEADS, 64, ROWS), F32),
            VMEM((5 * ROWS, 2 * COLS), BF16),
        ]
        + [block] * 7
        + [
            VMEM((ROWS, 2 * COLS), F32),
            VMEM((ROWS, D), BF16),
            VMEM((D, 384), F32),
            VMEM((4, 4, 80, D), BF16),
            VMEM((3, COLS, ROWS), BF16),
            VMEM((3, COLS, ROWS), BF16),
            VMEM((4, 8, 384), F32),
            VMEM((4, 8, 384), F32),
            VMEM((8, D), F32),
            VMEM((3, 40, D), F32),
            VMEM((1, 40, D), F32),
            DMA((9,)),
            DMA((5,)),
            DMA((5,)),
            DMA((4,)),
            DMA((4,)),
            DMA((4,)),
            DMA((4,)),
        ]
        + fold_scratch(3)
        + fold_scratch(1)
        + tally_scratch((8, D)),
        compiler_params=params(2),
        name="tail",
    )(*vmem_args, *placed_args)


def emit_kernel(sums, *refs):
    count = (len(refs) - 6) // 2
    for src, dst in zip(refs[:count], refs[count : 2 * count]):
        dst[...] = src[...]
    loss, attention, feedforward, score, up, gate = refs[2 * count :]
    loss[0] = jnp.sum(sums[5:6, 0:1] / sums[6:7, 0:1])
    score[...] = sums[2:3, 0:COLS].reshape(COLS)
    attention[...] = sums[3:4, 0:COLS].reshape(COLS)
    feedforward[...] = sums[4:5, 0:COLS].reshape(COLS)
    up[...] = sums[0:1, :].reshape(D)
    gate[...] = sums[1:2, :].reshape(D)


def emit(sums, arrays):
    sds = jax.ShapeDtypeStruct
    vectors = [sds((1,), F32)] + [sds((COLS,), F32)] * 3 + [sds((D,), F32)] * 2
    return pl.pallas_call(
        emit_kernel,
        out_shape=tuple(sds(a.shape, a.dtype) for a in arrays) + tuple(vectors),
        in_specs=[IN_VMEM] * (1 + len(arrays)),
        out_specs=(IN_VMEM,) * len(arrays) + (IN_SMEM,) + (IN_VMEM,) * 5,
        compiler_params=params(),
        name="emit",
    )(sums, *arrays)


def shards(
    hidden,
    teacher,
    valid_mask,
    segments,
    query_weight,
    key_weight,
    value_weight,
    out_weight,
    gate_weight,
    up_weight,
    down_weight,
    attention_rate,
    feedforward_rate,
    score_gain,
    up_gain,
    gate_gain,
):
    ropes = rope_constants()
    others = (query_weight, key_weight, value_weight, out_weight.T)
    others += (attention_rate, feedforward_rate, valid_mask, segments, score_gain, *ropes)
    (
        hid_t,
        hid_tok,
        tea_tok,
        rates,
        count,
        mask,
        gains,
        weights,
        raw,
        q_pad,
        win,
        att,
        out_t,
        lse,
        starts,
    ) = front(hidden.T, teacher.T, others)
    output, attn_grad, d_att, res_t, small, *grads = middle(
        (
            att,
            hid_tok,
            tea_tok,
            mask,
            count,
            rates,
            up_gain,
            gate_gain,
            gate_weight,
            up_weight,
            down_weight.T,
        ),
        weights,
    )
    results = tail(
        (starts, q_pad, out_t, lse, d_att, att, gains, *ropes, res_t, small, count),
        (win, raw, hid_t, weights, attn_grad) + tuple(g.reshape(4, 4, 80, D) for g in grads),
    )
    results = emit(results[8], (output,) + tuple(results[:8]))
    output, hidden_grad, query_g, key_g, value_g, out_g, gate_g, up_g, down_g = results[:9]
    return (
        results[9].reshape(()),
        output.T,
        hidden_grad.T,
        query_g,
        key_g,
        value_g,
        out_g.T,
        gate_g,
        up_g,
        down_g.T,
    ) + tuple(results[10:])


def solution(mesh):
    both = P(("dp", "row"), "col")
    turned = P("col", ("dp", "row"))
    vector = P("col")
    in_specs = (both, both, P(("dp", "row")), P("dp", None), both, both, both, turned, both, both)
    in_specs += (turned,) + (vector,) * 5
    out_specs = (P(), both, both, both, both, both, turned, both, both, turned) + (vector,) * 5
    return jax.shard_map(shards, mesh=mesh, in_specs=in_specs, out_specs=out_specs, check_vma=False)
```

```python
import math

import jax
import jax.numpy as jnp
import numpy as np
from jax import lax
from jax.experimental import pallas as pl
from jax.experimental.pallas import tpu as pltpu
from jax.sharding import PartitionSpec as P

D = 1280
HEAD_DIM = 64
EPS = 1e-06
HEADS = 5
ROWS = 512
TOK = 128
COLS = 320
TILE = 256
F32 = jnp.float32
BF16 = jnp.bfloat16
MESH = pl.DeviceIdType.MESH
DMA = pltpu.SemaphoreType.DMA
VMEM = pltpu.VMEM
IN_VMEM = pl.BlockSpec(memory_space=pltpu.VMEM)
IN_SMEM = pl.BlockSpec(memory_space=pltpu.SMEM)
IN_PLACE = pl.BlockSpec(memory_space=pl.ANY)
LIMIT = 60 << 20


def params(collective=None):
    if collective is None:
        return pltpu.CompilerParams(vmem_limit_bytes=LIMIT)
    return pltpu.CompilerParams(
        collective_id=collective, has_side_effects=True, vmem_limit_bytes=LIMIT
    )


def spot():
    row = lax.axis_index("row")
    return lax.axis_index("dp"), lax.div(row, 2), lax.rem(row, 2), lax.axis_index("col")


def wrap(i):
    return lax.rem(i + 8, 4)


def device(z, x, c, y):
    return (z, 2 * x + c, y)


def meet(others):
    barrier = pltpu.get_barrier_semaphore()
    for other in others:
        pl.semaphore_signal(barrier, inc=1, device_id=other, device_id_type=MESH)
    pl.semaphore_wait(barrier, len(others))


def remote(src, dst, send_sem, recv_sem, to):
    return pltpu.make_async_remote_copy(
        src_ref=src,
        dst_ref=dst,
        send_sem=send_sem,
        recv_sem=recv_sem,
        device_id=to,
        device_id_type=MESH,
    )


def dot_nn(a, b):
    return lax.dot_general(a, b, (((1,), (0,)), ((), ())), preferred_element_type=F32)


def dot_nt(a, b):
    return lax.dot_general(a, b, (((1,), (1,)), ((), ())), preferred_element_type=F32)


def dot_tn(a, b):
    return lax.dot_general(a, b, (((0,), (0,)), ((), ())), preferred_element_type=F32)


class Tally:
    def __init__(self, src, accs, parts, send, recv):
        z, x, c, y = spot()
        self.src, self.accs, self.parts, self.send, self.recv = src, accs, parts, send, recv
        self.peers = [
            [device(z, wrap(x + d), c, y) for d in (1, 2, 3)],
            [device(wrap(z + d), x, c, y) for d in (1, 2, 3)],
            [device(z, x, 1 - c, y)],
        ]
        self.copies = []

    def start(self, stage):
        src = self.src if stage == 0 else self.accs.at[stage - 1]
        for d, peer in enumerate(self.peers[stage]):
            at = 3 * stage + d
            copy = remote(src, self.parts.at[at], self.send.at[at], self.recv.at[at], peer)
            copy.start()
            self.copies.append(copy)

    def finish(self, stage):
        src = self.src if stage == 0 else self.accs.at[stage - 1]
        total = src[...]
        for d in range(len(self.peers[stage])):
            self.copies[3 * stage + d].wait_recv()
            total = total + self.parts[3 * stage + d]
        self.accs[stage] = total

    def close(self):
        for copy in self.copies:
            copy.wait_send()


TALLY_PEERS = 7


def tally_scratch(shape):
    return [
        VMEM((3,) + shape, F32),
        VMEM((7,) + shape, F32),
        DMA((7,)),
        DMA((7,)),
    ]


def torus(z, x, c, y, z_last=False):
    turn = 0 if z_last else c

    def first(d):
        return device(wrap(z + turn * d), wrap(x + (1 - turn) * d), c, y)

    def second(d):
        return device(wrap(z + (1 - turn) * d), wrap(x + turn * d), c, y)

    at_first = x * (1 - turn) + z * turn
    at_second = z * (1 - turn) + x * turn

    def block(d1, d2):
        a1, a2 = wrap(at_first + d1), wrap(at_second + d2)
        return (1 - turn) * (a2 * 4 + a1) + turn * (a1 * 4 + a2)

    return first, second, block


def half_mask(half):
    lane = lax.broadcasted_iota(jnp.int32, (1, 128), 1)
    return (lane < 64) if half == 0 else (lane >= 64)


def key_place(h):
    return h // 2, h % 2


def value_place(h):
    return (HEADS + h) // 2, (HEADS + h) % 2


def pad_head(wide, at, half):
    group = wide[:, 128 * at : 128 * at + 128]
    return jnp.where(half_mask(half), group, jnp.zeros_like(group))


LOW_ROWS = 48


def lane_halves(c):
    ours = pl.ds(pl.multiple_of(640 * c, 128), 640)
    theirs = pl.ds(pl.multiple_of(640 * (1 - c), 128), 640)
    return ours, theirs


def lane_slab(ref, lanes):
    return lambda at: ref.at[:, pl.ds(pl.multiple_of(80 * at, 16), 80), lanes]


def lane_part(ref, lanes):
    def part(at, way):
        if way > 0:
            rows = pl.ds(pl.multiple_of(80 * at, 16), LOW_ROWS)
        else:
            rows = pl.ds(pl.multiple_of(80 * at + LOW_ROWS, 16), 80 - LOW_ROWS)
        return ref.at[:, rows, lanes]

    return part


def join_cores(c, shard, shard_sib, own_block, ours):
    for j in range(own_block.shape[0]):
        near = shard[j, :, ours].astype(F32)
        far = shard_sib[j].astype(F32)
        upper = jnp.where(c == 0, near, far)
        lower = jnp.where(c == 0, far, near)
        own_block[j] = jnp.concatenate([upper, lower], axis=0).astype(BF16)


class Ring:
    def __init__(self, own, slab, part, send, recv, h_send, h_recv, z_last=False):
        z, x, c, y = spot()
        self.first, self.second, self.block = torus(z, x, c, y, z_last)
        self.sibling = device(z, x, 1 - c, y)
        self.own, self.slab, self.part = own, slab, part
        self.send, self.recv, self.h_send, self.h_recv = send, recv, h_send, h_recv

    def ship(self, src, dst, at, to):
        return remote(src, dst, self.send.at[at], self.recv.at[at], to)

    def one(self, way):
        at = self.block(0, 0)
        return self.ship(self.own, self.slab(at), 0 if way > 0 else 1, self.first(way))

    def one_on(self, way):
        piece = self.part(self.block(-way, 0), way)
        return self.ship(piece, piece, 2 if way > 0 else 3, self.first(way))

    def two(self, d1, way):
        at = self.block(d1, 0)
        src = self.own if d1 == 0 else self.slab(at)
        return self.ship(src, self.slab(at), 4 + 4 * d1 + (0 if way > 0 else 1), self.second(way))

    def two_on(self, d1, way):
        piece = self.part(self.block(d1, -way), way)
        return self.ship(piece, piece, 6 + 4 * d1 + (0 if way > 0 else 1), self.second(way))

    def hand(self, d1, d2):
        at = self.block(d1, d2)
        src = self.own if d1 == 0 and d2 == 0 else self.slab(at)
        k = 4 * d1 + d2
        return remote(src, self.slab(at), self.h_send.at[k], self.h_recv.at[k], self.sibling)

    def open(self):
        self.one(1).start()
        self.one(-1).start()
        self.spread(0)

    def spread(self, d1):
        self.two(d1, 1).start()
        self.two(d1, -1).start()
        self.hand(d1, 0).start()

    def near(self):
        self.one(1).wait_recv()
        self.one_on(1).start()
        self.spread(3)
        self.one(-1).wait_recv()
        self.one_on(-1).start()
        self.spread(1)

    def far(self):
        self.one_on(1).wait_recv()
        self.one_on(-1).wait_recv()
        self.spread(2)

    def turn(self, d1):
        self.two(d1, 1).wait_recv()
        self.two_on(d1, 1).start()
        self.hand(d1, 3).start()
        self.two(d1, -1).wait_recv()
        self.two_on(d1, -1).start()
        self.hand(d1, 1).start()

    def end(self, d1):
        self.two_on(d1, 1).wait_recv()
        self.two_on(d1, -1).wait_recv()
        self.hand(d1, 2).start()

    def arrive(self):
        for d1 in range(4):
            for d2 in range(4):
                self.hand(d1, d2).wait_recv()

    def close(self):
        for way in (1, -1):
            self.one(way).wait_send()
            self.one_on(way).wait_send()
            for d1 in range(4):
                self.two(d1, way).wait_send()
                self.two_on(d1, way).wait_send()
        for d1 in range(4):
            for d2 in range(4):
                self.hand(d1, d2).wait_send()

    def steps(self):
        return [
            self.near,
            lambda: self.turn(0),
            self.far,
            lambda: self.turn(3),
            lambda: self.turn(1),
            lambda: self.end(0),
            lambda: self.turn(2),
            lambda: self.end(3),
            lambda: self.end(1),
            lambda: self.end(2),
        ]


def ring_scratch():
    return [DMA((20,)), DMA((20,)), DMA((16,)), DMA((16,))]


def rope_wide(cos_block, sin_block, turn):
    place = lax.axis_index("row")
    cos_at = turn[place, 0:1, :]
    sin_at = turn[place, 1:2, :]
    cosine = cos_block[...] * cos_at - sin_block[...] * sin_at
    sine = sin_block[...] * cos_at + cos_block[...] * sin_at
    lane = lax.broadcasted_iota(jnp.int32, sine.shape, 1)
    return cosine, jnp.where(lax.rem(lane, 64) < 32, -sine, sine)


def swap_halves(v):
    lane = lax.broadcasted_iota(jnp.int32, v.shape, 1)
    return jnp.where(lax.rem(lane, 64) < 32, pltpu.roll(v, 96, 1), pltpu.roll(v, 32, 1))


def over_heads(v):
    low = half_mask(0)
    left = jnp.sum(jnp.where(low, v, 0.0), axis=1, keepdims=True)
    right = jnp.sum(jnp.where(low, 0.0, v), axis=1, keepdims=True)
    return jnp.where(low, left, right)


def head_norm(raw, cosine, sine):
    scale = lax.rsqrt(over_heads(raw * raw) + EPS)
    return (raw * cosine + swap_halves(raw) * sine) * scale, scale


def front_kernel(
    hid,
    tea,
    query_w,
    key_w,
    value_w,
    out_w,
    gate_w,
    up_w,
    down_w,
    rate_one,
    rate_two,
    valid,
    seg,
    score_gain,
    cos_block,
    sin_block,
    turn,
    hid_out,
    hid_tok,
    tea_tok,
    rates_out,
    count_out,
    mask_out,
    gains_out,
    weights,
    w_rest,
    raw_out,
    q_pad,
    win_out,
    att,
    out_t,
    lse,
    starts_out,
    hid_t,
    hid_n,
    tea_t,
    rates,
    count,
    count_rows,
    rate_buf,
    shard,
    shard_sib,
    own_block,
    shard_b,
    shard_b_sib,
    own_b,
    w_first,
    win,
    o_acc,
    l_acc,
    y_send,
    y_recv,
    s_send,
    s_recv,
    local_sem,
    k_send,
    k_recv,
    a_send,
    a_recv,
    a_hsend,
    a_hrecv,
    b_send,
    b_recv,
    b_hsend,
    b_hrecv,
    t_accs,
    t_parts,
    t_send,
    t_recv,
):
    z, x, c, y = spot()
    place = 2 * x + c
    sibling = device(z, x, 1 - c, y)
    across = [device(z, x, c, wrap(y + d)) for d in (1, 2, 3)]
    tally = Tally(count, t_accs, t_parts, t_send, t_recv)

    shard[0] = jnp.concatenate(
        [query_w[:, 256:], out_w[...], query_w[:, :256], key_w[...], value_w[...]], axis=1
    )
    shard_b[0] = gate_w[...]
    shard_b[1] = up_w[...]
    shard_b[2] = down_w[...]
    rates[0:1, :] = rate_one[...].reshape(1, COLS)
    rates[1:2, :] = rate_two[...].reshape(1, COLS)
    token_mask = valid[...].reshape(1, ROWS).astype(F32)
    count[...] = jnp.broadcast_to(jnp.sum(token_mask, axis=1, keepdims=True), (8, 128))
    meet(across + tally.peers[0] + tally.peers[1] + tally.peers[2])

    ours, theirs = lane_halves(c)
    ring_a = Ring(own_block, lane_slab(w_first, ours), lane_part(w_first, ours), a_send, a_recv, a_hsend, a_hrecv)
    ring_b = Ring(
        own_b, lane_slab(w_rest, ours), lane_part(w_rest, ours), b_send, b_recv, b_hsend, b_hrecv, True
    )
    head = remote(shard.at[:, :, theirs], shard_sib, s_send.at[0], s_recv.at[0], sibling)
    head.start()
    head_b = remote(shard_b.at[:, :, theirs], shard_b_sib, s_send.at[1], s_recv.at[1], sibling)
    head_b.start()
    my_feats = pl.ds(pl.multiple_of(COLS * y, 64), COLS)
    hid_r = remote(hid, hid_t.at[my_feats], y_send.at[0], y_recv.at[0], across[0])
    hid_l = remote(hid, hid_t.at[my_feats], y_send.at[1], y_recv.at[1], across[2])
    hid_r.start()
    hid_l.start()
    hid_own = pltpu.make_async_copy(hid, hid_t.at[my_feats], local_sem.at[0])
    hid_own.start()
    tea_own = pltpu.make_async_copy(
        tea.at[:, pl.ds(pl.multiple_of(TOK * y, TOK), TOK)], tea_t.at[my_feats], local_sem.at[1]
    )
    tea_own.start()

    head.wait()
    join_cores(c, shard, shard_sib, own_block, ours)
    ring_a.open()
    own_at = ring_a.block(0, 0)
    own_a = pltpu.make_async_copy(own_block, ring_a.slab(own_at), local_sem.at[2])
    own_a.start()
    tally.start(0)
    small = []
    for d in (1, 2, 3):
        rows = pl.ds(pl.multiple_of(TOK * wrap(y + d), TOK), TOK)
        pieces = ((tea.at[:, rows], tea_t.at[my_feats]), (rates, rate_buf.at[y]))
        for k, (src, dst) in enumerate(pieces):
            at = 4 + 2 * (d - 1) + k
            copy = remote(src, dst, y_send.at[at], y_recv.at[at], across[d - 1])
            copy.start()
            small.append(copy)
    rate_buf[y] = rates[...]
    gains = jnp.concatenate([score_gain[...].reshape(1, COLS), jnp.zeros((1, 64), F32)], axis=1)
    gains_out[...] = gains
    token = pl.ds(pl.multiple_of(TOK * y, TOK), TOK)
    count_rows[0:1, :] = token_mask
    mask_out[...] = jnp.broadcast_to(count_rows[0:1, token], (TOK, TOK)).T

    first = jnp.sum((seg[...] < 1).astype(jnp.int32), axis=1, keepdims=True)
    second = jnp.sum((seg[...] < 2).astype(jnp.int32), axis=1, keepdims=True)
    query_seg = seg[:, pl.ds(pl.multiple_of(ROWS * place, ROWS), ROWS)]
    starts = jnp.where(query_seg == 0, 0, jnp.where(query_seg == 1, first, second))
    starts_out[...] = starts - (place - 4) * ROWS
    o_acc[...] = jnp.zeros_like(o_acc)
    l_acc[...] = jnp.zeros_like(l_acc)

    ring_a.near()
    head_b.wait()
    join_cores(c, shard_b, shard_b_sib, own_b, ours)
    own_rest = pltpu.make_async_copy(own_b, ring_b.slab(ring_b.block(0, 0)), local_sem.at[3])
    own_rest.start()
    ring_a.turn(0)
    ring_a.far()
    ring_b.open()
    hid_r.wait_recv()
    hid_f_ref = hid_t.at[pl.ds(pl.multiple_of(COLS * wrap(y - 1), 64), 160)]
    hid_f = remote(hid_f_ref, hid_f_ref, y_send.at[2], y_recv.at[2], across[0])
    hid_f.start()
    hid_l.wait_recv()
    hid_g_ref = hid_t.at[pl.ds(pl.multiple_of(COLS * wrap(y + 1) + 160, 32), 160)]
    hid_g = remote(hid_g_ref, hid_g_ref, y_send.at[3], y_recv.at[3], across[2])
    hid_g.start()
    ring_a.turn(3)
    ring_a.turn(1)
    tally.finish(0)
    tally.start(1)
    ring_a.end(0)
    ring_a.turn(2)
    ring_a.end(3)
    ring_a.end(1)
    ring_a.end(2)
    tally.finish(1)
    tally.start(2)
    hid_own.wait()
    hid_f.wait_recv()
    hid_g.wait_recv()
    hid_save = pltpu.make_async_copy(hid_t, hid_out, local_sem.at[4])
    hid_save.start()
    for g in range(10):
        hid_n[:, 128 * g : 128 * g + 128] = hid_t[128 * g : 128 * g + 128, :].T
    own_a.wait()
    ring_a.arrive()
    ring_b.near()
    w_save = pltpu.make_async_copy(w_first.at[0], weights, local_sem.at[5])
    w_save.start()

    cosine, sine = rope_wide(cos_block, sin_block, turn)
    raw = dot_nn(hid_n[...], w_first[0, :, 640:1280])
    for g in range(3):
        group = raw[:, 128 * g : 128 * g + 128]
        raw_out[3 + g] = group
        normed, _ = head_norm(group, cosine, sine)
        keys = normed * gains[:, 128 * g : 128 * g + 128]
        if g == 2:
            keys = jnp.where(half_mask(0), keys, group)
        win[4 * ROWS :, 128 * g : 128 * g + 128] = keys.astype(BF16)
    win[4 * ROWS :, 384:640] = raw[:, 384:640].astype(BF16)

    def slot(s):
        return win.at[pl.ds(pl.multiple_of(ROWS * s, ROWS), ROWS)]

    one = remote(slot(4), slot(2), k_send.at[0], k_recv.at[0], device(z, wrap(x + 1), c, y))
    two = remote(slot(4), slot(0), k_send.at[1], k_recv.at[1], device(z, wrap(x + 2), c, y))
    own = remote(slot(4), slot(3), k_send.at[2], k_recv.at[2], sibling)
    one_on = remote(slot(2), slot(1 + 2 * c), k_send.at[3], k_recv.at[3], sibling)
    two_on = remote(slot(0), slot(1), k_send.at[4], k_recv.at[4], sibling)

    @pl.when(x < 3)
    def _():
        one.start()

    @pl.when(x < 2)
    def _():
        two.start()

    @pl.when(c == 0)
    def _():
        own.start()

    root = math.sqrt(HEAD_DIM)
    for g, at in enumerate((384, 512, 0)):
        group = dot_nn(hid_n[...], w_first[0, :, at : at + 128])
        raw_out[g] = group
        normed, _ = head_norm(group, cosine, sine)
        scaled = (normed * gains[:, 128 * g : 128 * g + 128]).astype(BF16) * jnp.asarray(root, BF16)
        for half in range(2 if g < 2 else 1):
            q_pad[2 * g + half] = jnp.where(half_mask(half), scaled, jnp.zeros_like(scaled))
    hid_tok[...] = hid_n[pl.ds(pl.multiple_of(TOK * y, TOK), TOK), :]

    ring_b.turn(0)
    ring_b.far()
    events = ring_b.steps()[3:]

    def tile(t):
        rows = pl.ds(pl.multiple_of(t * TILE, TILE), TILE)
        key_at = t * TILE + lax.broadcasted_iota(jnp.int32, (TILE, ROWS), 0)
        query_at = 4 * ROWS + lax.broadcasted_iota(jnp.int32, (TILE, ROWS), 1)
        allowed = (key_at >= starts_out[...]) & (key_at <= query_at)
        for h in range(HEADS):
            kg, _ = key_place(h)
            vg, vh = value_place(h)
            keys = win[rows, 128 * kg : 128 * kg + 128]
            values = win[rows, 128 * vg : 128 * vg + 128]
            scores = dot_nt(keys, q_pad[h])
            probs = jnp.where(allowed, jnp.exp(scores), 0.0)
            l_acc[h] += jnp.sum(probs.reshape(TILE // 8, 8, ROWS), axis=0)
            both = dot_tn(values, probs.astype(BF16))
            o_acc[h] += both[64 * vh : 64 * vh + 64, :]

    def step(i, carry):
        k = lax.div(i, 2)
        turned = k - 1 + 2 * lax.rem(k, 2)
        s = jnp.where(k == 0, 4, jnp.where(c == 1, 4 - k, 4 - turned))

        @pl.when((i == 2) & (c == 1))
        def _():
            own.wait_recv()

        @pl.when((x > 0) & (((i == 4) & (c == 1)) | ((i == 2) & (c == 0))))
        def _():
            one.wait_recv()
            one_on.start()

        @pl.when((x > 0) & (((i == 6) & (c == 1)) | ((i == 4) & (c == 0))))
        def _():
            one_on.wait_recv()

        @pl.when((x > 1) & (((i == 8) & (c == 1)) | ((i == 6) & (c == 0))))
        def _():
            two.wait_recv()

            @pl.when(c == 1)
            def _():
                two_on.start()

        @pl.when((x > 1) & (i == 8) & (c == 0))
        def _():
            two_on.wait_recv()

        for n, event in enumerate(events):

            @pl.when(i == n + 2)
            def _(event=event):
                event()

        @pl.when(place + s >= 4)
        def _():
            tile(2 * s + lax.rem(i, 2))

        return carry

    lax.fori_loop(0, 10, step, 0)
    win_save = pltpu.make_async_copy(win, win_out, local_sem.at[6])
    win_save.start()
    for copy in small:
        copy.wait_recv()
    tea_own.wait()
    for g in range(10):
        tea_tok[:, 128 * g : 128 * g + 128] = tea_t[128 * g : 128 * g + 128, :].T
    rates_out[...] = jnp.concatenate([rate_buf[k] for k in range(4)], axis=1)
    tally.finish(2)
    count_out[...] = t_accs[2]
    for h in range(HEADS):
        total = jnp.sum(l_acc[h], axis=0, keepdims=True)
        lse[h] = jnp.broadcast_to(jnp.log(total), (8, ROWS))
        out_t[64 * h : 64 * h + 64, :] = o_acc[h] / total
    wide = jnp.concatenate([jnp.zeros((64, ROWS), F32), out_t[...]], axis=0)
    att[...] = wide.T.astype(BF16)
    ring_b.arrive()
    own_rest.wait()
    ring_a.close()
    ring_b.close()
    hid_save.wait()
    w_save.wait()
    win_save.wait()
    for copy in small + [hid_r, hid_l, hid_f, hid_g]:
        copy.wait_send()

    @pl.when(x < 3)
    def _():
        one.wait_send()

    @pl.when(x < 2)
    def _():
        two.wait_send()

    @pl.when(c == 0)
    def _():
        own.wait_send()

    @pl.when(x > 0)
    def _():
        one_on.wait_send()

    @pl.when((x > 1) & (c == 1))
    def _():
        two_on.wait_send()

    tally.close()


def rope_constants():
    inverse = np.exp(np.arange(32) * (-2.0 * math.log(10000.0) / HEAD_DIM))
    inverse = np.tile(inverse, 4)
    inside = np.arange(ROWS)[:, None] * inverse[None, :]
    at = (ROWS * np.arange(8))[:, None] * inverse[None, :]
    turn = np.stack([np.cos(at), np.sin(at)], axis=1)
    return [jnp.asarray(v, F32) for v in (np.cos(inside), np.sin(inside), turn)]


def front(hidden, teacher, others):
    sds = jax.ShapeDtypeStruct
    outs = [
        (sds((D, ROWS), BF16), IN_PLACE),
        (sds((TOK, D), BF16), IN_VMEM),
        (sds((TOK, D), BF16), IN_VMEM),
        (sds((2, D), F32), IN_VMEM),
        (sds((8, 128), F32), IN_VMEM),
        (sds((TOK, TOK), F32), IN_VMEM),
        (sds((1, 384), F32), IN_VMEM),
        (sds((D, D), BF16), IN_PLACE),
        (sds((3, D, D), BF16), IN_PLACE),
        (sds((6, ROWS, 128), F32), IN_VMEM),
        (sds((HEADS, ROWS, 128), BF16), IN_VMEM),
        (sds((5 * ROWS, 2 * COLS), BF16), IN_PLACE),
        (sds((ROWS, 384), BF16), IN_VMEM),
        (sds((COLS, ROWS), F32), IN_VMEM),
        (sds((HEADS, 8, ROWS), F32), IN_VMEM),
        (sds((1, ROWS), jnp.int32), IN_VMEM),
    ]
    return pl.pallas_call(
        front_kernel,
        out_shape=tuple(o[0] for o in outs),
        in_specs=[IN_PLACE] * 2 + [IN_VMEM] * len(others),
        out_specs=tuple(o[1] for o in outs),
        scratch_shapes=[
            VMEM((D, ROWS), BF16),
            VMEM((ROWS, D), BF16),
            VMEM((D, TOK), BF16),
            VMEM((2, COLS), F32),
            VMEM((8, 128), F32),
            VMEM((8, ROWS), F32),
            VMEM((4, 2, COLS), F32),
            VMEM((1, 40, D), BF16),
            VMEM((1, 40, 640), BF16),
            VMEM((1, 80, 640), BF16),
            VMEM((3, 40, D), BF16),
            VMEM((3, 40, 640), BF16),
            VMEM((3, 80, 640), BF16),
            VMEM((1, D, D), BF16),
            VMEM((5 * ROWS, 2 * COLS), BF16),
            VMEM((HEADS, 64, ROWS), F32),
            VMEM((HEADS, 8, ROWS), F32),
            DMA((10,)),
            DMA((10,)),
            DMA((2,)),
            DMA((2,)),
            DMA((7,)),
            DMA((5,)),
            DMA((5,)),
        ]
        + ring_scratch()
        + ring_scratch()
        + tally_scratch((8, 128)),
        compiler_params=params(0),
        name="front",
    )(hidden, teacher, *others)


class Spread:
    def __init__(self, ref, send, recv):
        z, x, c, y = spot()
        self.ref, self.send, self.recv, self.y = ref, send, recv, y
        self.to = {way: device(z, x, c, wrap(y + way)) for way in (1, -1)}

    def full(self, way):
        rows = pl.ds(pl.multiple_of(TOK * self.y, TOK), TOK)
        k = 0 if way > 0 else 1
        return remote(self.ref.at[rows], self.ref.at[rows], self.send.at[k], self.recv.at[k], self.to[way])

    def relay(self, way):
        half = TOK // 2
        at = TOK * wrap(self.y - way) + (0 if way > 0 else half)
        rows = pl.ds(pl.multiple_of(at, half), half)
        k = 2 if way > 0 else 3
        return remote(self.ref.at[rows], self.ref.at[rows], self.send.at[k], self.recv.at[k], self.to[way])

    def start(self):
        self.full(1).start()
        self.full(-1).start()

    def sides(self):
        self.full(1).wait_recv()
        self.relay(1).start()
        self.full(-1).wait_recv()
        self.relay(-1).start()

    def opposite(self):
        self.relay(1).wait_recv()
        self.relay(-1).wait_recv()

    def close(self):
        for way in (1, -1):
            self.full(way).wait_send()
            self.relay(way).wait_send()


HALF = TOK // 2
OWN, LEFT, RIGHT, OPPOSITE = range(4)


def position(slot, h):
    if slot == OWN:
        at = HALF * h
    elif slot == OPPOSITE:
        at = 6 * HALF + HALF * h
    else:
        at = 2 * HALF * (1 + h) + (HALF if slot == RIGHT else 0)
    return at if isinstance(h, int) else pl.multiple_of(at, HALF)


class Halves:
    def __init__(self, ref, send, recv):
        z, x, c, y = spot()
        self.ref, self.send, self.recv = ref, send, recv
        self.to = {way: device(z, x, c, wrap(y + way)) for way in (1, -1)}

    def full(self, h, way):
        src = self.ref.at[pl.ds(position(OWN, h), HALF)]
        dst = self.ref.at[pl.ds(position(LEFT if way > 0 else RIGHT, h), HALF)]
        k = 0 if way > 0 else 1
        return remote(src, dst, self.send.at[h, k], self.recv.at[h, k], self.to[way])

    def relay(self, h, way):
        part = HALF // 2
        off = 0 if way > 0 else part
        src = pl.multiple_of(position(LEFT if way > 0 else RIGHT, h) + off, part)
        dst = pl.multiple_of(position(OPPOSITE, h) + off, part)
        k = 2 if way > 0 else 3
        return remote(
            self.ref.at[pl.ds(src, part)],
            self.ref.at[pl.ds(dst, part)],
            self.send.at[h, k],
            self.recv.at[h, k],
            self.to[way],
        )

    def start(self, h):
        self.full(h, 1).start()
        self.full(h, -1).start()

    def sides(self, h):
        self.full(h, 1).wait_recv()
        self.relay(h, 1).start()
        self.full(h, -1).wait_recv()
        self.relay(h, -1).start()

    def opposite(self, h):
        self.relay(h, 1).wait_recv()
        self.relay(h, -1).wait_recv()

    def close(self):
        for h in range(2):
            for way in (1, -1):
                self.full(h, way).wait_send()
                self.relay(h, way).wait_send()


def mix_forward(states, branch, alphas):
    branch_scale = lax.rsqrt(jnp.sum(branch * branch, axis=1, keepdims=True) + EPS)
    normed = branch * branch_scale
    mixed = states + alphas * (normed - states)
    mixed_scale = lax.rsqrt(jnp.sum(mixed * mixed, axis=1, keepdims=True) + EPS)
    return mixed * mixed_scale, normed, branch_scale, mixed_scale


def mix_backward(gradient, states, normed, branch_scale, mixed_out, mixed_scale, alphas):
    along = jnp.sum(mixed_out * gradient, axis=1, keepdims=True)
    mixed_grad = mixed_scale * (gradient - mixed_out * along)
    normed_grad = alphas * mixed_grad
    toward = jnp.sum(normed * normed_grad, axis=1, keepdims=True)
    branch_grad = branch_scale * (normed_grad - normed * toward)
    rate_grad = jnp.sum(mixed_grad * (normed - states), axis=0, keepdims=True)
    return (1.0 - alphas) * mixed_grad, branch_grad, rate_grad


def swiglu_parts(gate_raw, up_raw, gate_gain, up_gain):
    root = math.sqrt(D)
    g = gate_gain * gate_raw * root
    q = jax.nn.sigmoid(g)
    return g, q


def middle_kernel(
    att,
    hid_tok,
    tea,
    mask,
    count,
    rates,
    up_gain_in,
    gate_gain_in,
    weights,
    w_rest,
    output,
    attn_low,
    res_zero,
    small,
    gate_out,
    up_out,
    down_out,
    in_one,
    product,
    mlp_grad,
    gate_low,
    up_low,
    w_out,
    w_all,
    grads,
    raw_gate,
    raw_up,
    send_buf,
    got_buf,
    own_part,
    out_buf,
    state,
    normed,
    scales,
    turned,
    w_sem,
    g_sem,
    ag_send,
    ag_recv,
    rs_send,
    rs_recv,
    o_send,
    o_recv,
):
    z, x, c, y = spot()
    peers = [device(z, x, c, wrap(y + d)) for d in range(4)]
    load = pltpu.make_async_copy(weights.at[:, pl.ds(0, 384)], w_out, w_sem.at[0])
    load.start()
    load_rest = pltpu.make_async_copy(w_rest, w_all, w_sem.at[1])
    load_rest.start()
    up_gain = up_gain_in[...].reshape(1, D)
    gate_gain = gate_gain_in[...].reshape(1, D)
    w_gate, w_up, w_down = (w_all.at[k] for k in range(3))
    meet(peers[1:])
    places = {LEFT: 3, RIGHT: 1, OPPOSITE: 2}

    def rows_of(off):
        return pl.ds(pl.multiple_of(TOK * wrap(y + off), TOK), TOK)

    def feats(k):
        return pl.ds(pl.multiple_of(COLS * k, 64), COLS)

    def half_rows(h):
        return pl.ds(pl.multiple_of(HALF * h, HALF), HALF)

    def scatter(stage, h, slot):
        return remote(
            send_buf.at[stage, h, slot - 1],
            got_buf.at[stage, h, slot - 1],
            rs_send.at[stage, h, slot],
            rs_recv.at[stage, h, slot],
            device(z, x, c, wrap(y + places[slot])),
        )

    def give(stage, h, slot, part):
        send_buf[stage, h, slot - 1] = part.astype(BF16)
        scatter(stage, h, slot).start()

    def collect(stage, h):
        total = own_part[half_rows(h), :]
        for slot in (LEFT, RIGHT, OPPOSITE):
            scatter(stage, h, slot).wait_recv()
            total = total + got_buf[stage, h, slot - 1].astype(F32)
        return total

    def both(body):
        def step(h, carry):
            body(h)
            return carry

        lax.fori_loop(0, 2, step, 0)

    def flow(stage, spread, compute):
        def step(i, carry):
            @pl.when(i == 1)
            def _():
                spread.sides(0)

            part = compute(pl.ds(pl.multiple_of(TOK * i, TOK), TOK))

            @pl.when(i == 0)
            def _():
                own_part[...] = part

            @pl.when(i > 0)
            def _():
                h = i - 1
                give(stage, h, LEFT, part[:HALF])
                give(stage, h, RIGHT, part[HALF:])

                @pl.when(i == 1)
                def _():
                    spread.sides(1)

                spread.opposite(h)
                give(stage, h, OPPOSITE, compute(pl.ds(position(OPPOSITE, h), HALF)))

            return carry

        lax.fori_loop(0, 3, step, 0)

    ones = Halves(in_one, ag_send.at[0], ag_recv.at[0])
    backs = Halves(mlp_grad, ag_send.at[1], ag_recv.at[1])

    load.wait()
    for slot in (OPPOSITE, LEFT, RIGHT):
        part = dot_nt(att[rows_of(places[slot]), :], w_out[...])
        give(0, 0, slot, part[:HALF])
        send_buf[0, 1, slot - 1] = part[HALF:].astype(BF16)
    for slot in (OPPOSITE, LEFT, RIGHT):
        scatter(0, 1, slot).start()
    own_part[...] = dot_nt(att[rows_of(0), :], w_out[...])
    small[...] = jnp.zeros_like(small)

    def first_mix(h):
        rows = half_rows(h)
        attn = collect(0, h)
        states = hid_tok[rows, :].astype(F32)
        one, normed_one, branch_one, scale_one = mix_forward(states, attn, rates[0:1, :])
        in_one[rows, :] = one.astype(BF16)
        ones.start(h)
        state[0, rows, :] = one
        normed[rows, :] = normed_one
        scales[0, rows, :] = jnp.broadcast_to(branch_one, (HALF, 128))
        scales[1, rows, :] = jnp.broadcast_to(scale_one, (HALF, 128))

    both(first_mix)
    load_rest.wait()

    def feed(rows):
        block = in_one[rows, :]
        gate_raw = dot_nn(block, w_gate[...])
        raw_gate[rows, :] = gate_raw
        up_raw = dot_nn(block, w_up[...])
        raw_up[rows, :] = up_raw
        g, q = swiglu_parts(gate_raw, up_raw, gate_gain, up_gain)
        low = (up_gain * up_raw * (g * q)).astype(BF16)
        product[rows, :] = low
        return dot_nt(low, w_down[...])

    flow(1, ones, feed)
    factor = 16384 * math.sqrt(D) / count[0:1, 0:1]

    def second_mix(h):
        rows = half_rows(h)
        mlp = collect(1, h)
        one = state[0, rows, :]
        two, normed_two, branch_two, scale_two = mix_forward(one, mlp, rates[1:2, :])
        errors = two - tea[rows, :].astype(F32)
        weight = mask[rows, 0:1]
        seed = factor * (weight * errors)
        res_one, mlp_back, rate_two = mix_backward(
            seed, one, normed_two, branch_two, two, scale_two, rates[1:2, :]
        )
        mlp_grad[rows, :] = mlp_back.astype(BF16)
        backs.start(h)
        state[1, rows, :] = res_one
        turned[rows, :] = two
        small[1:2, :] += rate_two
        loss = jnp.sum(jnp.sum(weight * errors * errors, axis=1, keepdims=True), axis=0, keepdims=True)
        small[4:5, :] += jnp.broadcast_to(loss, (1, D))

    both(second_mix)
    for g in range(10):
        lanes = slice(128 * g, 128 * g + 128)
        out_buf[lanes, :] = turned[:, lanes].T.astype(BF16)
    out_copies = []
    for k in (1, 2, 3):
        copy = remote(
            out_buf.at[feats(wrap(y + k))],
            output.at[:, rows_of(0)],
            o_send.at[k],
            o_recv.at[k],
            device(z, x, c, wrap(y + k)),
        )
        copy.start()
        out_copies.append(copy)
    output[:, rows_of(0)] = out_buf[feats(y), :]

    def unfeed(rows):
        grad = dot_nn(mlp_grad[rows, :], w_down[...])
        gate_raw = raw_gate[rows, :]
        up_raw = raw_up[rows, :]
        g, q = swiglu_parts(gate_raw, up_raw, gate_gain, up_gain)
        silu = g * q
        up_term = grad * silu
        slope = grad * up_gain * up_raw * (q * (1.0 + g * (1.0 - q))) * math.sqrt(D)
        small[2:3, :] += jnp.sum(up_term * up_raw, axis=0, keepdims=True)
        small[3:4, :] += jnp.sum(slope * gate_raw, axis=0, keepdims=True)
        up_back = (up_term * up_gain).astype(BF16)
        gate_back = (slope * gate_gain).astype(BF16)
        up_low[rows, :] = up_back
        gate_low[rows, :] = gate_back
        return dot_nt(gate_back, w_gate[...]) + dot_nt(up_back, w_up[...])

    flow(2, backs, unfeed)

    def weight_grad(j, left, right, out):
        def step(k, carry):
            rows = pl.ds(pl.multiple_of(256 * k, 256), 256)
            grads[j, rows, :] = dot_tn(left[:, rows], right[...]).astype(BF16)
            return carry

        lax.fori_loop(0, 5, step, 0)
        pltpu.make_async_copy(grads.at[j], out, g_sem.at[j]).start()

    weight_grad(2, mlp_grad, product, down_out)
    weight_grad(0, in_one, gate_low, gate_out)
    weight_grad(1, in_one, up_low, up_out)

    def third_mix(h):
        rows = half_rows(h)
        grad_one = state[1, rows, :] + collect(2, h)
        res, attn_back, rate_one = mix_backward(
            grad_one,
            hid_tok[rows, :].astype(F32),
            normed[rows, :],
            scales[0, rows, 0:1],
            state[0, rows, :],
            scales[1, rows, 0:1],
            rates[0:1, :],
        )
        attn_low[rows, :] = attn_back.astype(BF16)
        small[0:1, :] += rate_one
        turned[rows, :] = res

    both(third_mix)
    for g in range(10):
        lanes = slice(128 * g, 128 * g + 128)
        res_zero[lanes, :] = turned[:, lanes].T
    for j, out in enumerate((gate_out, up_out, down_out)):
        pltpu.make_async_copy(grads.at[j], out, g_sem.at[j]).wait()
    for slot in (LEFT, RIGHT, OPPOSITE):
        for stage in range(3):
            for h in range(2):
                scatter(stage, h, slot).wait_send()
    ones.close()
    backs.close()
    for copy in out_copies:
        copy.wait()


def middle(vmem_args, placed_args):
    sds = jax.ShapeDtypeStruct
    wide = VMEM((ROWS, D), BF16)
    square = sds((D, D), BF16)
    return pl.pallas_call(
        middle_kernel,
        out_shape=(
            sds((COLS, ROWS), BF16),
            sds((TOK, D), BF16),
            sds((D, TOK), F32),
            sds((8, D), F32),
            square,
            square,
            square,
        ),
        in_specs=[IN_VMEM] * len(vmem_args) + [IN_PLACE] * len(placed_args),
        out_specs=(IN_VMEM,) * 4 + (IN_PLACE,) * 3,
        scratch_shapes=[
            wide,
            wide,
            wide,
            wide,
            wide,
            VMEM((D, 384), BF16),
            VMEM((3, D, D), BF16),
            VMEM((3, D, D), BF16),
            VMEM((ROWS, D), F32),
            VMEM((ROWS, D), F32),
            VMEM((3, 2, 3, HALF, D), BF16),
            VMEM((3, 2, 3, HALF, D), BF16),
            VMEM((TOK, D), F32),
            VMEM((D, TOK), BF16),
            VMEM((2, TOK, D), F32),
            VMEM((TOK, D), F32),
            VMEM((2, TOK, 128), F32),
            VMEM((TOK, D), F32),
            DMA((2,)),
            DMA((3,)),
            DMA((2, 2, 4)),
            DMA((2, 2, 4)),
            DMA((3, 2, 4)),
            DMA((3, 2, 4)),
            DMA((4,)),
            DMA((4,)),
        ],
        compiler_params=params(1),
        name="middle",
    )(*vmem_args, *placed_args)


class Fold:
    def __init__(self, bufs, sems, z_heavy):
        z, x, c, y = spot()
        self.z, self.x, self.c = z, x, c
        self.z_heavy = z_heavy
        self.first, self.second, _ = torus(z, x, c, y, z_heavy)
        self.at_first = x if z_heavy else x * (1 - c) + z * c
        self.sibling = device(z, x, 1 - c, y)
        self.own, self.sib, self.relays, self.got_two, self.mid, self.got_one, self.fin = bufs
        self.l_sem, self.h_send, self.h_recv, self.b_send, self.b_recv, self.a_send, self.a_recv, self.f_send, self.f_recv = sems
        self.count = self.own.shape[0]
        self.lanes = pl.ds(pl.multiple_of(640 * c, 128), 640)
        self.other = pl.ds(pl.multiple_of(640 * (1 - c), 128), 640)

    def handed(self, j, d, src):
        return remote(src, self.sib.at[j, d], self.h_send.at[j, d], self.h_recv.at[j, d], self.sibling)

    def fetched(self, j, d, src):
        return pltpu.make_async_copy(src, self.own.at[j, d], self.l_sem.at[j, d])

    def open(self, srcs):
        z, x = self.z, self.x
        if self.z_heavy:
            for d in (2, 1, 3, 0):
                for j, src in enumerate(srcs):
                    self.handed(j, d, src.at[wrap(z + d), :, :, self.other]).start()
                    self.fetched(j, d, src.at[wrap(z + d), :, :, self.lanes]).start()
            return

        @pl.when(self.c == 0)
        def _():
            for d in (2, 1, 3, 0):
                for j, src in enumerate(srcs):
                    self.handed(j, d, src.at[:, wrap(x + d), :, self.other]).start()
                    self.fetched(j, d, src.at[wrap(z + d), :, :, self.lanes]).start()

        @pl.when(self.c == 1)
        def _():
            for d in (2, 1, 3, 0):
                for j, src in enumerate(srcs):
                    self.handed(j, d, src.at[wrap(z + d), :, :, self.other]).start()
                    self.fetched(j, d, src.at[:, wrap(x + d), :, self.lanes]).start()

    def pair(self, k):
        way = 1 if k % 2 == 0 else -1
        at = pl.ds(0 if k in (0, 3, 4) else 2, 2)
        if k < 2:
            src, dst = self.own.at[:, 2, at], self.relays.at[:, k]
        else:
            src, dst = self.own.at[:, 1 if way > 0 else 3, at], self.got_two.at[:, k % 2, at]
        return remote(src, dst, self.b_send.at[k], self.b_recv.at[k], self.second(way))

    def last(self, e):
        return remote(
            self.mid.at[:, e - 1], self.got_one.at[:, e - 1], self.a_send.at[e], self.a_recv.at[e], self.first(e)
        )

    def add(self, d):
        for j in range(self.count):
            blank = self.sib.at[j, d]
            self.fetched(j, d, blank).wait()
            self.handed(j, d, blank).wait_recv()

        def each(i, carry):
            j, a = lax.div(i, 4), lax.rem(i, 4)
            total = self.own[j, d, a].astype(F32) + self.sib[j, d, a].astype(F32)
            self.own[j, d, a] = total.astype(BF16)
            return carry

        lax.fori_loop(0, 4 * self.count, each, 0)
        for k in {2: (0, 1), 1: (2,), 3: (3,), 0: ()}[d]:
            self.pair(k).start()

    def relay(self):
        for k, d, off in ((0, 1, 0), (1, 3, 2)):
            self.pair(k).wait_recv()

            def each(i, carry, k=k, d=d, off=off):
                j, a = lax.div(i, 2), lax.rem(i, 2)
                total = self.own[j, d, off + a].astype(F32) + self.relays[j, k, a].astype(F32)
                self.own[j, d, off + a] = total.astype(BF16)
                return carry

            lax.fori_loop(0, 2 * self.count, each, 0)
            self.pair(4 + k).start()

    def whole(self, j, at):
        total = self.own[j, 0, at].astype(F32)
        for k in range(2):
            total = total + self.got_two[j, k, at].astype(F32)
        return total

    def cross(self):
        for k in range(2, 6):
            self.pair(k).wait_recv()
        for e in (2, 1, 3):

            def each(j, carry, e=e):
                self.mid[j, e - 1] = self.whole(j, wrap(self.at_first + e)).astype(BF16)
                return carry

            lax.fori_loop(0, self.count, each, 0)
            self.last(e).start()

    def give(self, out):
        rows = pl.ds(pl.multiple_of(40 * (1 - self.c), 8), 40)
        return remote(self.fin.at[:, rows], out.at[:, :, self.lanes], self.f_send, self.f_recv, self.sibling)

    def finish(self, out):
        for e in (1, 2, 3):
            self.last(e).wait_recv()

        def each(j, carry):
            total = self.whole(j, self.at_first)
            for e in (1, 2, 3):
                total = total + self.got_one[j, e - 1].astype(F32)
            self.fin[j] = total
            return carry

        lax.fori_loop(0, self.count, each, 0)
        self.give(out).start()
        rows = pl.ds(pl.multiple_of(40 * self.c, 8), 40)
        for j in range(self.count):
            out[j, :, self.lanes] = self.fin[j, rows, :]

    def close(self, out):
        self.give(out).wait()
        for k in range(6):
            self.pair(k).wait_send()
        for e in (1, 2, 3):
            self.last(e).wait_send()
        for j in range(self.count):
            for d in range(4):
                self.handed(j, d, self.sib.at[j, d]).wait_send()


def fold_scratch(count):
    block = (80, 640)
    return [
        VMEM((count, 4, 4) + block, BF16),
        VMEM((count, 4, 4) + block, BF16),
        VMEM((count, 2, 2) + block, BF16),
        VMEM((count, 2, 4) + block, BF16),
        VMEM((count, 3) + block, BF16),
        VMEM((count, 3) + block, BF16),
        VMEM((count,) + block, F32),
        DMA((count, 4)),
        DMA((count, 4)),
        DMA((count, 4)),
        DMA((6,)),
        DMA((6,)),
        DMA((4,)),
        DMA((4,)),
        DMA,
        DMA,
    ]


def head_back(grad, raw, gain, cosine, sine):
    normed, scale = head_norm(raw, cosine, sine)
    gain_grad = jnp.sum(grad * normed, axis=0, keepdims=True)
    pulled = grad * gain
    turned = scale * (pulled - normed * over_heads(normed * pulled))
    return turned * cosine + swap_halves(turned * sine), gain_grad


def tail_kernel(
    starts,
    q_pad,
    out_t,
    lse,
    attn_low,
    att,
    gains,
    cos_block,
    sin_block,
    turn,
    res_t,
    small,
    count,
    win_in,
    raw_in,
    hid_in,
    w_in,
    m0,
    m1,
    m2,
    hidden_grad,
    query_g,
    key_g,
    value_g,
    out_g,
    gate_g,
    up_g,
    down_g,
    sums_out,
    win,
    raw,
    hid_t,
    w_first,
    attn,
    d_att,
    d_pad,
    delta,
    q_acc,
    d_win,
    sib_one,
    sib_two,
    sib_own,
    one_buf,
    two_buf,
    got_one,
    got_two,
    kv_sum,
    pack,
    out_part,
    first_g,
    y_send_buf,
    y_got_buf,
    side_src,
    side_got,
    sums,
    m_out,
    f_out,
    in_sem,
    k_send,
    k_recv,
    y_send,
    y_recv,
    v_send,
    v_recv,
    g_send,
    g_recv,
    *rest,
):
    m_bufs, m_sems, rest = rest[:7], rest[7:16], rest[16:]
    f_bufs, f_sems, rest = rest[:7], rest[7:16], rest[16:]
    t_accs, t_parts, t_send, t_recv = rest
    z, x, c, y = spot()
    place = 2 * x + c
    sibling = device(z, x, 1 - c, y)
    across = [device(z, x, c, wrap(y + d)) for d in (1, 2, 3)]
    tally = Tally(sums, t_accs, t_parts, t_send, t_recv)

    def slot(ref, s):
        return ref.at[pl.ds(pl.multiple_of(ROWS * s, ROWS), ROWS)]

    win_loads = [
        pltpu.make_async_copy(slot(win_in, s), slot(win, s), in_sem.at[s]) for s in range(5)
    ]
    for s in range(5):
        win_loads[s].start()
    loads = [
        pltpu.make_async_copy(src, dst, in_sem.at[5 + k])
        for k, (src, dst) in enumerate(
            ((w_in, w_first), (raw_in, raw), (hid_in, hid_t))
        )
    ]
    meet(across + tally.peers[0] + tally.peers[1] + tally.peers[2])
    fold_m = Fold(m_bufs, m_sems, True)
    fold_f = Fold(f_bufs, f_sems, False)
    my_rows = pl.ds(pl.multiple_of(TOK * y, TOK), TOK)
    attn[my_rows, :] = attn_low[...]
    spread = Spread(attn, g_send, g_recv)
    spread.start()
    fold_m.open([m0, m1, m2])
    for load in loads:
        load.start()
    side_src[...] = jnp.zeros_like(side_src)
    for k in range(4):
        lanes = slice(COLS * k, COLS * (k + 1))
        side_src[k, 0:2, 0:COLS] = small[0:2, lanes]
        side_src[k, 2:3, 0:COLS] = small[4:5, lanes]

    def side(k):
        return remote(side_src.at[wrap(y + k)], side_got.at[k], v_send.at[k], v_recv.at[k], across[k - 1])

    for k in (1, 2, 3):
        side(k).start()
    loads[0].wait()

    def unproject(k):
        rows = pl.ds(pl.multiple_of(TOK * wrap(y + k), TOK), TOK)
        d_att[rows, :] = dot_nn(attn[rows, :], w_first[:, 0:384]).astype(BF16)

    unproject(0)
    fold_m.add(2)
    spread.sides()
    fold_m.add(1)
    unproject(1)
    unproject(3)
    fold_m.add(3)
    spread.opposite()
    unproject(2)

    for h in range(HEADS):
        d_pad[h] = pad_head(d_att, (h + 1) // 2, (h + 1) % 2)
    wide = d_att[...].astype(F32).T[64:, :] * out_t[...]
    for h in range(HEADS):
        delta[h] = jnp.broadcast_to(
            jnp.sum(wide[64 * h : 64 * (h + 1), :], axis=0, keepdims=True), (8, ROWS)
        )
    q_acc[...] = jnp.zeros_like(q_acc)

    hand_one = remote(slot(d_win, 3 - 2 * c), sib_one, k_send.at[0], k_recv.at[0], sibling)
    hand_two = remote(slot(d_win, 1), sib_two, k_send.at[1], k_recv.at[1], sibling)
    hand_own = remote(slot(d_win, 3), sib_own, k_send.at[2], k_recv.at[2], sibling)
    one = remote(one_buf, got_one, k_send.at[3], k_recv.at[3], device(z, wrap(x + 3), c, y))
    two = remote(two_buf, got_two, k_send.at[4], k_recv.at[4], device(z, wrap(x + 2), c, y))

    def tile(t):
        rows = pl.ds(pl.multiple_of(t * TILE, TILE), TILE)
        key_at = t * TILE + lax.broadcasted_iota(jnp.int32, (TILE, ROWS), 0)
        query_at = 4 * ROWS + lax.broadcasted_iota(jnp.int32, (TILE, ROWS), 1)
        allowed = (key_at >= starts[...]) & (key_at <= query_at)
        terms = [None] * 5
        for h in range(HEADS):
            kg, kh = key_place(h)
            vg, _ = value_place(h)
            keys = win[rows, 128 * kg : 128 * kg + 128]
            values = win[rows, 128 * vg : 128 * vg + 128]
            scores = dot_nt(keys, q_pad[h])
            probs = jnp.where(allowed, jnp.exp(scores - lse[h, 0:1, :]), 0.0)
            prob_grad = dot_nt(values, d_pad[h])
            score_grad = (probs * (prob_grad - delta[h, 0:1, :])).astype(BF16)
            v_term = dot_nn(probs.astype(BF16), d_pad[h])
            k_term = dot_nn(score_grad, q_pad[h])
            for at, term in ((kg, k_term), (vg, v_term)):
                terms[at] = term if terms[at] is None else terms[at] + term
            both = dot_tn(keys, score_grad)
            q_acc[h] += both[64 * kh : 64 * kh + 64, :]
        for g in range(5):
            d_win[rows, 128 * g : 128 * g + 128] = terms[g].astype(BF16)

    def after(k):
        if k == 0:

            @pl.when((c == 0) & (x > 1))
            def _():
                two_buf[...] = d_win[0:ROWS, :]
                two.start()

        if k == 1:

            @pl.when((c == 0) & (x > 1))
            def _():
                hand_two.start()

            @pl.when((c == 1) & (x > 0))
            def _():
                hand_one.start()

        if k == 2:

            @pl.when((c == 0) & (x > 0))
            def _():
                hand_one.start()

            @pl.when((c == 1) & (x > 1))
            def _():
                hand_two.wait_recv()
                two_buf[...] = (
                    d_win[0:ROWS, :].astype(F32) + sib_two[...].astype(F32)
                ).astype(BF16)
                two.start()

        if k == 3:

            @pl.when(x > 0)
            def _():
                hand_one.wait_recv()
                one_buf[...] = (
                    d_win[2 * ROWS : 3 * ROWS, :].astype(F32) + sib_one[...].astype(F32)
                ).astype(BF16)
                one.start()

            @pl.when(c == 1)
            def _():
                hand_own.start()

    for load in win_loads:
        load.wait()
    folds = {3: 0}

    def step(i, carry):
        k = lax.div(i, 2)
        s = jnp.where((c == 0) & (k == 2), 3, jnp.where((c == 0) & (k == 3), 2, k))

        @pl.when(place + s >= 4)
        def _():
            tile(2 * s + lax.rem(i, 2))

        for k in range(4):

            @pl.when(i == 2 * k + 1)
            def _(k=k):
                after(k)

        for n, d in folds.items():

            @pl.when(i == n)
            def _(d=d):
                fold_m.add(d)

        @pl.when(i == 5)
        def _():
            fold_m.relay()

        return carry

    lax.fori_loop(0, 10, step, 0)
    for load in loads[1:]:
        load.wait()
    cosine, sine = rope_wide(cos_block, sin_block, turn)
    pack[:, 128:384] = jnp.zeros((ROWS, 256), BF16)
    gain_parts = []
    wide = jnp.concatenate([q_acc[h] for h in range(HEADS)] + [jnp.zeros((64, ROWS), F32)], axis=0)
    for g, at in enumerate((384, 512, 0)):
        grad = wide[128 * g : 128 * g + 128, :].T * math.sqrt(HEAD_DIM)
        term, gain_part = head_back(grad, raw[g], gains[:, 128 * g : 128 * g + 128], cosine, sine)
        if g == 2:
            term = jnp.where(half_mask(0), term, 0.0)
        pack[:, at : at + 128] = term.astype(BF16)
        gain_parts.append(gain_part)
    out_part[...] = dot_tn(attn[...], att[...])

    kv_sum[...] = d_win[4 * ROWS :, :].astype(F32)

    @pl.when(c == 0)
    def _():
        hand_own.wait_recv()
        kv_sum[...] += sib_own[...].astype(F32)

    @pl.when(x < 3)
    def _():
        one.wait_recv()
        kv_sum[...] += got_one[...].astype(F32)

    @pl.when(x < 2)
    def _():
        two.wait_recv()
        kv_sum[...] += got_two[...].astype(F32)

    for g in range(3):
        grad = kv_sum[:, 128 * g : 128 * g + 128]
        gain = gains[:, 128 * g : 128 * g + 128]
        term, gain_part = head_back(grad, raw[3 + g], gain, cosine, sine)
        if g == 2:
            term = jnp.where(half_mask(0), term, grad)
        at = 640 + 128 * g
        pack[:, at : at + 128] = term.astype(BF16)
        gain_parts[g] += gain_part
    pack[:, 1024:1280] = kv_sum[:, 384:640].astype(BF16)

    my_cols = pl.ds(pl.multiple_of(TOK * y, TOK), TOK)

    def project(to):
        rows = pl.ds(pl.multiple_of(COLS * to, 64), COLS)
        hidden_grad[...] = dot_nt(w_first[rows, :], pack[...])
        hidden_grad[:, my_cols] += res_t[rows, :]

    def grad_copy(k):
        return remote(y_send_buf.at[k - 1], y_got_buf.at[k - 1], y_send.at[k], y_recv.at[k], across[k - 1])

    for k in (2, 1, 3):
        project(wrap(y + k))
        y_send_buf[k - 1] = hidden_grad[...].astype(BF16)
        grad_copy(k).start()

    extra = side_src[y]
    for k in (1, 2, 3):
        side(k).wait_recv()
        extra = extra + side_got[k]
    sums[...] = jnp.zeros_like(sums)
    sums[0:2, :] = small[2:4, :]
    sums[2:3, 0:384] = jnp.concatenate(gain_parts, axis=1)
    sums[3:6, 0:384] = extra[0:3, :]
    tally.start(0)

    def first_grad(k, carry):
        rows = pl.ds(pl.multiple_of(COLS * k, 64), COLS)
        grad = dot_nn(hid_t[rows, :], pack[...])
        low = grad[:, 0:384] + out_part[rows, :]
        for a in range(4):
            first_g[k, a, :, 0:384] = low[80 * a : 80 * a + 80].astype(BF16)
            first_g[k, a, :, 384:] = grad[80 * a : 80 * a + 80, 384:].astype(BF16)
        return carry

    lax.fori_loop(0, 4, first_grad, 0)
    fold_f.open([first_g])
    fold_m.cross()
    tally.finish(0)
    tally.start(1)
    project(y)
    for d in (2, 1, 3, 0):
        fold_f.add(d)
    fold_f.relay()
    for k in (1, 2, 3):
        grad_copy(k).wait_recv()
        hidden_grad[...] += y_got_buf[k - 1].astype(F32)
    tally.finish(1)
    tally.start(2)
    fold_m.finish(m_out)
    fold_f.cross()
    fold_f.finish(f_out)
    tally.finish(2)
    fold_m.close(m_out)
    fold_f.close(f_out)
    gate_g[...] = m_out[0]
    up_g[...] = m_out[1]
    down_g[...] = m_out[2]
    query_g[:, 0:256] = f_out[0, :, 384:640]
    query_g[:, 256:320] = f_out[0, :, 0:64]
    key_g[...] = f_out[0, :, 640:960]
    value_g[...] = f_out[0, :, 960:1280]
    out_g[...] = f_out[0, :, 64:384]
    sums_out[...] = t_accs[2]
    sums_out[6:7, :] = jnp.broadcast_to(count[0:1, 0:1], (1, D))
    for k in (1, 2, 3):
        grad_copy(k).wait_send()
        side(k).wait_send()
    spread.close()

    @pl.when(x > 0)
    def _():
        hand_one.wait_send()
        one.wait_send()

    @pl.when(x > 1)
    def _():
        two.wait_send()

        @pl.when(c == 0)
        def _():
            hand_two.wait_send()

    @pl.when(c == 1)
    def _():
        hand_own.wait_send()

    tally.close()


def tail(vmem_args, placed_args):
    sds = jax.ShapeDtypeStruct
    block = VMEM((ROWS, 2 * COLS), BF16)
    shapes = [(COLS, ROWS)] + [(40, COLS)] * 4 + [(40, D)] * 3 + [(8, D)]
    return pl.pallas_call(
        tail_kernel,
        out_shape=tuple(sds(s, F32) for s in shapes),
        in_specs=[IN_VMEM] * len(vmem_args) + [IN_PLACE] * len(placed_args),
        out_specs=(IN_VMEM,) * len(shapes),
        scratch_shapes=[
            VMEM((5 * ROWS, 2 * COLS), BF16),
            VMEM((6, ROWS, 128), F32),
            VMEM((D, ROWS), BF16),
            VMEM((D, D), BF16),
            VMEM((ROWS, D), BF16),
            VMEM((ROWS, 384), BF16),
            VMEM((HEADS, ROWS, 128), BF16),
            VMEM((HEADS, 8, ROWS), F32),
            VMEM((HEADS, 64, ROWS), F32),
            VMEM((5 * ROWS, 2 * COLS), BF16),
        ]
        + [block] * 7
        + [
            VMEM((ROWS, 2 * COLS), F32),
            VMEM((ROWS, D), BF16),
            VMEM((D, 384), F32),
            VMEM((4, 4, 80, D), BF16),
            VMEM((3, COLS, ROWS), BF16),
            VMEM((3, COLS, ROWS), BF16),
            VMEM((4, 8, 384), F32),
            VMEM((4, 8, 384), F32),
            VMEM((8, D), F32),
            VMEM((3, 40, D), F32),
            VMEM((1, 40, D), F32),
            DMA((9,)),
            DMA((5,)),
            DMA((5,)),
            DMA((4,)),
            DMA((4,)),
            DMA((4,)),
            DMA((4,)),
            DMA((4,)),
            DMA((4,)),
        ]
        + fold_scratch(3)
        + fold_scratch(1)
        + tally_scratch((8, D)),
        compiler_params=params(2),
        name="tail",
    )(*vmem_args, *placed_args)


def emit_kernel(sums, *refs):
    count = (len(refs) - 6) // 2
    for src, dst in zip(refs[:count], refs[count : 2 * count]):
        dst[...] = src[...]
    loss, attention, feedforward, score, up, gate = refs[2 * count :]
    loss[0] = jnp.sum(sums[5:6, 0:1] / sums[6:7, 0:1])
    score[...] = sums[2:3, 0:COLS].reshape(COLS)
    attention[...] = sums[3:4, 0:COLS].reshape(COLS)
    feedforward[...] = sums[4:5, 0:COLS].reshape(COLS)
    up[...] = sums[0:1, :].reshape(D)
    gate[...] = sums[1:2, :].reshape(D)


def emit(sums, arrays):
    sds = jax.ShapeDtypeStruct
    vectors = [sds((1,), F32)] + [sds((COLS,), F32)] * 3 + [sds((D,), F32)] * 2
    return pl.pallas_call(
        emit_kernel,
        out_shape=tuple(sds(a.shape, a.dtype) for a in arrays) + tuple(vectors),
        in_specs=[IN_VMEM] * (1 + len(arrays)),
        out_specs=(IN_VMEM,) * len(arrays) + (IN_SMEM,) + (IN_VMEM,) * 5,
        compiler_params=params(),
        name="emit",
    )(sums, *arrays)


def shards(
    hidden,
    teacher,
    valid_mask,
    segments,
    query_weight,
    key_weight,
    value_weight,
    out_weight,
    gate_weight,
    up_weight,
    down_weight,
    attention_rate,
    feedforward_rate,
    score_gain,
    up_gain,
    gate_gain,
):
    ropes = rope_constants()
    others = (query_weight, key_weight, value_weight, out_weight.T)
    others += (gate_weight, up_weight, down_weight.T)
    others += (attention_rate, feedforward_rate, valid_mask, segments, score_gain, *ropes)
    (
        hid_t,
        hid_tok,
        tea_tok,
        rates,
        count,
        mask,
        gains,
        weights,
        w_rest,
        raw,
        q_pad,
        win,
        att,
        out_t,
        lse,
        starts,
    ) = front(hidden.T, teacher.T, others)
    output, attn_low, res_t, small, *grads = middle(
        (
            att,
            hid_tok,
            tea_tok,
            mask,
            count,
            rates,
            up_gain,
            gate_gain,
        ),
        (weights, w_rest),
    )
    results = tail(
        (starts, q_pad, out_t, lse, attn_low, att, gains, *ropes, res_t, small, count),
        (win, raw, hid_t, weights) + tuple(g.reshape(4, 4, 80, D) for g in grads),
    )
    results = emit(results[8], (output,) + tuple(results[:8]))
    output, hidden_grad, query_g, key_g, value_g, out_g, gate_g, up_g, down_g = results[:9]
    return (
        results[9].reshape(()),
        output.T,
        hidden_grad.T,
        query_g,
        key_g,
        value_g,
        out_g.T,
        gate_g,
        up_g,
        down_g.T,
    ) + tuple(results[10:])


def solution(mesh):
    both = P(("dp", "row"), "col")
    turned = P("col", ("dp", "row"))
    vector = P("col")
    in_specs = (both, both, P(("dp", "row")), P("dp", None), both, both, both, turned, both, both)
    in_specs += (turned,) + (vector,) * 5
    out_specs = (P(), both, both, both, both, both, turned, both, both, turned) + (vector,) * 5
    return jax.shard_map(shards, mesh=mesh, in_specs=in_specs, out_specs=out_specs, check_vma=False)
```

```python
import math

import jax
import jax.numpy as jnp
import numpy as np
from jax import lax
from jax.experimental import pallas as pl
from jax.experimental.pallas import tpu as pltpu
from jax.sharding import PartitionSpec as P

D = 1280
HEAD_DIM = 64
EPS = 1e-06
HEADS = 5
ROWS = 512
TOK = 128
COLS = 320
TILE = 256
UP = 176
F32 = jnp.float32
BF16 = jnp.bfloat16
MESH = pl.DeviceIdType.MESH
DMA = pltpu.SemaphoreType.DMA
VMEM = pltpu.VMEM
IN_VMEM = pl.BlockSpec(memory_space=pltpu.VMEM)
IN_SMEM = pl.BlockSpec(memory_space=pltpu.SMEM)
IN_PLACE = pl.BlockSpec(memory_space=pl.ANY)
LIMIT = 60 << 20


def params(collective=None):
    if collective is None:
        return pltpu.CompilerParams(vmem_limit_bytes=LIMIT)
    return pltpu.CompilerParams(
        collective_id=collective, has_side_effects=True, vmem_limit_bytes=LIMIT
    )


def spot():
    row = lax.axis_index("row")
    return lax.axis_index("dp"), lax.div(row, 2), lax.rem(row, 2), lax.axis_index("col")


def wrap(i):
    return lax.rem(i + 8, 4)


def device(z, x, c, y):
    return (z, 2 * x + c, y)


def meet(others):
    barrier = pltpu.get_barrier_semaphore()
    for other in others:
        pl.semaphore_signal(barrier, inc=1, device_id=other, device_id_type=MESH)
    pl.semaphore_wait(barrier, len(others))


def remote(src, dst, send_sem, recv_sem, to):
    return pltpu.make_async_remote_copy(
        src_ref=src,
        dst_ref=dst,
        send_sem=send_sem,
        recv_sem=recv_sem,
        device_id=to,
        device_id_type=MESH,
    )


def dot_nn(a, b):
    return lax.dot_general(a, b, (((1,), (0,)), ((), ())), preferred_element_type=F32)


def dot_nt(a, b):
    return lax.dot_general(a, b, (((1,), (1,)), ((), ())), preferred_element_type=F32)


def dot_tn(a, b):
    return lax.dot_general(a, b, (((0,), (0,)), ((), ())), preferred_element_type=F32)


class Tally:
    def __init__(self, src, accs, parts, send, recv):
        z, x, c, y = spot()
        self.src, self.accs, self.parts, self.send, self.recv = src, accs, parts, send, recv
        self.peers = [
            [device(z, wrap(x + d), c, y) for d in (1, 2, 3)],
            [device(wrap(z + d), x, c, y) for d in (1, 2, 3)],
            [device(z, x, 1 - c, y)],
        ]
        self.copies = []

    def start(self, stage):
        src = self.src if stage == 0 else self.accs.at[stage - 1]
        for d, peer in enumerate(self.peers[stage]):
            at = 3 * stage + d
            copy = remote(src, self.parts.at[at], self.send.at[at], self.recv.at[at], peer)
            copy.start()
            self.copies.append(copy)

    def finish(self, stage):
        src = self.src if stage == 0 else self.accs.at[stage - 1]
        total = src[...]
        for d in range(len(self.peers[stage])):
            self.copies[3 * stage + d].wait_recv()
            total = total + self.parts[3 * stage + d]
        self.accs[stage] = total

    def close(self):
        for copy in self.copies:
            copy.wait_send()


TALLY_PEERS = 7


def tally_scratch(shape):
    return [
        VMEM((3,) + shape, F32),
        VMEM((7,) + shape, F32),
        DMA((7,)),
        DMA((7,)),
    ]


def torus(z, x, c, y, z_last=False):
    turn = 0 if z_last else c

    def first(d):
        return device(wrap(z + turn * d), wrap(x + (1 - turn) * d), c, y)

    def second(d):
        return device(wrap(z + (1 - turn) * d), wrap(x + turn * d), c, y)

    at_first = x * (1 - turn) + z * turn
    at_second = z * (1 - turn) + x * turn

    def block(d1, d2):
        a1, a2 = wrap(at_first + d1), wrap(at_second + d2)
        return (1 - turn) * (a2 * 4 + a1) + turn * (a1 * 4 + a2)

    return first, second, block


def half_mask(half):
    lane = lax.broadcasted_iota(jnp.int32, (1, 128), 1)
    return (lane < 64) if half == 0 else (lane >= 64)


def key_place(h):
    return h // 2, h % 2


def value_place(h):
    return (HEADS + h) // 2, (HEADS + h) % 2


def pad_head(wide, at, half):
    group = wide[:, 128 * at : 128 * at + 128]
    return jnp.where(half_mask(half), group, jnp.zeros_like(group))


LOW_ROWS = 48


def lane_halves(c):
    ours = pl.ds(pl.multiple_of(640 * c, 128), 640)
    theirs = pl.ds(pl.multiple_of(640 * (1 - c), 128), 640)
    return ours, theirs


def lane_slab(ref, lanes):
    return lambda at: ref.at[:, pl.ds(pl.multiple_of(80 * at, 16), 80), lanes]


def lane_part(ref, lanes):
    def part(at, way):
        if way > 0:
            rows = pl.ds(pl.multiple_of(80 * at, 16), LOW_ROWS)
        else:
            rows = pl.ds(pl.multiple_of(80 * at + LOW_ROWS, 16), 80 - LOW_ROWS)
        return ref.at[:, rows, lanes]

    return part


def join_cores(c, shard, shard_sib, own_block, ours):
    for j in range(own_block.shape[0]):
        near = shard[j, :, ours].astype(F32)
        far = shard_sib[j].astype(F32)
        upper = jnp.where(c == 0, near, far)
        lower = jnp.where(c == 0, far, near)
        own_block[j] = jnp.concatenate([upper, lower], axis=0).astype(BF16)


class Ring:
    def __init__(self, own, slab, part, send, recv, h_send, h_recv, z_last=False):
        z, x, c, y = spot()
        self.first, self.second, self.block = torus(z, x, c, y, z_last)
        self.sibling = device(z, x, 1 - c, y)
        self.own, self.slab, self.part = own, slab, part
        self.send, self.recv, self.h_send, self.h_recv = send, recv, h_send, h_recv

    def ship(self, src, dst, at, to):
        return remote(src, dst, self.send.at[at], self.recv.at[at], to)

    def one(self, way):
        at = self.block(0, 0)
        return self.ship(self.own, self.slab(at), 0 if way > 0 else 1, self.first(way))

    def one_on(self, way):
        piece = self.part(self.block(-way, 0), way)
        return self.ship(piece, piece, 2 if way > 0 else 3, self.first(way))

    def two(self, d1, way):
        at = self.block(d1, 0)
        src = self.own if d1 == 0 else self.slab(at)
        return self.ship(src, self.slab(at), 4 + 4 * d1 + (0 if way > 0 else 1), self.second(way))

    def two_on(self, d1, way):
        piece = self.part(self.block(d1, -way), way)
        return self.ship(piece, piece, 6 + 4 * d1 + (0 if way > 0 else 1), self.second(way))

    def hand(self, d1, d2):
        at = self.block(d1, d2)
        src = self.own if d1 == 0 and d2 == 0 else self.slab(at)
        k = 4 * d1 + d2
        return remote(src, self.slab(at), self.h_send.at[k], self.h_recv.at[k], self.sibling)

    def open(self):
        self.one(1).start()
        self.one(-1).start()
        self.spread(0)

    def spread(self, d1):
        self.two(d1, 1).start()
        self.two(d1, -1).start()
        self.hand(d1, 0).start()

    def near(self):
        self.one(1).wait_recv()
        self.one_on(1).start()
        self.spread(3)
        self.one(-1).wait_recv()
        self.one_on(-1).start()
        self.spread(1)

    def far(self):
        self.one_on(1).wait_recv()
        self.one_on(-1).wait_recv()
        self.spread(2)

    def turn(self, d1):
        self.two(d1, 1).wait_recv()
        self.two_on(d1, 1).start()
        self.hand(d1, 3).start()
        self.two(d1, -1).wait_recv()
        self.two_on(d1, -1).start()
        self.hand(d1, 1).start()

    def end(self, d1):
        self.two_on(d1, 1).wait_recv()
        self.two_on(d1, -1).wait_recv()
        self.hand(d1, 2).start()

    def arrive(self):
        for d1 in range(4):
            for d2 in range(4):
                self.hand(d1, d2).wait_recv()

    def close(self):
        for way in (1, -1):
            self.one(way).wait_send()
            self.one_on(way).wait_send()
            for d1 in range(4):
                self.two(d1, way).wait_send()
                self.two_on(d1, way).wait_send()
        for d1 in range(4):
            for d2 in range(4):
                self.hand(d1, d2).wait_send()

    def steps(self):
        return [
            self.near,
            lambda: self.turn(0),
            self.far,
            lambda: self.turn(3),
            lambda: self.turn(1),
            lambda: self.end(0),
            lambda: self.turn(2),
            lambda: self.end(3),
            lambda: self.end(1),
            lambda: self.end(2),
        ]


def ring_scratch():
    return [DMA((20,)), DMA((20,)), DMA((16,)), DMA((16,))]


def rope_wide(cos_block, sin_block, turn):
    place = lax.axis_index("row")
    cos_at = turn[place, 0:1, :]
    sin_at = turn[place, 1:2, :]
    cosine = cos_block[...] * cos_at - sin_block[...] * sin_at
    sine = sin_block[...] * cos_at + cos_block[...] * sin_at
    lane = lax.broadcasted_iota(jnp.int32, sine.shape, 1)
    return cosine, jnp.where(lax.rem(lane, 64) < 32, -sine, sine)


def swap_halves(v):
    lane = lax.broadcasted_iota(jnp.int32, v.shape, 1)
    return jnp.where(lax.rem(lane, 64) < 32, pltpu.roll(v, 96, 1), pltpu.roll(v, 32, 1))


def over_heads(v):
    low = half_mask(0)
    left = jnp.sum(jnp.where(low, v, 0.0), axis=1, keepdims=True)
    right = jnp.sum(jnp.where(low, 0.0, v), axis=1, keepdims=True)
    return jnp.where(low, left, right)


def head_norm(raw, cosine, sine):
    scale = lax.rsqrt(over_heads(raw * raw) + EPS)
    return (raw * cosine + swap_halves(raw) * sine) * scale, scale


def front_kernel(
    hid,
    tea,
    query_w,
    key_w,
    value_w,
    out_w,
    gate_w,
    up_w,
    down_w,
    rate_one,
    rate_two,
    valid,
    seg,
    score_gain,
    cos_block,
    sin_block,
    turn,
    hid_out,
    hid_tok,
    tea_tok,
    rates_out,
    count_out,
    mask_out,
    gains_out,
    weights,
    w_rest,
    raw_out,
    q_pad,
    win_out,
    att,
    out_t,
    lse,
    starts_out,
    hid_t,
    hid_n,
    tea_t,
    rates,
    count,
    count_rows,
    rate_buf,
    shard,
    shard_sib,
    own_block,
    shard_b,
    shard_b_sib,
    own_b,
    w_first,
    win,
    transit,
    o_acc,
    l_acc,
    y_send,
    y_recv,
    s_send,
    s_recv,
    local_sem,
    k_send,
    k_recv,
    a_send,
    a_recv,
    a_hsend,
    a_hrecv,
    b_send,
    b_recv,
    b_hsend,
    b_hrecv,
    c_send,
    c_recv,
    c_hsend,
    c_hrecv,
    t_accs,
    t_parts,
    t_send,
    t_recv,
):
    z, x, c, y = spot()
    place = 2 * x + c
    sibling = device(z, x, 1 - c, y)
    across = [device(z, x, c, wrap(y + d)) for d in (1, 2, 3)]
    tally = Tally(count, t_accs, t_parts, t_send, t_recv)

    shard[0] = jnp.concatenate(
        [query_w[:, 256:], out_w[...], query_w[:, :256], key_w[...], value_w[...]], axis=1
    )
    shard_b[0] = gate_w[...]
    shard_b[1] = up_w[...]
    shard_b[2] = down_w[...]
    rates[0:1, :] = rate_one[...].reshape(1, COLS)
    rates[1:2, :] = rate_two[...].reshape(1, COLS)
    token_mask = valid[...].reshape(1, ROWS).astype(F32)
    count[...] = jnp.broadcast_to(jnp.sum(token_mask, axis=1, keepdims=True), (8, 128))
    meet(across + tally.peers[0] + tally.peers[1] + tally.peers[2])

    ours, theirs = lane_halves(c)
    ring_a = Ring(own_block, lane_slab(w_first, ours), lane_part(w_first, ours), a_send, a_recv, a_hsend, a_hrecv)
    w_pair, w_last = w_rest.at[pl.ds(0, 2)], w_rest.at[pl.ds(2, 1)]
    ring_b = Ring(
        own_b.at[pl.ds(0, 2)],
        lane_slab(w_pair, ours),
        lane_part(w_pair, ours),
        b_send,
        b_recv,
        b_hsend,
        b_hrecv,
        True,
    )
    ring_c = Ring(
        own_b.at[pl.ds(2, 1)],
        lane_slab(w_last, ours),
        lane_part(w_last, ours),
        c_send,
        c_recv,
        c_hsend,
        c_hrecv,
    )
    head = remote(shard.at[:, :, theirs], shard_sib, s_send.at[0], s_recv.at[0], sibling)
    head.start()
    head_b = remote(shard_b.at[:, :, theirs], shard_b_sib, s_send.at[1], s_recv.at[1], sibling)
    head_b.start()
    my_feats = pl.ds(pl.multiple_of(COLS * y, 64), COLS)
    hid_r = remote(hid, hid_t.at[my_feats], y_send.at[0], y_recv.at[0], across[0])
    hid_l = remote(hid, hid_t.at[my_feats], y_send.at[1], y_recv.at[1], across[2])
    hid_r.start()
    hid_l.start()
    hid_own = pltpu.make_async_copy(hid, hid_t.at[my_feats], local_sem.at[0])
    hid_own.start()
    tea_own = pltpu.make_async_copy(
        tea.at[:, pl.ds(pl.multiple_of(TOK * y, TOK), TOK)], tea_t.at[my_feats], local_sem.at[1]
    )
    tea_own.start()

    head.wait()
    join_cores(c, shard, shard_sib, own_block, ours)
    ring_a.open()
    own_at = ring_a.block(0, 0)
    own_a = pltpu.make_async_copy(own_block, ring_a.slab(own_at), local_sem.at[2])
    own_a.start()
    tally.start(0)
    small = []
    for d in (1, 2, 3):
        rows = pl.ds(pl.multiple_of(TOK * wrap(y + d), TOK), TOK)
        pieces = ((tea.at[:, rows], tea_t.at[my_feats]), (rates, rate_buf.at[y]))
        for k, (src, dst) in enumerate(pieces):
            at = 4 + 2 * (d - 1) + k
            copy = remote(src, dst, y_send.at[at], y_recv.at[at], across[d - 1])
            copy.start()
            small.append(copy)
    rate_buf[y] = rates[...]
    gains = jnp.concatenate([score_gain[...].reshape(1, COLS), jnp.zeros((1, 64), F32)], axis=1)
    gains_out[...] = gains
    token = pl.ds(pl.multiple_of(TOK * y, TOK), TOK)
    count_rows[0:1, :] = token_mask
    mask_out[...] = jnp.broadcast_to(count_rows[0:1, token], (TOK, TOK)).T

    first = jnp.sum((seg[...] < 1).astype(jnp.int32), axis=1, keepdims=True)
    second = jnp.sum((seg[...] < 2).astype(jnp.int32), axis=1, keepdims=True)
    query_seg = seg[:, pl.ds(pl.multiple_of(ROWS * place, ROWS), ROWS)]
    starts = jnp.where(query_seg == 0, 0, jnp.where(query_seg == 1, first, second))
    starts_out[...] = starts - (place - 4) * ROWS
    o_acc[...] = jnp.zeros_like(o_acc)
    l_acc[...] = jnp.zeros_like(l_acc)

    ring_a.near()
    head_b.wait()
    join_cores(c, shard_b, shard_b_sib, own_b, ours)
    own_rest = pltpu.make_async_copy(own_b, lane_slab(w_rest, ours)(ring_b.block(0, 0)), local_sem.at[3])
    own_rest.start()
    ring_a.turn(0)
    ring_a.far()
    ring_b.open()
    ring_c.open()
    hid_r.wait_recv()
    hid_f_ref = hid_t.at[pl.ds(pl.multiple_of(COLS * wrap(y - 1), 64), 160)]
    hid_f = remote(hid_f_ref, hid_f_ref, y_send.at[2], y_recv.at[2], across[0])
    hid_f.start()
    hid_l.wait_recv()
    hid_g_ref = hid_t.at[pl.ds(pl.multiple_of(COLS * wrap(y + 1) + 160, 32), 160)]
    hid_g = remote(hid_g_ref, hid_g_ref, y_send.at[3], y_recv.at[3], across[2])
    hid_g.start()
    ring_a.turn(3)
    ring_a.turn(1)
    tally.finish(0)
    tally.start(1)
    ring_a.end(0)
    ring_a.turn(2)
    ring_a.end(3)
    ring_a.end(1)
    ring_a.end(2)
    tally.finish(1)
    tally.start(2)
    hid_own.wait()
    hid_f.wait_recv()
    hid_g.wait_recv()
    hid_save = pltpu.make_async_copy(hid_t, hid_out, local_sem.at[4])
    hid_save.start()
    for g in range(10):
        hid_n[:, 128 * g : 128 * g + 128] = hid_t[128 * g : 128 * g + 128, :].T
    own_a.wait()
    ring_a.arrive()
    ring_b.near()
    ring_c.near()
    w_save = pltpu.make_async_copy(w_first.at[0], weights, local_sem.at[5])
    w_save.start()

    cosine, sine = rope_wide(cos_block, sin_block, turn)
    raw = dot_nn(hid_n[...], w_first[0, :, 640:1280])
    for g in range(3):
        group = raw[:, 128 * g : 128 * g + 128]
        raw_out[3 + g] = group
        normed, _ = head_norm(group, cosine, sine)
        keys = normed * gains[:, 128 * g : 128 * g + 128]
        if g == 2:
            keys = jnp.where(half_mask(0), keys, group)
        win[4 * ROWS :, 128 * g : 128 * g + 128] = keys.astype(BF16)
    win[4 * ROWS :, 384:640] = raw[:, 384:640].astype(BF16)

    def slot(s):
        return win.at[pl.ds(pl.multiple_of(ROWS * s, ROWS), ROWS)]

    one = remote(slot(4), slot(2), k_send.at[0], k_recv.at[0], device(z, wrap(x + 1), c, y))
    up = remote(
        win.at[pl.ds(2 * ROWS, UP)],
        win.at[pl.ds(0, UP)],
        k_send.at[1],
        k_recv.at[1],
        device(z, wrap(x + 1), c, y),
    )
    down = remote(
        win.at[pl.ds(4 * ROWS + UP, ROWS - UP)],
        transit,
        k_send.at[5],
        k_recv.at[5],
        device(z, wrap(x - 1), c, y),
    )
    down_on = remote(
        transit,
        win.at[pl.ds(UP, ROWS - UP)],
        k_send.at[6],
        k_recv.at[6],
        device(z, wrap(x - 1), c, y),
    )
    own = remote(slot(4), slot(3), k_send.at[2], k_recv.at[2], sibling)
    one_on = remote(slot(2), slot(1 + 2 * c), k_send.at[3], k_recv.at[3], sibling)
    two_on = remote(slot(0), slot(1), k_send.at[4], k_recv.at[4], sibling)

    @pl.when(x < 3)
    def _():
        one.start()

    @pl.when(x < 2)
    def _():
        down.start()

    @pl.when(c == 0)
    def _():
        own.start()

    root = math.sqrt(HEAD_DIM)
    for g, at in enumerate((384, 512, 0)):
        group = dot_nn(hid_n[...], w_first[0, :, at : at + 128])
        raw_out[g] = group
        normed, _ = head_norm(group, cosine, sine)
        scaled = (normed * gains[:, 128 * g : 128 * g + 128]).astype(BF16) * jnp.asarray(root, BF16)
        for half in range(2 if g < 2 else 1):
            q_pad[2 * g + half] = jnp.where(half_mask(half), scaled, jnp.zeros_like(scaled))
    hid_tok[...] = hid_n[pl.ds(pl.multiple_of(TOK * y, TOK), TOK), :]

    ring_b.turn(0)
    ring_b.far()
    ring_c.turn(0)
    ring_c.far()
    events = list(zip(ring_b.steps()[3:], ring_c.steps()[3:]))

    def tile(t):
        rows = pl.ds(pl.multiple_of(t * TILE, TILE), TILE)
        key_at = t * TILE + lax.broadcasted_iota(jnp.int32, (TILE, ROWS), 0)
        query_at = 4 * ROWS + lax.broadcasted_iota(jnp.int32, (TILE, ROWS), 1)
        allowed = (key_at >= starts_out[...]) & (key_at <= query_at)
        for h in range(HEADS):
            kg, _ = key_place(h)
            vg, vh = value_place(h)
            keys = win[rows, 128 * kg : 128 * kg + 128]
            values = win[rows, 128 * vg : 128 * vg + 128]
            scores = dot_nt(keys, q_pad[h])
            probs = jnp.where(allowed, jnp.exp(scores), 0.0)
            l_acc[h] += jnp.sum(probs.reshape(TILE // 8, 8, ROWS), axis=0)
            both = dot_tn(values, probs.astype(BF16))
            o_acc[h] += both[64 * vh : 64 * vh + 64, :]

    def step(i, carry):
        k = lax.div(i, 2)
        turned = k - 1 + 2 * lax.rem(k, 2)
        s = jnp.where(k == 0, 4, jnp.where(c == 1, 4 - k, 4 - turned))

        @pl.when((i == 2) & (c == 1))
        def _():
            own.wait_recv()

        @pl.when((x > 0) & (((i == 4) & (c == 1)) | ((i == 2) & (c == 0))))
        def _():
            one.wait_recv()
            one_on.start()

            @pl.when(x < 3)
            def _():
                up.start()

        @pl.when((i == 3) & ((x == 0) | (x == 3)))
        def _():
            down.wait_recv()
            down_on.start()

        @pl.when((x > 0) & (((i == 6) & (c == 1)) | ((i == 4) & (c == 0))))
        def _():
            one_on.wait_recv()

        @pl.when((x > 1) & (((i == 8) & (c == 1)) | ((i == 6) & (c == 0))))
        def _():
            up.wait_recv()
            down_on.wait_recv()

            @pl.when(c == 1)
            def _():
                two_on.start()

        @pl.when((x > 1) & (i == 8) & (c == 0))
        def _():
            two_on.wait_recv()

        for n, event in enumerate(events):

            @pl.when(i == n + 2)
            def _(event=event):
                event[0]()
                event[1]()

        @pl.when(place + s >= 4)
        def _():
            tile(2 * s + lax.rem(i, 2))

        return carry

    lax.fori_loop(0, 10, step, 0)
    win_save = pltpu.make_async_copy(win, win_out, local_sem.at[6])
    win_save.start()
    for copy in small:
        copy.wait_recv()
    tea_own.wait()
    for g in range(10):
        tea_tok[:, 128 * g : 128 * g + 128] = tea_t[128 * g : 128 * g + 128, :].T
    rates_out[...] = jnp.concatenate([rate_buf[k] for k in range(4)], axis=1)
    tally.finish(2)
    count_out[...] = t_accs[2]
    for h in range(HEADS):
        total = jnp.sum(l_acc[h], axis=0, keepdims=True)
        lse[h] = jnp.broadcast_to(jnp.log(total), (8, ROWS))
        out_t[64 * h : 64 * h + 64, :] = o_acc[h] / total
    wide = jnp.concatenate([jnp.zeros((64, ROWS), F32), out_t[...]], axis=0)
    att[...] = wide.T.astype(BF16)
    ring_b.arrive()
    ring_c.arrive()
    own_rest.wait()
    ring_a.close()
    ring_b.close()
    ring_c.close()
    hid_save.wait()
    w_save.wait()
    win_save.wait()
    for copy in small + [hid_r, hid_l, hid_f, hid_g]:
        copy.wait_send()

    @pl.when(x < 3)
    def _():
        one.wait_send()

    @pl.when(x < 2)
    def _():
        down.wait_send()

    @pl.when((x == 0) | (x == 3))
    def _():
        down_on.wait_send()

    @pl.when((x == 1) | (x == 2))
    def _():
        up.wait_send()

    @pl.when(c == 0)
    def _():
        own.wait_send()

    @pl.when(x > 0)
    def _():
        one_on.wait_send()

    @pl.when((x > 1) & (c == 1))
    def _():
        two_on.wait_send()

    tally.close()


def rope_constants():
    inverse = np.exp(np.arange(32) * (-2.0 * math.log(10000.0) / HEAD_DIM))
    inverse = np.tile(inverse, 4)
    inside = np.arange(ROWS)[:, None] * inverse[None, :]
    at = (ROWS * np.arange(8))[:, None] * inverse[None, :]
    turn = np.stack([np.cos(at), np.sin(at)], axis=1)
    return [jnp.asarray(v, F32) for v in (np.cos(inside), np.sin(inside), turn)]


def front(hidden, teacher, others):
    sds = jax.ShapeDtypeStruct
    outs = [
        (sds((D, ROWS), BF16), IN_PLACE),
        (sds((TOK, D), BF16), IN_VMEM),
        (sds((TOK, D), BF16), IN_VMEM),
        (sds((2, D), F32), IN_VMEM),
        (sds((8, 128), F32), IN_VMEM),
        (sds((TOK, TOK), F32), IN_VMEM),
        (sds((1, 384), F32), IN_VMEM),
        (sds((D, D), BF16), IN_PLACE),
        (sds((3, D, D), BF16), IN_PLACE),
        (sds((6, ROWS, 128), F32), IN_VMEM),
        (sds((HEADS, ROWS, 128), BF16), IN_VMEM),
        (sds((5 * ROWS, 2 * COLS), BF16), IN_PLACE),
        (sds((ROWS, 384), BF16), IN_VMEM),
        (sds((COLS, ROWS), F32), IN_VMEM),
        (sds((HEADS, 8, ROWS), F32), IN_VMEM),
        (sds((1, ROWS), jnp.int32), IN_VMEM),
    ]
    return pl.pallas_call(
        front_kernel,
        out_shape=tuple(o[0] for o in outs),
        in_specs=[IN_PLACE] * 2 + [IN_VMEM] * len(others),
        out_specs=tuple(o[1] for o in outs),
        scratch_shapes=[
            VMEM((D, ROWS), BF16),
            VMEM((ROWS, D), BF16),
            VMEM((D, TOK), BF16),
            VMEM((2, COLS), F32),
            VMEM((8, 128), F32),
            VMEM((8, ROWS), F32),
            VMEM((4, 2, COLS), F32),
            VMEM((1, 40, D), BF16),
            VMEM((1, 40, 640), BF16),
            VMEM((1, 80, 640), BF16),
            VMEM((3, 40, D), BF16),
            VMEM((3, 40, 640), BF16),
            VMEM((3, 80, 640), BF16),
            VMEM((1, D, D), BF16),
            VMEM((5 * ROWS, 2 * COLS), BF16),
            VMEM((ROWS - UP, 2 * COLS), BF16),
            VMEM((HEADS, 64, ROWS), F32),
            VMEM((HEADS, 8, ROWS), F32),
            DMA((10,)),
            DMA((10,)),
            DMA((2,)),
            DMA((2,)),
            DMA((7,)),
            DMA((7,)),
            DMA((7,)),
        ]
        + ring_scratch()
        + ring_scratch()
        + ring_scratch()
        + tally_scratch((8, 128)),
        compiler_params=params(0),
        name="front",
    )(hidden, teacher, *others)


class Spread:
    def __init__(self, ref, send, recv):
        z, x, c, y = spot()
        self.ref, self.send, self.recv, self.y = ref, send, recv, y
        self.to = {way: device(z, x, c, wrap(y + way)) for way in (1, -1)}

    def full(self, way):
        rows = pl.ds(pl.multiple_of(TOK * self.y, TOK), TOK)
        k = 0 if way > 0 else 1
        return remote(self.ref.at[rows], self.ref.at[rows], self.send.at[k], self.recv.at[k], self.to[way])

    def relay(self, way):
        half = TOK // 2
        at = TOK * wrap(self.y - way) + (0 if way > 0 else half)
        rows = pl.ds(pl.multiple_of(at, half), half)
        k = 2 if way > 0 else 3
        return remote(self.ref.at[rows], self.ref.at[rows], self.send.at[k], self.recv.at[k], self.to[way])

    def start(self):
        self.full(1).start()
        self.full(-1).start()

    def sides(self):
        self.full(1).wait_recv()
        self.relay(1).start()
        self.full(-1).wait_recv()
        self.relay(-1).start()

    def opposite(self):
        self.relay(1).wait_recv()
        self.relay(-1).wait_recv()

    def close(self):
        for way in (1, -1):
            self.full(way).wait_send()
            self.relay(way).wait_send()


HALF = TOK // 2
OWN, LEFT, RIGHT, OPPOSITE = range(4)


def position(slot, h):
    if slot == OWN:
        at = HALF * h
    elif slot == OPPOSITE:
        at = 6 * HALF + HALF * h
    else:
        at = 2 * HALF * (1 + h) + (HALF if slot == RIGHT else 0)
    return at if isinstance(h, int) else pl.multiple_of(at, HALF)


class Halves:
    def __init__(self, ref, send, recv):
        z, x, c, y = spot()
        self.ref, self.send, self.recv = ref, send, recv
        self.to = {way: device(z, x, c, wrap(y + way)) for way in (1, -1)}

    def full(self, h, way):
        src = self.ref.at[pl.ds(position(OWN, h), HALF)]
        dst = self.ref.at[pl.ds(position(LEFT if way > 0 else RIGHT, h), HALF)]
        k = 0 if way > 0 else 1
        return remote(src, dst, self.send.at[h, k], self.recv.at[h, k], self.to[way])

    def relay(self, h, way):
        part = HALF // 2
        off = 0 if way > 0 else part
        src = pl.multiple_of(position(LEFT if way > 0 else RIGHT, h) + off, part)
        dst = pl.multiple_of(position(OPPOSITE, h) + off, part)
        k = 2 if way > 0 else 3
        return remote(
            self.ref.at[pl.ds(src, part)],
            self.ref.at[pl.ds(dst, part)],
            self.send.at[h, k],
            self.recv.at[h, k],
            self.to[way],
        )

    def start(self, h):
        self.full(h, 1).start()
        self.full(h, -1).start()

    def sides(self, h):
        self.full(h, 1).wait_recv()
        self.relay(h, 1).start()
        self.full(h, -1).wait_recv()
        self.relay(h, -1).start()

    def opposite(self, h):
        self.relay(h, 1).wait_recv()
        self.relay(h, -1).wait_recv()

    def close(self):
        for h in range(2):
            for way in (1, -1):
                self.full(h, way).wait_send()
                self.relay(h, way).wait_send()


def mix_forward(states, branch, alphas):
    branch_scale = lax.rsqrt(jnp.sum(branch * branch, axis=1, keepdims=True) + EPS)
    normed = branch * branch_scale
    mixed = states + alphas * (normed - states)
    mixed_scale = lax.rsqrt(jnp.sum(mixed * mixed, axis=1, keepdims=True) + EPS)
    return mixed * mixed_scale, normed, branch_scale, mixed_scale


def mix_backward(gradient, states, normed, branch_scale, mixed_out, mixed_scale, alphas):
    along = jnp.sum(mixed_out * gradient, axis=1, keepdims=True)
    mixed_grad = mixed_scale * (gradient - mixed_out * along)
    normed_grad = alphas * mixed_grad
    toward = jnp.sum(normed * normed_grad, axis=1, keepdims=True)
    branch_grad = branch_scale * (normed_grad - normed * toward)
    rate_grad = jnp.sum(mixed_grad * (normed - states), axis=0, keepdims=True)
    return (1.0 - alphas) * mixed_grad, branch_grad, rate_grad


def swiglu_parts(gate_raw, up_raw, gate_gain, up_gain):
    root = math.sqrt(D)
    g = gate_gain * gate_raw * root
    q = jax.nn.sigmoid(g)
    return g, q


def middle_kernel(
    att,
    hid_tok,
    tea,
    mask,
    count,
    rates,
    up_gain_in,
    gate_gain_in,
    weights,
    w_rest,
    output,
    attn_low,
    res_zero,
    small,
    gate_out,
    up_out,
    down_out,
    in_one,
    product,
    mlp_grad,
    gate_low,
    up_low,
    w_out,
    w_all,
    grads,
    raw_gate,
    raw_up,
    send_buf,
    got_buf,
    own_part,
    out_buf,
    state,
    normed,
    scales,
    turned,
    w_sem,
    g_sem,
    ag_send,
    ag_recv,
    rs_send,
    rs_recv,
    o_send,
    o_recv,
):
    z, x, c, y = spot()
    peers = [device(z, x, c, wrap(y + d)) for d in range(4)]
    load = pltpu.make_async_copy(weights.at[:, pl.ds(0, 384)], w_out, w_sem.at[0])
    load.start()
    load_rest = pltpu.make_async_copy(w_rest, w_all, w_sem.at[1])
    load_rest.start()
    up_gain = up_gain_in[...].reshape(1, D)
    gate_gain = gate_gain_in[...].reshape(1, D)
    w_gate, w_up, w_down = (w_all.at[k] for k in range(3))
    meet(peers[1:])
    places = {LEFT: 3, RIGHT: 1, OPPOSITE: 2}

    def rows_of(off):
        return pl.ds(pl.multiple_of(TOK * wrap(y + off), TOK), TOK)

    def feats(k):
        return pl.ds(pl.multiple_of(COLS * k, 64), COLS)

    def half_rows(h):
        return pl.ds(pl.multiple_of(HALF * h, HALF), HALF)

    def scatter(stage, h, slot):
        return remote(
            send_buf.at[stage, h, slot - 1],
            got_buf.at[stage, h, slot - 1],
            rs_send.at[stage, h, slot],
            rs_recv.at[stage, h, slot],
            device(z, x, c, wrap(y + places[slot])),
        )

    def give(stage, h, slot, part):
        send_buf[stage, h, slot - 1] = part.astype(BF16)
        scatter(stage, h, slot).start()

    def collect(stage, h):
        total = own_part[half_rows(h), :]
        for slot in (LEFT, RIGHT, OPPOSITE):
            scatter(stage, h, slot).wait_recv()
            total = total + got_buf[stage, h, slot - 1].astype(F32)
        return total

    def both(body):
        def step(h, carry):
            body(h)
            return carry

        lax.fori_loop(0, 2, step, 0)

    def flow(stage, spread, compute):
        def step(i, carry):
            @pl.when(i == 1)
            def _():
                spread.sides(0)

            part = compute(pl.ds(pl.multiple_of(TOK * i, TOK), TOK))

            @pl.when(i == 0)
            def _():
                own_part[...] = part

            @pl.when(i > 0)
            def _():
                h = i - 1
                give(stage, h, LEFT, part[:HALF])
                give(stage, h, RIGHT, part[HALF:])

                @pl.when(i == 1)
                def _():
                    spread.sides(1)

                spread.opposite(h)
                give(stage, h, OPPOSITE, compute(pl.ds(position(OPPOSITE, h), HALF)))

            return carry

        lax.fori_loop(0, 3, step, 0)

    ones = Halves(in_one, ag_send.at[0], ag_recv.at[0])
    backs = Halves(mlp_grad, ag_send.at[1], ag_recv.at[1])

    load.wait()
    for slot in (OPPOSITE, LEFT, RIGHT):
        part = dot_nt(att[rows_of(places[slot]), :], w_out[...])
        give(0, 0, slot, part[:HALF])
        send_buf[0, 1, slot - 1] = part[HALF:].astype(BF16)
    for slot in (OPPOSITE, LEFT, RIGHT):
        scatter(0, 1, slot).start()
    own_part[...] = dot_nt(att[rows_of(0), :], w_out[...])
    small[...] = jnp.zeros_like(small)

    def first_mix(h):
        rows = half_rows(h)
        attn = collect(0, h)
        states = hid_tok[rows, :].astype(F32)
        one, normed_one, branch_one, scale_one = mix_forward(states, attn, rates[0:1, :])
        in_one[rows, :] = one.astype(BF16)
        ones.start(h)
        state[0, rows, :] = one
        normed[rows, :] = normed_one
        scales[0, rows, :] = jnp.broadcast_to(branch_one, (HALF, 128))
        scales[1, rows, :] = jnp.broadcast_to(scale_one, (HALF, 128))

    both(first_mix)
    load_rest.wait()

    def feed(rows):
        block = in_one[rows, :]
        gate_raw = dot_nn(block, w_gate[...])
        raw_gate[rows, :] = gate_raw
        up_raw = dot_nn(block, w_up[...])
        raw_up[rows, :] = up_raw
        g, q = swiglu_parts(gate_raw, up_raw, gate_gain, up_gain)
        low = (up_gain * up_raw * (g * q)).astype(BF16)
        product[rows, :] = low
        return dot_nt(low, w_down[...])

    flow(1, ones, feed)
    factor = 16384 * math.sqrt(D) / count[0:1, 0:1]

    def second_mix(h):
        rows = half_rows(h)
        mlp = collect(1, h)
        one = state[0, rows, :]
        two, normed_two, branch_two, scale_two = mix_forward(one, mlp, rates[1:2, :])
        errors = two - tea[rows, :].astype(F32)
        weight = mask[rows, 0:1]
        seed = factor * (weight * errors)
        res_one, mlp_back, rate_two = mix_backward(
            seed, one, normed_two, branch_two, two, scale_two, rates[1:2, :]
        )
        mlp_grad[rows, :] = mlp_back.astype(BF16)
        backs.start(h)
        state[1, rows, :] = res_one
        turned[rows, :] = two
        small[1:2, :] += rate_two
        loss = jnp.sum(jnp.sum(weight * errors * errors, axis=1, keepdims=True), axis=0, keepdims=True)
        small[4:5, :] += jnp.broadcast_to(loss, (1, D))

    both(second_mix)
    for g in range(10):
        lanes = slice(128 * g, 128 * g + 128)
        out_buf[lanes, :] = turned[:, lanes].T.astype(BF16)
    out_copies = []
    for k in (1, 2, 3):
        copy = remote(
            out_buf.at[feats(wrap(y + k))],
            output.at[:, rows_of(0)],
            o_send.at[k],
            o_recv.at[k],
            device(z, x, c, wrap(y + k)),
        )
        copy.start()
        out_copies.append(copy)
    output[:, rows_of(0)] = out_buf[feats(y), :]

    def unfeed(rows):
        grad = dot_nn(mlp_grad[rows, :], w_down[...])
        gate_raw = raw_gate[rows, :]
        up_raw = raw_up[rows, :]
        g, q = swiglu_parts(gate_raw, up_raw, gate_gain, up_gain)
        silu = g * q
        up_term = grad * silu
        slope = grad * up_gain * up_raw * (q * (1.0 + g * (1.0 - q))) * math.sqrt(D)
        small[2:3, :] += jnp.sum(up_term * up_raw, axis=0, keepdims=True)
        small[3:4, :] += jnp.sum(slope * gate_raw, axis=0, keepdims=True)
        up_back = (up_term * up_gain).astype(BF16)
        gate_back = (slope * gate_gain).astype(BF16)
        up_low[rows, :] = up_back
        gate_low[rows, :] = gate_back
        return dot_nt(gate_back, w_gate[...]) + dot_nt(up_back, w_up[...])

    flow(2, backs, unfeed)

    def weight_grad(j, left, right, out):
        def step(k, carry):
            rows = pl.ds(pl.multiple_of(256 * k, 256), 256)
            grads[j, rows, :] = dot_tn(left[:, rows], right[...]).astype(BF16)
            return carry

        lax.fori_loop(0, 5, step, 0)
        pltpu.make_async_copy(grads.at[j], out, g_sem.at[j]).start()

    weight_grad(2, mlp_grad, product, down_out)
    weight_grad(0, in_one, gate_low, gate_out)
    weight_grad(1, in_one, up_low, up_out)

    def third_mix(h):
        rows = half_rows(h)
        grad_one = state[1, rows, :] + collect(2, h)
        res, attn_back, rate_one = mix_backward(
            grad_one,
            hid_tok[rows, :].astype(F32),
            normed[rows, :],
            scales[0, rows, 0:1],
            state[0, rows, :],
            scales[1, rows, 0:1],
            rates[0:1, :],
        )
        attn_low[rows, :] = attn_back.astype(BF16)
        small[0:1, :] += rate_one
        turned[rows, :] = res

    both(third_mix)
    for g in range(10):
        lanes = slice(128 * g, 128 * g + 128)
        res_zero[lanes, :] = turned[:, lanes].T
    for j, out in enumerate((gate_out, up_out, down_out)):
        pltpu.make_async_copy(grads.at[j], out, g_sem.at[j]).wait()
    for slot in (LEFT, RIGHT, OPPOSITE):
        for stage in range(3):
            for h in range(2):
                scatter(stage, h, slot).wait_send()
    ones.close()
    backs.close()
    for copy in out_copies:
        copy.wait()


def middle(vmem_args, placed_args):
    sds = jax.ShapeDtypeStruct
    wide = VMEM((ROWS, D), BF16)
    square = sds((D, D), BF16)
    return pl.pallas_call(
        middle_kernel,
        out_shape=(
            sds((COLS, ROWS), BF16),
            sds((TOK, D), BF16),
            sds((D, TOK), F32),
            sds((8, D), F32),
            square,
            square,
            square,
        ),
        in_specs=[IN_VMEM] * len(vmem_args) + [IN_PLACE] * len(placed_args),
        out_specs=(IN_VMEM,) * 4 + (IN_PLACE,) * 3,
        scratch_shapes=[
            wide,
            wide,
            wide,
            wide,
            wide,
            VMEM((D, 384), BF16),
            VMEM((3, D, D), BF16),
            VMEM((3, D, D), BF16),
            VMEM((ROWS, D), F32),
            VMEM((ROWS, D), F32),
            VMEM((3, 2, 3, HALF, D), BF16),
            VMEM((3, 2, 3, HALF, D), BF16),
            VMEM((TOK, D), F32),
            VMEM((D, TOK), BF16),
            VMEM((2, TOK, D), F32),
            VMEM((TOK, D), F32),
            VMEM((2, TOK, 128), F32),
            VMEM((TOK, D), F32),
            DMA((2,)),
            DMA((3,)),
            DMA((2, 2, 4)),
            DMA((2, 2, 4)),
            DMA((3, 2, 4)),
            DMA((3, 2, 4)),
            DMA((4,)),
            DMA((4,)),
        ],
        compiler_params=params(1),
        name="middle",
    )(*vmem_args, *placed_args)


class Fold:
    def __init__(self, bufs, sems, z_heavy):
        z, x, c, y = spot()
        self.z, self.x, self.c = z, x, c
        self.z_heavy = z_heavy
        self.first, self.second, _ = torus(z, x, c, y, z_heavy)
        self.at_first = x if z_heavy else x * (1 - c) + z * c
        self.sibling = device(z, x, 1 - c, y)
        self.own, self.sib, self.relays, self.got_two, self.mid, self.got_one, self.fin = bufs
        self.l_sem, self.h_send, self.h_recv, self.b_send, self.b_recv, self.a_send, self.a_recv, self.f_send, self.f_recv = sems
        self.count = self.own.shape[0]
        self.lanes = pl.ds(pl.multiple_of(640 * c, 128), 640)
        self.other = pl.ds(pl.multiple_of(640 * (1 - c), 128), 640)

    def handed(self, j, d, src):
        return remote(src, self.sib.at[j, d], self.h_send.at[j, d], self.h_recv.at[j, d], self.sibling)

    def fetched(self, j, d, src):
        return pltpu.make_async_copy(src, self.own.at[j, d], self.l_sem.at[j, d])

    def open(self, srcs):
        z, x = self.z, self.x
        if self.z_heavy:
            for d in (2, 1, 3, 0):
                for j, src in enumerate(srcs):
                    self.handed(j, d, src.at[wrap(z + d), :, :, self.other]).start()
                    self.fetched(j, d, src.at[wrap(z + d), :, :, self.lanes]).start()
            return

        @pl.when(self.c == 0)
        def _():
            for d in (2, 1, 3, 0):
                for j, src in enumerate(srcs):
                    self.handed(j, d, src.at[:, wrap(x + d), :, self.other]).start()
                    self.fetched(j, d, src.at[wrap(z + d), :, :, self.lanes]).start()

        @pl.when(self.c == 1)
        def _():
            for d in (2, 1, 3, 0):
                for j, src in enumerate(srcs):
                    self.handed(j, d, src.at[wrap(z + d), :, :, self.other]).start()
                    self.fetched(j, d, src.at[:, wrap(x + d), :, self.lanes]).start()

    def pair(self, k):
        way = 1 if k % 2 == 0 else -1
        at = pl.ds(0 if k in (0, 3, 4) else 2, 2)
        if k < 2:
            src, dst = self.own.at[:, 2, at], self.relays.at[:, k]
        else:
            src, dst = self.own.at[:, 1 if way > 0 else 3, at], self.got_two.at[:, k % 2, at]
        return remote(src, dst, self.b_send.at[k], self.b_recv.at[k], self.second(way))

    def last(self, e):
        return remote(
            self.mid.at[:, e - 1], self.got_one.at[:, e - 1], self.a_send.at[e], self.a_recv.at[e], self.first(e)
        )

    def add(self, d):
        for j in range(self.count):
            blank = self.sib.at[j, d]
            self.fetched(j, d, blank).wait()
            self.handed(j, d, blank).wait_recv()

        def each(i, carry):
            j, a = lax.div(i, 4), lax.rem(i, 4)
            total = self.own[j, d, a].astype(F32) + self.sib[j, d, a].astype(F32)
            self.own[j, d, a] = total.astype(BF16)
            return carry

        lax.fori_loop(0, 4 * self.count, each, 0)
        for k in {2: (0, 1), 1: (2,), 3: (3,), 0: ()}[d]:
            self.pair(k).start()

    def relay(self):
        for k, d, off in ((0, 1, 0), (1, 3, 2)):
            self.pair(k).wait_recv()

            def each(i, carry, k=k, d=d, off=off):
                j, a = lax.div(i, 2), lax.rem(i, 2)
                total = self.own[j, d, off + a].astype(F32) + self.relays[j, k, a].astype(F32)
                self.own[j, d, off + a] = total.astype(BF16)
                return carry

            lax.fori_loop(0, 2 * self.count, each, 0)
            self.pair(4 + k).start()

    def whole(self, j, at):
        total = self.own[j, 0, at].astype(F32)
        for k in range(2):
            total = total + self.got_two[j, k, at].astype(F32)
        return total

    def cross(self):
        for k in range(2, 6):
            self.pair(k).wait_recv()
        for e in (2, 1, 3):

            def each(j, carry, e=e):
                self.mid[j, e - 1] = self.whole(j, wrap(self.at_first + e)).astype(BF16)
                return carry

            lax.fori_loop(0, self.count, each, 0)
            self.last(e).start()

    def give(self, out):
        rows = pl.ds(pl.multiple_of(40 * (1 - self.c), 8), 40)
        return remote(self.fin.at[:, rows], out.at[:, :, self.lanes], self.f_send, self.f_recv, self.sibling)

    def finish(self, out):
        for e in (1, 2, 3):
            self.last(e).wait_recv()

        def each(j, carry):
            total = self.whole(j, self.at_first)
            for e in (1, 2, 3):
                total = total + self.got_one[j, e - 1].astype(F32)
            self.fin[j] = total
            return carry

        lax.fori_loop(0, self.count, each, 0)
        self.give(out).start()
        rows = pl.ds(pl.multiple_of(40 * self.c, 8), 40)
        for j in range(self.count):
            out[j, :, self.lanes] = self.fin[j, rows, :]

    def close(self, out):
        self.give(out).wait()
        for k in range(6):
            self.pair(k).wait_send()
        for e in (1, 2, 3):
            self.last(e).wait_send()
        for j in range(self.count):
            for d in range(4):
                self.handed(j, d, self.sib.at[j, d]).wait_send()


def fold_scratch(count):
    block = (80, 640)
    return [
        VMEM((count, 4, 4) + block, BF16),
        VMEM((count, 4, 4) + block, BF16),
        VMEM((count, 2, 2) + block, BF16),
        VMEM((count, 2, 4) + block, BF16),
        VMEM((count, 3) + block, BF16),
        VMEM((count, 3) + block, BF16),
        VMEM((count,) + block, F32),
        DMA((count, 4)),
        DMA((count, 4)),
        DMA((count, 4)),
        DMA((6,)),
        DMA((6,)),
        DMA((4,)),
        DMA((4,)),
        DMA,
        DMA,
    ]


def head_back(grad, raw, gain, cosine, sine):
    normed, scale = head_norm(raw, cosine, sine)
    gain_grad = jnp.sum(grad * normed, axis=0, keepdims=True)
    pulled = grad * gain
    turned = scale * (pulled - normed * over_heads(normed * pulled))
    return turned * cosine + swap_halves(turned * sine), gain_grad


def tail_kernel(
    starts,
    q_pad,
    out_t,
    lse,
    attn_low,
    att,
    gains,
    cos_block,
    sin_block,
    turn,
    res_t,
    small,
    count,
    win_in,
    raw_in,
    hid_in,
    w_in,
    m0,
    m1,
    m2,
    hidden_grad,
    query_g,
    key_g,
    value_g,
    out_g,
    gate_g,
    up_g,
    down_g,
    sums_out,
    win,
    raw,
    hid_t,
    w_first,
    attn,
    d_att,
    d_pad,
    delta,
    q_acc,
    d_win,
    sib_one,
    sib_two,
    one_buf,
    two_buf,
    got_one,
    got_two,
    got_part,
    transit,
    kv_sum,
    pack,
    out_part,
    first_g,
    y_send_buf,
    y_got_buf,
    side_src,
    side_got,
    sums,
    m_out,
    f_out,
    in_sem,
    k_send,
    k_recv,
    y_send,
    y_recv,
    v_send,
    v_recv,
    g_send,
    g_recv,
    *rest,
):
    m_bufs, m_sems, rest = rest[:7], rest[7:16], rest[16:]
    f_bufs, f_sems, rest = rest[:7], rest[7:16], rest[16:]
    t_accs, t_parts, t_send, t_recv = rest
    z, x, c, y = spot()
    place = 2 * x + c
    sibling = device(z, x, 1 - c, y)
    across = [device(z, x, c, wrap(y + d)) for d in (1, 2, 3)]
    tally = Tally(sums, t_accs, t_parts, t_send, t_recv)

    def slot(ref, s):
        return ref.at[pl.ds(pl.multiple_of(ROWS * s, ROWS), ROWS)]

    win_loads = [
        pltpu.make_async_copy(slot(win_in, s), slot(win, s), in_sem.at[s]) for s in range(5)
    ]
    for s in range(5):
        win_loads[s].start()
    loads = [
        pltpu.make_async_copy(src, dst, in_sem.at[5 + k])
        for k, (src, dst) in enumerate(
            ((w_in, w_first), (raw_in, raw), (hid_in, hid_t))
        )
    ]
    meet(across + tally.peers[0] + tally.peers[1] + tally.peers[2])
    fold_m = Fold(m_bufs, m_sems, True)
    fold_f = Fold(f_bufs, f_sems, False)
    my_rows = pl.ds(pl.multiple_of(TOK * y, TOK), TOK)
    attn[my_rows, :] = attn_low[...]
    spread = Spread(attn, g_send, g_recv)
    spread.start()
    fold_m.open([m0, m1, m2])
    for load in loads:
        load.start()
    side_src[...] = jnp.zeros_like(side_src)
    for k in range(4):
        lanes = slice(COLS * k, COLS * (k + 1))
        side_src[k, 0:2, 0:COLS] = small[0:2, lanes]
        side_src[k, 2:3, 0:COLS] = small[4:5, lanes]

    def side(k):
        return remote(side_src.at[wrap(y + k)], side_got.at[k], v_send.at[k], v_recv.at[k], across[k - 1])

    for k in (1, 2, 3):
        side(k).start()
    loads[0].wait()

    def unproject(k):
        rows = pl.ds(pl.multiple_of(TOK * wrap(y + k), TOK), TOK)
        d_att[rows, :] = dot_nn(attn[rows, :], w_first[:, 0:384]).astype(BF16)

    unproject(0)
    fold_m.add(2)
    spread.sides()
    fold_m.add(1)
    unproject(1)
    unproject(3)
    fold_m.add(3)
    spread.opposite()
    unproject(2)

    for h in range(HEADS):
        d_pad[h] = pad_head(d_att, (h + 1) // 2, (h + 1) % 2)
    wide = d_att[...].astype(F32).T[64:, :] * out_t[...]
    for h in range(HEADS):
        delta[h] = jnp.broadcast_to(
            jnp.sum(wide[64 * h : 64 * (h + 1), :], axis=0, keepdims=True), (8, ROWS)
        )
    q_acc[...] = jnp.zeros_like(q_acc)

    hand_one = remote(slot(d_win, 3 - 2 * c), sib_one, k_send.at[0], k_recv.at[0], sibling)
    hand_two = remote(slot(d_win, 1), sib_two, k_send.at[1], k_recv.at[1], sibling)
    hand_own = remote(slot(d_win, 3), sib_two, k_send.at[2], k_recv.at[2], sibling)
    one = remote(one_buf, got_one, k_send.at[3], k_recv.at[3], device(z, wrap(x + 3), c, y))
    part_a = remote(
        two_buf.at[pl.ds(0, UP)], got_part, k_send.at[4], k_recv.at[4], device(z, wrap(x - 1), c, y)
    )
    part_b = remote(
        two_buf.at[pl.ds(UP, ROWS - UP)],
        transit,
        k_send.at[5],
        k_recv.at[5],
        device(z, wrap(x + 1), c, y),
    )
    part_on = remote(transit, got_two, k_send.at[6], k_recv.at[6], device(z, wrap(x + 1), c, y))

    def tile(t):
        rows = pl.ds(pl.multiple_of(t * TILE, TILE), TILE)
        key_at = t * TILE + lax.broadcasted_iota(jnp.int32, (TILE, ROWS), 0)
        query_at = 4 * ROWS + lax.broadcasted_iota(jnp.int32, (TILE, ROWS), 1)
        allowed = (key_at >= starts[...]) & (key_at <= query_at)
        terms = [None] * 5
        for h in range(HEADS):
            kg, kh = key_place(h)
            vg, _ = value_place(h)
            keys = win[rows, 128 * kg : 128 * kg + 128]
            values = win[rows, 128 * vg : 128 * vg + 128]
            scores = dot_nt(keys, q_pad[h])
            probs = jnp.where(allowed, jnp.exp(scores - lse[h, 0:1, :]), 0.0)
            prob_grad = dot_nt(values, d_pad[h])
            score_grad = (probs * (prob_grad - delta[h, 0:1, :])).astype(BF16)
            v_term = dot_nn(probs.astype(BF16), d_pad[h])
            k_term = dot_nn(score_grad, q_pad[h])
            for at, term in ((kg, k_term), (vg, v_term)):
                terms[at] = term if terms[at] is None else terms[at] + term
            both = dot_tn(keys, score_grad)
            q_acc[h] += both[64 * kh : 64 * kh + 64, :]
        for g in range(5):
            d_win[rows, 128 * g : 128 * g + 128] = terms[g].astype(BF16)

    def after(k):
        if k == 0:

            @pl.when((c == 0) & (x > 1))
            def _():
                two_buf[...] = d_win[0:ROWS, :]
                part_b.start()
                part_a.start()

        if k == 1:

            @pl.when((c == 0) & (x > 1))
            def _():
                hand_two.start()

            @pl.when((c == 1) & (x > 0))
            def _():
                hand_one.start()

        if k == 2:

            @pl.when((c == 0) & (x > 0))
            def _():
                hand_one.start()

            @pl.when((c == 1) & (x > 1))
            def _():
                hand_two.wait_recv()
                two_buf[...] = (
                    d_win[0:ROWS, :].astype(F32) + sib_two[...].astype(F32)
                ).astype(BF16)
                part_b.start()
                part_a.start()

        if k == 3:

            @pl.when(x > 0)
            def _():
                hand_one.wait_recv()
                one_buf[...] = (
                    d_win[2 * ROWS : 3 * ROWS, :].astype(F32) + sib_one[...].astype(F32)
                ).astype(BF16)

                @pl.when(x < 3)
                def _():
                    part_a.wait_recv()
                    one_buf[0:UP, :] = (
                        one_buf[0:UP, :].astype(F32) + got_part[...].astype(F32)
                    ).astype(BF16)

                one.start()

            @pl.when(c == 1)
            def _():
                hand_own.start()

    for load in win_loads:
        load.wait()
    folds = {3: 0}

    def step(i, carry):
        k = lax.div(i, 2)
        s = jnp.where((c == 0) & (k == 2), 3, jnp.where((c == 0) & (k == 3), 2, k))

        @pl.when(place + s >= 4)
        def _():
            tile(2 * s + lax.rem(i, 2))

        for k in range(4):

            @pl.when(i == 2 * k + 1)
            def _(k=k):
                after(k)

        for n, d in folds.items():

            @pl.when(i == n)
            def _(d=d):
                fold_m.add(d)

        @pl.when((i == 6) & ((x == 0) | (x == 3)))
        def _():
            part_b.wait_recv()
            part_on.start()

        @pl.when(i == 5)
        def _():
            fold_m.relay()

        return carry

    lax.fori_loop(0, 10, step, 0)
    for load in loads[1:]:
        load.wait()
    cosine, sine = rope_wide(cos_block, sin_block, turn)
    pack[:, 128:384] = jnp.zeros((ROWS, 256), BF16)
    gain_parts = []
    wide = jnp.concatenate([q_acc[h] for h in range(HEADS)] + [jnp.zeros((64, ROWS), F32)], axis=0)
    for g, at in enumerate((384, 512, 0)):
        grad = wide[128 * g : 128 * g + 128, :].T * math.sqrt(HEAD_DIM)
        term, gain_part = head_back(grad, raw[g], gains[:, 128 * g : 128 * g + 128], cosine, sine)
        if g == 2:
            term = jnp.where(half_mask(0), term, 0.0)
        pack[:, at : at + 128] = term.astype(BF16)
        gain_parts.append(gain_part)
    out_part[...] = dot_tn(attn[...], att[...])

    fold_m.cross()
    kv_sum[...] = d_win[4 * ROWS :, :].astype(F32)

    @pl.when(c == 0)
    def _():
        hand_own.wait_recv()
        kv_sum[...] += sib_two[...].astype(F32)

    @pl.when(x < 3)
    def _():
        one.wait_recv()
        kv_sum[...] += got_one[...].astype(F32)

    @pl.when(x < 2)
    def _():
        part_on.wait_recv()
        kv_sum[UP:, :] += got_two[...].astype(F32)

    for g in range(3):
        grad = kv_sum[:, 128 * g : 128 * g + 128]
        gain = gains[:, 128 * g : 128 * g + 128]
        term, gain_part = head_back(grad, raw[3 + g], gain, cosine, sine)
        if g == 2:
            term = jnp.where(half_mask(0), term, grad)
        at = 640 + 128 * g
        pack[:, at : at + 128] = term.astype(BF16)
        gain_parts[g] += gain_part
    pack[:, 1024:1280] = kv_sum[:, 384:640].astype(BF16)

    my_cols = pl.ds(pl.multiple_of(TOK * y, TOK), TOK)

    def project(to):
        rows = pl.ds(pl.multiple_of(COLS * to, 64), COLS)
        hidden_grad[...] = dot_nt(w_first[rows, :], pack[...])
        hidden_grad[:, my_cols] += res_t[rows, :]

    def grad_copy(k):
        return remote(y_send_buf.at[k - 1], y_got_buf.at[k - 1], y_send.at[k], y_recv.at[k], across[k - 1])

    extra = side_src[y]
    for k in (1, 2, 3):
        side(k).wait_recv()
        extra = extra + side_got[k]
    sums[...] = jnp.zeros_like(sums)
    sums[0:2, :] = small[2:4, :]
    sums[2:3, 0:384] = jnp.concatenate(gain_parts, axis=1)
    sums[3:6, 0:384] = extra[0:3, :]
    tally.start(0)

    def first_grad(k, carry):
        rows = pl.ds(pl.multiple_of(COLS * k, 64), COLS)
        grad = dot_nn(hid_t[rows, :], pack[...])
        low = grad[:, 0:384] + out_part[rows, :]
        for a in range(4):
            first_g[k, a, :, 0:384] = low[80 * a : 80 * a + 80].astype(BF16)
            first_g[k, a, :, 384:] = grad[80 * a : 80 * a + 80, 384:].astype(BF16)
        return carry

    lax.fori_loop(0, 4, first_grad, 0)
    fold_f.open([first_g])
    for k in (2, 1, 3):
        project(wrap(y + k))
        y_send_buf[k - 1] = hidden_grad[...].astype(BF16)
        grad_copy(k).start()

    tally.finish(0)
    tally.start(1)
    for d in (2, 1, 3):
        fold_f.add(d)
    project(y)
    fold_f.relay()
    fold_f.add(0)
    for k in (1, 2, 3):
        grad_copy(k).wait_recv()
        hidden_grad[...] += y_got_buf[k - 1].astype(F32)
    tally.finish(1)
    tally.start(2)
    fold_m.finish(m_out)
    fold_f.cross()
    fold_f.finish(f_out)
    tally.finish(2)
    fold_m.close(m_out)
    fold_f.close(f_out)
    gate_g[...] = m_out[0]
    up_g[...] = m_out[1]
    down_g[...] = m_out[2]
    query_g[:, 0:256] = f_out[0, :, 384:640]
    query_g[:, 256:320] = f_out[0, :, 0:64]
    key_g[...] = f_out[0, :, 640:960]
    value_g[...] = f_out[0, :, 960:1280]
    out_g[...] = f_out[0, :, 64:384]
    sums_out[...] = t_accs[2]
    sums_out[6:7, :] = jnp.broadcast_to(count[0:1, 0:1], (1, D))
    for k in (1, 2, 3):
        grad_copy(k).wait_send()
        side(k).wait_send()
    spread.close()

    @pl.when(x > 0)
    def _():
        hand_one.wait_send()
        one.wait_send()

    @pl.when((x == 0) | (x == 3))
    def _():
        part_on.wait_send()

    @pl.when(x > 1)
    def _():
        part_a.wait_send()
        part_b.wait_send()

        @pl.when(c == 0)
        def _():
            hand_two.wait_send()

    @pl.when(c == 1)
    def _():
        hand_own.wait_send()

    tally.close()


def tail(vmem_args, placed_args):
    sds = jax.ShapeDtypeStruct
    block = VMEM((ROWS, 2 * COLS), BF16)
    shapes = [(COLS, ROWS)] + [(40, COLS)] * 4 + [(40, D)] * 3 + [(8, D)]
    return pl.pallas_call(
        tail_kernel,
        out_shape=tuple(sds(s, F32) for s in shapes),
        in_specs=[IN_VMEM] * len(vmem_args) + [IN_PLACE] * len(placed_args),
        out_specs=(IN_VMEM,) * len(shapes),
        scratch_shapes=[
            VMEM((5 * ROWS, 2 * COLS), BF16),
            VMEM((6, ROWS, 128), F32),
            VMEM((D, ROWS), BF16),
            VMEM((D, D), BF16),
            VMEM((ROWS, D), BF16),
            VMEM((ROWS, 384), BF16),
            VMEM((HEADS, ROWS, 128), BF16),
            VMEM((HEADS, 8, ROWS), F32),
            VMEM((HEADS, 64, ROWS), F32),
            VMEM((5 * ROWS, 2 * COLS), BF16),
        ]
        + [block] * 5
        + [
            VMEM((ROWS - UP, 2 * COLS), BF16),
            VMEM((UP, 2 * COLS), BF16),
            VMEM((ROWS - UP, 2 * COLS), BF16),
            VMEM((ROWS, 2 * COLS), F32),
            VMEM((ROWS, D), BF16),
            VMEM((D, 384), F32),
            VMEM((4, 4, 80, D), BF16),
            VMEM((3, COLS, ROWS), BF16),
            VMEM((3, COLS, ROWS), BF16),
            VMEM((4, 8, 384), F32),
            VMEM((4, 8, 384), F32),
            VMEM((8, D), F32),
            VMEM((3, 40, D), F32),
            VMEM((1, 40, D), F32),
            DMA((9,)),
            DMA((7,)),
            DMA((7,)),
            DMA((4,)),
            DMA((4,)),
            DMA((4,)),
            DMA((4,)),
            DMA((4,)),
            DMA((4,)),
        ]
        + fold_scratch(3)
        + fold_scratch(1)
        + tally_scratch((8, D)),
        compiler_params=params(2),
        name="tail",
    )(*vmem_args, *placed_args)


def emit_kernel(sums, *refs):
    count = (len(refs) - 6) // 2
    for src, dst in zip(refs[:count], refs[count : 2 * count]):
        dst[...] = src[...]
    loss, attention, feedforward, score, up, gate = refs[2 * count :]
    loss[0] = jnp.sum(sums[5:6, 0:1] / sums[6:7, 0:1])
    score[...] = sums[2:3, 0:COLS].reshape(COLS)
    attention[...] = sums[3:4, 0:COLS].reshape(COLS)
    feedforward[...] = sums[4:5, 0:COLS].reshape(COLS)
    up[...] = sums[0:1, :].reshape(D)
    gate[...] = sums[1:2, :].reshape(D)


def emit(sums, arrays):
    sds = jax.ShapeDtypeStruct
    vectors = [sds((1,), F32)] + [sds((COLS,), F32)] * 3 + [sds((D,), F32)] * 2
    return pl.pallas_call(
        emit_kernel,
        out_shape=tuple(sds(a.shape, a.dtype) for a in arrays) + tuple(vectors),
        in_specs=[IN_VMEM] * (1 + len(arrays)),
        out_specs=(IN_VMEM,) * len(arrays) + (IN_SMEM,) + (IN_VMEM,) * 5,
        compiler_params=params(),
        name="emit",
    )(sums, *arrays)


def shards(
    hidden,
    teacher,
    valid_mask,
    segments,
    query_weight,
    key_weight,
    value_weight,
    out_weight,
    gate_weight,
    up_weight,
    down_weight,
    attention_rate,
    feedforward_rate,
    score_gain,
    up_gain,
    gate_gain,
):
    ropes = rope_constants()
    others = (query_weight, key_weight, value_weight, out_weight.T)
    others += (gate_weight, up_weight, down_weight.T)
    others += (attention_rate, feedforward_rate, valid_mask, segments, score_gain, *ropes)
    (
        hid_t,
        hid_tok,
        tea_tok,
        rates,
        count,
        mask,
        gains,
        weights,
        w_rest,
        raw,
        q_pad,
        win,
        att,
        out_t,
        lse,
        starts,
    ) = front(hidden.T, teacher.T, others)
    output, attn_low, res_t, small, *grads = middle(
        (
            att,
            hid_tok,
            tea_tok,
            mask,
            count,
            rates,
            up_gain,
            gate_gain,
        ),
        (weights, w_rest),
    )
    results = tail(
        (starts, q_pad, out_t, lse, attn_low, att, gains, *ropes, res_t, small, count),
        (win, raw, hid_t, weights) + tuple(g.reshape(4, 4, 80, D) for g in grads),
    )
    results = emit(results[8], (output,) + tuple(results[:8]))
    output, hidden_grad, query_g, key_g, value_g, out_g, gate_g, up_g, down_g = results[:9]
    return (
        results[9].reshape(()),
        output.T,
        hidden_grad.T,
        query_g,
        key_g,
        value_g,
        out_g.T,
        gate_g,
        up_g,
        down_g.T,
    ) + tuple(results[10:])


def solution(mesh):
    both = P(("dp", "row"), "col")
    turned = P("col", ("dp", "row"))
    vector = P("col")
    in_specs = (both, both, P(("dp", "row")), P("dp", None), both, both, both, turned, both, both)
    in_specs += (turned,) + (vector,) * 5
    out_specs = (P(), both, both, both, both, both, turned, both, both, turned) + (vector,) * 5
    return jax.shard_map(shards, mesh=mesh, in_specs=in_specs, out_specs=out_specs, check_vma=False)
```

```python
import math

import jax
import jax.numpy as jnp
import numpy as np
from jax import lax
from jax.experimental import pallas as pl
from jax.experimental.pallas import tpu as pltpu
from jax.sharding import PartitionSpec as P

D = 1280
HEAD_DIM = 64
EPS = 1e-06
HEADS = 5
ROWS = 512
TOK = 128
COLS = 320
TILE = 256
UP = 176
F32 = jnp.float32
BF16 = jnp.bfloat16
MESH = pl.DeviceIdType.MESH
DMA = pltpu.SemaphoreType.DMA
VMEM = pltpu.VMEM
IN_VMEM = pl.BlockSpec(memory_space=pltpu.VMEM)
IN_SMEM = pl.BlockSpec(memory_space=pltpu.SMEM)
IN_PLACE = pl.BlockSpec(memory_space=pl.ANY)
LIMIT = 60 << 20


def params(collective=None):
    if collective is None:
        return pltpu.CompilerParams(vmem_limit_bytes=LIMIT)
    return pltpu.CompilerParams(
        collective_id=collective, has_side_effects=True, vmem_limit_bytes=LIMIT
    )


def spot():
    row = lax.axis_index("row")
    return lax.axis_index("dp"), lax.div(row, 2), lax.rem(row, 2), lax.axis_index("col")


def wrap(i):
    return lax.rem(i + 8, 4)


def device(z, x, c, y):
    return (z, 2 * x + c, y)


def meet(others):
    barrier = pltpu.get_barrier_semaphore()
    for other in others:
        pl.semaphore_signal(barrier, inc=1, device_id=other, device_id_type=MESH)
    pl.semaphore_wait(barrier, len(others))


def remote(src, dst, send_sem, recv_sem, to):
    return pltpu.make_async_remote_copy(
        src_ref=src,
        dst_ref=dst,
        send_sem=send_sem,
        recv_sem=recv_sem,
        device_id=to,
        device_id_type=MESH,
    )


def dot_nn(a, b):
    return lax.dot_general(a, b, (((1,), (0,)), ((), ())), preferred_element_type=F32)


def dot_nt(a, b):
    return lax.dot_general(a, b, (((1,), (1,)), ((), ())), preferred_element_type=F32)


def dot_tn(a, b):
    return lax.dot_general(a, b, (((0,), (0,)), ((), ())), preferred_element_type=F32)


class Tally:
    def __init__(self, src, accs, parts, send, recv):
        z, x, c, y = spot()
        self.src, self.accs, self.parts, self.send, self.recv = src, accs, parts, send, recv
        self.peers = [
            [device(z, wrap(x + d), c, y) for d in (1, 2, 3)],
            [device(wrap(z + d), x, c, y) for d in (1, 2, 3)],
            [device(z, x, 1 - c, y)],
        ]
        self.copies = []

    def start(self, stage):
        src = self.src if stage == 0 else self.accs.at[stage - 1]
        for d, peer in enumerate(self.peers[stage]):
            at = 3 * stage + d
            copy = remote(src, self.parts.at[at], self.send.at[at], self.recv.at[at], peer)
            copy.start()
            self.copies.append(copy)

    def finish(self, stage):
        src = self.src if stage == 0 else self.accs.at[stage - 1]
        total = src[...]
        for d in range(len(self.peers[stage])):
            self.copies[3 * stage + d].wait_recv()
            total = total + self.parts[3 * stage + d]
        self.accs[stage] = total

    def close(self):
        for copy in self.copies:
            copy.wait_send()


TALLY_PEERS = 7


def tally_scratch(shape):
    return [
        VMEM((3,) + shape, F32),
        VMEM((7,) + shape, F32),
        DMA((7,)),
        DMA((7,)),
    ]


def torus(z, x, c, y, z_last=False):
    turn = 0 if z_last else c

    def first(d):
        return device(wrap(z + turn * d), wrap(x + (1 - turn) * d), c, y)

    def second(d):
        return device(wrap(z + (1 - turn) * d), wrap(x + turn * d), c, y)

    at_first = x * (1 - turn) + z * turn
    at_second = z * (1 - turn) + x * turn

    def block(d1, d2):
        a1, a2 = wrap(at_first + d1), wrap(at_second + d2)
        return (1 - turn) * (a2 * 4 + a1) + turn * (a1 * 4 + a2)

    return first, second, block


def half_mask(half):
    lane = lax.broadcasted_iota(jnp.int32, (1, 128), 1)
    return (lane < 64) if half == 0 else (lane >= 64)


def key_place(h):
    return h // 2, h % 2


def value_place(h):
    return (HEADS + h) // 2, (HEADS + h) % 2


def pad_head(wide, at, half):
    group = wide[:, 128 * at : 128 * at + 128]
    return jnp.where(half_mask(half), group, jnp.zeros_like(group))


LOW_ROWS = 48


def lane_halves(c):
    ours = pl.ds(pl.multiple_of(640 * c, 128), 640)
    theirs = pl.ds(pl.multiple_of(640 * (1 - c), 128), 640)
    return ours, theirs


def lane_slab(ref, lanes):
    return lambda at: ref.at[:, pl.ds(pl.multiple_of(80 * at, 16), 80), lanes]


def lane_part(ref, lanes):
    def part(at, way):
        if way > 0:
            rows = pl.ds(pl.multiple_of(80 * at, 16), LOW_ROWS)
        else:
            rows = pl.ds(pl.multiple_of(80 * at + LOW_ROWS, 16), 80 - LOW_ROWS)
        return ref.at[:, rows, lanes]

    return part


def join_cores(c, shard, shard_sib, own_block, ours):
    for j in range(own_block.shape[0]):
        near = shard[j, :, ours].astype(F32)
        far = shard_sib[j].astype(F32)
        upper = jnp.where(c == 0, near, far)
        lower = jnp.where(c == 0, far, near)
        own_block[j] = jnp.concatenate([upper, lower], axis=0).astype(BF16)


class Ring:
    def __init__(self, own, slab, part, send, recv, h_send, h_recv, z_last=False):
        z, x, c, y = spot()
        self.first, self.second, self.block = torus(z, x, c, y, z_last)
        self.sibling = device(z, x, 1 - c, y)
        self.own, self.slab, self.part = own, slab, part
        self.send, self.recv, self.h_send, self.h_recv = send, recv, h_send, h_recv

    def ship(self, src, dst, at, to):
        return remote(src, dst, self.send.at[at], self.recv.at[at], to)

    def one(self, way):
        at = self.block(0, 0)
        return self.ship(self.own, self.slab(at), 0 if way > 0 else 1, self.first(way))

    def one_on(self, way):
        piece = self.part(self.block(-way, 0), way)
        return self.ship(piece, piece, 2 if way > 0 else 3, self.first(way))

    def two(self, d1, way):
        at = self.block(d1, 0)
        src = self.own if d1 == 0 else self.slab(at)
        return self.ship(src, self.slab(at), 4 + 4 * d1 + (0 if way > 0 else 1), self.second(way))

    def two_on(self, d1, way):
        piece = self.part(self.block(d1, -way), way)
        return self.ship(piece, piece, 6 + 4 * d1 + (0 if way > 0 else 1), self.second(way))

    def hand(self, d1, d2):
        at = self.block(d1, d2)
        src = self.own if d1 == 0 and d2 == 0 else self.slab(at)
        k = 4 * d1 + d2
        return remote(src, self.slab(at), self.h_send.at[k], self.h_recv.at[k], self.sibling)

    def open(self):
        self.one(1).start()
        self.one(-1).start()
        self.spread(0)

    def spread(self, d1):
        self.two(d1, 1).start()
        self.two(d1, -1).start()
        self.hand(d1, 0).start()

    def near(self):
        self.one(1).wait_recv()
        self.one_on(1).start()
        self.spread(3)
        self.one(-1).wait_recv()
        self.one_on(-1).start()
        self.spread(1)

    def far(self):
        self.one_on(1).wait_recv()
        self.one_on(-1).wait_recv()
        self.spread(2)

    def turn(self, d1):
        self.two(d1, 1).wait_recv()
        self.two_on(d1, 1).start()
        self.hand(d1, 3).start()
        self.two(d1, -1).wait_recv()
        self.two_on(d1, -1).start()
        self.hand(d1, 1).start()

    def end(self, d1):
        self.two_on(d1, 1).wait_recv()
        self.two_on(d1, -1).wait_recv()
        self.hand(d1, 2).start()

    def arrive(self):
        for d1 in range(4):
            for d2 in range(4):
                self.hand(d1, d2).wait_recv()

    def close(self):
        for way in (1, -1):
            self.one(way).wait_send()
            self.one_on(way).wait_send()
            for d1 in range(4):
                self.two(d1, way).wait_send()
                self.two_on(d1, way).wait_send()
        for d1 in range(4):
            for d2 in range(4):
                self.hand(d1, d2).wait_send()

    def steps(self):
        return [
            self.near,
            lambda: self.turn(0),
            self.far,
            lambda: self.turn(3),
            lambda: self.turn(1),
            lambda: self.end(0),
            lambda: self.turn(2),
            lambda: self.end(3),
            lambda: self.end(1),
            lambda: self.end(2),
        ]


def ring_scratch():
    return [DMA((20,)), DMA((20,)), DMA((16,)), DMA((16,))]


def rope_wide(cos_block, sin_block, turn):
    place = lax.axis_index("row")
    cos_at = turn[place, 0:1, :]
    sin_at = turn[place, 1:2, :]
    cosine = cos_block[...] * cos_at - sin_block[...] * sin_at
    sine = sin_block[...] * cos_at + cos_block[...] * sin_at
    lane = lax.broadcasted_iota(jnp.int32, sine.shape, 1)
    return cosine, jnp.where(lax.rem(lane, 64) < 32, -sine, sine)


def swap_halves(v):
    lane = lax.broadcasted_iota(jnp.int32, v.shape, 1)
    return jnp.where(lax.rem(lane, 64) < 32, pltpu.roll(v, 96, 1), pltpu.roll(v, 32, 1))


def over_heads(v):
    low = half_mask(0)
    left = jnp.sum(jnp.where(low, v, 0.0), axis=1, keepdims=True)
    right = jnp.sum(jnp.where(low, 0.0, v), axis=1, keepdims=True)
    return jnp.where(low, left, right)


def head_norm(raw, cosine, sine):
    scale = lax.rsqrt(over_heads(raw * raw) + EPS)
    return (raw * cosine + swap_halves(raw) * sine) * scale, scale


def front_kernel(
    hid,
    tea,
    query_w,
    key_w,
    value_w,
    out_w,
    gate_w,
    up_w,
    down_w,
    rate_one,
    rate_two,
    valid,
    seg,
    score_gain,
    cos_block,
    sin_block,
    turn,
    hid_out,
    hid_tok,
    tea_tok,
    rates_out,
    count_out,
    mask_out,
    gains_out,
    weights,
    w_rest,
    raw_out,
    q_pad,
    win_out,
    att,
    out_t,
    lse,
    starts_out,
    hid_t,
    hid_n,
    tea_t,
    rates,
    count,
    count_rows,
    rate_buf,
    shard,
    shard_sib,
    own_block,
    shard_b,
    shard_b_sib,
    own_b,
    w_first,
    win,
    transit,
    o_acc,
    l_acc,
    y_send,
    y_recv,
    s_send,
    s_recv,
    local_sem,
    k_send,
    k_recv,
    a_send,
    a_recv,
    a_hsend,
    a_hrecv,
    b_send,
    b_recv,
    b_hsend,
    b_hrecv,
    c_send,
    c_recv,
    c_hsend,
    c_hrecv,
    t_accs,
    t_parts,
    t_send,
    t_recv,
):
    z, x, c, y = spot()
    place = 2 * x + c
    sibling = device(z, x, 1 - c, y)
    across = [device(z, x, c, wrap(y + d)) for d in (1, 2, 3)]
    tally = Tally(count, t_accs, t_parts, t_send, t_recv)

    shard[0] = jnp.concatenate(
        [query_w[:, 256:], out_w[...], query_w[:, :256], key_w[...], value_w[...]], axis=1
    )
    shard_b[0] = gate_w[...]
    shard_b[1] = up_w[...]
    shard_b[2] = down_w[...]
    rates[0:1, :] = rate_one[...].reshape(1, COLS)
    rates[1:2, :] = rate_two[...].reshape(1, COLS)
    token_mask = valid[...].reshape(1, ROWS).astype(F32)
    count[...] = jnp.broadcast_to(jnp.sum(token_mask, axis=1, keepdims=True), (8, 128))
    meet(across + tally.peers[0] + tally.peers[1] + tally.peers[2])

    ours, theirs = lane_halves(c)
    ring_a = Ring(own_block, lane_slab(w_first, ours), lane_part(w_first, ours), a_send, a_recv, a_hsend, a_hrecv)
    w_pair, w_last = w_rest.at[pl.ds(0, 2)], w_rest.at[pl.ds(2, 1)]
    ring_b = Ring(
        own_b.at[pl.ds(0, 2)],
        lane_slab(w_pair, ours),
        lane_part(w_pair, ours),
        b_send,
        b_recv,
        b_hsend,
        b_hrecv,
        True,
    )
    ring_c = Ring(
        own_b.at[pl.ds(2, 1)],
        lane_slab(w_last, ours),
        lane_part(w_last, ours),
        c_send,
        c_recv,
        c_hsend,
        c_hrecv,
    )
    head = remote(shard.at[:, :, theirs], shard_sib, s_send.at[0], s_recv.at[0], sibling)
    head.start()
    head_b = remote(shard_b.at[:, :, theirs], shard_b_sib, s_send.at[1], s_recv.at[1], sibling)
    head_b.start()
    my_feats = pl.ds(pl.multiple_of(COLS * y, 64), COLS)
    hid_r = remote(hid, hid_t.at[my_feats], y_send.at[0], y_recv.at[0], across[0])
    hid_l = remote(hid, hid_t.at[my_feats], y_send.at[1], y_recv.at[1], across[2])
    hid_r.start()
    hid_l.start()
    hid_own = pltpu.make_async_copy(hid, hid_t.at[my_feats], local_sem.at[0])
    hid_own.start()
    tea_own = pltpu.make_async_copy(
        tea.at[:, pl.ds(pl.multiple_of(TOK * y, TOK), TOK)], tea_t.at[my_feats], local_sem.at[1]
    )
    tea_own.start()

    head.wait()
    join_cores(c, shard, shard_sib, own_block, ours)
    ring_a.open()
    own_at = ring_a.block(0, 0)
    own_a = pltpu.make_async_copy(own_block, ring_a.slab(own_at), local_sem.at[2])
    own_a.start()
    tally.start(0)
    small = []
    for d in (1, 2, 3):
        rows = pl.ds(pl.multiple_of(TOK * wrap(y + d), TOK), TOK)
        pieces = ((tea.at[:, rows], tea_t.at[my_feats]), (rates, rate_buf.at[y]))
        for k, (src, dst) in enumerate(pieces):
            at = 4 + 2 * (d - 1) + k
            copy = remote(src, dst, y_send.at[at], y_recv.at[at], across[d - 1])
            copy.start()
            small.append(copy)
    rate_buf[y] = rates[...]
    gains = jnp.concatenate([score_gain[...].reshape(1, COLS), jnp.zeros((1, 64), F32)], axis=1)
    gains_out[...] = gains
    token = pl.ds(pl.multiple_of(TOK * y, TOK), TOK)
    count_rows[0:1, :] = token_mask
    mask_out[...] = jnp.broadcast_to(count_rows[0:1, token], (TOK, TOK)).T

    first = jnp.sum((seg[...] < 1).astype(jnp.int32), axis=1, keepdims=True)
    second = jnp.sum((seg[...] < 2).astype(jnp.int32), axis=1, keepdims=True)
    query_seg = seg[:, pl.ds(pl.multiple_of(ROWS * place, ROWS), ROWS)]
    starts = jnp.where(query_seg == 0, 0, jnp.where(query_seg == 1, first, second))
    starts_out[...] = starts - (place - 4) * ROWS
    o_acc[...] = jnp.zeros_like(o_acc)
    l_acc[...] = jnp.zeros_like(l_acc)

    ring_a.near()
    head_b.wait()
    join_cores(c, shard_b, shard_b_sib, own_b, ours)
    own_rest = pltpu.make_async_copy(own_b, lane_slab(w_rest, ours)(ring_b.block(0, 0)), local_sem.at[3])
    own_rest.start()
    ring_a.turn(0)
    ring_a.far()
    ring_b.open()
    ring_c.open()
    hid_r.wait_recv()
    hid_f_ref = hid_t.at[pl.ds(pl.multiple_of(COLS * wrap(y - 1), 64), 160)]
    hid_f = remote(hid_f_ref, hid_f_ref, y_send.at[2], y_recv.at[2], across[0])
    hid_f.start()
    hid_l.wait_recv()
    hid_g_ref = hid_t.at[pl.ds(pl.multiple_of(COLS * wrap(y + 1) + 160, 32), 160)]
    hid_g = remote(hid_g_ref, hid_g_ref, y_send.at[3], y_recv.at[3], across[2])
    hid_g.start()
    ring_a.turn(3)
    ring_a.turn(1)
    tally.finish(0)
    tally.start(1)
    ring_a.end(0)
    ring_a.turn(2)
    ring_a.end(3)
    ring_a.end(1)
    ring_a.end(2)
    tally.finish(1)
    tally.start(2)
    hid_own.wait()
    hid_f.wait_recv()
    hid_g.wait_recv()
    hid_save = pltpu.make_async_copy(hid_t, hid_out, local_sem.at[4])
    hid_save.start()
    for g in range(10):
        hid_n[:, 128 * g : 128 * g + 128] = hid_t[128 * g : 128 * g + 128, :].T
    own_a.wait()
    ring_a.arrive()
    ring_b.near()
    ring_c.near()
    w_save = pltpu.make_async_copy(w_first.at[0], weights, local_sem.at[5])
    w_save.start()

    cosine, sine = rope_wide(cos_block, sin_block, turn)
    raw = dot_nn(hid_n[...], w_first[0, :, 640:1280])
    for g in range(3):
        group = raw[:, 128 * g : 128 * g + 128]
        raw_out[3 + g] = group
        normed, _ = head_norm(group, cosine, sine)
        keys = normed * gains[:, 128 * g : 128 * g + 128]
        if g == 2:
            keys = jnp.where(half_mask(0), keys, group)
        win[4 * ROWS :, 128 * g : 128 * g + 128] = keys.astype(BF16)
    win[4 * ROWS :, 384:640] = raw[:, 384:640].astype(BF16)

    def slot(s):
        return win.at[pl.ds(pl.multiple_of(ROWS * s, ROWS), ROWS)]

    one = remote(slot(4), slot(2), k_send.at[0], k_recv.at[0], device(z, wrap(x + 1), c, y))
    up = remote(
        win.at[pl.ds(2 * ROWS, UP)],
        win.at[pl.ds(0, UP)],
        k_send.at[1],
        k_recv.at[1],
        device(z, wrap(x + 1), c, y),
    )
    down = remote(
        win.at[pl.ds(4 * ROWS + UP, ROWS - UP)],
        transit,
        k_send.at[5],
        k_recv.at[5],
        device(z, wrap(x - 1), c, y),
    )
    down_on = remote(
        transit,
        win.at[pl.ds(UP, ROWS - UP)],
        k_send.at[6],
        k_recv.at[6],
        device(z, wrap(x - 1), c, y),
    )
    own = remote(slot(4), slot(3), k_send.at[2], k_recv.at[2], sibling)
    one_on = remote(slot(2), slot(1 + 2 * c), k_send.at[3], k_recv.at[3], sibling)
    two_on = remote(slot(0), slot(1), k_send.at[4], k_recv.at[4], sibling)

    @pl.when(x < 3)
    def _():
        one.start()

    @pl.when(x < 2)
    def _():
        down.start()

    @pl.when(c == 0)
    def _():
        own.start()

    root = math.sqrt(HEAD_DIM)
    for g, at in enumerate((384, 512, 0)):
        group = dot_nn(hid_n[...], w_first[0, :, at : at + 128])
        raw_out[g] = group
        normed, _ = head_norm(group, cosine, sine)
        scaled = (normed * gains[:, 128 * g : 128 * g + 128]).astype(BF16) * jnp.asarray(root, BF16)
        for half in range(2 if g < 2 else 1):
            q_pad[2 * g + half] = jnp.where(half_mask(half), scaled, jnp.zeros_like(scaled))
    hid_tok[...] = hid_n[pl.ds(pl.multiple_of(TOK * y, TOK), TOK), :]

    ring_b.turn(0)
    ring_b.far()
    ring_c.turn(0)
    ring_c.far()
    events = list(zip(ring_b.steps()[3:], ring_c.steps()[3:]))

    def tile(t):
        rows = pl.ds(pl.multiple_of(t * TILE, TILE), TILE)
        key_at = t * TILE + lax.broadcasted_iota(jnp.int32, (TILE, ROWS), 0)
        query_at = 4 * ROWS + lax.broadcasted_iota(jnp.int32, (TILE, ROWS), 1)
        allowed = (key_at >= starts_out[...]) & (key_at <= query_at)
        for h in range(HEADS):
            kg, _ = key_place(h)
            vg, vh = value_place(h)
            keys = win[rows, 128 * kg : 128 * kg + 128]
            values = win[rows, 128 * vg : 128 * vg + 128]
            scores = dot_nt(keys, q_pad[h])
            probs = jnp.where(allowed, jnp.exp(scores), 0.0)
            l_acc[h] += jnp.sum(probs.reshape(TILE // 8, 8, ROWS), axis=0)
            both = dot_tn(values, probs.astype(BF16))
            o_acc[h] += both[64 * vh : 64 * vh + 64, :]

    def step(i, carry):
        k = lax.div(i, 2)
        turned = k - 1 + 2 * lax.rem(k, 2)
        s = jnp.where(k == 0, 4, jnp.where(c == 1, 4 - k, 4 - turned))

        @pl.when((i == 2) & (c == 1))
        def _():
            own.wait_recv()

        @pl.when((x > 0) & (((i == 4) & (c == 1)) | ((i == 2) & (c == 0))))
        def _():
            one.wait_recv()
            one_on.start()

            @pl.when(x < 3)
            def _():
                up.start()

        @pl.when((i == 3) & ((x == 0) | (x == 3)))
        def _():
            down.wait_recv()
            down_on.start()

        @pl.when((x > 0) & (((i == 6) & (c == 1)) | ((i == 4) & (c == 0))))
        def _():
            one_on.wait_recv()

        @pl.when((x > 1) & (((i == 8) & (c == 1)) | ((i == 6) & (c == 0))))
        def _():
            up.wait_recv()
            down_on.wait_recv()

            @pl.when(c == 1)
            def _():
                two_on.start()

        @pl.when((x > 1) & (i == 8) & (c == 0))
        def _():
            two_on.wait_recv()

        for n, event in enumerate(events):

            @pl.when(i == n + 2)
            def _(event=event):
                event[0]()
                event[1]()

        @pl.when(place + s >= 4)
        def _():
            tile(2 * s + lax.rem(i, 2))

        return carry

    lax.fori_loop(0, 10, step, 0)
    win_save = pltpu.make_async_copy(win, win_out, local_sem.at[6])
    win_save.start()
    for copy in small:
        copy.wait_recv()
    tea_own.wait()
    for g in range(10):
        tea_tok[:, 128 * g : 128 * g + 128] = tea_t[128 * g : 128 * g + 128, :].T
    rates_out[...] = jnp.concatenate([rate_buf[k] for k in range(4)], axis=1)
    tally.finish(2)
    count_out[...] = t_accs[2]
    for h in range(HEADS):
        total = jnp.sum(l_acc[h], axis=0, keepdims=True)
        lse[h] = jnp.broadcast_to(jnp.log(total), (8, ROWS))
        out_t[64 * h : 64 * h + 64, :] = o_acc[h] / total
    wide = jnp.concatenate([jnp.zeros((64, ROWS), F32), out_t[...]], axis=0)
    att[...] = wide.T.astype(BF16)
    ring_b.arrive()
    ring_c.arrive()
    own_rest.wait()
    ring_a.close()
    ring_b.close()
    ring_c.close()
    hid_save.wait()
    w_save.wait()
    win_save.wait()
    for copy in small + [hid_r, hid_l, hid_f, hid_g]:
        copy.wait_send()

    @pl.when(x < 3)
    def _():
        one.wait_send()

    @pl.when(x < 2)
    def _():
        down.wait_send()

    @pl.when((x == 0) | (x == 3))
    def _():
        down_on.wait_send()

    @pl.when((x == 1) | (x == 2))
    def _():
        up.wait_send()

    @pl.when(c == 0)
    def _():
        own.wait_send()

    @pl.when(x > 0)
    def _():
        one_on.wait_send()

    @pl.when((x > 1) & (c == 1))
    def _():
        two_on.wait_send()

    tally.close()


def rope_constants():
    inverse = np.exp(np.arange(32) * (-2.0 * math.log(10000.0) / HEAD_DIM))
    inverse = np.tile(inverse, 4)
    inside = np.arange(ROWS)[:, None] * inverse[None, :]
    at = (ROWS * np.arange(8))[:, None] * inverse[None, :]
    turn = np.stack([np.cos(at), np.sin(at)], axis=1)
    return [jnp.asarray(v, F32) for v in (np.cos(inside), np.sin(inside), turn)]


def front(hidden, teacher, others):
    sds = jax.ShapeDtypeStruct
    outs = [
        (sds((D, ROWS), BF16), IN_PLACE),
        (sds((TOK, D), BF16), IN_VMEM),
        (sds((TOK, D), BF16), IN_VMEM),
        (sds((2, D), F32), IN_VMEM),
        (sds((8, 128), F32), IN_VMEM),
        (sds((TOK, TOK), F32), IN_VMEM),
        (sds((1, 384), F32), IN_VMEM),
        (sds((D, D), BF16), IN_PLACE),
        (sds((3, D, D), BF16), IN_PLACE),
        (sds((6, ROWS, 128), F32), IN_VMEM),
        (sds((HEADS, ROWS, 128), BF16), IN_VMEM),
        (sds((5 * ROWS, 2 * COLS), BF16), IN_PLACE),
        (sds((ROWS, 384), BF16), IN_VMEM),
        (sds((COLS, ROWS), F32), IN_VMEM),
        (sds((HEADS, 8, ROWS), F32), IN_VMEM),
        (sds((1, ROWS), jnp.int32), IN_VMEM),
    ]
    return pl.pallas_call(
        front_kernel,
        out_shape=tuple(o[0] for o in outs),
        in_specs=[IN_PLACE] * 2 + [IN_VMEM] * len(others),
        out_specs=tuple(o[1] for o in outs),
        scratch_shapes=[
            VMEM((D, ROWS), BF16),
            VMEM((ROWS, D), BF16),
            VMEM((D, TOK), BF16),
            VMEM((2, COLS), F32),
            VMEM((8, 128), F32),
            VMEM((8, ROWS), F32),
            VMEM((4, 2, COLS), F32),
            VMEM((1, 40, D), BF16),
            VMEM((1, 40, 640), BF16),
            VMEM((1, 80, 640), BF16),
            VMEM((3, 40, D), BF16),
            VMEM((3, 40, 640), BF16),
            VMEM((3, 80, 640), BF16),
            VMEM((1, D, D), BF16),
            VMEM((5 * ROWS, 2 * COLS), BF16),
            VMEM((ROWS - UP, 2 * COLS), BF16),
            VMEM((HEADS, 64, ROWS), F32),
            VMEM((HEADS, 8, ROWS), F32),
            DMA((10,)),
            DMA((10,)),
            DMA((2,)),
            DMA((2,)),
            DMA((7,)),
            DMA((7,)),
            DMA((7,)),
        ]
        + ring_scratch()
        + ring_scratch()
        + ring_scratch()
        + tally_scratch((8, 128)),
        compiler_params=params(0),
        name="front",
    )(hidden, teacher, *others)


class Spread:
    def __init__(self, ref, send, recv):
        z, x, c, y = spot()
        self.ref, self.send, self.recv, self.y = ref, send, recv, y
        self.to = {way: device(z, x, c, wrap(y + way)) for way in (1, -1)}

    def full(self, way):
        rows = pl.ds(pl.multiple_of(TOK * self.y, TOK), TOK)
        k = 0 if way > 0 else 1
        return remote(self.ref.at[rows], self.ref.at[rows], self.send.at[k], self.recv.at[k], self.to[way])

    def relay(self, way):
        half = TOK // 2
        at = TOK * wrap(self.y - way) + (0 if way > 0 else half)
        rows = pl.ds(pl.multiple_of(at, half), half)
        k = 2 if way > 0 else 3
        return remote(self.ref.at[rows], self.ref.at[rows], self.send.at[k], self.recv.at[k], self.to[way])

    def start(self):
        self.full(1).start()
        self.full(-1).start()

    def sides(self):
        self.full(1).wait_recv()
        self.relay(1).start()
        self.full(-1).wait_recv()
        self.relay(-1).start()

    def opposite(self):
        self.relay(1).wait_recv()
        self.relay(-1).wait_recv()

    def close(self):
        for way in (1, -1):
            self.full(way).wait_send()
            self.relay(way).wait_send()


HALF = TOK // 2
OWN, LEFT, RIGHT, OPPOSITE = range(4)


def position(slot, h):
    if slot == OWN:
        at = HALF * h
    elif slot == OPPOSITE:
        at = 6 * HALF + HALF * h
    else:
        at = 2 * HALF * (1 + h) + (HALF if slot == RIGHT else 0)
    return at if isinstance(h, int) else pl.multiple_of(at, HALF)


class Halves:
    def __init__(self, ref, send, recv):
        z, x, c, y = spot()
        self.ref, self.send, self.recv = ref, send, recv
        self.to = {way: device(z, x, c, wrap(y + way)) for way in (1, -1)}

    def full(self, h, way):
        src = self.ref.at[pl.ds(position(OWN, h), HALF)]
        dst = self.ref.at[pl.ds(position(LEFT if way > 0 else RIGHT, h), HALF)]
        k = 0 if way > 0 else 1
        return remote(src, dst, self.send.at[h, k], self.recv.at[h, k], self.to[way])

    def relay(self, h, way):
        part = HALF // 2
        off = 0 if way > 0 else part
        src = pl.multiple_of(position(LEFT if way > 0 else RIGHT, h) + off, part)
        dst = pl.multiple_of(position(OPPOSITE, h) + off, part)
        k = 2 if way > 0 else 3
        return remote(
            self.ref.at[pl.ds(src, part)],
            self.ref.at[pl.ds(dst, part)],
            self.send.at[h, k],
            self.recv.at[h, k],
            self.to[way],
        )

    def start(self, h):
        self.full(h, 1).start()
        self.full(h, -1).start()

    def sides(self, h):
        self.full(h, 1).wait_recv()
        self.relay(h, 1).start()
        self.full(h, -1).wait_recv()
        self.relay(h, -1).start()

    def opposite(self, h):
        self.relay(h, 1).wait_recv()
        self.relay(h, -1).wait_recv()

    def close(self):
        for h in range(2):
            for way in (1, -1):
                self.full(h, way).wait_send()
                self.relay(h, way).wait_send()


def mix_forward(states, branch, alphas):
    branch_scale = lax.rsqrt(jnp.sum(branch * branch, axis=1, keepdims=True) + EPS)
    normed = branch * branch_scale
    mixed = states + alphas * (normed - states)
    mixed_scale = lax.rsqrt(jnp.sum(mixed * mixed, axis=1, keepdims=True) + EPS)
    return mixed * mixed_scale, normed, branch_scale, mixed_scale


def mix_backward(gradient, states, normed, branch_scale, mixed_out, mixed_scale, alphas):
    along = jnp.sum(mixed_out * gradient, axis=1, keepdims=True)
    mixed_grad = mixed_scale * (gradient - mixed_out * along)
    normed_grad = alphas * mixed_grad
    toward = jnp.sum(normed * normed_grad, axis=1, keepdims=True)
    branch_grad = branch_scale * (normed_grad - normed * toward)
    rate_grad = jnp.sum(mixed_grad * (normed - states), axis=0, keepdims=True)
    return (1.0 - alphas) * mixed_grad, branch_grad, rate_grad


def swiglu_parts(gate_raw, up_raw, gate_gain, up_gain):
    root = math.sqrt(D)
    g = gate_gain * gate_raw * root
    q = jax.nn.sigmoid(g)
    return g, q


def middle_kernel(
    att,
    hid_tok,
    tea,
    mask,
    count,
    rates,
    up_gain_in,
    gate_gain_in,
    weights,
    w_rest,
    output,
    attn_low,
    res_zero,
    small,
    gate_out,
    up_out,
    down_out,
    in_one,
    product,
    mlp_grad,
    gate_low,
    up_low,
    w_out,
    w_all,
    grads,
    raw_gate,
    raw_up,
    send_buf,
    got_buf,
    own_part,
    out_buf,
    state,
    normed,
    scales,
    turned,
    w_sem,
    g_sem,
    ag_send,
    ag_recv,
    rs_send,
    rs_recv,
    o_send,
    o_recv,
):
    z, x, c, y = spot()
    peers = [device(z, x, c, wrap(y + d)) for d in range(4)]
    load = pltpu.make_async_copy(weights.at[:, pl.ds(0, 384)], w_out, w_sem.at[0])
    load.start()
    load_rest = pltpu.make_async_copy(w_rest, w_all, w_sem.at[1])
    load_rest.start()
    up_gain = up_gain_in[...].reshape(1, D)
    gate_gain = gate_gain_in[...].reshape(1, D)
    w_gate, w_up, w_down = (w_all.at[k] for k in range(3))
    meet(peers[1:])
    places = {LEFT: 3, RIGHT: 1, OPPOSITE: 2}

    def rows_of(off):
        return pl.ds(pl.multiple_of(TOK * wrap(y + off), TOK), TOK)

    def feats(k):
        return pl.ds(pl.multiple_of(COLS * k, 64), COLS)

    def half_rows(h):
        return pl.ds(pl.multiple_of(HALF * h, HALF), HALF)

    def scatter(stage, h, slot):
        return remote(
            send_buf.at[stage, h, slot - 1],
            got_buf.at[stage, h, slot - 1],
            rs_send.at[stage, h, slot],
            rs_recv.at[stage, h, slot],
            device(z, x, c, wrap(y + places[slot])),
        )

    def give(stage, h, slot, part):
        send_buf[stage, h, slot - 1] = part.astype(BF16)
        scatter(stage, h, slot).start()

    def collect(stage, h):
        total = own_part[half_rows(h), :]
        for slot in (LEFT, RIGHT, OPPOSITE):
            scatter(stage, h, slot).wait_recv()
            total = total + got_buf[stage, h, slot - 1].astype(F32)
        return total

    def both(body):
        def step(h, carry):
            body(h)
            return carry

        lax.fori_loop(0, 2, step, 0)

    def flow(stage, spread, compute):
        def step(i, carry):
            @pl.when(i == 1)
            def _():
                spread.sides(0)

            part = compute(pl.ds(pl.multiple_of(TOK * i, TOK), TOK))

            @pl.when(i == 0)
            def _():
                own_part[...] = part

            @pl.when(i > 0)
            def _():
                h = i - 1
                give(stage, h, LEFT, part[:HALF])
                give(stage, h, RIGHT, part[HALF:])

                @pl.when(i == 1)
                def _():
                    spread.sides(1)

                spread.opposite(h)
                give(stage, h, OPPOSITE, compute(pl.ds(position(OPPOSITE, h), HALF)))

            return carry

        lax.fori_loop(0, 3, step, 0)

    ones = Halves(in_one, ag_send.at[0], ag_recv.at[0])
    backs = Halves(mlp_grad, ag_send.at[1], ag_recv.at[1])

    load.wait()
    for slot in (OPPOSITE, LEFT, RIGHT):
        part = dot_nt(att[rows_of(places[slot]), :], w_out[...])
        give(0, 0, slot, part[:HALF])
        send_buf[0, 1, slot - 1] = part[HALF:].astype(BF16)
    for slot in (OPPOSITE, LEFT, RIGHT):
        scatter(0, 1, slot).start()
    own_part[...] = dot_nt(att[rows_of(0), :], w_out[...])
    small[...] = jnp.zeros_like(small)

    def first_mix(h):
        rows = half_rows(h)
        attn = collect(0, h)
        states = hid_tok[rows, :].astype(F32)
        one, normed_one, branch_one, scale_one = mix_forward(states, attn, rates[0:1, :])
        in_one[rows, :] = one.astype(BF16)
        ones.start(h)
        state[0, rows, :] = one
        normed[rows, :] = normed_one
        scales[0, rows, :] = jnp.broadcast_to(branch_one, (HALF, 128))
        scales[1, rows, :] = jnp.broadcast_to(scale_one, (HALF, 128))

    both(first_mix)
    load_rest.wait()

    def feed(rows):
        block = in_one[rows, :]
        gate_raw = dot_nn(block, w_gate[...])
        raw_gate[rows, :] = gate_raw
        up_raw = dot_nn(block, w_up[...])
        raw_up[rows, :] = up_raw
        g, q = swiglu_parts(gate_raw, up_raw, gate_gain, up_gain)
        low = (up_gain * up_raw * (g * q)).astype(BF16)
        product[rows, :] = low
        return dot_nt(low, w_down[...])

    flow(1, ones, feed)
    factor = 16384 * math.sqrt(D) / count[0:1, 0:1]

    def second_mix(h):
        rows = half_rows(h)
        mlp = collect(1, h)
        one = state[0, rows, :]
        two, normed_two, branch_two, scale_two = mix_forward(one, mlp, rates[1:2, :])
        errors = two - tea[rows, :].astype(F32)
        weight = mask[rows, 0:1]
        seed = factor * (weight * errors)
        res_one, mlp_back, rate_two = mix_backward(
            seed, one, normed_two, branch_two, two, scale_two, rates[1:2, :]
        )
        mlp_grad[rows, :] = mlp_back.astype(BF16)
        backs.start(h)
        state[1, rows, :] = res_one
        turned[rows, :] = two
        small[1:2, :] += rate_two
        loss = jnp.sum(jnp.sum(weight * errors * errors, axis=1, keepdims=True), axis=0, keepdims=True)
        small[4:5, :] += jnp.broadcast_to(loss, (1, D))

    both(second_mix)
    for g in range(10):
        lanes = slice(128 * g, 128 * g + 128)
        out_buf[lanes, :] = turned[:, lanes].T.astype(BF16)
    out_copies = []
    for k in (1, 2, 3):
        copy = remote(
            out_buf.at[feats(wrap(y + k))],
            output.at[:, rows_of(0)],
            o_send.at[k],
            o_recv.at[k],
            device(z, x, c, wrap(y + k)),
        )
        copy.start()
        out_copies.append(copy)
    output[:, rows_of(0)] = out_buf[feats(y), :]

    def unfeed(rows):
        grad = dot_nn(mlp_grad[rows, :], w_down[...])
        gate_raw = raw_gate[rows, :]
        up_raw = raw_up[rows, :]
        g, q = swiglu_parts(gate_raw, up_raw, gate_gain, up_gain)
        silu = g * q
        up_term = grad * silu
        slope = grad * up_gain * up_raw * (q * (1.0 + g * (1.0 - q))) * math.sqrt(D)
        small[2:3, :] += jnp.sum(up_term * up_raw, axis=0, keepdims=True)
        small[3:4, :] += jnp.sum(slope * gate_raw, axis=0, keepdims=True)
        up_back = (up_term * up_gain).astype(BF16)
        gate_back = (slope * gate_gain).astype(BF16)
        up_low[rows, :] = up_back
        gate_low[rows, :] = gate_back
        return dot_nt(gate_back, w_gate[...]) + dot_nt(up_back, w_up[...])

    flow(2, backs, unfeed)

    def weight_grad(j, left, right, out):
        def step(k, carry):
            rows = pl.ds(pl.multiple_of(256 * k, 256), 256)
            grads[j, rows, :] = dot_tn(left[:, rows], right[...]).astype(BF16)
            return carry

        lax.fori_loop(0, 5, step, 0)
        pltpu.make_async_copy(grads.at[j], out, g_sem.at[j]).start()

    weight_grad(2, mlp_grad, product, down_out)
    weight_grad(0, in_one, gate_low, gate_out)
    weight_grad(1, in_one, up_low, up_out)

    def third_mix(h):
        rows = half_rows(h)
        grad_one = state[1, rows, :] + collect(2, h)
        res, attn_back, rate_one = mix_backward(
            grad_one,
            hid_tok[rows, :].astype(F32),
            normed[rows, :],
            scales[0, rows, 0:1],
            state[0, rows, :],
            scales[1, rows, 0:1],
            rates[0:1, :],
        )
        attn_low[rows, :] = attn_back.astype(BF16)
        small[0:1, :] += rate_one
        turned[rows, :] = res

    both(third_mix)
    for g in range(10):
        lanes = slice(128 * g, 128 * g + 128)
        res_zero[lanes, :] = turned[:, lanes].T
    for j, out in enumerate((gate_out, up_out, down_out)):
        pltpu.make_async_copy(grads.at[j], out, g_sem.at[j]).wait()
    for slot in (LEFT, RIGHT, OPPOSITE):
        for stage in range(3):
            for h in range(2):
                scatter(stage, h, slot).wait_send()
    ones.close()
    backs.close()
    for copy in out_copies:
        copy.wait()


def middle(vmem_args, placed_args):
    sds = jax.ShapeDtypeStruct
    wide = VMEM((ROWS, D), BF16)
    square = sds((D, D), BF16)
    return pl.pallas_call(
        middle_kernel,
        out_shape=(
            sds((COLS, ROWS), BF16),
            sds((TOK, D), BF16),
            sds((D, TOK), F32),
            sds((8, D), F32),
            square,
            square,
            square,
        ),
        in_specs=[IN_VMEM] * len(vmem_args) + [IN_PLACE] * len(placed_args),
        out_specs=(IN_VMEM,) * 4 + (IN_PLACE,) * 3,
        scratch_shapes=[
            wide,
            wide,
            wide,
            wide,
            wide,
            VMEM((D, 384), BF16),
            VMEM((3, D, D), BF16),
            VMEM((3, D, D), BF16),
            VMEM((ROWS, D), F32),
            VMEM((ROWS, D), F32),
            VMEM((3, 2, 3, HALF, D), BF16),
            VMEM((3, 2, 3, HALF, D), BF16),
            VMEM((TOK, D), F32),
            VMEM((D, TOK), BF16),
            VMEM((2, TOK, D), F32),
            VMEM((TOK, D), F32),
            VMEM((2, TOK, 128), F32),
            VMEM((TOK, D), F32),
            DMA((2,)),
            DMA((3,)),
            DMA((2, 2, 4)),
            DMA((2, 2, 4)),
            DMA((3, 2, 4)),
            DMA((3, 2, 4)),
            DMA((4,)),
            DMA((4,)),
        ],
        compiler_params=params(1),
        name="middle",
    )(*vmem_args, *placed_args)


class Fold:
    def __init__(self, bufs, sems, z_heavy):
        z, x, c, y = spot()
        self.z, self.x, self.c = z, x, c
        self.z_heavy = z_heavy
        self.first, self.second, _ = torus(z, x, c, y, z_heavy)
        self.at_first = x if z_heavy else x * (1 - c) + z * c
        self.sibling = device(z, x, 1 - c, y)
        self.own, self.sib, self.relays, self.got_two, self.mid, self.got_one, self.fin = bufs
        self.l_sem, self.h_send, self.h_recv, self.b_send, self.b_recv, self.a_send, self.a_recv, self.f_send, self.f_recv = sems
        self.count = self.own.shape[0]
        self.lanes = pl.ds(pl.multiple_of(640 * c, 128), 640)
        self.other = pl.ds(pl.multiple_of(640 * (1 - c), 128), 640)

    def handed(self, j, d, src):
        return remote(src, self.sib.at[j, d], self.h_send.at[j, d], self.h_recv.at[j, d], self.sibling)

    def fetched(self, j, d, src):
        return pltpu.make_async_copy(src, self.own.at[j, d], self.l_sem.at[j, d])

    def open(self, srcs):
        z, x = self.z, self.x
        if self.z_heavy:
            for d in (2, 1, 3, 0):
                for j, src in enumerate(srcs):
                    self.handed(j, d, src.at[wrap(z + d), :, :, self.other]).start()
                    self.fetched(j, d, src.at[wrap(z + d), :, :, self.lanes]).start()
            return

        @pl.when(self.c == 0)
        def _():
            for d in (2, 1, 3, 0):
                for j, src in enumerate(srcs):
                    self.handed(j, d, src.at[:, wrap(x + d), :, self.other]).start()
                    self.fetched(j, d, src.at[wrap(z + d), :, :, self.lanes]).start()

        @pl.when(self.c == 1)
        def _():
            for d in (2, 1, 3, 0):
                for j, src in enumerate(srcs):
                    self.handed(j, d, src.at[wrap(z + d), :, :, self.other]).start()
                    self.fetched(j, d, src.at[:, wrap(x + d), :, self.lanes]).start()

    def pair(self, k):
        way = 1 if k % 2 == 0 else -1
        at = pl.ds(0 if k in (0, 3, 4) else 2, 2)
        if k < 2:
            src, dst = self.own.at[:, 2, at], self.relays.at[:, k]
        else:
            src, dst = self.own.at[:, 1 if way > 0 else 3, at], self.got_two.at[:, k % 2, at]
        return remote(src, dst, self.b_send.at[k], self.b_recv.at[k], self.second(way))

    def last(self, e):
        return remote(
            self.mid.at[:, e - 1], self.got_one.at[:, e - 1], self.a_send.at[e], self.a_recv.at[e], self.first(e)
        )

    def add(self, d):
        for j in range(self.count):
            blank = self.sib.at[j, d]
            self.fetched(j, d, blank).wait()
            self.handed(j, d, blank).wait_recv()

        def each(i, carry):
            j, a = lax.div(i, 4), lax.rem(i, 4)
            total = self.own[j, d, a].astype(F32) + self.sib[j, d, a].astype(F32)
            self.own[j, d, a] = total.astype(BF16)
            return carry

        lax.fori_loop(0, 4 * self.count, each, 0)
        for k in {2: (0, 1), 1: (2,), 3: (3,), 0: ()}[d]:
            self.pair(k).start()

    def relay(self):
        for k, d, off in ((0, 1, 0), (1, 3, 2)):
            self.pair(k).wait_recv()

            def each(i, carry, k=k, d=d, off=off):
                j, a = lax.div(i, 2), lax.rem(i, 2)
                total = self.own[j, d, off + a].astype(F32) + self.relays[j, k, a].astype(F32)
                self.own[j, d, off + a] = total.astype(BF16)
                return carry

            lax.fori_loop(0, 2 * self.count, each, 0)
            self.pair(4 + k).start()

    def whole(self, j, at):
        total = self.own[j, 0, at].astype(F32)
        for k in range(2):
            total = total + self.got_two[j, k, at].astype(F32)
        return total

    def cross(self):
        for k in range(2, 6):
            self.pair(k).wait_recv()
        for e in (2, 1, 3):

            def each(j, carry, e=e):
                self.mid[j, e - 1] = self.whole(j, wrap(self.at_first + e)).astype(BF16)
                return carry

            lax.fori_loop(0, self.count, each, 0)
            self.last(e).start()

    def give(self, out):
        rows = pl.ds(pl.multiple_of(40 * (1 - self.c), 8), 40)
        return remote(self.fin.at[:, rows], out.at[:, :, self.lanes], self.f_send, self.f_recv, self.sibling)

    def finish(self, out):
        for e in (1, 2, 3):
            self.last(e).wait_recv()

        def each(j, carry):
            total = self.whole(j, self.at_first)
            for e in (1, 2, 3):
                total = total + self.got_one[j, e - 1].astype(F32)
            self.fin[j] = total
            return carry

        lax.fori_loop(0, self.count, each, 0)
        self.give(out).start()
        rows = pl.ds(pl.multiple_of(40 * self.c, 8), 40)
        for j in range(self.count):
            out[j, :, self.lanes] = self.fin[j, rows, :]

    def close(self, out):
        self.give(out).wait()
        for k in range(6):
            self.pair(k).wait_send()
        for e in (1, 2, 3):
            self.last(e).wait_send()
        for j in range(self.count):
            for d in range(4):
                self.handed(j, d, self.sib.at[j, d]).wait_send()


def fold_scratch(count):
    block = (80, 640)
    return [
        VMEM((count, 4, 4) + block, BF16),
        VMEM((count, 4, 4) + block, BF16),
        VMEM((count, 2, 2) + block, BF16),
        VMEM((count, 2, 4) + block, BF16),
        VMEM((count, 3) + block, BF16),
        VMEM((count, 3) + block, BF16),
        VMEM((count,) + block, F32),
        DMA((count, 4)),
        DMA((count, 4)),
        DMA((count, 4)),
        DMA((6,)),
        DMA((6,)),
        DMA((4,)),
        DMA((4,)),
        DMA,
        DMA,
    ]


def head_back(grad, raw, gain, cosine, sine):
    normed, scale = head_norm(raw, cosine, sine)
    gain_grad = jnp.sum(grad * normed, axis=0, keepdims=True)
    pulled = grad * gain
    turned = scale * (pulled - normed * over_heads(normed * pulled))
    return turned * cosine + swap_halves(turned * sine), gain_grad


def tail_kernel(
    starts,
    q_pad,
    out_t,
    lse,
    attn_low,
    att,
    gains,
    cos_block,
    sin_block,
    turn,
    res_t,
    small,
    count,
    win_in,
    raw_in,
    hid_in,
    w_in,
    m0,
    m1,
    m2,
    hidden_grad,
    query_g,
    key_g,
    value_g,
    out_g,
    gate_g,
    up_g,
    down_g,
    sums_out,
    win,
    raw,
    hid_t,
    w_first,
    attn,
    d_att,
    d_pad,
    delta,
    q_acc,
    d_win,
    sib_one,
    sib_two,
    one_buf,
    two_buf,
    got_one,
    got_two,
    got_part,
    transit,
    kv_sum,
    pack,
    out_part,
    first_g,
    y_send_buf,
    y_got_buf,
    side_src,
    side_got,
    sums,
    m_out,
    n_out,
    f_out,
    in_sem,
    k_send,
    k_recv,
    y_send,
    y_recv,
    v_send,
    v_recv,
    g_send,
    g_recv,
    *rest,
):
    m_bufs, m_sems, rest = rest[:7], rest[7:16], rest[16:]
    n_bufs, n_sems, rest = rest[:7], rest[7:16], rest[16:]
    f_bufs, f_sems, rest = rest[:7], rest[7:16], rest[16:]
    t_accs, t_parts, t_send, t_recv = rest
    z, x, c, y = spot()
    place = 2 * x + c
    sibling = device(z, x, 1 - c, y)
    across = [device(z, x, c, wrap(y + d)) for d in (1, 2, 3)]
    tally = Tally(sums, t_accs, t_parts, t_send, t_recv)

    def slot(ref, s):
        return ref.at[pl.ds(pl.multiple_of(ROWS * s, ROWS), ROWS)]

    win_loads = [
        pltpu.make_async_copy(slot(win_in, s), slot(win, s), in_sem.at[s]) for s in range(5)
    ]
    for s in range(5):
        win_loads[s].start()
    loads = [
        pltpu.make_async_copy(src, dst, in_sem.at[5 + k])
        for k, (src, dst) in enumerate(
            ((w_in, w_first), (raw_in, raw), (hid_in, hid_t))
        )
    ]
    meet(across + tally.peers[0] + tally.peers[1] + tally.peers[2])
    fold_m = Fold(m_bufs, m_sems, True)
    fold_n = Fold(n_bufs, n_sems, False)
    fold_f = Fold(f_bufs, f_sems, False)
    my_rows = pl.ds(pl.multiple_of(TOK * y, TOK), TOK)
    attn[my_rows, :] = attn_low[...]
    spread = Spread(attn, g_send, g_recv)
    spread.start()
    fold_m.open([m0, m1])
    fold_n.open([m2])
    for load in loads:
        load.start()
    side_src[...] = jnp.zeros_like(side_src)
    for k in range(4):
        lanes = slice(COLS * k, COLS * (k + 1))
        side_src[k, 0:2, 0:COLS] = small[0:2, lanes]
        side_src[k, 2:3, 0:COLS] = small[4:5, lanes]

    def side(k):
        return remote(side_src.at[wrap(y + k)], side_got.at[k], v_send.at[k], v_recv.at[k], across[k - 1])

    for k in (1, 2, 3):
        side(k).start()
    loads[0].wait()

    def unproject(k):
        rows = pl.ds(pl.multiple_of(TOK * wrap(y + k), TOK), TOK)
        d_att[rows, :] = dot_nn(attn[rows, :], w_first[:, 0:384]).astype(BF16)

    unproject(0)
    fold_m.add(2)
    fold_n.add(2)
    spread.sides()
    fold_m.add(1)
    fold_n.add(1)
    unproject(1)
    unproject(3)
    fold_m.add(3)
    fold_n.add(3)
    spread.opposite()
    unproject(2)

    for h in range(HEADS):
        d_pad[h] = pad_head(d_att, (h + 1) // 2, (h + 1) % 2)
    wide = d_att[...].astype(F32).T[64:, :] * out_t[...]
    for h in range(HEADS):
        delta[h] = jnp.broadcast_to(
            jnp.sum(wide[64 * h : 64 * (h + 1), :], axis=0, keepdims=True), (8, ROWS)
        )
    q_acc[...] = jnp.zeros_like(q_acc)

    hand_one = remote(slot(d_win, 3 - 2 * c), sib_one, k_send.at[0], k_recv.at[0], sibling)
    hand_two = remote(slot(d_win, 1), sib_two, k_send.at[1], k_recv.at[1], sibling)
    hand_own = remote(slot(d_win, 3), sib_two, k_send.at[2], k_recv.at[2], sibling)
    one = remote(one_buf, got_one, k_send.at[3], k_recv.at[3], device(z, wrap(x + 3), c, y))
    part_a = remote(
        two_buf.at[pl.ds(0, UP)], got_part, k_send.at[4], k_recv.at[4], device(z, wrap(x - 1), c, y)
    )
    part_b = remote(
        two_buf.at[pl.ds(UP, ROWS - UP)],
        transit,
        k_send.at[5],
        k_recv.at[5],
        device(z, wrap(x + 1), c, y),
    )
    part_on = remote(transit, got_two, k_send.at[6], k_recv.at[6], device(z, wrap(x + 1), c, y))

    def tile(t):
        rows = pl.ds(pl.multiple_of(t * TILE, TILE), TILE)
        key_at = t * TILE + lax.broadcasted_iota(jnp.int32, (TILE, ROWS), 0)
        query_at = 4 * ROWS + lax.broadcasted_iota(jnp.int32, (TILE, ROWS), 1)
        allowed = (key_at >= starts[...]) & (key_at <= query_at)
        terms = [None] * 5
        for h in range(HEADS):
            kg, kh = key_place(h)
            vg, _ = value_place(h)
            keys = win[rows, 128 * kg : 128 * kg + 128]
            values = win[rows, 128 * vg : 128 * vg + 128]
            scores = dot_nt(keys, q_pad[h])
            probs = jnp.where(allowed, jnp.exp(scores - lse[h, 0:1, :]), 0.0)
            prob_grad = dot_nt(values, d_pad[h])
            score_grad = (probs * (prob_grad - delta[h, 0:1, :])).astype(BF16)
            v_term = dot_nn(probs.astype(BF16), d_pad[h])
            k_term = dot_nn(score_grad, q_pad[h])
            for at, term in ((kg, k_term), (vg, v_term)):
                terms[at] = term if terms[at] is None else terms[at] + term
            both = dot_tn(keys, score_grad)
            q_acc[h] += both[64 * kh : 64 * kh + 64, :]
        for g in range(5):
            d_win[rows, 128 * g : 128 * g + 128] = terms[g].astype(BF16)

    def after(k):
        if k == 0:

            @pl.when((c == 0) & (x > 1))
            def _():
                two_buf[...] = d_win[0:ROWS, :]
                part_b.start()
                part_a.start()

        if k == 1:

            @pl.when((c == 0) & (x > 1))
            def _():
                hand_two.start()

            @pl.when((c == 1) & (x > 0))
            def _():
                hand_one.start()

        if k == 2:

            @pl.when((c == 0) & (x > 0))
            def _():
                hand_one.start()

            @pl.when((c == 1) & (x > 1))
            def _():
                hand_two.wait_recv()
                two_buf[...] = (
                    d_win[0:ROWS, :].astype(F32) + sib_two[...].astype(F32)
                ).astype(BF16)
                part_b.start()
                part_a.start()

        if k == 3:

            @pl.when(x > 0)
            def _():
                hand_one.wait_recv()
                one_buf[...] = (
                    d_win[2 * ROWS : 3 * ROWS, :].astype(F32) + sib_one[...].astype(F32)
                ).astype(BF16)

                @pl.when(x < 3)
                def _():
                    part_a.wait_recv()
                    one_buf[0:UP, :] = (
                        one_buf[0:UP, :].astype(F32) + got_part[...].astype(F32)
                    ).astype(BF16)

                one.start()

            @pl.when(c == 1)
            def _():
                hand_own.start()

    for load in win_loads:
        load.wait()
    folds = {3: 0}

    def step(i, carry):
        k = lax.div(i, 2)
        s = jnp.where((c == 0) & (k == 2), 3, jnp.where((c == 0) & (k == 3), 2, k))

        @pl.when(place + s >= 4)
        def _():
            tile(2 * s + lax.rem(i, 2))

        for k in range(4):

            @pl.when(i == 2 * k + 1)
            def _(k=k):
                after(k)

        for n, d in folds.items():

            @pl.when(i == n)
            def _(d=d):
                fold_m.add(d)
                fold_n.add(d)

        @pl.when((i == 6) & ((x == 0) | (x == 3)))
        def _():
            part_b.wait_recv()
            part_on.start()

        @pl.when(i == 5)
        def _():
            fold_m.relay()
            fold_n.relay()

        return carry

    lax.fori_loop(0, 10, step, 0)
    for load in loads[1:]:
        load.wait()
    cosine, sine = rope_wide(cos_block, sin_block, turn)
    pack[:, 128:384] = jnp.zeros((ROWS, 256), BF16)
    gain_parts = []
    wide = jnp.concatenate([q_acc[h] for h in range(HEADS)] + [jnp.zeros((64, ROWS), F32)], axis=0)
    for g, at in enumerate((384, 512, 0)):
        grad = wide[128 * g : 128 * g + 128, :].T * math.sqrt(HEAD_DIM)
        term, gain_part = head_back(grad, raw[g], gains[:, 128 * g : 128 * g + 128], cosine, sine)
        if g == 2:
            term = jnp.where(half_mask(0), term, 0.0)
        pack[:, at : at + 128] = term.astype(BF16)
        gain_parts.append(gain_part)
    out_part[...] = dot_tn(attn[...], att[...])

    fold_m.cross()
    fold_n.cross()
    kv_sum[...] = d_win[4 * ROWS :, :].astype(F32)

    @pl.when(c == 0)
    def _():
        hand_own.wait_recv()
        kv_sum[...] += sib_two[...].astype(F32)

    @pl.when(x < 3)
    def _():
        one.wait_recv()
        kv_sum[...] += got_one[...].astype(F32)

    @pl.when(x < 2)
    def _():
        part_on.wait_recv()
        kv_sum[UP:, :] += got_two[...].astype(F32)

    for g in range(3):
        grad = kv_sum[:, 128 * g : 128 * g + 128]
        gain = gains[:, 128 * g : 128 * g + 128]
        term, gain_part = head_back(grad, raw[3 + g], gain, cosine, sine)
        if g == 2:
            term = jnp.where(half_mask(0), term, grad)
        at = 640 + 128 * g
        pack[:, at : at + 128] = term.astype(BF16)
        gain_parts[g] += gain_part
    pack[:, 1024:1280] = kv_sum[:, 384:640].astype(BF16)

    my_cols = pl.ds(pl.multiple_of(TOK * y, TOK), TOK)

    def project(to):
        rows = pl.ds(pl.multiple_of(COLS * to, 64), COLS)
        hidden_grad[...] = dot_nt(w_first[rows, :], pack[...])
        hidden_grad[:, my_cols] += res_t[rows, :]

    def grad_copy(k):
        return remote(y_send_buf.at[k - 1], y_got_buf.at[k - 1], y_send.at[k], y_recv.at[k], across[k - 1])

    extra = side_src[y]
    for k in (1, 2, 3):
        side(k).wait_recv()
        extra = extra + side_got[k]
    sums[...] = jnp.zeros_like(sums)
    sums[0:2, :] = small[2:4, :]
    sums[2:3, 0:384] = jnp.concatenate(gain_parts, axis=1)
    sums[3:6, 0:384] = extra[0:3, :]
    tally.start(0)

    def first_grad(k, carry):
        rows = pl.ds(pl.multiple_of(COLS * k, 64), COLS)
        grad = dot_nn(hid_t[rows, :], pack[...])
        low = grad[:, 0:384] + out_part[rows, :]
        for a in range(4):
            first_g[k, a, :, 0:384] = low[80 * a : 80 * a + 80].astype(BF16)
            first_g[k, a, :, 384:] = grad[80 * a : 80 * a + 80, 384:].astype(BF16)
        return carry

    lax.fori_loop(0, 4, first_grad, 0)
    fold_f.open([first_g])
    for k in (2, 1, 3):
        project(wrap(y + k))
        y_send_buf[k - 1] = hidden_grad[...].astype(BF16)
        grad_copy(k).start()

    tally.finish(0)
    tally.start(1)
    for d in (2, 1, 3):
        fold_f.add(d)
    project(y)
    fold_f.relay()
    fold_f.add(0)
    for k in (1, 2, 3):
        grad_copy(k).wait_recv()
        hidden_grad[...] += y_got_buf[k - 1].astype(F32)
    tally.finish(1)
    tally.start(2)
    fold_m.finish(m_out)
    fold_n.finish(n_out)
    fold_f.cross()
    fold_f.finish(f_out)
    tally.finish(2)
    fold_m.close(m_out)
    fold_n.close(n_out)
    fold_f.close(f_out)
    gate_g[...] = m_out[0]
    up_g[...] = m_out[1]
    down_g[...] = n_out[0]
    query_g[:, 0:256] = f_out[0, :, 384:640]
    query_g[:, 256:320] = f_out[0, :, 0:64]
    key_g[...] = f_out[0, :, 640:960]
    value_g[...] = f_out[0, :, 960:1280]
    out_g[...] = f_out[0, :, 64:384]
    sums_out[...] = t_accs[2]
    sums_out[6:7, :] = jnp.broadcast_to(count[0:1, 0:1], (1, D))
    for k in (1, 2, 3):
        grad_copy(k).wait_send()
        side(k).wait_send()
    spread.close()

    @pl.when(x > 0)
    def _():
        hand_one.wait_send()
        one.wait_send()

    @pl.when((x == 0) | (x == 3))
    def _():
        part_on.wait_send()

    @pl.when(x > 1)
    def _():
        part_a.wait_send()
        part_b.wait_send()

        @pl.when(c == 0)
        def _():
            hand_two.wait_send()

    @pl.when(c == 1)
    def _():
        hand_own.wait_send()

    tally.close()


def tail(vmem_args, placed_args):
    sds = jax.ShapeDtypeStruct
    block = VMEM((ROWS, 2 * COLS), BF16)
    shapes = [(COLS, ROWS)] + [(40, COLS)] * 4 + [(40, D)] * 3 + [(8, D)]
    return pl.pallas_call(
        tail_kernel,
        out_shape=tuple(sds(s, F32) for s in shapes),
        in_specs=[IN_VMEM] * len(vmem_args) + [IN_PLACE] * len(placed_args),
        out_specs=(IN_VMEM,) * len(shapes),
        scratch_shapes=[
            VMEM((5 * ROWS, 2 * COLS), BF16),
            VMEM((6, ROWS, 128), F32),
            VMEM((D, ROWS), BF16),
            VMEM((D, D), BF16),
            VMEM((ROWS, D), BF16),
            VMEM((ROWS, 384), BF16),
            VMEM((HEADS, ROWS, 128), BF16),
            VMEM((HEADS, 8, ROWS), F32),
            VMEM((HEADS, 64, ROWS), F32),
            VMEM((5 * ROWS, 2 * COLS), BF16),
        ]
        + [block] * 5
        + [
            VMEM((ROWS - UP, 2 * COLS), BF16),
            VMEM((UP, 2 * COLS), BF16),
            VMEM((ROWS - UP, 2 * COLS), BF16),
            VMEM((ROWS, 2 * COLS), F32),
            VMEM((ROWS, D), BF16),
            VMEM((D, 384), F32),
            VMEM((4, 4, 80, D), BF16),
            VMEM((3, COLS, ROWS), BF16),
            VMEM((3, COLS, ROWS), BF16),
            VMEM((4, 8, 384), F32),
            VMEM((4, 8, 384), F32),
            VMEM((8, D), F32),
            VMEM((2, 40, D), F32),
            VMEM((1, 40, D), F32),
            VMEM((1, 40, D), F32),
            DMA((9,)),
            DMA((7,)),
            DMA((7,)),
            DMA((4,)),
            DMA((4,)),
            DMA((4,)),
            DMA((4,)),
            DMA((4,)),
            DMA((4,)),
        ]
        + fold_scratch(2)
        + fold_scratch(1)
        + fold_scratch(1)
        + tally_scratch((8, D)),
        compiler_params=params(2),
        name="tail",
    )(*vmem_args, *placed_args)


def emit_kernel(sums, *refs):
    count = (len(refs) - 6) // 2
    for src, dst in zip(refs[:count], refs[count : 2 * count]):
        dst[...] = src[...]
    loss, attention, feedforward, score, up, gate = refs[2 * count :]
    loss[0] = jnp.sum(sums[5:6, 0:1] / sums[6:7, 0:1])
    score[...] = sums[2:3, 0:COLS].reshape(COLS)
    attention[...] = sums[3:4, 0:COLS].reshape(COLS)
    feedforward[...] = sums[4:5, 0:COLS].reshape(COLS)
    up[...] = sums[0:1, :].reshape(D)
    gate[...] = sums[1:2, :].reshape(D)


def emit(sums, arrays):
    sds = jax.ShapeDtypeStruct
    vectors = [sds((1,), F32)] + [sds((COLS,), F32)] * 3 + [sds((D,), F32)] * 2
    return pl.pallas_call(
        emit_kernel,
        out_shape=tuple(sds(a.shape, a.dtype) for a in arrays) + tuple(vectors),
        in_specs=[IN_VMEM] * (1 + len(arrays)),
        out_specs=(IN_VMEM,) * len(arrays) + (IN_SMEM,) + (IN_VMEM,) * 5,
        compiler_params=params(),
        name="emit",
    )(sums, *arrays)


def shards(
    hidden,
    teacher,
    valid_mask,
    segments,
    query_weight,
    key_weight,
    value_weight,
    out_weight,
    gate_weight,
    up_weight,
    down_weight,
    attention_rate,
    feedforward_rate,
    score_gain,
    up_gain,
    gate_gain,
):
    ropes = rope_constants()
    others = (query_weight, key_weight, value_weight, out_weight.T)
    others += (gate_weight, up_weight, down_weight.T)
    others += (attention_rate, feedforward_rate, valid_mask, segments, score_gain, *ropes)
    (
        hid_t,
        hid_tok,
        tea_tok,
        rates,
        count,
        mask,
        gains,
        weights,
        w_rest,
        raw,
        q_pad,
        win,
        att,
        out_t,
        lse,
        starts,
    ) = front(hidden.T, teacher.T, others)
    output, attn_low, res_t, small, *grads = middle(
        (
            att,
            hid_tok,
            tea_tok,
            mask,
            count,
            rates,
            up_gain,
            gate_gain,
        ),
        (weights, w_rest),
    )
    results = tail(
        (starts, q_pad, out_t, lse, attn_low, att, gains, *ropes, res_t, small, count),
        (win, raw, hid_t, weights) + tuple(g.reshape(4, 4, 80, D) for g in grads),
    )
    results = emit(results[8], (output,) + tuple(results[:8]))
    output, hidden_grad, query_g, key_g, value_g, out_g, gate_g, up_g, down_g = results[:9]
    return (
        results[9].reshape(()),
        output.T,
        hidden_grad.T,
        query_g,
        key_g,
        value_g,
        out_g.T,
        gate_g,
        up_g,
        down_g.T,
    ) + tuple(results[10:])


def solution(mesh):
    both = P(("dp", "row"), "col")
    turned = P("col", ("dp", "row"))
    vector = P("col")
    in_specs = (both, both, P(("dp", "row")), P("dp", None), both, both, both, turned, both, both)
    in_specs += (turned,) + (vector,) * 5
    out_specs = (P(), both, both, both, both, both, turned, both, both, turned) + (vector,) * 5
    return jax.shard_map(shards, mesh=mesh, in_specs=in_specs, out_specs=out_specs, check_vma=False)
```

```python
import math

import jax
import jax.numpy as jnp
import numpy as np
from jax import lax
from jax.experimental import pallas as pl
from jax.experimental.pallas import tpu as pltpu
from jax.sharding import PartitionSpec as P

D = 1280
HEAD_DIM = 64
EPS = 1e-06
HEADS = 5
ROWS = 512
TOK = 128
COLS = 320
TILE = 256
UP = 176
F32 = jnp.float32
BF16 = jnp.bfloat16
MESH = pl.DeviceIdType.MESH
DMA = pltpu.SemaphoreType.DMA
VMEM = pltpu.VMEM
IN_VMEM = pl.BlockSpec(memory_space=pltpu.VMEM)
IN_SMEM = pl.BlockSpec(memory_space=pltpu.SMEM)
IN_PLACE = pl.BlockSpec(memory_space=pl.ANY)
LIMIT = 60 << 20


def params(collective=None):
    if collective is None:
        return pltpu.CompilerParams(vmem_limit_bytes=LIMIT)
    return pltpu.CompilerParams(
        collective_id=collective, has_side_effects=True, vmem_limit_bytes=LIMIT
    )


def spot():
    row = lax.axis_index("row")
    return lax.axis_index("dp"), lax.div(row, 2), lax.rem(row, 2), lax.axis_index("col")


def wrap(i):
    return lax.rem(i + 8, 4)


def device(z, x, c, y):
    return (z, 2 * x + c, y)


def meet(others):
    barrier = pltpu.get_barrier_semaphore()
    for other in others:
        pl.semaphore_signal(barrier, inc=1, device_id=other, device_id_type=MESH)
    pl.semaphore_wait(barrier, len(others))


def remote(src, dst, send_sem, recv_sem, to):
    return pltpu.make_async_remote_copy(
        src_ref=src,
        dst_ref=dst,
        send_sem=send_sem,
        recv_sem=recv_sem,
        device_id=to,
        device_id_type=MESH,
    )


def dot_nn(a, b):
    return lax.dot_general(a, b, (((1,), (0,)), ((), ())), preferred_element_type=F32)


def dot_nt(a, b):
    return lax.dot_general(a, b, (((1,), (1,)), ((), ())), preferred_element_type=F32)


def dot_tn(a, b):
    return lax.dot_general(a, b, (((0,), (0,)), ((), ())), preferred_element_type=F32)


class Tally:
    def __init__(self, src, accs, parts, send, recv):
        z, x, c, y = spot()
        self.src, self.accs, self.parts, self.send, self.recv = src, accs, parts, send, recv
        self.peers = [
            [device(z, wrap(x + d), c, y) for d in (1, 2, 3)],
            [device(wrap(z + d), x, c, y) for d in (1, 2, 3)],
            [device(z, x, 1 - c, y)],
        ]
        self.copies = []

    def start(self, stage):
        src = self.src if stage == 0 else self.accs.at[stage - 1]
        for d, peer in enumerate(self.peers[stage]):
            at = 3 * stage + d
            copy = remote(src, self.parts.at[at], self.send.at[at], self.recv.at[at], peer)
            copy.start()
            self.copies.append(copy)

    def finish(self, stage):
        src = self.src if stage == 0 else self.accs.at[stage - 1]
        total = src[...]
        for d in range(len(self.peers[stage])):
            self.copies[3 * stage + d].wait_recv()
            total = total + self.parts[3 * stage + d]
        self.accs[stage] = total

    def close(self):
        for copy in self.copies:
            copy.wait_send()


TALLY_PEERS = 7


def tally_scratch(shape):
    return [
        VMEM((3,) + shape, F32),
        VMEM((7,) + shape, F32),
        DMA((7,)),
        DMA((7,)),
    ]


def torus(z, x, c, y, z_last=False):
    turn = 0 if z_last else c

    def first(d):
        return device(wrap(z + turn * d), wrap(x + (1 - turn) * d), c, y)

    def second(d):
        return device(wrap(z + (1 - turn) * d), wrap(x + turn * d), c, y)

    at_first = x * (1 - turn) + z * turn
    at_second = z * (1 - turn) + x * turn

    def block(d1, d2):
        a1, a2 = wrap(at_first + d1), wrap(at_second + d2)
        return (1 - turn) * (a2 * 4 + a1) + turn * (a1 * 4 + a2)

    return first, second, block


def half_mask(half):
    lane = lax.broadcasted_iota(jnp.int32, (1, 128), 1)
    return (lane < 64) if half == 0 else (lane >= 64)


def key_place(h):
    return h // 2, h % 2


def value_place(h):
    return (HEADS + h) // 2, (HEADS + h) % 2


def pad_head(wide, at, half):
    group = wide[:, 128 * at : 128 * at + 128]
    return jnp.where(half_mask(half), group, jnp.zeros_like(group))


LOW_ROWS = 48


def lane_halves(c):
    ours = pl.ds(pl.multiple_of(640 * c, 128), 640)
    theirs = pl.ds(pl.multiple_of(640 * (1 - c), 128), 640)
    return ours, theirs


def lane_slab(ref, lanes):
    return lambda at: ref.at[:, pl.ds(pl.multiple_of(80 * at, 16), 80), lanes]


def lane_part(ref, lanes):
    def part(at, way):
        if way > 0:
            rows = pl.ds(pl.multiple_of(80 * at, 16), LOW_ROWS)
        else:
            rows = pl.ds(pl.multiple_of(80 * at + LOW_ROWS, 16), 80 - LOW_ROWS)
        return ref.at[:, rows, lanes]

    return part


def join_cores(c, shard, shard_sib, own_block, ours):
    for j in range(own_block.shape[0]):
        near = shard[j, :, ours].astype(F32)
        far = shard_sib[j].astype(F32)
        upper = jnp.where(c == 0, near, far)
        lower = jnp.where(c == 0, far, near)
        own_block[j] = jnp.concatenate([upper, lower], axis=0).astype(BF16)


class Ring:
    def __init__(self, own, slab, part, send, recv, h_send, h_recv, z_last=False):
        z, x, c, y = spot()
        self.first, self.second, self.block = torus(z, x, c, y, z_last)
        self.sibling = device(z, x, 1 - c, y)
        self.own, self.slab, self.part = own, slab, part
        self.send, self.recv, self.h_send, self.h_recv = send, recv, h_send, h_recv

    def ship(self, src, dst, at, to):
        return remote(src, dst, self.send.at[at], self.recv.at[at], to)

    def one(self, way):
        at = self.block(0, 0)
        return self.ship(self.own, self.slab(at), 0 if way > 0 else 1, self.first(way))

    def one_on(self, way):
        piece = self.part(self.block(-way, 0), way)
        return self.ship(piece, piece, 2 if way > 0 else 3, self.first(way))

    def two(self, d1, way):
        at = self.block(d1, 0)
        src = self.own if d1 == 0 else self.slab(at)
        return self.ship(src, self.slab(at), 4 + 4 * d1 + (0 if way > 0 else 1), self.second(way))

    def two_on(self, d1, way):
        piece = self.part(self.block(d1, -way), way)
        return self.ship(piece, piece, 6 + 4 * d1 + (0 if way > 0 else 1), self.second(way))

    def hand(self, d1, d2):
        at = self.block(d1, d2)
        src = self.own if d1 == 0 and d2 == 0 else self.slab(at)
        k = 4 * d1 + d2
        return remote(src, self.slab(at), self.h_send.at[k], self.h_recv.at[k], self.sibling)

    def open(self):
        self.one(1).start()
        self.one(-1).start()
        self.spread(0)

    def spread(self, d1):
        self.two(d1, 1).start()
        self.two(d1, -1).start()
        self.hand(d1, 0).start()

    def near(self):
        self.one(1).wait_recv()
        self.one_on(1).start()
        self.spread(3)
        self.one(-1).wait_recv()
        self.one_on(-1).start()
        self.spread(1)

    def far(self):
        self.one_on(1).wait_recv()
        self.one_on(-1).wait_recv()
        self.spread(2)

    def turn(self, d1):
        self.two(d1, 1).wait_recv()
        self.two_on(d1, 1).start()
        self.hand(d1, 3).start()
        self.two(d1, -1).wait_recv()
        self.two_on(d1, -1).start()
        self.hand(d1, 1).start()

    def end(self, d1):
        self.two_on(d1, 1).wait_recv()
        self.two_on(d1, -1).wait_recv()
        self.hand(d1, 2).start()

    def arrive(self):
        for d1 in range(4):
            for d2 in range(4):
                self.hand(d1, d2).wait_recv()

    def close(self):
        for way in (1, -1):
            self.one(way).wait_send()
            self.one_on(way).wait_send()
            for d1 in range(4):
                self.two(d1, way).wait_send()
                self.two_on(d1, way).wait_send()
        for d1 in range(4):
            for d2 in range(4):
                self.hand(d1, d2).wait_send()

    def steps(self):
        return [
            self.near,
            lambda: self.turn(0),
            self.far,
            lambda: self.turn(3),
            lambda: self.turn(1),
            lambda: self.end(0),
            lambda: self.turn(2),
            lambda: self.end(3),
            lambda: self.end(1),
            lambda: self.end(2),
        ]


def ring_scratch():
    return [DMA((20,)), DMA((20,)), DMA((16,)), DMA((16,))]


def rope_wide(cos_block, sin_block, turn):
    place = lax.axis_index("row")
    cos_at = turn[place, 0:1, :]
    sin_at = turn[place, 1:2, :]
    cosine = cos_block[...] * cos_at - sin_block[...] * sin_at
    sine = sin_block[...] * cos_at + cos_block[...] * sin_at
    lane = lax.broadcasted_iota(jnp.int32, sine.shape, 1)
    return cosine, jnp.where(lax.rem(lane, 64) < 32, -sine, sine)


def swap_halves(v):
    lane = lax.broadcasted_iota(jnp.int32, v.shape, 1)
    return jnp.where(lax.rem(lane, 64) < 32, pltpu.roll(v, 96, 1), pltpu.roll(v, 32, 1))


def over_heads(v):
    low = half_mask(0)
    left = jnp.sum(jnp.where(low, v, 0.0), axis=1, keepdims=True)
    right = jnp.sum(jnp.where(low, 0.0, v), axis=1, keepdims=True)
    return jnp.where(low, left, right)


def head_norm(raw, cosine, sine):
    scale = lax.rsqrt(over_heads(raw * raw) + EPS)
    return (raw * cosine + swap_halves(raw) * sine) * scale, scale


def front_kernel(
    hid,
    tea,
    query_w,
    key_w,
    value_w,
    out_w,
    gate_w,
    up_w,
    down_w,
    rate_one,
    rate_two,
    valid,
    seg,
    score_gain,
    cos_block,
    sin_block,
    turn,
    hid_out,
    hid_tok,
    tea_tok,
    rates_out,
    count_out,
    mask_out,
    gains_out,
    weights,
    w_rest,
    raw_out,
    q_pad,
    win_out,
    att,
    out_t,
    lse,
    starts_out,
    hid_t,
    hid_n,
    tea_t,
    rates,
    count,
    count_rows,
    rate_buf,
    shard,
    shard_sib,
    own_block,
    shard_b,
    shard_b_sib,
    own_b,
    w_first,
    win,
    transit,
    o_acc,
    l_acc,
    y_send,
    y_recv,
    s_send,
    s_recv,
    local_sem,
    k_send,
    k_recv,
    a_send,
    a_recv,
    a_hsend,
    a_hrecv,
    b_send,
    b_recv,
    b_hsend,
    b_hrecv,
    c_send,
    c_recv,
    c_hsend,
    c_hrecv,
    t_accs,
    t_parts,
    t_send,
    t_recv,
):
    z, x, c, y = spot()
    place = 2 * x + c
    sibling = device(z, x, 1 - c, y)
    across = [device(z, x, c, wrap(y + d)) for d in (1, 2, 3)]
    tally = Tally(count, t_accs, t_parts, t_send, t_recv)

    shard[0] = jnp.concatenate(
        [query_w[:, 256:], out_w[...], query_w[:, :256], key_w[...], value_w[...]], axis=1
    )
    shard_b[0] = gate_w[...]
    shard_b[1] = up_w[...]
    shard_b[2] = down_w[...]
    rates[0:1, :] = rate_one[...].reshape(1, COLS)
    rates[1:2, :] = rate_two[...].reshape(1, COLS)
    token_mask = valid[...].reshape(1, ROWS).astype(F32)
    count[...] = jnp.broadcast_to(jnp.sum(token_mask, axis=1, keepdims=True), (8, 128))
    meet(across + tally.peers[0] + tally.peers[1] + tally.peers[2])

    ours, theirs = lane_halves(c)
    ring_a = Ring(own_block, lane_slab(w_first, ours), lane_part(w_first, ours), a_send, a_recv, a_hsend, a_hrecv)
    w_pair, w_last = w_rest.at[pl.ds(0, 2)], w_rest.at[pl.ds(2, 1)]
    ring_b = Ring(
        own_b.at[pl.ds(0, 2)],
        lane_slab(w_pair, ours),
        lane_part(w_pair, ours),
        b_send,
        b_recv,
        b_hsend,
        b_hrecv,
        True,
    )
    ring_c = Ring(
        own_b.at[pl.ds(2, 1)],
        lane_slab(w_last, ours),
        lane_part(w_last, ours),
        c_send,
        c_recv,
        c_hsend,
        c_hrecv,
    )
    head = remote(shard.at[:, :, theirs], shard_sib, s_send.at[0], s_recv.at[0], sibling)
    head.start()
    head_b = remote(shard_b.at[:, :, theirs], shard_b_sib, s_send.at[1], s_recv.at[1], sibling)
    head_b.start()
    my_feats = pl.ds(pl.multiple_of(COLS * y, 64), COLS)
    hid_r = remote(hid, hid_t.at[my_feats], y_send.at[0], y_recv.at[0], across[0])
    hid_l = remote(hid, hid_t.at[my_feats], y_send.at[1], y_recv.at[1], across[2])
    hid_r.start()
    hid_l.start()
    hid_own = pltpu.make_async_copy(hid, hid_t.at[my_feats], local_sem.at[0])
    hid_own.start()
    tea_own = pltpu.make_async_copy(
        tea.at[:, pl.ds(pl.multiple_of(TOK * y, TOK), TOK)], tea_t.at[my_feats], local_sem.at[1]
    )
    tea_own.start()

    head.wait()
    join_cores(c, shard, shard_sib, own_block, ours)
    ring_a.open()
    own_at = ring_a.block(0, 0)
    own_a = pltpu.make_async_copy(own_block, ring_a.slab(own_at), local_sem.at[2])
    own_a.start()
    tally.start(0)
    small = []
    for d in (1, 2, 3):
        rows = pl.ds(pl.multiple_of(TOK * wrap(y + d), TOK), TOK)
        pieces = ((tea.at[:, rows], tea_t.at[my_feats]), (rates, rate_buf.at[y]))
        for k, (src, dst) in enumerate(pieces):
            at = 4 + 2 * (d - 1) + k
            copy = remote(src, dst, y_send.at[at], y_recv.at[at], across[d - 1])
            copy.start()
            small.append(copy)
    rate_buf[y] = rates[...]
    gains = jnp.concatenate([score_gain[...].reshape(1, COLS), jnp.zeros((1, 64), F32)], axis=1)
    gains_out[...] = gains
    token = pl.ds(pl.multiple_of(TOK * y, TOK), TOK)
    count_rows[0:1, :] = token_mask
    mask_out[...] = jnp.broadcast_to(count_rows[0:1, token], (TOK, TOK)).T

    first = jnp.sum((seg[...] < 1).astype(jnp.int32), axis=1, keepdims=True)
    second = jnp.sum((seg[...] < 2).astype(jnp.int32), axis=1, keepdims=True)
    query_seg = seg[:, pl.ds(pl.multiple_of(ROWS * place, ROWS), ROWS)]
    starts = jnp.where(query_seg == 0, 0, jnp.where(query_seg == 1, first, second))
    starts_out[...] = starts - (place - 4) * ROWS
    o_acc[...] = jnp.zeros_like(o_acc)
    l_acc[...] = jnp.zeros_like(l_acc)

    ring_a.near()
    head_b.wait()
    join_cores(c, shard_b, shard_b_sib, own_b, ours)
    own_rest = pltpu.make_async_copy(own_b, lane_slab(w_rest, ours)(ring_b.block(0, 0)), local_sem.at[3])
    own_rest.start()
    ring_a.turn(0)
    ring_a.far()
    ring_b.open()
    ring_c.open()
    hid_r.wait_recv()
    hid_f_ref = hid_t.at[pl.ds(pl.multiple_of(COLS * wrap(y - 1), 64), 160)]
    hid_f = remote(hid_f_ref, hid_f_ref, y_send.at[2], y_recv.at[2], across[0])
    hid_f.start()
    hid_l.wait_recv()
    hid_g_ref = hid_t.at[pl.ds(pl.multiple_of(COLS * wrap(y + 1) + 160, 32), 160)]
    hid_g = remote(hid_g_ref, hid_g_ref, y_send.at[3], y_recv.at[3], across[2])
    hid_g.start()
    ring_a.turn(3)
    ring_a.turn(1)
    tally.finish(0)
    tally.start(1)
    ring_a.end(0)
    ring_a.turn(2)
    ring_a.end(3)
    ring_a.end(1)
    ring_a.end(2)
    tally.finish(1)
    tally.start(2)
    hid_own.wait()
    hid_f.wait_recv()
    hid_g.wait_recv()
    hid_save = pltpu.make_async_copy(hid_t, hid_out, local_sem.at[4])
    hid_save.start()
    for g in range(10):
        hid_n[:, 128 * g : 128 * g + 128] = hid_t[128 * g : 128 * g + 128, :].T
    own_a.wait()
    ring_a.arrive()
    ring_b.near()
    ring_c.near()
    w_save = pltpu.make_async_copy(w_first.at[0], weights, local_sem.at[5])
    w_save.start()

    cosine, sine = rope_wide(cos_block, sin_block, turn)
    raw = dot_nn(hid_n[...], w_first[0, :, 640:1280])
    for g in range(3):
        group = raw[:, 128 * g : 128 * g + 128]
        raw_out[3 + g] = group
        normed, _ = head_norm(group, cosine, sine)
        keys = normed * gains[:, 128 * g : 128 * g + 128]
        if g == 2:
            keys = jnp.where(half_mask(0), keys, group)
        win[4 * ROWS :, 128 * g : 128 * g + 128] = keys.astype(BF16)
    win[4 * ROWS :, 384:640] = raw[:, 384:640].astype(BF16)

    def slot(s):
        return win.at[pl.ds(pl.multiple_of(ROWS * s, ROWS), ROWS)]

    one = remote(slot(4), slot(2), k_send.at[0], k_recv.at[0], device(z, wrap(x + 1), c, y))
    up = remote(
        win.at[pl.ds(2 * ROWS, UP)],
        win.at[pl.ds(0, UP)],
        k_send.at[1],
        k_recv.at[1],
        device(z, wrap(x + 1), c, y),
    )
    down = remote(
        win.at[pl.ds(4 * ROWS + UP, ROWS - UP)],
        transit,
        k_send.at[5],
        k_recv.at[5],
        device(z, wrap(x - 1), c, y),
    )
    down_on = remote(
        transit,
        win.at[pl.ds(UP, ROWS - UP)],
        k_send.at[6],
        k_recv.at[6],
        device(z, wrap(x - 1), c, y),
    )
    own = remote(slot(4), slot(3), k_send.at[2], k_recv.at[2], sibling)
    one_on = remote(slot(2), slot(1 + 2 * c), k_send.at[3], k_recv.at[3], sibling)
    two_on = remote(slot(0), slot(1), k_send.at[4], k_recv.at[4], sibling)

    @pl.when(x < 3)
    def _():
        one.start()

    @pl.when(x < 2)
    def _():
        down.start()

    @pl.when(c == 0)
    def _():
        own.start()

    root = math.sqrt(HEAD_DIM)
    for g, at in enumerate((384, 512, 0)):
        group = dot_nn(hid_n[...], w_first[0, :, at : at + 128])
        raw_out[g] = group
        normed, _ = head_norm(group, cosine, sine)
        scaled = (normed * gains[:, 128 * g : 128 * g + 128]).astype(BF16) * jnp.asarray(root, BF16)
        for half in range(2 if g < 2 else 1):
            q_pad[2 * g + half] = jnp.where(half_mask(half), scaled, jnp.zeros_like(scaled))
    hid_tok[...] = hid_n[pl.ds(pl.multiple_of(TOK * y, TOK), TOK), :]

    ring_b.turn(0)
    ring_b.far()
    ring_c.turn(0)
    ring_c.far()
    events = list(zip(ring_b.steps()[3:], ring_c.steps()[3:]))

    def tile(t):
        rows = pl.ds(pl.multiple_of(t * TILE, TILE), TILE)
        key_at = t * TILE + lax.broadcasted_iota(jnp.int32, (TILE, ROWS), 0)
        query_at = 4 * ROWS + lax.broadcasted_iota(jnp.int32, (TILE, ROWS), 1)
        allowed = (key_at >= starts_out[...]) & (key_at <= query_at)
        for h in range(HEADS):
            kg, _ = key_place(h)
            vg, vh = value_place(h)
            keys = win[rows, 128 * kg : 128 * kg + 128]
            values = win[rows, 128 * vg : 128 * vg + 128]
            scores = dot_nt(keys, q_pad[h])
            probs = jnp.where(allowed, jnp.exp(scores), 0.0)
            l_acc[h] += jnp.sum(probs.reshape(TILE // 8, 8, ROWS), axis=0)
            both = dot_tn(values, probs.astype(BF16))
            o_acc[h] += both[64 * vh : 64 * vh + 64, :]

    def step(i, carry):
        k = lax.div(i, 2)
        turned = k - 1 + 2 * lax.rem(k, 2)
        s = jnp.where(k == 0, 4, jnp.where(c == 1, 4 - k, 4 - turned))

        @pl.when((i == 2) & (c == 1))
        def _():
            own.wait_recv()

        @pl.when((x > 0) & (((i == 4) & (c == 1)) | ((i == 2) & (c == 0))))
        def _():
            one.wait_recv()
            one_on.start()

            @pl.when(x < 3)
            def _():
                up.start()

        @pl.when((i == 3) & ((x == 0) | (x == 3)))
        def _():
            down.wait_recv()
            down_on.start()

        @pl.when((x > 0) & (((i == 6) & (c == 1)) | ((i == 4) & (c == 0))))
        def _():
            one_on.wait_recv()

        @pl.when((x > 1) & (((i == 8) & (c == 1)) | ((i == 6) & (c == 0))))
        def _():
            up.wait_recv()
            down_on.wait_recv()

            @pl.when(c == 1)
            def _():
                two_on.start()

        @pl.when((x > 1) & (i == 8) & (c == 0))
        def _():
            two_on.wait_recv()

        for n, event in enumerate(events):

            @pl.when(i == n + 2)
            def _(event=event):
                event[0]()
                event[1]()

        @pl.when(place + s >= 4)
        def _():
            tile(2 * s + lax.rem(i, 2))

        return carry

    lax.fori_loop(0, 10, step, 0)
    win_save = pltpu.make_async_copy(win, win_out, local_sem.at[6])
    win_save.start()
    for copy in small:
        copy.wait_recv()
    tea_own.wait()
    for g in range(10):
        tea_tok[:, 128 * g : 128 * g + 128] = tea_t[128 * g : 128 * g + 128, :].T
    rates_out[...] = jnp.concatenate([rate_buf[k] for k in range(4)], axis=1)
    tally.finish(2)
    count_out[...] = t_accs[2]
    for h in range(HEADS):
        total = jnp.sum(l_acc[h], axis=0, keepdims=True)
        lse[h] = jnp.broadcast_to(jnp.log(total), (8, ROWS))
        out_t[64 * h : 64 * h + 64, :] = o_acc[h] / total
    wide = jnp.concatenate([jnp.zeros((64, ROWS), F32), out_t[...]], axis=0)
    att[...] = wide.T.astype(BF16)
    ring_b.arrive()
    ring_c.arrive()
    own_rest.wait()
    ring_a.close()
    ring_b.close()
    ring_c.close()
    hid_save.wait()
    w_save.wait()
    win_save.wait()
    for copy in small + [hid_r, hid_l, hid_f, hid_g]:
        copy.wait_send()

    @pl.when(x < 3)
    def _():
        one.wait_send()

    @pl.when(x < 2)
    def _():
        down.wait_send()

    @pl.when((x == 0) | (x == 3))
    def _():
        down_on.wait_send()

    @pl.when((x == 1) | (x == 2))
    def _():
        up.wait_send()

    @pl.when(c == 0)
    def _():
        own.wait_send()

    @pl.when(x > 0)
    def _():
        one_on.wait_send()

    @pl.when((x > 1) & (c == 1))
    def _():
        two_on.wait_send()

    tally.close()


def rope_constants():
    inverse = np.exp(np.arange(32) * (-2.0 * math.log(10000.0) / HEAD_DIM))
    inverse = np.tile(inverse, 4)
    inside = np.arange(ROWS)[:, None] * inverse[None, :]
    at = (ROWS * np.arange(8))[:, None] * inverse[None, :]
    turn = np.stack([np.cos(at), np.sin(at)], axis=1)
    return [jnp.asarray(v, F32) for v in (np.cos(inside), np.sin(inside), turn)]


def front(hidden, teacher, others):
    sds = jax.ShapeDtypeStruct
    outs = [
        (sds((D, ROWS), BF16), IN_PLACE),
        (sds((TOK, D), BF16), IN_VMEM),
        (sds((TOK, D), BF16), IN_VMEM),
        (sds((2, D), F32), IN_VMEM),
        (sds((8, 128), F32), IN_VMEM),
        (sds((TOK, TOK), F32), IN_VMEM),
        (sds((1, 384), F32), IN_VMEM),
        (sds((D, D), BF16), IN_PLACE),
        (sds((3, D, D), BF16), IN_PLACE),
        (sds((6, ROWS, 128), F32), IN_VMEM),
        (sds((HEADS, ROWS, 128), BF16), IN_VMEM),
        (sds((5 * ROWS, 2 * COLS), BF16), IN_PLACE),
        (sds((ROWS, 384), BF16), IN_VMEM),
        (sds((COLS, ROWS), F32), IN_VMEM),
        (sds((HEADS, 8, ROWS), F32), IN_VMEM),
        (sds((1, ROWS), jnp.int32), IN_VMEM),
    ]
    return pl.pallas_call(
        front_kernel,
        out_shape=tuple(o[0] for o in outs),
        in_specs=[IN_PLACE] * 2 + [IN_VMEM] * len(others),
        out_specs=tuple(o[1] for o in outs),
        scratch_shapes=[
            VMEM((D, ROWS), BF16),
            VMEM((ROWS, D), BF16),
            VMEM((D, TOK), BF16),
            VMEM((2, COLS), F32),
            VMEM((8, 128), F32),
            VMEM((8, ROWS), F32),
            VMEM((4, 2, COLS), F32),
            VMEM((1, 40, D), BF16),
            VMEM((1, 40, 640), BF16),
            VMEM((1, 80, 640), BF16),
            VMEM((3, 40, D), BF16),
            VMEM((3, 40, 640), BF16),
            VMEM((3, 80, 640), BF16),
            VMEM((1, D, D), BF16),
            VMEM((5 * ROWS, 2 * COLS), BF16),
            VMEM((ROWS - UP, 2 * COLS), BF16),
            VMEM((HEADS, 64, ROWS), F32),
            VMEM((HEADS, 8, ROWS), F32),
            DMA((10,)),
            DMA((10,)),
            DMA((2,)),
            DMA((2,)),
            DMA((7,)),
            DMA((7,)),
            DMA((7,)),
        ]
        + ring_scratch()
        + ring_scratch()
        + ring_scratch()
        + tally_scratch((8, 128)),
        compiler_params=params(0),
        name="front",
    )(hidden, teacher, *others)


class Spread:
    def __init__(self, ref, send, recv):
        z, x, c, y = spot()
        self.ref, self.send, self.recv, self.y = ref, send, recv, y
        self.to = {way: device(z, x, c, wrap(y + way)) for way in (1, -1)}

    def full(self, way):
        rows = pl.ds(pl.multiple_of(TOK * self.y, TOK), TOK)
        k = 0 if way > 0 else 1
        return remote(self.ref.at[rows], self.ref.at[rows], self.send.at[k], self.recv.at[k], self.to[way])

    def relay(self, way):
        half = TOK // 2
        at = TOK * wrap(self.y - way) + (0 if way > 0 else half)
        rows = pl.ds(pl.multiple_of(at, half), half)
        k = 2 if way > 0 else 3
        return remote(self.ref.at[rows], self.ref.at[rows], self.send.at[k], self.recv.at[k], self.to[way])

    def start(self):
        self.full(1).start()
        self.full(-1).start()

    def sides(self):
        self.full(1).wait_recv()
        self.relay(1).start()
        self.full(-1).wait_recv()
        self.relay(-1).start()

    def opposite(self):
        self.relay(1).wait_recv()
        self.relay(-1).wait_recv()

    def close(self):
        for way in (1, -1):
            self.full(way).wait_send()
            self.relay(way).wait_send()


HALF = TOK // 2
OWN, LEFT, RIGHT, OPPOSITE = range(4)


def position(slot, h):
    if slot == OWN:
        at = HALF * h
    elif slot == OPPOSITE:
        at = 6 * HALF + HALF * h
    else:
        at = 2 * HALF * (1 + h) + (HALF if slot == RIGHT else 0)
    return at if isinstance(h, int) else pl.multiple_of(at, HALF)


class Halves:
    def __init__(self, ref, send, recv):
        z, x, c, y = spot()
        self.ref, self.send, self.recv = ref, send, recv
        self.to = {way: device(z, x, c, wrap(y + way)) for way in (1, -1)}

    def full(self, h, way):
        src = self.ref.at[pl.ds(position(OWN, h), HALF)]
        dst = self.ref.at[pl.ds(position(LEFT if way > 0 else RIGHT, h), HALF)]
        k = 0 if way > 0 else 1
        return remote(src, dst, self.send.at[h, k], self.recv.at[h, k], self.to[way])

    def relay(self, h, way):
        part = HALF // 2
        off = 0 if way > 0 else part
        src = pl.multiple_of(position(LEFT if way > 0 else RIGHT, h) + off, part)
        dst = pl.multiple_of(position(OPPOSITE, h) + off, part)
        k = 2 if way > 0 else 3
        return remote(
            self.ref.at[pl.ds(src, part)],
            self.ref.at[pl.ds(dst, part)],
            self.send.at[h, k],
            self.recv.at[h, k],
            self.to[way],
        )

    def start(self, h):
        self.full(h, 1).start()
        self.full(h, -1).start()

    def sides(self, h):
        self.full(h, 1).wait_recv()
        self.relay(h, 1).start()
        self.full(h, -1).wait_recv()
        self.relay(h, -1).start()

    def opposite(self, h):
        self.relay(h, 1).wait_recv()
        self.relay(h, -1).wait_recv()

    def close(self):
        for h in range(2):
            for way in (1, -1):
                self.full(h, way).wait_send()
                self.relay(h, way).wait_send()


def mix_forward(states, branch, alphas):
    branch_scale = lax.rsqrt(jnp.sum(branch * branch, axis=1, keepdims=True) + EPS)
    normed = branch * branch_scale
    mixed = states + alphas * (normed - states)
    mixed_scale = lax.rsqrt(jnp.sum(mixed * mixed, axis=1, keepdims=True) + EPS)
    return mixed * mixed_scale, normed, branch_scale, mixed_scale


def mix_backward(gradient, states, normed, branch_scale, mixed_out, mixed_scale, alphas):
    along = jnp.sum(mixed_out * gradient, axis=1, keepdims=True)
    mixed_grad = mixed_scale * (gradient - mixed_out * along)
    normed_grad = alphas * mixed_grad
    toward = jnp.sum(normed * normed_grad, axis=1, keepdims=True)
    branch_grad = branch_scale * (normed_grad - normed * toward)
    rate_grad = jnp.sum(mixed_grad * (normed - states), axis=0, keepdims=True)
    return (1.0 - alphas) * mixed_grad, branch_grad, rate_grad


def swiglu_parts(gate_raw, up_raw, gate_gain, up_gain):
    root = math.sqrt(D)
    g = gate_gain * gate_raw * root
    q = jax.nn.sigmoid(g)
    return g, q


def middle_kernel(
    att,
    hid_tok,
    tea,
    mask,
    count,
    rates,
    up_gain_in,
    gate_gain_in,
    weights,
    w_rest,
    output,
    attn_low,
    res_zero,
    small,
    gate_out,
    up_out,
    down_out,
    in_one,
    product,
    mlp_grad,
    gate_low,
    up_low,
    w_out,
    w_all,
    grads,
    raw_gate,
    raw_up,
    send_buf,
    got_buf,
    own_part,
    out_buf,
    state,
    normed,
    scales,
    turned,
    w_sem,
    g_sem,
    ag_send,
    ag_recv,
    rs_send,
    rs_recv,
    o_send,
    o_recv,
):
    z, x, c, y = spot()
    peers = [device(z, x, c, wrap(y + d)) for d in range(4)]
    load = pltpu.make_async_copy(weights.at[:, pl.ds(0, 384)], w_out, w_sem.at[0])
    load.start()
    load_rest = pltpu.make_async_copy(w_rest, w_all, w_sem.at[1])
    load_rest.start()
    up_gain = up_gain_in[...].reshape(1, D)
    gate_gain = gate_gain_in[...].reshape(1, D)
    w_gate, w_up, w_down = (w_all.at[k] for k in range(3))
    meet(peers[1:])
    places = {LEFT: 3, RIGHT: 1, OPPOSITE: 2}

    def rows_of(off):
        return pl.ds(pl.multiple_of(TOK * wrap(y + off), TOK), TOK)

    def feats(k):
        return pl.ds(pl.multiple_of(COLS * k, 64), COLS)

    def half_rows(h):
        return pl.ds(pl.multiple_of(HALF * h, HALF), HALF)

    def scatter(stage, h, slot):
        return remote(
            send_buf.at[stage, h, slot - 1],
            got_buf.at[stage, h, slot - 1],
            rs_send.at[stage, h, slot],
            rs_recv.at[stage, h, slot],
            device(z, x, c, wrap(y + places[slot])),
        )

    def give(stage, h, slot, part):
        send_buf[stage, h, slot - 1] = part.astype(BF16)
        scatter(stage, h, slot).start()

    def collect(stage, h):
        total = own_part[half_rows(h), :]
        for slot in (LEFT, RIGHT, OPPOSITE):
            scatter(stage, h, slot).wait_recv()
            total = total + got_buf[stage, h, slot - 1].astype(F32)
        return total

    def both(body):
        def step(h, carry):
            body(h)
            return carry

        lax.fori_loop(0, 2, step, 0)

    def flow(stage, spread, compute):
        def step(i, carry):
            @pl.when(i == 1)
            def _():
                spread.sides(0)

            part = compute(pl.ds(pl.multiple_of(TOK * i, TOK), TOK))

            @pl.when(i == 0)
            def _():
                own_part[...] = part

            @pl.when(i > 0)
            def _():
                h = i - 1
                give(stage, h, LEFT, part[:HALF])
                give(stage, h, RIGHT, part[HALF:])

                @pl.when(i == 1)
                def _():
                    spread.sides(1)

                spread.opposite(h)
                give(stage, h, OPPOSITE, compute(pl.ds(position(OPPOSITE, h), HALF)))

            return carry

        lax.fori_loop(0, 3, step, 0)

    ones = Halves(in_one, ag_send.at[0], ag_recv.at[0])
    backs = Halves(mlp_grad, ag_send.at[1], ag_recv.at[1])

    load.wait()
    for slot in (OPPOSITE, LEFT, RIGHT):
        part = dot_nt(att[rows_of(places[slot]), :], w_out[...])
        give(0, 0, slot, part[:HALF])
        send_buf[0, 1, slot - 1] = part[HALF:].astype(BF16)
    for slot in (OPPOSITE, LEFT, RIGHT):
        scatter(0, 1, slot).start()
    own_part[...] = dot_nt(att[rows_of(0), :], w_out[...])
    small[...] = jnp.zeros_like(small)

    def first_mix(h):
        rows = half_rows(h)
        attn = collect(0, h)
        states = hid_tok[rows, :].astype(F32)
        one, normed_one, branch_one, scale_one = mix_forward(states, attn, rates[0:1, :])
        in_one[rows, :] = one.astype(BF16)
        ones.start(h)
        state[0, rows, :] = one
        normed[rows, :] = normed_one
        scales[0, rows, :] = jnp.broadcast_to(branch_one, (HALF, 128))
        scales[1, rows, :] = jnp.broadcast_to(scale_one, (HALF, 128))

    both(first_mix)
    load_rest.wait()

    def feed(rows):
        block = in_one[rows, :]
        gate_raw = dot_nn(block, w_gate[...])
        raw_gate[rows, :] = gate_raw
        up_raw = dot_nn(block, w_up[...])
        raw_up[rows, :] = up_raw
        g, q = swiglu_parts(gate_raw, up_raw, gate_gain, up_gain)
        low = (up_gain * up_raw * (g * q)).astype(BF16)
        product[rows, :] = low
        return dot_nt(low, w_down[...])

    flow(1, ones, feed)
    factor = 16384 * math.sqrt(D) / count[0:1, 0:1]

    def second_mix(h):
        rows = half_rows(h)
        mlp = collect(1, h)
        one = state[0, rows, :]
        two, normed_two, branch_two, scale_two = mix_forward(one, mlp, rates[1:2, :])
        errors = two - tea[rows, :].astype(F32)
        weight = mask[rows, 0:1]
        seed = factor * (weight * errors)
        res_one, mlp_back, rate_two = mix_backward(
            seed, one, normed_two, branch_two, two, scale_two, rates[1:2, :]
        )
        mlp_grad[rows, :] = mlp_back.astype(BF16)
        backs.start(h)
        state[1, rows, :] = res_one
        turned[rows, :] = two
        small[1:2, :] += rate_two
        loss = jnp.sum(jnp.sum(weight * errors * errors, axis=1, keepdims=True), axis=0, keepdims=True)
        small[4:5, :] += jnp.broadcast_to(loss, (1, D))

    both(second_mix)
    for g in range(10):
        lanes = slice(128 * g, 128 * g + 128)
        out_buf[lanes, :] = turned[:, lanes].T.astype(BF16)
    out_copies = []
    for k in (1, 2, 3):
        copy = remote(
            out_buf.at[feats(wrap(y + k))],
            output.at[:, rows_of(0)],
            o_send.at[k],
            o_recv.at[k],
            device(z, x, c, wrap(y + k)),
        )
        copy.start()
        out_copies.append(copy)
    output[:, rows_of(0)] = out_buf[feats(y), :]

    def unfeed(rows):
        grad = dot_nn(mlp_grad[rows, :], w_down[...])
        gate_raw = raw_gate[rows, :]
        up_raw = raw_up[rows, :]
        g, q = swiglu_parts(gate_raw, up_raw, gate_gain, up_gain)
        silu = g * q
        up_term = grad * silu
        slope = grad * up_gain * up_raw * (q * (1.0 + g * (1.0 - q))) * math.sqrt(D)
        small[2:3, :] += jnp.sum(up_term * up_raw, axis=0, keepdims=True)
        small[3:4, :] += jnp.sum(slope * gate_raw, axis=0, keepdims=True)
        up_back = (up_term * up_gain).astype(BF16)
        gate_back = (slope * gate_gain).astype(BF16)
        up_low[rows, :] = up_back
        gate_low[rows, :] = gate_back
        return dot_nt(gate_back, w_gate[...]) + dot_nt(up_back, w_up[...])

    flow(2, backs, unfeed)

    def weight_grad(j, left, right, out):
        def step(k, carry):
            rows = pl.ds(pl.multiple_of(256 * k, 256), 256)
            grads[j, rows, :] = dot_tn(left[:, rows], right[...]).astype(BF16)
            return carry

        lax.fori_loop(0, 5, step, 0)
        pltpu.make_async_copy(grads.at[j], out, g_sem.at[j]).start()

    weight_grad(2, mlp_grad, product, down_out)
    weight_grad(0, in_one, gate_low, gate_out)
    weight_grad(1, in_one, up_low, up_out)

    def third_mix(h):
        rows = half_rows(h)
        grad_one = state[1, rows, :] + collect(2, h)
        res, attn_back, rate_one = mix_backward(
            grad_one,
            hid_tok[rows, :].astype(F32),
            normed[rows, :],
            scales[0, rows, 0:1],
            state[0, rows, :],
            scales[1, rows, 0:1],
            rates[0:1, :],
        )
        attn_low[rows, :] = attn_back.astype(BF16)
        small[0:1, :] += rate_one
        turned[rows, :] = res

    both(third_mix)
    for g in range(10):
        lanes = slice(128 * g, 128 * g + 128)
        res_zero[lanes, :] = turned[:, lanes].T
    for j, out in enumerate((gate_out, up_out, down_out)):
        pltpu.make_async_copy(grads.at[j], out, g_sem.at[j]).wait()
    for slot in (LEFT, RIGHT, OPPOSITE):
        for stage in range(3):
            for h in range(2):
                scatter(stage, h, slot).wait_send()
    ones.close()
    backs.close()
    for copy in out_copies:
        copy.wait()


def middle(vmem_args, placed_args):
    sds = jax.ShapeDtypeStruct
    wide = VMEM((ROWS, D), BF16)
    square = sds((D, D), BF16)
    return pl.pallas_call(
        middle_kernel,
        out_shape=(
            sds((COLS, ROWS), BF16),
            sds((TOK, D), BF16),
            sds((D, TOK), F32),
            sds((8, D), F32),
            square,
            square,
            square,
        ),
        in_specs=[IN_VMEM] * len(vmem_args) + [IN_PLACE] * len(placed_args),
        out_specs=(IN_VMEM,) * 4 + (IN_PLACE,) * 3,
        scratch_shapes=[
            wide,
            wide,
            wide,
            wide,
            wide,
            VMEM((D, 384), BF16),
            VMEM((3, D, D), BF16),
            VMEM((3, D, D), BF16),
            VMEM((ROWS, D), F32),
            VMEM((ROWS, D), F32),
            VMEM((3, 2, 3, HALF, D), BF16),
            VMEM((3, 2, 3, HALF, D), BF16),
            VMEM((TOK, D), F32),
            VMEM((D, TOK), BF16),
            VMEM((2, TOK, D), F32),
            VMEM((TOK, D), F32),
            VMEM((2, TOK, 128), F32),
            VMEM((TOK, D), F32),
            DMA((2,)),
            DMA((3,)),
            DMA((2, 2, 4)),
            DMA((2, 2, 4)),
            DMA((3, 2, 4)),
            DMA((3, 2, 4)),
            DMA((4,)),
            DMA((4,)),
        ],
        compiler_params=params(1),
        name="middle",
    )(*vmem_args, *placed_args)


class Fold:
    def __init__(self, bufs, sems, z_heavy):
        z, x, c, y = spot()
        self.z, self.x, self.c = z, x, c
        self.z_heavy = z_heavy
        self.first, self.second, _ = torus(z, x, c, y, z_heavy)
        self.at_first = x if z_heavy else x * (1 - c) + z * c
        self.sibling = device(z, x, 1 - c, y)
        self.own, self.sib, self.relays, self.got_two, self.mid, self.got_one, self.fin = bufs
        self.l_sem, self.h_send, self.h_recv, self.b_send, self.b_recv, self.a_send, self.a_recv, self.f_send, self.f_recv = sems
        self.count = self.own.shape[0]
        self.lanes = pl.ds(pl.multiple_of(640 * c, 128), 640)
        self.other = pl.ds(pl.multiple_of(640 * (1 - c), 128), 640)

    def handed(self, j, d, src):
        return remote(src, self.sib.at[j, d], self.h_send.at[j, d], self.h_recv.at[j, d], self.sibling)

    def fetched(self, j, d, src):
        return pltpu.make_async_copy(src, self.own.at[j, d], self.l_sem.at[j, d])

    def open(self, srcs):
        z, x = self.z, self.x
        if self.z_heavy:
            for d in (2, 1, 3, 0):
                for j, src in enumerate(srcs):
                    self.handed(j, d, src.at[wrap(z + d), :, :, self.other]).start()
                    self.fetched(j, d, src.at[wrap(z + d), :, :, self.lanes]).start()
            return

        @pl.when(self.c == 0)
        def _():
            for d in (2, 1, 3, 0):
                for j, src in enumerate(srcs):
                    self.handed(j, d, src.at[:, wrap(x + d), :, self.other]).start()
                    self.fetched(j, d, src.at[wrap(z + d), :, :, self.lanes]).start()

        @pl.when(self.c == 1)
        def _():
            for d in (2, 1, 3, 0):
                for j, src in enumerate(srcs):
                    self.handed(j, d, src.at[wrap(z + d), :, :, self.other]).start()
                    self.fetched(j, d, src.at[:, wrap(x + d), :, self.lanes]).start()

    def pair(self, k):
        way = 1 if k % 2 == 0 else -1
        at = pl.ds(0 if k in (0, 3, 4) else 2, 2)
        if k < 2:
            src, dst = self.own.at[:, 2, at], self.relays.at[:, k]
        else:
            src, dst = self.own.at[:, 1 if way > 0 else 3, at], self.got_two.at[:, k % 2, at]
        return remote(src, dst, self.b_send.at[k], self.b_recv.at[k], self.second(way))

    def last(self, e):
        return remote(
            self.mid.at[:, e - 1], self.got_one.at[:, e - 1], self.a_send.at[e], self.a_recv.at[e], self.first(e)
        )

    def add(self, d):
        for j in range(self.count):
            blank = self.sib.at[j, d]
            self.fetched(j, d, blank).wait()
            self.handed(j, d, blank).wait_recv()

        def each(i, carry):
            j, a = lax.div(i, 4), lax.rem(i, 4)
            total = self.own[j, d, a].astype(F32) + self.sib[j, d, a].astype(F32)
            self.own[j, d, a] = total.astype(BF16)
            return carry

        lax.fori_loop(0, 4 * self.count, each, 0)
        for k in {2: (0, 1), 1: (2,), 3: (3,), 0: ()}[d]:
            self.pair(k).start()

    def relay(self):
        for k, d, off in ((0, 1, 0), (1, 3, 2)):
            self.pair(k).wait_recv()

            def each(i, carry, k=k, d=d, off=off):
                j, a = lax.div(i, 2), lax.rem(i, 2)
                total = self.own[j, d, off + a].astype(F32) + self.relays[j, k, a].astype(F32)
                self.own[j, d, off + a] = total.astype(BF16)
                return carry

            lax.fori_loop(0, 2 * self.count, each, 0)
            self.pair(4 + k).start()

    def whole(self, j, at):
        total = self.own[j, 0, at].astype(F32)
        for k in range(2):
            total = total + self.got_two[j, k, at].astype(F32)
        return total

    def cross(self):
        for k in range(2, 6):
            self.pair(k).wait_recv()
        for e in (2, 1, 3):

            def each(j, carry, e=e):
                self.mid[j, e - 1] = self.whole(j, wrap(self.at_first + e)).astype(BF16)
                return carry

            lax.fori_loop(0, self.count, each, 0)
            self.last(e).start()

    def give(self, out):
        rows = pl.ds(pl.multiple_of(40 * (1 - self.c), 8), 40)
        return remote(self.fin.at[:, rows], out.at[:, :, self.lanes], self.f_send, self.f_recv, self.sibling)

    def finish(self, out):
        for e in (1, 2, 3):
            self.last(e).wait_recv()

        def each(j, carry):
            total = self.whole(j, self.at_first)
            for e in (1, 2, 3):
                total = total + self.got_one[j, e - 1].astype(F32)
            self.fin[j] = total
            return carry

        lax.fori_loop(0, self.count, each, 0)
        self.give(out).start()
        rows = pl.ds(pl.multiple_of(40 * self.c, 8), 40)
        for j in range(self.count):
            out[j, :, self.lanes] = self.fin[j, rows, :]

    def close(self, out):
        self.give(out).wait()
        for k in range(6):
            self.pair(k).wait_send()
        for e in (1, 2, 3):
            self.last(e).wait_send()
        for j in range(self.count):
            for d in range(4):
                self.handed(j, d, self.sib.at[j, d]).wait_send()


def fold_scratch(count):
    block = (80, 640)
    return [
        VMEM((count, 4, 4) + block, BF16),
        VMEM((count, 4, 4) + block, BF16),
        VMEM((count, 2, 2) + block, BF16),
        VMEM((count, 2, 4) + block, BF16),
        VMEM((count, 3) + block, BF16),
        VMEM((count, 3) + block, BF16),
        VMEM((count,) + block, F32),
        DMA((count, 4)),
        DMA((count, 4)),
        DMA((count, 4)),
        DMA((6,)),
        DMA((6,)),
        DMA((4,)),
        DMA((4,)),
        DMA,
        DMA,
    ]


def head_back(grad, raw, gain, cosine, sine):
    normed, scale = head_norm(raw, cosine, sine)
    gain_grad = jnp.sum(grad * normed, axis=0, keepdims=True)
    pulled = grad * gain
    turned = scale * (pulled - normed * over_heads(normed * pulled))
    return turned * cosine + swap_halves(turned * sine), gain_grad


def tail_kernel(
    starts,
    q_pad,
    out_t,
    lse,
    attn_low,
    att,
    gains,
    cos_block,
    sin_block,
    turn,
    res_t,
    small,
    count,
    win_in,
    raw_in,
    hid_in,
    w_in,
    m0,
    m1,
    m2,
    hidden_grad,
    query_g,
    key_g,
    value_g,
    out_g,
    gate_g,
    up_g,
    down_g,
    sums_out,
    win,
    raw,
    hid_t,
    w_first,
    attn,
    d_att,
    d_pad,
    delta,
    q_acc,
    d_win,
    sib_one,
    sib_two,
    one_buf,
    two_buf,
    got_one,
    got_two,
    got_part,
    transit,
    kv_sum,
    pack,
    out_part,
    first_g,
    y_send_buf,
    y_got_buf,
    side_src,
    side_got,
    sums,
    m_out,
    n_out,
    f_out,
    in_sem,
    k_send,
    k_recv,
    y_send,
    y_recv,
    v_send,
    v_recv,
    g_send,
    g_recv,
    *rest,
):
    m_bufs, m_sems, rest = rest[:7], rest[7:16], rest[16:]
    n_bufs, n_sems, rest = rest[:7], rest[7:16], rest[16:]
    f_bufs, f_sems, rest = rest[:7], rest[7:16], rest[16:]
    t_accs, t_parts, t_send, t_recv = rest
    z, x, c, y = spot()
    place = 2 * x + c
    sibling = device(z, x, 1 - c, y)
    across = [device(z, x, c, wrap(y + d)) for d in (1, 2, 3)]
    tally = Tally(sums, t_accs, t_parts, t_send, t_recv)

    def slot(ref, s):
        return ref.at[pl.ds(pl.multiple_of(ROWS * s, ROWS), ROWS)]

    win_loads = [
        pltpu.make_async_copy(slot(win_in, s), slot(win, s), in_sem.at[s]) for s in range(5)
    ]
    for s in range(5):
        win_loads[s].start()
    loads = [
        pltpu.make_async_copy(src, dst, in_sem.at[5 + k])
        for k, (src, dst) in enumerate(
            ((w_in, w_first), (raw_in, raw), (hid_in, hid_t))
        )
    ]
    meet(across + tally.peers[0] + tally.peers[1] + tally.peers[2])
    fold_m = Fold(m_bufs, m_sems, True)
    fold_n = Fold(n_bufs, n_sems, False)
    fold_f = Fold(f_bufs, f_sems, False)
    my_rows = pl.ds(pl.multiple_of(TOK * y, TOK), TOK)
    attn[my_rows, :] = attn_low[...]
    spread = Spread(attn, g_send, g_recv)
    spread.start()
    fold_m.open([m0, m1])
    fold_n.open([m2])
    for load in loads:
        load.start()
    side_src[...] = jnp.zeros_like(side_src)
    for k in range(4):
        lanes = slice(COLS * k, COLS * (k + 1))
        side_src[k, 0:2, 0:COLS] = small[0:2, lanes]
        side_src[k, 2:3, 0:COLS] = small[4:5, lanes]

    def side(k):
        return remote(side_src.at[wrap(y + k)], side_got.at[k], v_send.at[k], v_recv.at[k], across[k - 1])

    for k in (1, 2, 3):
        side(k).start()
    loads[0].wait()

    def unproject(k):
        rows = pl.ds(pl.multiple_of(TOK * wrap(y + k), TOK), TOK)
        d_att[rows, :] = dot_nn(attn[rows, :], w_first[:, 0:384]).astype(BF16)

    unproject(0)
    fold_m.add(2)
    fold_n.add(2)
    spread.sides()
    fold_m.add(1)
    fold_n.add(1)
    unproject(1)
    unproject(3)
    fold_m.add(3)
    fold_n.add(3)
    spread.opposite()
    unproject(2)

    for h in range(HEADS):
        d_pad[h] = pad_head(d_att, (h + 1) // 2, (h + 1) % 2)
    wide = d_att[...].astype(F32).T[64:, :] * out_t[...]
    for h in range(HEADS):
        delta[h] = jnp.broadcast_to(
            jnp.sum(wide[64 * h : 64 * (h + 1), :], axis=0, keepdims=True), (8, ROWS)
        )
    q_acc[...] = jnp.zeros_like(q_acc)

    hand_one = remote(slot(d_win, 3 - 2 * c), sib_one, k_send.at[0], k_recv.at[0], sibling)
    hand_two = remote(slot(d_win, 1), sib_two, k_send.at[1], k_recv.at[1], sibling)
    hand_own = remote(slot(d_win, 3), sib_two, k_send.at[2], k_recv.at[2], sibling)
    one = remote(one_buf, got_one, k_send.at[3], k_recv.at[3], device(z, wrap(x + 3), c, y))
    part_a = remote(
        two_buf.at[pl.ds(0, UP)], got_part, k_send.at[4], k_recv.at[4], device(z, wrap(x - 1), c, y)
    )
    part_b = remote(
        two_buf.at[pl.ds(UP, ROWS - UP)],
        transit,
        k_send.at[5],
        k_recv.at[5],
        device(z, wrap(x + 1), c, y),
    )
    part_on = remote(transit, got_two, k_send.at[6], k_recv.at[6], device(z, wrap(x + 1), c, y))

    def tile(t):
        rows = pl.ds(pl.multiple_of(t * TILE, TILE), TILE)
        key_at = t * TILE + lax.broadcasted_iota(jnp.int32, (TILE, ROWS), 0)
        query_at = 4 * ROWS + lax.broadcasted_iota(jnp.int32, (TILE, ROWS), 1)
        allowed = (key_at >= starts[...]) & (key_at <= query_at)
        terms = [None] * 5
        for h in range(HEADS):
            kg, kh = key_place(h)
            vg, _ = value_place(h)
            keys = win[rows, 128 * kg : 128 * kg + 128]
            values = win[rows, 128 * vg : 128 * vg + 128]
            scores = dot_nt(keys, q_pad[h])
            probs = jnp.where(allowed, jnp.exp(scores - lse[h, 0:1, :]), 0.0)
            prob_grad = dot_nt(values, d_pad[h])
            score_grad = (probs * (prob_grad - delta[h, 0:1, :])).astype(BF16)
            v_term = dot_nn(probs.astype(BF16), d_pad[h])
            k_term = dot_nn(score_grad, q_pad[h])
            for at, term in ((kg, k_term), (vg, v_term)):
                terms[at] = term if terms[at] is None else terms[at] + term
            both = dot_tn(keys, score_grad)
            q_acc[h] += both[64 * kh : 64 * kh + 64, :]
        for g in range(5):
            d_win[rows, 128 * g : 128 * g + 128] = terms[g].astype(BF16)

    def after(k):
        if k == 0:

            @pl.when((c == 0) & (x > 1))
            def _():
                two_buf[...] = d_win[0:ROWS, :]
                part_b.start()
                part_a.start()

        if k == 1:

            @pl.when((c == 0) & (x > 1))
            def _():
                hand_two.start()

            @pl.when((c == 1) & (x > 0))
            def _():
                hand_one.start()

        if k == 2:

            @pl.when((c == 0) & (x > 0))
            def _():
                hand_one.start()

            @pl.when((c == 1) & (x > 1))
            def _():
                hand_two.wait_recv()
                two_buf[...] = (
                    d_win[0:ROWS, :].astype(F32) + sib_two[...].astype(F32)
                ).astype(BF16)
                part_b.start()
                part_a.start()

        if k == 3:

            @pl.when(x > 0)
            def _():
                hand_one.wait_recv()
                one_buf[...] = (
                    d_win[2 * ROWS : 3 * ROWS, :].astype(F32) + sib_one[...].astype(F32)
                ).astype(BF16)

                @pl.when(x < 3)
                def _():
                    part_a.wait_recv()
                    one_buf[0:UP, :] = (
                        one_buf[0:UP, :].astype(F32) + got_part[...].astype(F32)
                    ).astype(BF16)

                one.start()

            @pl.when(c == 1)
            def _():
                hand_own.start()

    for load in win_loads:
        load.wait()
    folds = {3: 0}

    def step(i, carry):
        k = lax.div(i, 2)
        s = jnp.where((c == 0) & (k == 2), 3, jnp.where((c == 0) & (k == 3), 2, k))

        @pl.when(place + s >= 4)
        def _():
            tile(2 * s + lax.rem(i, 2))

        for k in range(4):

            @pl.when(i == 2 * k + 1)
            def _(k=k):
                after(k)

        for n, d in folds.items():

            @pl.when(i == n)
            def _(d=d):
                fold_m.add(d)
                fold_n.add(d)

        @pl.when((i == 6) & ((x == 0) | (x == 3)))
        def _():
            part_b.wait_recv()
            part_on.start()

        @pl.when(i == 5)
        def _():
            fold_n.relay()
            fold_m.relay()

        return carry

    lax.fori_loop(0, 10, step, 0)
    for load in loads[1:]:
        load.wait()
    cosine, sine = rope_wide(cos_block, sin_block, turn)
    pack[:, 128:384] = jnp.zeros((ROWS, 256), BF16)
    gain_parts = []
    wide = jnp.concatenate([q_acc[h] for h in range(HEADS)] + [jnp.zeros((64, ROWS), F32)], axis=0)
    for g, at in enumerate((384, 512, 0)):
        grad = wide[128 * g : 128 * g + 128, :].T * math.sqrt(HEAD_DIM)
        term, gain_part = head_back(grad, raw[g], gains[:, 128 * g : 128 * g + 128], cosine, sine)
        if g == 2:
            term = jnp.where(half_mask(0), term, 0.0)
        pack[:, at : at + 128] = term.astype(BF16)
        gain_parts.append(gain_part)
    out_part[...] = dot_tn(attn[...], att[...])

    fold_n.cross()
    fold_m.cross()
    kv_sum[...] = d_win[4 * ROWS :, :].astype(F32)

    @pl.when(c == 0)
    def _():
        hand_own.wait_recv()
        kv_sum[...] += sib_two[...].astype(F32)

    @pl.when(x < 3)
    def _():
        one.wait_recv()
        kv_sum[...] += got_one[...].astype(F32)

    @pl.when(x < 2)
    def _():
        part_on.wait_recv()
        kv_sum[UP:, :] += got_two[...].astype(F32)

    for g in range(3):
        grad = kv_sum[:, 128 * g : 128 * g + 128]
        gain = gains[:, 128 * g : 128 * g + 128]
        term, gain_part = head_back(grad, raw[3 + g], gain, cosine, sine)
        if g == 2:
            term = jnp.where(half_mask(0), term, grad)
        at = 640 + 128 * g
        pack[:, at : at + 128] = term.astype(BF16)
        gain_parts[g] += gain_part
    pack[:, 1024:1280] = kv_sum[:, 384:640].astype(BF16)

    my_cols = pl.ds(pl.multiple_of(TOK * y, TOK), TOK)

    def project(to):
        rows = pl.ds(pl.multiple_of(COLS * to, 64), COLS)
        hidden_grad[...] = dot_nt(w_first[rows, :], pack[...])
        hidden_grad[:, my_cols] += res_t[rows, :]

    def grad_copy(k):
        return remote(y_send_buf.at[k - 1], y_got_buf.at[k - 1], y_send.at[k], y_recv.at[k], across[k - 1])

    extra = side_src[y]
    for k in (1, 2, 3):
        side(k).wait_recv()
        extra = extra + side_got[k]
    sums[...] = jnp.zeros_like(sums)
    sums[0:2, :] = small[2:4, :]
    sums[2:3, 0:384] = jnp.concatenate(gain_parts, axis=1)
    sums[3:6, 0:384] = extra[0:3, :]
    tally.start(0)

    def first_grad(k, carry):
        rows = pl.ds(pl.multiple_of(COLS * k, 64), COLS)
        grad = dot_nn(hid_t[rows, :], pack[...])
        low = grad[:, 0:384] + out_part[rows, :]
        for a in range(4):
            first_g[k, a, :, 0:384] = low[80 * a : 80 * a + 80].astype(BF16)
            first_g[k, a, :, 384:] = grad[80 * a : 80 * a + 80, 384:].astype(BF16)
        return carry

    lax.fori_loop(0, 4, first_grad, 0)
    fold_f.open([first_g])
    for k in (2, 1, 3):
        project(wrap(y + k))
        y_send_buf[k - 1] = hidden_grad[...].astype(BF16)
        grad_copy(k).start()

    tally.finish(0)
    tally.start(1)
    for d in (2, 1, 3):
        fold_f.add(d)
    project(y)
    fold_f.relay()
    fold_f.add(0)
    for k in (1, 2, 3):
        grad_copy(k).wait_recv()
        hidden_grad[...] += y_got_buf[k - 1].astype(F32)
    tally.finish(1)
    tally.start(2)
    fold_m.finish(m_out)
    fold_n.finish(n_out)
    fold_f.cross()
    fold_f.finish(f_out)
    tally.finish(2)
    fold_m.close(m_out)
    fold_n.close(n_out)
    fold_f.close(f_out)
    gate_g[...] = m_out[0]
    up_g[...] = m_out[1]
    down_g[...] = n_out[0]
    query_g[:, 0:256] = f_out[0, :, 384:640]
    query_g[:, 256:320] = f_out[0, :, 0:64]
    key_g[...] = f_out[0, :, 640:960]
    value_g[...] = f_out[0, :, 960:1280]
    out_g[...] = f_out[0, :, 64:384]
    sums_out[...] = t_accs[2]
    sums_out[6:7, :] = jnp.broadcast_to(count[0:1, 0:1], (1, D))
    for k in (1, 2, 3):
        grad_copy(k).wait_send()
        side(k).wait_send()
    spread.close()

    @pl.when(x > 0)
    def _():
        hand_one.wait_send()
        one.wait_send()

    @pl.when((x == 0) | (x == 3))
    def _():
        part_on.wait_send()

    @pl.when(x > 1)
    def _():
        part_a.wait_send()
        part_b.wait_send()

        @pl.when(c == 0)
        def _():
            hand_two.wait_send()

    @pl.when(c == 1)
    def _():
        hand_own.wait_send()

    tally.close()


def tail(vmem_args, placed_args):
    sds = jax.ShapeDtypeStruct
    block = VMEM((ROWS, 2 * COLS), BF16)
    shapes = [(COLS, ROWS)] + [(40, COLS)] * 4 + [(40, D)] * 3 + [(8, D)]
    return pl.pallas_call(
        tail_kernel,
        out_shape=tuple(sds(s, F32) for s in shapes),
        in_specs=[IN_VMEM] * len(vmem_args) + [IN_PLACE] * len(placed_args),
        out_specs=(IN_VMEM,) * len(shapes),
        scratch_shapes=[
            VMEM((5 * ROWS, 2 * COLS), BF16),
            VMEM((6, ROWS, 128), F32),
            VMEM((D, ROWS), BF16),
            VMEM((D, D), BF16),
            VMEM((ROWS, D), BF16),
            VMEM((ROWS, 384), BF16),
            VMEM((HEADS, ROWS, 128), BF16),
            VMEM((HEADS, 8, ROWS), F32),
            VMEM((HEADS, 64, ROWS), F32),
            VMEM((5 * ROWS, 2 * COLS), BF16),
        ]
        + [block] * 5
        + [
            VMEM((ROWS - UP, 2 * COLS), BF16),
            VMEM((UP, 2 * COLS), BF16),
            VMEM((ROWS - UP, 2 * COLS), BF16),
            VMEM((ROWS, 2 * COLS), F32),
            VMEM((ROWS, D), BF16),
            VMEM((D, 384), F32),
            VMEM((4, 4, 80, D), BF16),
            VMEM((3, COLS, ROWS), BF16),
            VMEM((3, COLS, ROWS), BF16),
            VMEM((4, 8, 384), F32),
            VMEM((4, 8, 384), F32),
            VMEM((8, D), F32),
            VMEM((2, 40, D), F32),
            VMEM((1, 40, D), F32),
            VMEM((1, 40, D), F32),
            DMA((9,)),
            DMA((7,)),
            DMA((7,)),
            DMA((4,)),
            DMA((4,)),
            DMA((4,)),
            DMA((4,)),
            DMA((4,)),
            DMA((4,)),
        ]
        + fold_scratch(2)
        + fold_scratch(1)
        + fold_scratch(1)
        + tally_scratch((8, D)),
        compiler_params=params(2),
        name="tail",
    )(*vmem_args, *placed_args)


def emit_kernel(sums, *refs):
    count = (len(refs) - 6) // 2
    for src, dst in zip(refs[:count], refs[count : 2 * count]):
        dst[...] = src[...]
    loss, attention, feedforward, score, up, gate = refs[2 * count :]
    loss[0] = jnp.sum(sums[5:6, 0:1] / sums[6:7, 0:1])
    score[...] = sums[2:3, 0:COLS].reshape(COLS)
    attention[...] = sums[3:4, 0:COLS].reshape(COLS)
    feedforward[...] = sums[4:5, 0:COLS].reshape(COLS)
    up[...] = sums[0:1, :].reshape(D)
    gate[...] = sums[1:2, :].reshape(D)


def emit(sums, arrays):
    sds = jax.ShapeDtypeStruct
    vectors = [sds((1,), F32)] + [sds((COLS,), F32)] * 3 + [sds((D,), F32)] * 2
    return pl.pallas_call(
        emit_kernel,
        out_shape=tuple(sds(a.shape, a.dtype) for a in arrays) + tuple(vectors),
        in_specs=[IN_VMEM] * (1 + len(arrays)),
        out_specs=(IN_VMEM,) * len(arrays) + (IN_SMEM,) + (IN_VMEM,) * 5,
        compiler_params=params(),
        name="emit",
    )(sums, *arrays)


def shards(
    hidden,
    teacher,
    valid_mask,
    segments,
    query_weight,
    key_weight,
    value_weight,
    out_weight,
    gate_weight,
    up_weight,
    down_weight,
    attention_rate,
    feedforward_rate,
    score_gain,
    up_gain,
    gate_gain,
):
    ropes = rope_constants()
    others = (query_weight, key_weight, value_weight, out_weight.T)
    others += (gate_weight, up_weight, down_weight.T)
    others += (attention_rate, feedforward_rate, valid_mask, segments, score_gain, *ropes)
    (
        hid_t,
        hid_tok,
        tea_tok,
        rates,
        count,
        mask,
        gains,
        weights,
        w_rest,
        raw,
        q_pad,
        win,
        att,
        out_t,
        lse,
        starts,
    ) = front(hidden.T, teacher.T, others)
    output, attn_low, res_t, small, *grads = middle(
        (
            att,
            hid_tok,
            tea_tok,
            mask,
            count,
            rates,
            up_gain,
            gate_gain,
        ),
        (weights, w_rest),
    )
    results = tail(
        (starts, q_pad, out_t, lse, attn_low, att, gains, *ropes, res_t, small, count),
        (win, raw, hid_t, weights) + tuple(g.reshape(4, 4, 80, D) for g in grads),
    )
    results = emit(results[8], (output,) + tuple(results[:8]))
    output, hidden_grad, query_g, key_g, value_g, out_g, gate_g, up_g, down_g = results[:9]
    return (
        results[9].reshape(()),
        output.T,
        hidden_grad.T,
        query_g,
        key_g,
        value_g,
        out_g.T,
        gate_g,
        up_g,
        down_g.T,
    ) + tuple(results[10:])


def solution(mesh):
    both = P(("dp", "row"), "col")
    turned = P("col", ("dp", "row"))
    vector = P("col")
    in_specs = (both, both, P(("dp", "row")), P("dp", None), both, both, both, turned, both, both)
    in_specs += (turned,) + (vector,) * 5
    out_specs = (P(), both, both, both, both, both, turned, both, both, turned) + (vector,) * 5
    return jax.shard_map(shards, mesh=mesh, in_specs=in_specs, out_specs=out_specs, check_vma=False)
```
